32 devices in a mesh: dp: 16 (over z, y, core), tensor: 2 (over x).
Axes of the slice: x: 2, y: 2, z: 4, core: 2. Of those that a mesh axis runs over, the one named last changes fastest.
Arguments:
- tokens: bfloat16 [16, 256, 2048], P('dp', 'tensor'), may hold values from -6 to 6
- segment_ids: int32 [16, 256], P('dp'), may hold values from 0 to 3, never falling along the last dimension, each value on 1 to 128 neighbouring positions
- norm_gain: float32 [2048], replicated, may hold values from 0.5 to 1.5
- w_query: bfloat16 [2048, 1536], P('dp', 'tensor'), may hold values from -0.125 to 0.125
- w_key: bfloat16 [2048, 1536], P('dp', 'tensor'), may hold values from -0.125 to 0.125
- w_value: bfloat16 [2048, 3072], P('dp', 'tensor'), may hold values from -0.125 to 0.125
- w_outgate: bfloat16 [2048, 3072], P('dp', 'tensor'), may hold values from -0.125 to 0.125
- w_beta: bfloat16 [2048, 12], P('dp', 'tensor'), may hold values from -0.125 to 0.125
- w_decay: bfloat16 [2048, 12], P('dp', 'tensor'), may hold values from -0.125 to 0.125
- conv_query: float32 [4, 1536], replicated, may hold values from -3 to 3
- conv_key: float32 [4, 1536], replicated, may hold values from -3 to 3
- conv_value: float32 [4, 3072], replicated, may hold values from -3 to 3
- decay_log: float32 [12], replicated, may hold values from -4 to 1.5
- decay_bias: float32 [12], replicated, may hold values from -4 to 0
- out_gain: float32 [256], replicated, may hold values from 0.5 to 1.5
- w_output: bfloat16 [3072, 2048], P('tensor', 'dp'), may hold values from -0.15625 to 0.15625
- mlp_gain: float32 [2048], replicated, may hold values from 0.5 to 1.5
- w_gate: bfloat16 [2048, 5632], P('dp', 'tensor'), may hold values from -0.125 to 0.125
- w_up: bfloat16 [2048, 5632], P('dp', 'tensor'), may hold values from -0.125 to 0.125
- w_down: bfloat16 [5632, 2048], P('tensor', 'dp'), may hold values from -0.109375 to 0.109375
- cotangent: bfloat16 [16, 256, 2048], P('dp', 'tensor'), may hold values from -6 to 6
Outputs:
- out_tokens: float32 [16, 256, 2048], P('dp', 'tensor')
- grad_tokens: float32 [16, 256, 2048], P('dp', 'tensor')
- grad_norm_gain: float32 [2048], replicated
- grad_w_query: float32 [2048, 1536], P('dp', 'tensor')
- grad_w_key: float32 [2048, 1536], P('dp', 'tensor')
- grad_w_value: float32 [2048, 3072], P('dp', 'tensor')
- grad_w_outgate: float32 [2048, 3072], P('dp', 'tensor')
- grad_w_beta: float32 [2048, 12], P('dp', 'tensor')
- grad_w_decay: float32 [2048, 12], P('dp', 'tensor')
- grad_conv_query: float32 [4, 1536], replicated
- grad_conv_key: float32 [4, 1536], replicated
- grad_conv_value: float32 [4, 3072], replicated
- grad_decay_log: float32 [12], replicated
- grad_decay_bias: float32 [12], replicated
- grad_out_gain: float32 [256], replicated
- grad_w_output: float32 [3072, 2048], P('tensor', 'dp')
- grad_mlp_gain: float32 [2048], replicated
- grad_w_gate: float32 [2048, 5632], P('dp', 'tensor')
- grad_w_up: float32 [2048, 5632], P('dp', 'tensor')
- grad_w_down: float32 [5632, 2048], P('tensor', 'dp')
The draws below stay inside these ranges and needn't reach their ends.
Inputs may be any that keep to these rules, and one draw needn't show every extreme that they name: `segment_ids`: along each sequence the document numbers never fall; one document spans at most 128 tokens.
All inputs are finite; a program needn't handle non-finite values.
Results may differ from the reference program's by a relative error of at most 0.01145.
Values may be sent and summed in bfloat16 or wider, within the bound.
A program may use at most 256 MiB of HBM per device.

```python
import math
import jax
import jax.numpy as jnp
import numpy as np
from jax import lax

D = 2048
HEADS = 12
VALUE_SIZE = 256
FF = 5632
STRETCH = 64
KEYW = 1536
VALW = 3072
LEN = 256
NSEQ = 16


def block_levels(key, extent, cuts, least, largest):
    gain, own = 1.0, jax.random.fold_in(key, 6)
    for axis_at, shards_of in cuts:
        draws = jnp.exp(jax.random.uniform(jax.random.fold_in(own, axis_at), (shards_of,), jnp.float32, least / len(cuts), largest / len(cuts)))
        gain = gain * jnp.repeat(draws, extent[axis_at] // shards_of).reshape([-1 if axis == axis_at else 1 for axis in range(len(extent))])
    return gain


def split_up(number_of, total, most, lean):
    weights = [(1 << 20) // math.isqrt(rank ** lean) + 1 for rank in range(2, number_of + 1)]
    spare, holding = total - most - (number_of - 1), [1] * (number_of - 1)
    while spare > 0:
        free = [i for i in range(number_of - 1) if holding[i] < most]
        pool, left = sum([weights[i] for i in free]), spare
        for i in free:
            more = min(most - holding[i], max(1, left * weights[i] // pool), spare)
            holding[i] = holding[i] + more
            spare = spare - more
    return np.array([most] + holding)


def ragged(key, number_of, total, bound, slope):
    if number_of == 2:
        one = jax.random.randint(key, (), max(1, total - bound), min(bound, total - 1) + 1)
        return jnp.stack([one, total - one])
    lengths = jnp.asarray(split_up(number_of, total, bound, slope), jnp.int32)
    twos = (number_of - 1) // 2
    source_of, taker = lengths[1:1 + 2 * twos:2], lengths[2:2 + 2 * twos:2]
    slack = jnp.minimum(source_of - 1, bound - taker)
    shifted = jax.random.randint(jax.random.fold_in(key, 1), (twos,), 0, 1 << 20) % (slack + 1)
    lengths = lengths.at[1:1 + 2 * twos:2].set(source_of - shifted).at[2:2 + 2 * twos:2].set(taker + shifted)
    return lengths[jax.random.permutation(jax.random.fold_in(key, 2), number_of)]


def centred(own_key, dims, scale, reach, cuts=(), kind=jnp.bfloat16):
    array = scale * jax.random.normal(own_key, dims, jnp.float32)
    if cuts:
        array = array * block_levels(own_key, dims, cuts, -0.22, 0.18)
    return jnp.clip(array, -reach, reach).astype(kind)


def setup_inputs(seed: int = 0) -> dict:
    key_list = jax.random.split(jax.random.key(seed), 22)
    return {
        "tokens": centred(key_list[0], (NSEQ, LEN, D), 1.0, 6.0, ((0, 16), (1, 2))),
        "segment_ids": jax.vmap(lambda own: jnp.searchsorted(jnp.cumsum(ragged(own, 4, LEN, LEN // 2, 2)), jnp.arange(LEN), side="right"))(jax.random.split(key_list[1], NSEQ)).reshape((NSEQ, LEN)).astype(jnp.int32),
        "norm_gain": jnp.clip(1.0 + 0.1 * jax.random.normal(key_list[2], (D,), jnp.float32), 0.5, 1.5),
        "w_query": centred(key_list[3], (D, KEYW), D ** -0.5, 0.125, ((0, 16), (1, 2))),
        "w_key": centred(key_list[4], (D, KEYW), D ** -0.5, 0.125, ((0, 16), (1, 2))),
        "w_value": centred(key_list[5], (D, VALW), D ** -0.5, 0.125, ((0, 16), (1, 2))),
        "w_outgate": centred(key_list[6], (D, VALW), D ** -0.5, 0.125, ((0, 16), (1, 2))),
        "w_beta": centred(key_list[7], (D, HEADS), D ** -0.5, 0.125, ((0, 16), (1, 2))),
        "w_decay": centred(key_list[8], (D, HEADS), D ** -0.5, 0.125, ((0, 16), (1, 2))),
        "conv_query": centred(key_list[9], (4, KEYW), 0.5, 3.0, (), jnp.float32),
        "conv_key": centred(key_list[10], (4, KEYW), 0.5, 3.0, (), jnp.float32),
        "conv_value": centred(key_list[11], (4, VALW), 0.5, 3.0, (), jnp.float32),
        "decay_log": jnp.clip(jax.random.uniform(key_list[12], (HEADS,), jnp.float32, -4.0, 1.5), -4.0, 1.5),
        "decay_bias": jnp.clip(jax.random.uniform(key_list[13], (HEADS,), jnp.float32, -4.0, 0.0), -4.0, 0.0),
        "out_gain": jnp.clip(1.0 + 0.1 * jax.random.normal(key_list[14], (VALUE_SIZE,), jnp.float32), 0.5, 1.5),
        "w_output": centred(key_list[15], (VALW, D), (VALW // 2) ** -0.5, 0.15625, ((0, 2), (1, 16))),
        "mlp_gain": jnp.clip(1.0 + 0.1 * jax.random.normal(key_list[16], (D,), jnp.float32), 0.5, 1.5),
        "w_gate": centred(key_list[17], (D, FF), D ** -0.5, 0.125, ((0, 16), (1, 2))),
        "w_up": centred(key_list[18], (D, FF), D ** -0.5, 0.125, ((0, 16), (1, 2))),
        "w_down": centred(key_list[19], (FF, D), (FF // 2) ** -0.5, 0.109375, ((0, 2), (1, 16))),
        "cotangent": centred(key_list[20], (NSEQ, LEN, D), 1.0, 6.0, ((0, 16), (1, 2))),
    }


@jax.custom_vjp
def low(v):
    return lax.optimization_barrier(v.astype(jnp.bfloat16)).astype(jnp.float32)

@jax.custom_vjp
def low_back(v):
    return v

def low_keep(v):
    return (low(v), None)

def low_pass(kept, grad):
    return (grad,)

def back_keep(v):
    return (v, None)

def back_low(kept, grad):
    return (low(grad),)
low.defvjp(low_keep, low_pass)
low_back.defvjp(back_keep, back_low)
HIGHEST = lax.Precision.HIGHEST

def scale_rows(values, factor):
    return values * lax.rsqrt(lax.optimization_barrier(jnp.mean(values * values, axis=-1, keepdims=True)) + 1e-06) * factor

def short_conv(inputs, kernel, segments):
    total = inputs * kernel[0]
    for offset in range(1, kernel.shape[0]):
        moved = jnp.pad(inputs, ((0, 0), (offset, 0), (0, 0)))[:, :-offset]
        moved_ids = jnp.pad(segments, ((0, 0), (offset, 0)), constant_values=-1)[:, :-offset]
        keeping = (moved_ids == segments).astype(jnp.float32)[..., None]
        total = total + kernel[offset] * moved * keeping
    return jax.nn.silu(total)

def unit_heads(values, heads):
    batch, length, width = values.shape
    values = values.reshape(batch, length, heads, width // heads)
    return values * lax.rsqrt(lax.optimization_barrier(jnp.sum(values * values, axis=-1, keepdims=True)) + 1e-06)

def stretch_step(state, block):
    queries, keys, values, betas, cumulative, same_doc, carried = block
    size = queries.shape[2]
    row_ids = lax.broadcasted_iota(jnp.int32, (size, size), 0)
    col_ids = lax.broadcasted_iota(jnp.int32, (size, size), 1)
    lower = (col_ids <= row_ids).astype(jnp.float32)
    strict = (col_ids < row_ids).astype(jnp.float32)
    masking = same_doc[:, None] * lower
    spread = cumulative[..., :, None] - cumulative[..., None, :]
    decays = jnp.exp(spread * masking) * masking
    key_key = jnp.einsum('bhid,bhjd->bhij', keys, keys, precision=HIGHEST)
    query_key = jnp.einsum('bhid,bhjd->bhij', queries, keys, precision=HIGHEST)
    mix_keys = decays * key_key * betas[..., None, :] * strict
    mix_query = decays * query_key * betas[..., None, :]
    identity = jnp.eye(size, dtype=jnp.float32)
    starting = carried[:, None, :] * jnp.exp(cumulative)
    stacked = jnp.concatenate([values, starting[..., None] * keys], axis=-1)
    solved = lax.linalg.triangular_solve(identity + mix_keys, stacked, left_side=True, lower=True)
    value_width = values.shape[-1]
    errors = solved[..., :value_width] - jnp.einsum('bhik,bhkv->bhiv', solved[..., value_width:], state, precision=HIGHEST)
    outputs = starting[..., None] * jnp.einsum('bhik,bhkv->bhiv', queries, state, precision=HIGHEST)
    outputs = outputs + jnp.einsum('bhij,bhjv->bhiv', mix_query, errors, precision=HIGHEST)
    closing = decays[..., size - 1, :] * betas
    new_state = starting[..., size - 1][..., None, None] * state
    new_state = new_state + jnp.einsum('bhjk,bhjv->bhkv', keys * closing[..., None], errors, precision=HIGHEST)
    return (new_state, outputs)

def delta_mixer(query_pre, key_pre, value_pre, beta_pre, decay_pre, outgate_pre, conv_query, conv_key, conv_value, decay_log, decay_bias, out_gain, segments, heads):
    batch, length, _ = query_pre.shape
    key_size = query_pre.shape[-1] // heads
    value_size = value_pre.shape[-1] // heads
    queries = unit_heads(short_conv(query_pre, conv_query, segments), heads) * (1.0 / math.sqrt(key_size))
    keys = unit_heads(short_conv(key_pre, conv_key, segments), heads)
    values = short_conv(value_pre, conv_value, segments).reshape(batch, length, heads, value_size)
    betas = jax.nn.sigmoid(beta_pre)
    rates = -jnp.exp(decay_log) * jax.nn.softplus(decay_pre + decay_bias)
    blocks = length // STRETCH

    def split(tensor):
        return tensor.reshape(batch, blocks, STRETCH, heads, -1).transpose(1, 0, 3, 2, 4)
    cumulative = jnp.cumsum(rates.reshape(batch, blocks, STRETCH, heads), axis=2).transpose(1, 0, 3, 2)
    beta_blocks = betas.reshape(batch, blocks, STRETCH, heads).transpose(1, 0, 3, 2)
    id_blocks = segments.reshape(batch, blocks, STRETCH)
    same_doc = (id_blocks[..., :, None] == id_blocks[..., None, :]).astype(jnp.float32).transpose(1, 0, 2, 3)
    previous = jnp.concatenate([jnp.full((batch, 1), -1, jnp.int32), id_blocks[:, :-1, STRETCH - 1]], axis=1)
    carried = (id_blocks == previous[..., None]).astype(jnp.float32).transpose(1, 0, 2)
    initial = jnp.zeros((batch, heads, key_size, value_size), jnp.float32)
    _, outputs = lax.scan(jax.checkpoint(stretch_step), initial, (split(queries), split(keys), split(values), beta_blocks, cumulative, same_doc, carried))
    raw = outputs.transpose(1, 0, 3, 2, 4).reshape(batch, length, heads, value_size)
    raw = raw * lax.rsqrt(lax.optimization_barrier(jnp.mean(raw * raw, axis=-1, keepdims=True)) + 1e-05) * out_gain
    return raw.reshape(batch, length, heads * value_size) * jax.nn.silu(outgate_pre)

def project(rows, weight):
    return jnp.einsum('bld,de->ble', rows, weight, precision=HIGHEST)

def layer(stream, segments, params):
    norm_gain, w_query, w_key, w_value, w_outgate, w_beta, w_decay, conv_query, conv_key, conv_value, decay_log, decay_bias, out_gain, w_output, mlp_gain, w_gate, w_up, w_down = params
    normed = low(scale_rows(stream, norm_gain))
    query_pre = low_back(project(normed, w_query))
    key_pre = low_back(project(normed, w_key))
    value_pre = low_back(project(normed, w_value))
    outgate_pre = low_back(project(normed, w_outgate))
    beta_pre = low_back(project(normed, w_beta))
    decay_pre = low_back(project(normed, w_decay))
    heads_out = low(delta_mixer(query_pre, key_pre, value_pre, beta_pre, decay_pre, outgate_pre, conv_query, conv_key, conv_value, decay_log, decay_bias, out_gain, segments, HEADS))
    mixed = low_back(project(heads_out, w_output))
    middle = stream + mixed
    normed_mlp = low(scale_rows(middle, mlp_gain))
    gate = low_back(project(normed_mlp, w_gate))
    upper = low_back(project(normed_mlp, w_up))
    hidden = low(jax.nn.silu(gate) * upper)
    return middle + low_back(project(hidden, w_down))

def reference(tokens, segment_ids, norm_gain, w_query, w_key, w_value, w_outgate, w_beta, w_decay, conv_query, conv_key, conv_value, decay_log, decay_bias, out_gain, w_output, mlp_gain, w_gate, w_up, w_down, cotangent):
    params = tuple((p.astype(jnp.float32) for p in (norm_gain, w_query, w_key, w_value, w_outgate, w_beta, w_decay, conv_query, conv_key, conv_value, decay_log, decay_bias, out_gain, w_output, mlp_gain, w_gate, w_up, w_down)))
    streams = tokens.astype(jnp.float32).reshape(NSEQ // 8, 8, LEN, D)
    id_groups = segment_ids.reshape(NSEQ // 8, 8, LEN)
    incoming = cotangent.astype(jnp.float32).reshape(NSEQ // 8, 8, LEN, D)

    def group_step(totals, pieces):
        stream, segments, upstream = pieces
        result, pullback = jax.vjp(lambda values, weights: layer(values, segments, weights), stream, params)
        grad_stream, grad_params = pullback(upstream)
        return (jax.tree.map(lambda a, b: a + b, totals, grad_params), (result, grad_stream))
    zeros = jax.tree.map(jnp.zeros_like, params)
    totals, (results, grads) = lax.scan(group_step, zeros, (streams, id_groups, incoming))
    return (results.reshape(NSEQ, LEN, D), grads.reshape(NSEQ, LEN, D), totals[0], totals[1], totals[2], totals[3], totals[4], totals[5], totals[6], totals[7], totals[8], totals[9], totals[10], totals[11], totals[12], totals[13], totals[14], totals[15], totals[16], totals[17])
```

```python
from functools import partial
import math

import jax
import jax.numpy as jnp
from jax import lax
from jax.sharding import PartitionSpec as P

HIGH = lax.Precision.HIGH
HIGHEST = lax.Precision.HIGHEST
BF = jnp.bfloat16
F32 = jnp.float32


def scale_rows(values, factor):
    return values * lax.rsqrt(jnp.mean(values * values, axis=-1, keepdims=True) + 1e-06) * factor


def short_conv(inputs, kernel, keeping):
    total = inputs * kernel[0]
    for offset in range(1, kernel.shape[0]):
        moved = jnp.pad(inputs, ((offset, 0), (0, 0)))[:-offset]
        total = total + kernel[offset] * moved * keeping[offset]
    return jax.nn.silu(total)


def unit_heads(values, heads):
    length, width = values.shape
    values = values.reshape(length, heads, width // heads)
    return values * lax.rsqrt(jnp.sum(values * values, axis=-1, keepdims=True) + 1e-06)


def inverse_of(mixing):
    size = mixing.shape[-1]
    row = lax.broadcasted_iota(jnp.int32, (size, size), 0)
    col = lax.broadcasted_iota(jnp.int32, (size, size), 1)
    result = jnp.where(row == col, 1.0, 0.0) - jnp.where((row // 2) == (col // 2), mixing, 0.0)
    span = 2
    while span < size:
        picked = ((row // (2 * span)) == (col // (2 * span))) & ((row // span) != (col // span))
        part = jnp.where(picked, mixing, 0.0)
        half = jnp.einsum("hij,hjk->hik", result, part, precision=HIGH)
        result = result - jnp.einsum("hij,hjk->hik", half, result, precision=HIGH)
        span *= 2
    return result


@jax.custom_vjp
def solve(mixing, values):
    return solve_keep(mixing, values)[0]


def solve_keep(mixing, values):
    inverse = inverse_of(mixing)
    errors = jnp.einsum("hij,hjv->hiv", inverse, values, precision=HIGH)
    return errors, (inverse, errors)


def solve_back(kept, grad):
    inverse, errors = kept
    grad_values = jnp.einsum("hij,hiv->hjv", inverse, grad, precision=HIGH)
    return -jnp.einsum("hiv,hjv->hij", grad_values, errors, precision=HIGH), grad_values


solve.defvjp(solve_keep, solve_back)


def delta_mixer(
    query_pre,
    key_pre,
    value_pre,
    beta_pre,
    decay_pre,
    outgate_pre,
    conv_query,
    conv_key,
    conv_value,
    decay_log,
    decay_bias,
    out_gain,
    segments,
    heads,
):
    length = query_pre.shape[0]
    key_size = query_pre.shape[1] // heads
    value_size = value_pre.shape[1] // heads
    keeping = [None]
    for offset in range(1, conv_query.shape[0]):
        moved_ids = jnp.pad(segments, (offset, 0), constant_values=-1)[:-offset]
        keeping.append((moved_ids == segments).astype(F32)[:, None])
    queries = unit_heads(short_conv(query_pre, conv_query, keeping), heads) * (
        1.0 / math.sqrt(key_size)
    )
    keys = unit_heads(short_conv(key_pre, conv_key, keeping), heads)
    values = short_conv(value_pre, conv_value, keeping).reshape(length, heads, value_size)
    betas = jax.nn.sigmoid(beta_pre).T
    rates = -jnp.exp(decay_log) * jax.nn.softplus(decay_pre + decay_bias)
    row = lax.broadcasted_iota(jnp.int32, (length, length), 0)
    col = lax.broadcasted_iota(jnp.int32, (length, length), 1)
    same = segments[:, None] == segments[None, :]
    masking = (same & (col <= row)).astype(F32)
    strict = (col < row).astype(F32)
    cumulative = jnp.einsum("ij,jh->hi", masking, rates, precision=HIGHEST)
    spread = cumulative[:, :, None] - cumulative[:, None, :]
    decays = jnp.exp(spread * masking) * masking * betas[:, None, :]
    key_key = jnp.einsum("ihd,jhd->hij", keys, keys, precision=HIGH)
    query_key = jnp.einsum("ihd,jhd->hij", queries, keys, precision=HIGH)
    errors = solve(decays * key_key * strict, values.transpose(1, 0, 2))
    raw = jnp.einsum("hij,hjv->ihv", decays * query_key, errors, precision=HIGH)
    raw = raw * lax.rsqrt(jnp.mean(raw * raw, axis=-1, keepdims=True) + 1e-05) * out_gain
    return raw.reshape(length, heads * value_size) * jax.nn.silu(outgate_pre)


def rows_product(left, right):
    return lax.dot_general(left, right, (((0,), (0,)), ((), ())), preferred_element_type=F32)


def cols_product(left, right):
    return lax.dot_general(left, right, (((1,), (1,)), ((), ())), preferred_element_type=F32)


def dot(left, right):
    return jnp.dot(left, right, preferred_element_type=F32)


class Ring:
    def __init__(self, devices):
        self.devices = devices
        self.line = devices // 4
        self.me = lax.axis_index("dp")

    def swap(self, value, offset):
        pairs = [(at, at ^ offset) for at in range(self.devices)]
        return lax.ppermute(value, "dp", pairs)

    def offset(self, place):
        return (place % self.line) * 4 + ((place // self.line) % 2) * 2 + place // (2 * self.line)

    def place(self, offset):
        return (offset & 1) * (2 * self.line) + ((offset >> 1) & 1) * self.line + (offset >> 2)

    def into(self, value):
        width = value.shape[-1] // self.devices
        blocks = [
            lax.dynamic_slice_in_dim(value, (self.me ^ self.offset(p)) * width, width, -1)
            for p in range(self.devices)
        ]
        return jnp.concatenate(blocks, axis=-1)

    def out_of(self, value):
        width = value.shape[-1] // self.devices
        blocks = [
            lax.dynamic_slice_in_dim(value, self.place(self.me ^ j) * width, width, -1)
            for j in range(self.devices)
        ]
        return jnp.concatenate(blocks, axis=-1)

    def gather(self, shard, after):
        shard, _ = lax.optimization_barrier((shard, after))
        line = [shard] + [self.swap(shard, 4 * k) for k in range(1, self.line)]
        pair = line + [self.swap(piece, 2) for piece in line]
        return jnp.concatenate(pair + [self.swap(piece, 1) for piece in pair], axis=0), line[1:]

    def scatter(self, left, right):
        half = left.shape[1] // 2
        sent = rows_product(left[:, half:], right).astype(BF)
        kept = rows_product(left[:, :half], right)
        kept = kept + self.swap(sent, 1).astype(F32)
        half //= 2
        kept = kept[:half] + self.swap(kept[half:].astype(BF), 2).astype(F32)
        rows = half // self.line
        total = kept[:rows]
        for k in range(1, self.line):
            total = total + self.swap(kept[k * rows : (k + 1) * rows].astype(BF), 4 * k).astype(F32)
        return total

    def total(self, value):
        step = 1
        while step < self.devices:
            value = value + self.swap(value, step)
            step *= 2
        return value


def other(value):
    return lax.ppermute(value, "tensor", [(0, 1), (1, 0)])


def both_rows(own, member):
    peer = other(own)
    first = member == 0
    return jnp.concatenate([jnp.where(first, own, peer), jnp.where(first, peer, own)], axis=0)


def own_rows(value, member, dtype):
    half = value.shape[0] // 2
    mine = lax.dynamic_slice_in_dim(value, member * half, half, 0)
    theirs = lax.dynamic_slice_in_dim(value, (1 - member) * half, half, 0)
    return mine + other(theirs.astype(dtype)).astype(F32)


def per_device(
    tokens,
    segment_ids,
    norm_gain,
    w_query,
    w_key,
    w_value,
    w_outgate,
    w_beta,
    w_decay,
    conv_query,
    conv_key,
    conv_value,
    decay_log,
    decay_bias,
    out_gain,
    w_output,
    mlp_gain,
    w_gate,
    w_up,
    w_down,
    cotangent,
    *,
    devices,
):
    member = lax.axis_index("tensor")
    ring = Ring(devices)
    heads = w_beta.shape[1]
    keyw = w_query.shape[1]
    valw = w_value.shape[1]
    stream = ring.into(tokens[0]).astype(F32)
    cot_own = ring.into(cotangent[0])
    norm_gain = ring.into(norm_gain)
    mlp_gain = ring.into(mlp_gain)

    spare = (-2 * heads) % 128
    first = jnp.concatenate(
        [w_query, w_key, w_beta, w_decay, jnp.zeros((w_beta.shape[0], spare), BF)], axis=1
    )
    second = jnp.concatenate([w_value, w_outgate], axis=1)

    normed, norm_back = jax.vjp(scale_rows, stream, norm_gain)
    rows_mix = both_rows(normed.astype(BF), member)
    cot_rows = both_rows(cot_own, member)

    wqk, token = ring.gather(first, ())
    wvg, token = ring.gather(second, token)
    wout, token = ring.gather(w_output.T, token)
    gate_full, token = ring.gather(w_gate, token)
    up_full, token = ring.gather(w_up, token)
    down_full, token = ring.gather(w_down.T, token)

    pre_qk = dot(rows_mix, wqk)
    pre_vg = dot(rows_mix, wvg)
    own_cq = lax.dynamic_slice_in_dim(conv_query, member * keyw, keyw, 1)
    own_ck = lax.dynamic_slice_in_dim(conv_key, member * keyw, keyw, 1)
    own_cv = lax.dynamic_slice_in_dim(conv_value, member * valw, valw, 1)
    own_log = lax.dynamic_slice_in_dim(decay_log, member * heads, heads, 0)
    own_bias = lax.dynamic_slice_in_dim(decay_bias, member * heads, heads, 0)

    def mixer_local(qk, vg, cq, ck, cv, log_part, bias_part, gain_part):
        at = 2 * keyw
        return delta_mixer(
            qk[:, :keyw],
            qk[:, keyw:at],
            vg[:, :valw],
            qk[:, at : at + heads],
            qk[:, at + heads : at + 2 * heads],
            vg[:, valw:],
            cq,
            ck,
            cv,
            log_part,
            bias_part,
            gain_part,
            segment_ids[0],
            heads,
        )

    heads_raw, mixer_back = jax.vjp(
        mixer_local, pre_qk, pre_vg, own_cq, own_ck, own_cv, own_log, own_bias, out_gain
    )
    heads_out = heads_raw.astype(BF)
    mixed_own = own_rows(cols_product(heads_out, wout), member, F32)
    middle = stream + mixed_own
    normed_mlp, mlp_norm_back = jax.vjp(scale_rows, middle, mlp_gain)
    rows_mlp = both_rows(normed_mlp.astype(BF), member)
    gate = dot(rows_mlp, gate_full)
    upper = dot(rows_mlp, up_full)
    sigmoid_gate = jax.nn.sigmoid(gate)
    hidden = (gate * sigmoid_gate * upper).astype(BF)
    grad_wdown = ring.scatter(cot_rows, hidden).T
    ff_own = own_rows(cols_product(hidden, down_full), member, BF)
    out_tokens = ring.out_of(middle + ff_own)[None]
    grad_hidden = dot(cot_rows, down_full)
    grad_gate = (grad_hidden * upper * sigmoid_gate * (1.0 + gate * (1.0 - sigmoid_gate))).astype(BF)
    grad_upper = (grad_hidden * gate * sigmoid_gate).astype(BF)
    grad_wgate = ring.scatter(rows_mlp, grad_gate)
    grad_wup = ring.scatter(rows_mlp, grad_upper)
    back_part = cols_product(grad_gate, gate_full) + cols_product(grad_upper, up_full)
    middle_norm_grad, grad_mlp_gain = mlp_norm_back(own_rows(back_part, member, F32))
    grad_middle = cot_own.astype(F32) + middle_norm_grad
    grad_mixed = both_rows(grad_middle.astype(BF), member)
    grad_wout = ring.scatter(grad_mixed, heads_out).T
    grad_qk, grad_vg, *core_grads = mixer_back(dot(grad_mixed, wout))
    grad_qk = grad_qk.astype(BF)
    grad_vg = grad_vg.astype(BF)
    grad_wvg = ring.scatter(rows_mix, grad_vg)
    grad_wqk = ring.scatter(rows_mix, grad_qk)
    back_mix = cols_product(grad_vg, wvg) + cols_product(grad_qk, wqk)
    stream_norm_grad, grad_norm_gain = norm_back(own_rows(back_mix, member, BF))
    grad_tokens = ring.out_of(grad_middle + stream_norm_grad)[None]

    grad_cq, grad_ck, grad_cv, grad_log, grad_bias, grad_gain = core_grads
    shared = jnp.concatenate([ring.out_of(grad_norm_gain), ring.out_of(grad_mlp_gain), grad_gain])
    halves = [grad_cq, grad_ck, grad_cv, grad_log, grad_bias]
    sizes = [piece.size for piece in halves]
    packed = jnp.concatenate([shared] + [piece.reshape(-1) for piece in halves])
    packed = jnp.pad(packed, (0, (-packed.size) % 1024)).reshape(-1, 128)
    packed = ring.total(packed).reshape(-1)
    peer = other(packed)
    shared = packed[: shared.size] + peer[: shared.size]
    wholes = []
    at = shared.size
    for piece, size in zip(halves, sizes):
        mine = packed[at : at + size].reshape(piece.shape)
        theirs = peer[at : at + size].reshape(piece.shape)
        low = jnp.where(member == 0, mine, theirs)
        high = jnp.where(member == 0, theirs, mine)
        wholes.append(jnp.concatenate([low, high], axis=-1))
        at += size
    width = norm_gain.shape[0]
    at = 2 * keyw
    return (
        out_tokens,
        grad_tokens,
        shared[:width],
        grad_wqk[:, :keyw],
        grad_wqk[:, keyw:at],
        grad_wvg[:, :valw],
        grad_wvg[:, valw:],
        grad_wqk[:, at : at + heads],
        grad_wqk[:, at + heads : at + 2 * heads],
        wholes[0],
        wholes[1],
        wholes[2],
        wholes[3],
        wholes[4],
        shared[2 * width :],
        grad_wout,
        shared[width : 2 * width],
        grad_wgate,
        grad_wup,
        grad_wdown,
    )


def solution(mesh):
    rows = P("dp", "tensor")
    cols = P("tensor", "dp")
    tokens = P("dp", "tensor", None)
    placed = (tokens, P("dp", None), P()) + (rows,) * 6 + (P(),) * 6
    placed = placed + (cols, P(), rows, rows, cols, tokens)
    given = (tokens, tokens, P()) + (rows,) * 6 + (P(),) * 6 + (cols, P(), rows, rows, cols)
    return jax.shard_map(
        partial(per_device, devices=mesh.shape["dp"]),
        mesh=mesh,
        in_specs=placed,
        out_specs=given,
        check_vma=False,
    )
```

```python
from functools import partial
import math

import jax
import jax.numpy as jnp
from jax import lax
from jax.experimental import pallas as pl
from jax.experimental.pallas import tpu as pltpu
from jax.sharding import PartitionSpec as P

HIGH = lax.Precision.HIGH
HIGHEST = lax.Precision.HIGHEST
BF = jnp.bfloat16
F32 = jnp.float32


def scale_rows(values, factor):
    return values * lax.rsqrt(jnp.mean(values * values, axis=-1, keepdims=True) + 1e-06) * factor


def short_conv(inputs, kernel, keeping):
    total = inputs * kernel[0]
    for offset in range(1, kernel.shape[0]):
        moved = jnp.pad(inputs, ((0, 0), (offset, 0), (0, 0)))[:, :-offset]
        total = total + kernel[offset] * moved * keeping[offset]
    return jax.nn.silu(total)


def unit_heads(values, heads):
    batch, length, width = values.shape
    values = values.reshape(batch, length, heads, width // heads)
    return values * lax.rsqrt(jnp.sum(values * values, axis=-1, keepdims=True) + 1e-06)


def inverse_of(mixing):
    size = mixing.shape[-1]
    row = lax.broadcasted_iota(jnp.int32, (size, size), 0)
    col = lax.broadcasted_iota(jnp.int32, (size, size), 1)
    result = jnp.where(row == col, 1.0, 0.0) - jnp.where((row // 2) == (col // 2), mixing, 0.0)
    span = 2
    while span < size:
        picked = ((row // (2 * span)) == (col // (2 * span))) & ((row // span) != (col // span))
        part = jnp.where(picked, mixing, 0.0)
        half = jnp.einsum("shij,shjk->shik", result, part, precision=HIGH)
        result = result - jnp.einsum("shij,shjk->shik", half, result, precision=HIGH)
        span *= 2
    return result


def solve_keep(mixing, values):
    inverse = inverse_of(mixing)
    errors = jnp.einsum("shij,shjv->shiv", inverse, values, precision=HIGH)
    return errors, (inverse, errors)


def solve_back(kept, grad):
    inverse, errors = kept
    grad_values = jnp.einsum("shij,shiv->shjv", inverse, grad, precision=HIGH)
    return -jnp.einsum("shiv,shjv->shij", grad_values, errors, precision=HIGH), grad_values


def mixer_inputs(qk, value_pre, cq, ck, cv, decay_log, decay_bias, segments, heads):
    batch, length = segments.shape
    qk = qk.reshape(batch, length, -1)
    keyw, valw = cq.shape[1], cv.shape[1]
    keeping = [None]
    for offset in range(1, cq.shape[0]):
        moved_ids = jnp.pad(segments, ((0, 0), (offset, 0)), constant_values=-1)[:, :-offset]
        keeping.append((moved_ids == segments).astype(F32)[..., None])
    queries = unit_heads(short_conv(qk[..., :keyw], cq, keeping), heads)
    queries = queries * (1.0 / math.sqrt(queries.shape[-1]))
    keys = unit_heads(short_conv(qk[..., keyw : 2 * keyw], ck, keeping), heads)
    values = short_conv(value_pre.reshape(batch, length, valw), cv, keeping)
    values = values.reshape(batch, length, heads, -1).transpose(0, 2, 1, 3)
    at = 2 * keyw
    betas = jax.nn.sigmoid(qk[..., at : at + heads]).transpose(0, 2, 1)
    decay_pre = qk[..., at + heads : at + 2 * heads]
    rates = -jnp.exp(decay_log) * jax.nn.softplus(decay_pre + decay_bias)
    row = lax.broadcasted_iota(jnp.int32, (length, length), 0)
    col = lax.broadcasted_iota(jnp.int32, (length, length), 1)
    same = segments[:, :, None] == segments[:, None, :]
    masking = (same & (col <= row)).astype(F32)
    strict = (col < row).astype(F32)
    cumulative = jnp.einsum("sij,sjh->shi", masking, rates, precision=HIGHEST)
    spread = cumulative[..., :, None] - cumulative[..., None, :]
    masking = masking[:, None]
    decays = jnp.exp(spread * masking) * masking * betas[:, :, None, :]
    key_key = jnp.einsum("sihd,sjhd->shij", keys, keys, precision=HIGH)
    query_key = jnp.einsum("sihd,sjhd->shij", queries, keys, precision=HIGH)
    return decays * key_key * strict, decays * query_key, values


def mixer_outputs(mixing, errors, outgate_pre, out_gain):
    raw = jnp.einsum("shij,shjv->sihv", mixing, errors, precision=HIGH)
    raw = raw * lax.rsqrt(jnp.mean(raw * raw, axis=-1, keepdims=True) + 1e-05) * out_gain
    return raw.reshape(outgate_pre.shape) * jax.nn.silu(outgate_pre)


def rows_product(left, right):
    return lax.dot_general(left, right, (((0,), (0,)), ((), ())), preferred_element_type=F32)


def cols_product(left, right):
    return lax.dot_general(left, right, (((1,), (1,)), ((), ())), preferred_element_type=F32)


def dot(left, right):
    return jnp.dot(left, right, preferred_element_type=F32)


def tied(value, after):
    return lax.optimization_barrier((value, after))[0]


def first_of(flag, own, peer, axis):
    return jnp.concatenate([jnp.where(flag, own, peer), jnp.where(flag, peer, own)], axis=axis)


def part_of(value, index, size, axis):
    return lax.dynamic_slice_in_dim(value, index * size, size, axis)


class Grid:
    def __init__(self, devices):
        self.devices = devices
        self.chips = devices // 2
        me = lax.axis_index("dp")
        self.core = me % 2
        self.spot = ring_spot(me // 2, self.chips)
        self.member = lax.axis_index("tensor")
        self.quarter = 2 * self.member + self.core

    def swap(self, value, offset):
        pairs = [(at, at ^ offset) for at in range(self.devices)]
        return lax.ppermute(value, "dp", pairs)

    def over_core(self, value):
        return self.swap(value, 1)

    def over_tensor(self, value):
        return lax.ppermute(value, "tensor", [(0, 1), (1, 0)])

    def shift(self, value, step):
        pairs = []
        for at in range(self.devices):
            spot = (ring_spot(at // 2, self.chips) + step) % self.chips
            pairs.append((at, 2 * ring_chip(spot, self.chips) + at % 2))
        return lax.ppermute(value, "dp", pairs)

    def into(self, value):
        width = value.shape[-1] // self.chips
        blocks = []
        for place in range(self.chips):
            chip = ring_chip((self.spot + place) % self.chips, self.chips)
            blocks.append(part_of(value, chip, width, -1))
        return jnp.concatenate(blocks, axis=-1)

    def out_of(self, value):
        width = value.shape[-1] // self.chips
        blocks = []
        for chip in range(self.chips):
            place = (ring_spot(chip, self.chips) - self.spot + self.chips) % self.chips
            blocks.append(part_of(value, place, width, -1))
        return jnp.concatenate(blocks, axis=-1)

    def gather_rows(self, own):
        whole = first_of(self.member == 0, own, self.over_tensor(own), 0)
        return jnp.concatenate([whole, self.over_core(whole)], axis=0)

    def scatter_rows(self, value):
        half = value.shape[0] // 2
        whole = value[:half] + self.over_core(value[half:])
        half //= 2
        theirs = part_of(whole, 1 - self.member, half, 0)
        peer = self.over_tensor(theirs.astype(BF)).astype(F32)
        return part_of(whole, self.member, half, 0) + peer

    def gather(self, chunk):
        half = self.chips // 2
        mid = chunk.shape[0] // 2
        rights, lefts = [chunk], [chunk]
        for _ in range(1, half):
            rights.append(self.shift(rights[-1], 1))
            lefts.append(self.shift(lefts[-1], -1))
        top, low = self.shift(rights[-1][:mid], 1), self.shift(lefts[-1][mid:], -1)
        hops = list(zip(rights, lefts))[1:] + [(top, low)]
        return hops, jnp.concatenate(lefts + [top, low] + rights[:0:-1], axis=0)

    def scatter(self, left, right, after):
        half = self.chips // 2
        width = left.shape[1] // self.chips

        def piece(place, lo=0, hi=width):
            at = (place % self.chips) * width
            return rows_product(left[:, at + lo : at + hi], right)

        mid = width // 2
        goes_right, goes_left = tied(
            (piece(half, 0, mid).astype(BF), piece(half, mid, width).astype(BF)), after
        )
        hops = []
        for place in range(half - 1, -1, -1):
            from_left = self.shift(goes_right, 1).astype(F32)
            from_right = self.shift(goes_left, -1).astype(F32)
            hops.append((from_left, from_right))
            if place == half - 1:
                from_left = jnp.pad(from_left, ((0, width - mid), (0, 0)))
                from_right = jnp.pad(from_right, ((mid, 0), (0, 0)))
            if place:
                goes_right = (piece(place) + from_left).astype(BF)
                goes_left = (piece(-place) + from_right).astype(BF)
        return piece(0) + from_left + from_right, hops

    def own_block(self, total):
        half = total.shape[0] // 2
        peer = self.over_core(part_of(total, 1 - self.core, half, 0))
        return part_of(total, self.core, half, 0), peer

    def join(self, own, peer):
        return first_of(self.core == 0, own, peer, 1)

    def total(self, value):
        step = 1
        while step < self.devices:
            value = value + self.swap(value, step)
            step *= 2
        return value + self.over_tensor(value)


def ring_spot(chip, chips):
    line, pair = chip // 2, chip % 2
    return line * (1 - pair) + (chips - 1 - line) * pair


def ring_chip(spot, chips):
    pair = spot // (chips // 2)
    return 2 * (spot * (1 - pair) + (chips - 1 - spot) * pair) + pair


def spread_kernel(chips, layout, ringed, *refs):
    count = len(layout)
    totals = 1 + max(out for out, _, _ in layout)
    sources, outs = refs[:count], refs[count : count + totals]
    near_sem, send_core, recv_core, send_right, recv_right, send_left, recv_left = refs[count + totals :]
    me, member = lax.axis_index("dp"), lax.axis_index("tensor")
    core, chip = me % 2, me // 2
    spot = ring_spot(chip, chips)
    right = (2 * ring_chip((spot + 1) % chips, chips) + core, member)
    left = (2 * ring_chip((spot + chips - 1) % chips, chips) + core, member)
    peer = (2 * chip + 1 - core, member)
    barrier = pltpu.get_barrier_semaphore()
    for device in (right, left, peer):
        pl.semaphore_signal(barrier, inc=1, device_id=device, device_id_type=pl.DeviceIdType.MESH)
    pl.semaphore_wait(barrier, 3)

    def home(out):
        return outs[out].at[0] if out < ringed else outs[out]

    near, far = [], []
    for i, (out, at, width) in enumerate(layout):
        rows = sources[i].shape[0]
        place = home(out).at[pl.ds(pl.multiple_of(core * rows, rows), rows), pl.ds(at, width)]
        mine = sources[i].at[:, pl.ds(pl.multiple_of(core * width, 128), width)]
        theirs = sources[i].at[:, pl.ds(pl.multiple_of((1 - core) * width, 128), width)]
        near.append(pltpu.make_async_copy(mine, place, near_sem.at[i]))
        far.append(
            pltpu.make_async_remote_copy(
                src_ref=theirs,
                dst_ref=place,
                send_sem=send_core.at[i],
                recv_sem=recv_core.at[i],
                device_id=peer,
                device_id_type=pl.DeviceIdType.MESH,
            )
        )
        far[-1].start()
        near[-1].start()

    def hop(out, step, way):
        last = step == chips // 2
        ref = outs[out]
        mid = ref.shape[1] // 2
        if way > 0:
            at, to, device, sends, receives = -(step - 1) % chips, chips - step, right, send_right, recv_right
            rows = pl.ds(0, mid)
        else:
            at, to, device, sends, receives = step - 1, step, left, send_left, recv_left
            rows = pl.ds(mid, mid)
        source, target = ref.at[at], ref.at[to]
        if last:
            source, target = source.at[rows], target.at[rows]
        return pltpu.make_async_remote_copy(
            src_ref=source,
            dst_ref=target,
            send_sem=sends.at[out, step - 1],
            recv_sem=receives.at[out, step - 1],
            device_id=device,
            device_id_type=pl.DeviceIdType.MESH,
        )

    started = []
    for step in range(1, chips // 2 + 1):
        for out in range(ringed):
            if step == 1:
                for i, item in enumerate(layout):
                    if item[0] == out:
                        near[i].wait()
                        far[i].wait()
            for way in (1, -1):
                if step > 1:
                    hop(out, step - 1, way).wait_recv()
                copy = hop(out, step, way)
                copy.start()
                started.append(copy)
    for i, item in enumerate(layout):
        if item[0] >= ringed:
            near[i].wait()
            far[i].wait()
    for out in range(ringed):
        for way in (1, -1):
            hop(out, chips // 2, way).wait_recv()
    for copy in started:
        copy.wait_send()


def spread(grid, groups, ringed):
    chips = grid.chips
    sources, layout, shapes = [], [], []
    for out, group in enumerate(groups):
        at = 0
        for shard in group:
            width = shard.shape[1] // 2
            layout.append((out, at, width))
            sources.append(shard)
            at += width
        rows = 2 * group[0].shape[0]
        shapes.append(jax.ShapeDtypeStruct(((chips,) if out < ringed else ()) + (rows, at), BF))
    dma = pltpu.SemaphoreType.DMA
    hops = (ringed, chips // 2)
    anywhere = pl.BlockSpec(memory_space=pl.ANY)
    return pl.pallas_call(
        partial(spread_kernel, chips, layout, ringed),
        out_shape=shapes,
        in_specs=[anywhere] * len(sources),
        out_specs=[anywhere] * len(shapes),
        scratch_shapes=[dma((len(sources),))] * 3 + [dma(hops)] * 4,
        compiler_params=pltpu.CompilerParams(collective_id=0, has_side_effects=True),
        name="spread",
    )(*sources)


def whole_rows(stack):
    return stack.reshape(-1, stack.shape[-1])


def per_device(
    tokens,
    segment_ids,
    norm_gain,
    w_query,
    w_key,
    w_value,
    w_outgate,
    w_beta,
    w_decay,
    conv_query,
    conv_key,
    conv_value,
    decay_log,
    decay_bias,
    out_gain,
    w_output,
    mlp_gain,
    w_gate,
    w_up,
    w_down,
    cotangent,
    *,
    devices,
):
    grid = Grid(devices)
    heads = w_beta.shape[1] // 2
    keyw = w_query.shape[1] // 2
    valw = w_value.shape[1] // 2
    ffw = w_gate.shape[1] // 2
    small = -(-2 * heads // 128) * 128

    filler = jnp.zeros((w_beta.shape[0], small - 2 * heads), BF)
    rates = []
    for at in (0, heads):
        rates += [w_beta[:, at : at + heads], w_decay[:, at : at + heads], filler]
    rates = jnp.concatenate(rates, axis=1)
    groups = [[w_query, w_key, rates], [w_value, w_outgate], [w_output.T], [w_gate, w_up], [w_down.T]]
    wqk, wvg, wout, gate_up_chunk, down_chunk = spread(grid, groups, 3)
    wqk, wvg, wout = whole_rows(wqk), whole_rows(wvg), whole_rows(wout)

    stream = grid.into(tokens[0]).astype(F32)
    norm_gain = grid.into(norm_gain)
    mlp_gain = grid.into(mlp_gain)
    normed, norm_back = jax.vjp(scale_rows, stream, norm_gain)
    rows_mix = grid.gather_rows(normed.astype(BF))
    segments = jnp.concatenate([segment_ids, grid.over_core(segment_ids)], axis=0)

    hops, gate_up = grid.gather(gate_up_chunk)
    down_hops, down_full = grid.gather(tied(down_chunk, hops[-1]))

    conv_parts = [
        part_of(conv_query, grid.quarter, keyw, 1),
        part_of(conv_key, grid.quarter, keyw, 1),
        part_of(conv_value, grid.quarter, valw, 1),
        part_of(decay_log, grid.quarter, heads, 0),
        part_of(decay_bias, grid.quarter, heads, 0),
    ]
    pre_qk = dot(rows_mix, wqk)
    pre_vg = dot(rows_mix, wvg)
    (mixing, reading, values), inputs_back = jax.vjp(
        partial(mixer_inputs, segments=segments, heads=heads), pre_qk, pre_vg[:, :valw], *conv_parts
    )
    mixing = tied(mixing, hops[0])
    errors, kept = solve_keep(mixing, values)
    errors = tied(errors, hops[1])
    heads_raw, outputs_back = jax.vjp(mixer_outputs, reading, errors, pre_vg[:, valw:], out_gain)
    heads_out = heads_raw.astype(BF)
    middle = stream + tied(grid.scatter_rows(cols_product(heads_out, wout)), hops[2:3])
    normed_mlp, mlp_norm_back = jax.vjp(scale_rows, middle, mlp_gain)
    rows_mlp = grid.gather_rows(normed_mlp.astype(BF))
    cot_own = grid.into(cotangent[0])
    cot_rows = grid.gather_rows(tied(cot_own, normed_mlp))
    both = dot(rows_mlp, gate_up)
    gate, upper = both[:, :ffw], both[:, ffw:]
    sigmoid_gate = jax.nn.sigmoid(gate)
    hidden = (gate * sigmoid_gate * upper).astype(BF)
    grad_down, sent = grid.scatter(cot_rows, hidden, down_hops[-1])
    grad_hidden = dot(cot_rows, down_full)
    grad_gate = (grad_hidden * upper * sigmoid_gate * (1.0 + gate * (1.0 - sigmoid_gate))).astype(BF)
    grad_upper = (grad_hidden * gate * sigmoid_gate).astype(BF)
    grad_both = jnp.concatenate([grad_gate, grad_upper], axis=1)
    back_part = cols_product(grad_both, gate_up)
    middle_norm_grad, grad_mlp_gain = mlp_norm_back(grid.scatter_rows(back_part))
    grad_gate_up, sent = grid.scatter(rows_mlp, grad_both, sent[-1])
    grad_middle = cot_own.astype(F32) + middle_norm_grad
    grad_mixed = grid.gather_rows(grad_middle.astype(BF))
    ff_own = grid.scatter_rows(tied(cols_product(hidden, down_full), grad_mixed))
    out_tokens = grid.out_of(middle + ff_own)[None]
    grad_heads = tied(dot(grad_mixed, wout), (ff_own, sent[0]))
    grad_reading, grad_errors, grad_g, grad_gain = outputs_back(grad_heads)
    grad_mixing, grad_values = solve_back(kept, tied(grad_errors, sent[1]))
    grad_mixing = tied(grad_mixing, sent[2:3])
    grad_qk, grad_v, *core_grads = inputs_back((grad_mixing, grad_reading, grad_values))
    grad_wout, sent = grid.scatter(grad_mixed, heads_out, sent[-1])
    grad_qk = grad_qk.astype(BF)
    grad_vg = jnp.concatenate([grad_v, grad_g], axis=1).astype(BF)
    grad_wvg, sent = grid.scatter(rows_mix, grad_vg, sent[-1])
    grad_wqk, sent = grid.scatter(rows_mix, grad_qk, sent[-1])
    back_mix = cols_product(grad_vg, wvg) + cols_product(grad_qk, wqk)
    stream_norm_grad, grad_norm_gain = norm_back(grid.scatter_rows(back_mix))
    grad_tokens = grid.out_of(grad_middle + stream_norm_grad)[None]

    def placed(piece, whole):
        start = grid.quarter * piece.shape[-1]
        return lax.dynamic_update_slice_in_dim(jnp.zeros(whole.shape, F32), piece, start, -1)

    wholes = (conv_query, conv_key, conv_value, decay_log, decay_bias)
    pieces = [grid.out_of(grad_norm_gain), grid.out_of(grad_mlp_gain), grad_gain]
    pieces += [placed(piece, whole) for piece, whole in zip(core_grads, wholes)]
    packed = jnp.concatenate([piece.reshape(-1) for piece in pieces])
    packed = jnp.pad(packed, (0, (-packed.size) % 1024)).reshape(-1, 128)
    packed = grid.total(packed).reshape(-1)
    sums = []
    at = 0
    for piece in pieces:
        sums.append(packed[at : at + piece.size].reshape(piece.shape))
        at += piece.size

    def columns(total, *widths):
        own, peer = grid.own_block(total)
        parts = []
        at = 0
        for width in widths:
            parts.append(grid.join(own[:, at : at + width], peer[:, at : at + width]))
            at += width
        return parts

    (whole_down,) = columns(grad_down, ffw)
    whole_gate, whole_up = columns(grad_gate_up, ffw, ffw)
    (whole_out,) = columns(grad_wout, valw)
    whole_value, whole_outgate = columns(grad_wvg, valw, valw)
    whole_query, whole_key, whole_beta, whole_decay = columns(grad_wqk, keyw, keyw, heads, heads)
    return (
        out_tokens,
        grad_tokens,
        sums[0],
        whole_query,
        whole_key,
        whole_value,
        whole_outgate,
        whole_beta,
        whole_decay,
        sums[3],
        sums[4],
        sums[5],
        sums[6],
        sums[7],
        sums[2],
        whole_out.T,
        sums[1],
        whole_gate,
        whole_up,
        whole_down.T,
    )


def solution(mesh):
    rows = P("dp", "tensor")
    cols = P("tensor", "dp")
    tokens = P("dp", "tensor", None)
    placed = (tokens, P("dp", None), P()) + (rows,) * 6 + (P(),) * 6
    placed = placed + (cols, P(), rows, rows, cols, tokens)
    given = (tokens, tokens, P()) + (rows,) * 6 + (P(),) * 6 + (cols, P(), rows, rows, cols)
    return jax.shard_map(
        partial(per_device, devices=mesh.shape["dp"]),
        mesh=mesh,
        in_specs=placed,
        out_specs=given,
        check_vma=False,
    )
```

```python
from functools import partial
import math

import jax
import jax.numpy as jnp
from jax import lax
from jax.experimental import pallas as pl
from jax.experimental.pallas import tpu as pltpu
from jax.sharding import PartitionSpec as P

HIGH = lax.Precision.HIGH
HIGHEST = lax.Precision.HIGHEST
BF = jnp.bfloat16
F32 = jnp.float32


def scale_rows(values, factor):
    return values * lax.rsqrt(jnp.mean(values * values, axis=-1, keepdims=True) + 1e-06) * factor


def split3(value):
    high = value.astype(BF)
    return high, (value - high.astype(F32)).astype(BF)


def product(left, right, dims):
    dims = (dims, ((), ()))
    total = lax.dot_general(left[0], right[0], dims, preferred_element_type=F32)
    total = total + lax.dot_general(left[0], right[1], dims, preferred_element_type=F32)
    return total + lax.dot_general(left[1], right[0], dims, preferred_element_type=F32)


ROWS_COLS = ((1,), (0,))
ROWS_ROWS = ((1,), (1,))
COLS_ROWS = ((0,), (0,))


def exact_sum(mask, value, dims):
    high, low = split3(value)
    last = (value - high.astype(F32) - low.astype(F32)).astype(BF)
    dims = (dims, ((), ()))
    total = lax.dot_general(mask, last, dims, preferred_element_type=F32)
    total = total + lax.dot_general(mask, low, dims, preferred_element_type=F32)
    return total + lax.dot_general(mask, high, dims, preferred_element_type=F32)


def conv_parts(values, taps, keeping):
    moved = [values] + [pltpu.roll(values, j, 0) * keeping[j] for j in range(1, 4)]
    total = moved[0] * taps[0:1]
    for j in range(1, 4):
        total = total + moved[j] * taps[j : j + 1]
    return moved, total


def conv_back(grad, moved, taps, keeping):
    rows = grad.shape[0]
    total = grad * taps[0:1]
    for j in range(1, 4):
        total = total + pltpu.roll(grad * keeping[j], rows - j, 0) * taps[j : j + 1]
    parts = [jnp.sum(grad * moved[j], axis=0, keepdims=True) for j in range(4)]
    return total, jnp.concatenate(parts, axis=0)


def silu_back(total, gate):
    return gate * (1.0 + total * (1.0 - gate))


def softplus(value):
    return jnp.maximum(value, 0.0) + jnp.log1p(jnp.exp(-jnp.abs(value)))


def block_masks(seg_col, seg_row):
    size = seg_col.shape[0]
    row = lax.broadcasted_iota(jnp.int32, (size, size), 0)
    col = lax.broadcasted_iota(jnp.int32, (size, size), 1)
    masking = ((seg_col == seg_row) & (col <= row)).astype(F32)
    spot = lax.broadcasted_iota(jnp.int32, (size, 1), 0)
    keeping = [None]
    for j in range(1, 4):
        keeping.append(((pltpu.roll(seg_col, j, 0) == seg_col) & (spot >= j)).astype(F32))
    return row, col, masking, keeping


def head_rates(small, log, bias, masking, heads):
    decay_in = pltpu.roll(small, small.shape[1] - heads, 1) + bias
    factor = -jnp.exp(log)
    rates = factor * softplus(decay_in)
    betas = jax.nn.sigmoid(small)
    summed = exact_sum(masking.astype(BF), rates, ROWS_COLS)
    return decay_in, factor, rates, betas, summed


def invert(mixing, row, col):
    size = mixing.shape[0]
    result = jnp.where(row == col, 1.0, 0.0) - jnp.where((row >> 1) == (col >> 1), mixing, 0.0)
    level = 1
    while (1 << level) < size:
        picked = ((row >> (level + 1)) == (col >> (level + 1))) & ((row >> level) != (col >> level))
        part = split3(jnp.where(picked, mixing, 0.0))
        halves = split3(result)
        step = product(halves, part, ROWS_COLS)
        result = result - product(split3(step), halves, ROWS_COLS)
        level += 1
    return result


def unit(values):
    return lax.rsqrt(jnp.sum(values * values, axis=1, keepdims=True) + 1e-06)


def mixer_kernel(heads, qk, vg, seg_col, seg_row, cq, ck, cv, log, bias, gain, *outs):
    heads_out, inverses, all_errors, all_kk, all_qk, all_raw = outs
    keyw, valw = cq.shape[1] // heads, cv.shape[1] // heads
    row, col, masking, keeping = block_masks(seg_col[0], seg_row[0])
    small = qk[:, 2 * heads * keyw :]
    _, _, _, betas, summed = head_rates(small, log[...], bias[...], masking, heads)
    betas_t, summed_t = betas.T, summed.T
    strict = (col < row).astype(F32)
    for h in range(heads):
        at = pl.ds(h * keyw, keyw)
        query = jax.nn.silu(conv_parts(qk[:, at], cq[:, at], keeping)[1])
        query = query * (unit(query) * (1.0 / math.sqrt(keyw)))
        key = jax.nn.silu(
            conv_parts(qk[:, pl.ds((heads + h) * keyw, keyw)], ck[:, at], keeping)[1]
        )
        key = key * unit(key)
        at = pl.ds(h * valw, valw)
        value = jax.nn.silu(conv_parts(vg[:, at], cv[:, at], keeping)[1])
        spread = summed[:, h : h + 1] - summed_t[h : h + 1]
        decays = jnp.exp(spread * masking) * masking * betas_t[h : h + 1]
        keys = split3(key)
        key_key = product(keys, keys, ROWS_ROWS)
        query_key = product(split3(query), keys, ROWS_ROWS)
        inverse = invert(decays * key_key * strict, row, col)
        errors = product(split3(inverse), split3(value), ROWS_COLS)
        raw = product(split3(decays * query_key), split3(errors), ROWS_COLS)
        inverses[0, h] = inverse
        all_errors[0, h] = errors
        all_kk[0, h] = key_key
        all_qk[0, h] = query_key
        all_raw[:, at] = raw
        scaled = raw * lax.rsqrt(jnp.mean(raw * raw, axis=1, keepdims=True) + 1e-05) * gain[...]
        gate = vg[:, pl.ds((heads + h) * valw, valw)]
        heads_out[:, at] = (scaled * jax.nn.silu(gate)).astype(BF)


def mixer_back_kernel(heads, grad, qk, vg, seg_col, seg_row, cq, ck, cv, log, bias, gain, *refs):
    inverses, all_errors, all_kk, all_qk, all_raw = refs[:5]
    grad_qk, grad_vg, grad_cq, grad_ck, grad_cv, grad_rate, grad_gain = refs[5:]
    keyw, valw = cq.shape[1] // heads, cv.shape[1] // heads
    size = qk.shape[0]

    @pl.when(pl.program_id(0) == 0)
    def _():
        for ref in (grad_cq, grad_ck, grad_cv, grad_rate, grad_gain):
            ref[...] = jnp.zeros_like(ref)

    row, col, masking, keeping = block_masks(seg_col[0], seg_row[0])
    small = qk[:, 2 * heads * keyw :]
    decay_in, factor, rates, betas, summed = head_rates(small, log[...], bias[...], masking, heads)
    betas_t, summed_t = betas.T, summed.T
    strict = (col < row).astype(F32)
    lanes = lax.broadcasted_iota(jnp.int32, (1, small.shape[1]), 1)
    spots = lax.broadcasted_iota(jnp.int32, (small.shape[1], 1), 0)
    grad_summed = jnp.zeros_like(small)
    from_cols = jnp.zeros((small.shape[1], size), F32)
    for h in range(heads):
        at = pl.ds(h * valw, valw)
        raw, gate_in = all_raw[:, at], vg[:, pl.ds((heads + h) * valw, valw)]
        gate = jax.nn.sigmoid(gate_in)
        scale = lax.rsqrt(jnp.mean(raw * raw, axis=1, keepdims=True) + 1e-05)
        above = grad[:, at]
        grad_vg[:, pl.ds((heads + h) * valw, valw)] = (
            above * (raw * scale * gain[...]) * silu_back(gate_in, gate)
        ).astype(BF)
        above = above * (gate_in * gate)
        grad_gain[...] += jnp.sum(above * raw * scale, axis=0, keepdims=True)
        above = above * gain[...]
        grad_raw = scale * (above - raw * (scale * scale * jnp.mean(above * raw, axis=1, keepdims=True)))

        spread = summed[:, h : h + 1] - summed_t[h : h + 1]
        plain = jnp.exp(spread * masking) * masking
        decays = plain * betas_t[h : h + 1]
        key_key, query_key = all_kk[0, h] * strict, all_qk[0, h]
        grad_raws, errors = split3(grad_raw), split3(all_errors[0, h])
        grad_reading = product(grad_raws, errors, ROWS_ROWS)
        grad_errors = product(split3(decays * query_key), grad_raws, COLS_ROWS)
        grad_value = product(split3(inverses[0, h]), split3(grad_errors), COLS_ROWS)
        grad_mixing = -product(split3(grad_value), errors, ROWS_ROWS)
        both = (grad_mixing * key_key + grad_reading * query_key) * plain
        grad_beta = jnp.sum(both, axis=0, keepdims=True)
        both = both * betas_t[h : h + 1]
        from_rows = jnp.sum(both, axis=1, keepdims=True)
        grad_summed = grad_summed + jnp.where(lanes == heads + h, from_rows, 0.0)
        from_cols = from_cols + jnp.where(spots == h, grad_beta, 0.0)
        from_cols = from_cols - jnp.where(spots == heads + h, jnp.sum(both, axis=0, keepdims=True), 0.0)

        at = pl.ds(h * keyw, keyw)
        query_moved, query_total = conv_parts(qk[:, at], cq[:, at], keeping)
        query_gate = jax.nn.sigmoid(query_total)
        query = query_total * query_gate
        query_scale = unit(query)
        query = query * query_scale
        key_at = pl.ds((heads + h) * keyw, keyw)
        key_moved, key_total = conv_parts(qk[:, key_at], ck[:, at], keeping)
        key_gate = jax.nn.sigmoid(key_total)
        key = key_total * key_gate
        key_scale = unit(key)
        key = key * key_scale
        keys = split3(key)
        grad_kk = split3(grad_mixing * decays * strict)
        grad_qk_product = split3(grad_reading * (decays * (1.0 / math.sqrt(keyw))))
        grad_query = product(grad_qk_product, keys, ROWS_COLS)
        grad_key = product(grad_qk_product, split3(query), COLS_ROWS)
        grad_key = grad_key + product(grad_kk, keys, ROWS_COLS) + product(grad_kk, keys, COLS_ROWS)

        grad_query = query_scale * (grad_query - query * jnp.sum(grad_query * query, axis=1, keepdims=True))
        grad_query = grad_query * silu_back(query_total, query_gate)
        grad_query, taps = conv_back(grad_query, query_moved, cq[:, at], keeping)
        grad_qk[:, at] = grad_query.astype(BF)
        grad_cq[:, at] += taps
        grad_key = key_scale * (grad_key - key * jnp.sum(grad_key * key, axis=1, keepdims=True))
        grad_key = grad_key * silu_back(key_total, key_gate)
        grad_key, taps = conv_back(grad_key, key_moved, ck[:, at], keeping)
        grad_qk[:, key_at] = grad_key.astype(BF)
        grad_ck[:, at] += taps

        at = pl.ds(h * valw, valw)
        moved, total = conv_parts(vg[:, at], cv[:, at], keeping)
        grad_value = grad_value * silu_back(total, jax.nn.sigmoid(total))
        grad_value, taps = conv_back(grad_value, moved, cv[:, at], keeping)
        grad_vg[:, at] = grad_value.astype(BF)
        grad_cv[:, at] += taps

    from_cols = from_cols.T
    grad_summed = grad_summed + jnp.where(lanes >= heads, from_cols, 0.0)
    grad_rates = exact_sum(masking.astype(BF), grad_summed, COLS_ROWS)
    decay_lanes = (lanes >= heads) & (lanes < 2 * heads)
    shifted = [pltpu.roll(value, heads, 1) for value in (decay_in, rates)]
    grad_decay = grad_rates * pltpu.roll(factor, heads, 1) * jax.nn.sigmoid(shifted[0])
    grad_rate[0:1] += jnp.sum(grad_rates * shifted[1], axis=0, keepdims=True)
    grad_rate[1:2] += jnp.sum(grad_decay, axis=0, keepdims=True)
    grad_small = jnp.where(decay_lanes, grad_decay, from_cols * betas * (1.0 - betas))
    grad_small = jnp.where(lanes < 2 * heads, grad_small, 0.0)
    grad_qk[:, 2 * heads * keyw :] = grad_small.astype(BF)


def mixer_specs(heads, qk, vg, cq, cv, small):
    length = qk.shape[0] // 2

    def by_rows(width):
        return pl.BlockSpec((length, width), lambda s: (s, 0))

    def fixed(*shape):
        return pl.BlockSpec(shape, lambda s: (0,) * len(shape))

    shared = [
        by_rows(qk.shape[1]),
        by_rows(vg.shape[1]),
        pl.BlockSpec((1, length, 1), lambda s: (s, 0, 0)),
        pl.BlockSpec((1, 1, length), lambda s: (s, 0, 0)),
        fixed(*cq.shape),
        fixed(*cq.shape),
        fixed(*cv.shape),
        fixed(1, small),
        fixed(1, small),
        fixed(1, cv.shape[1] // heads),
    ]
    valw = cv.shape[1] // heads
    square = (heads, length, length)
    kept = [square, (heads, length, valw), square, square]
    kept_specs = [pl.BlockSpec((1,) + shape, lambda s: (s, 0, 0, 0)) for shape in kept]
    kept_specs.append(by_rows(cv.shape[1]))
    kept_shapes = [jax.ShapeDtypeStruct((2,) + shape, F32) for shape in kept]
    kept_shapes.append(jax.ShapeDtypeStruct((2 * length, cv.shape[1]), F32))
    return by_rows, fixed, shared, kept_specs, kept_shapes


def mixer(heads, inputs):
    qk, vg, _, _, cq, _, cv, log, _, _ = inputs
    by_rows, _, shared, kept_specs, kept_shapes = mixer_specs(heads, qk, vg, cq, cv, log.shape[1])
    heads_out, *kept = pl.pallas_call(
        partial(mixer_kernel, heads),
        grid=(2,),
        out_shape=[jax.ShapeDtypeStruct((qk.shape[0], cv.shape[1]), BF)] + kept_shapes,
        in_specs=shared,
        out_specs=[by_rows(cv.shape[1])] + kept_specs,
        compiler_params=pltpu.CompilerParams(vmem_limit_bytes=48 << 20),
        name="mixer",
    )(*inputs)
    return heads_out, kept


def mixer_back(heads, grad, inputs, kept):
    qk, vg, _, _, cq, _, cv, log, _, gain = inputs
    by_rows, fixed, shared, kept_specs, _ = mixer_specs(heads, qk, vg, cq, cv, log.shape[1])
    sums = [cq.shape, cq.shape, cv.shape, (2, log.shape[1]), gain.shape]
    return pl.pallas_call(
        partial(mixer_back_kernel, heads),
        grid=(2,),
        out_shape=[jax.ShapeDtypeStruct(qk.shape, BF), jax.ShapeDtypeStruct(vg.shape, BF)]
        + [jax.ShapeDtypeStruct(shape, F32) for shape in sums],
        in_specs=[by_rows(cv.shape[1])] + shared + kept_specs,
        out_specs=[by_rows(qk.shape[1]), by_rows(vg.shape[1])] + [fixed(*shape) for shape in sums],
        compiler_params=pltpu.CompilerParams(vmem_limit_bytes=48 << 20),
        name="mixer_back",
    )(grad, *inputs, *kept)


def rows_product(left, right):
    return lax.dot_general(left, right, (((0,), (0,)), ((), ())), preferred_element_type=F32)


def cols_product(left, right):
    return lax.dot_general(left, right, (((1,), (1,)), ((), ())), preferred_element_type=F32)


def dot(left, right):
    return jnp.dot(left, right, preferred_element_type=F32)


def tied(value, after):
    return lax.optimization_barrier((value, after))[0]


def first_of(flag, own, peer, axis):
    return jnp.concatenate([jnp.where(flag, own, peer), jnp.where(flag, peer, own)], axis=axis)


def part_of(value, index, size, axis):
    return lax.dynamic_slice_in_dim(value, index * size, size, axis)


class Grid:
    def __init__(self, devices):
        self.devices = devices
        self.chips = devices // 2
        me = lax.axis_index("dp")
        self.core = me % 2
        self.spot = ring_spot(me // 2, self.chips)
        self.member = lax.axis_index("tensor")
        self.quarter = 2 * self.member + self.core

    def swap(self, value, offset):
        pairs = [(at, at ^ offset) for at in range(self.devices)]
        return lax.ppermute(value, "dp", pairs)

    def over_core(self, value):
        return self.swap(value, 1)

    def over_tensor(self, value):
        return lax.ppermute(value, "tensor", [(0, 1), (1, 0)])

    def shift(self, value, step):
        pairs = []
        for at in range(self.devices):
            spot = (ring_spot(at // 2, self.chips) + step) % self.chips
            pairs.append((at, 2 * ring_chip(spot, self.chips) + at % 2))
        return lax.ppermute(value, "dp", pairs)

    def into(self, value):
        width = value.shape[-1] // self.chips
        blocks = []
        for place in range(self.chips):
            chip = ring_chip((self.spot + place) % self.chips, self.chips)
            blocks.append(part_of(value, chip, width, -1))
        return jnp.concatenate(blocks, axis=-1)

    def out_of(self, value):
        width = value.shape[-1] // self.chips
        blocks = []
        for chip in range(self.chips):
            place = (ring_spot(chip, self.chips) - self.spot + self.chips) % self.chips
            blocks.append(part_of(value, place, width, -1))
        return jnp.concatenate(blocks, axis=-1)

    def gather_rows(self, own):
        whole = first_of(self.member == 0, own, self.over_tensor(own), 0)
        return jnp.concatenate([whole, self.over_core(whole)], axis=0)

    def scatter_rows(self, value):
        half = value.shape[0] // 2
        whole = value[:half] + self.over_core(value[half:])
        half //= 2
        theirs = part_of(whole, 1 - self.member, half, 0)
        peer = self.over_tensor(theirs.astype(BF)).astype(F32)
        return part_of(whole, self.member, half, 0) + peer

    def gather(self, chunk, gates):
        half = self.chips // 2
        mid = chunk.shape[0] // 2
        rights, lefts = [chunk], [chunk]
        for step in range(1, half):
            pair = tied((rights[-1], lefts[-1]), gates[step - 1 : step])
            rights.append(self.shift(pair[0], 1))
            lefts.append(self.shift(pair[1], -1))
        top, low = self.shift(rights[-1][:mid], 1), self.shift(lefts[-1][mid:], -1)
        return jnp.concatenate(lefts + [top, low] + rights[:0:-1], axis=0)

    def scatter(self, pairs, after):
        half = self.chips // 2
        width = pairs[0][0].shape[1] // self.chips

        def piece(place, lo=0, hi=width):
            at = (place % self.chips) * width
            parts = [rows_product(left[:, at + lo : at + hi], right) for left, right in pairs]
            return jnp.concatenate(parts, axis=1)

        mid = width // 2
        goes_right, goes_left = tied(
            (piece(half, 0, mid).astype(BF), piece(half, mid, width).astype(BF)), after
        )
        hops = []
        for place in range(half - 1, -1, -1):
            from_left, from_right = self.shift(goes_right, 1), self.shift(goes_left, -1)
            hops.append((from_left, from_right))
            from_left, from_right = from_left.astype(F32), from_right.astype(F32)
            if place == half - 1:
                from_left = jnp.pad(from_left, ((0, width - mid), (0, 0)))
                from_right = jnp.pad(from_right, ((mid, 0), (0, 0)))
            if place:
                goes_right = (piece(place) + from_left).astype(BF)
                goes_left = (piece(-place) + from_right).astype(BF)
        return piece(0) + from_left + from_right, hops

    def own_block(self, total):
        half = total.shape[0] // 2
        peer = self.over_core(part_of(total, 1 - self.core, half, 0))
        return part_of(total, self.core, half, 0), peer

    def join(self, own, peer):
        return first_of(self.core == 0, own, peer, 1)

    def total(self, value):
        step = 1
        while step < self.devices:
            value = value + self.swap(value, step)
            step *= 2
        return value + self.over_tensor(value)


def ring_spot(chip, chips):
    line, pair = chip // 2, chip % 2
    return line * (1 - pair) + (chips - 1 - line) * pair


def ring_chip(spot, chips):
    pair = spot // (chips // 2)
    return 2 * (spot * (1 - pair) + (chips - 1 - spot) * pair) + pair


def signal_all(devices):
    barrier = pltpu.get_barrier_semaphore()
    for device in devices:
        pl.semaphore_signal(barrier, inc=1, device_id=device, device_id_type=pl.DeviceIdType.MESH)
    pl.semaphore_wait(barrier, len(devices))


def send(source, target, send_sem, recv_sem, device):
    return pltpu.make_async_remote_copy(
        src_ref=source,
        dst_ref=target,
        send_sem=send_sem,
        recv_sem=recv_sem,
        device_id=device,
        device_id_type=pl.DeviceIdType.MESH,
    )


def spread_kernel(chips, layout, ringed, *refs):
    count = len(layout)
    totals = 1 + max(out for out, _, _ in layout)
    sources, (tokens, cot, gain) = refs[:count], refs[count : count + 3]
    outs = refs[count + 3 : count + 3 + totals]
    stream, cot_own, rows_mix, rows_cot = refs[count + 3 + totals : count + 7 + totals]
    normed, near_sem, send_core, recv_core, send_right, recv_right, send_left, recv_left = refs[
        count + 7 + totals : count + 15 + totals
    ]
    own_sem, send_half, recv_half, send_whole, recv_whole = refs[count + 15 + totals :]
    me, member = lax.axis_index("dp"), lax.axis_index("tensor")
    core, chip = me % 2, me // 2
    spot = ring_spot(chip, chips)
    right = (2 * ring_chip((spot + 1) % chips, chips) + core, member)
    left = (2 * ring_chip((spot + chips - 1) % chips, chips) + core, member)
    peer = (2 * chip + 1 - core, member)
    across = (me, 1 - member)
    signal_all((right, left, peer, across))

    def home(out):
        return outs[out].at[0] if out < ringed else outs[out]

    near, far = [], []
    for i, (out, at, width) in enumerate(layout):
        rows = sources[i].shape[0]
        place = home(out).at[pl.ds(pl.multiple_of(core * rows, rows), rows), pl.ds(at, width)]
        mine = sources[i].at[:, pl.ds(pl.multiple_of(core * width, 128), width)]
        theirs = sources[i].at[:, pl.ds(pl.multiple_of((1 - core) * width, 128), width)]
        near.append(pltpu.make_async_copy(mine, place, near_sem.at[i]))
        far.append(send(theirs, place, send_core.at[i], recv_core.at[i], peer))
        far[-1].start()
        near[-1].start()

    def hop(out, step, way):
        last = step == chips // 2
        ref = outs[out]
        mid = ref.shape[1] // 2
        if way > 0:
            at, to, device, sends, receives = -(step - 1) % chips, chips - step, right, send_right, recv_right
            rows = pl.ds(0, mid)
        else:
            at, to, device, sends, receives = step - 1, step, left, send_left, recv_left
            rows = pl.ds(mid, mid)
        source, target = ref.at[at], ref.at[to]
        if last:
            source, target = source.at[rows], target.at[rows]
        return send(source, target, sends.at[out, step - 1], receives.at[out, step - 1], device)

    started, own = [], []
    pairs = ((normed, rows_mix), (cot_own, rows_cot))
    halves = [
        send(value, rows.at[0, member], send_half.at[i], recv_half.at[i], across)
        for i, (value, rows) in enumerate(pairs)
    ]
    wholes = [
        send(rows.at[0], rows.at[1], send_whole.at[i], recv_whole.at[i], peer)
        for i, (_, rows) in enumerate(pairs)
    ]
    for step in range(1, chips // 2 + 1):
        for out in range(ringed):
            if step == 1:
                for i, item in enumerate(layout):
                    if item[0] == out:
                        near[i].wait()
                        far[i].wait()
            for way in (1, -1):
                if step > 1:
                    hop(out, step - 1, way).wait_recv()
                copy = hop(out, step, way)
                copy.start()
                started.append(copy)
        if step == 1:
            width = tokens.shape[1] // chips
            aligned = width % 128 == 0
            squares = jnp.zeros((tokens.shape[0], 1), F32)
            for place in range(chips):
                to = pl.ds(place * width, width)
                at = to
                if aligned:
                    at = ring_chip((spot + place) % chips, chips) * width
                    at = pl.ds(pl.multiple_of(at, 128), width)
                stream[:, to] = tokens[:, at]
                cot_own[:, to] = cot[:, at]
                block = stream[:, to].astype(F32)
                squares = squares + jnp.sum(block * block, axis=1, keepdims=True)
            scale = lax.rsqrt(squares / tokens.shape[1] + 1e-06)
            normed[...] = (stream[...].astype(F32) * scale * gain[...]).astype(BF)
            for i, (value, rows) in enumerate(pairs):
                own.append(pltpu.make_async_copy(value, rows.at[0, member], own_sem.at[i]))
                own[-1].start()
                halves[i].start()
        if step == 2:
            for i in range(2):
                own[i].wait()
                halves[i].wait()
                wholes[i].start()
    for i, item in enumerate(layout):
        if item[0] >= ringed:
            near[i].wait()
            far[i].wait()
    for copy in wholes:
        copy.wait()
    for out in range(ringed):
        for way in (1, -1):
            hop(out, chips // 2, way).wait_recv()
    for copy in started:
        copy.wait_send()


def spread(grid, groups, ringed, tokens, cot, gain):
    chips = grid.chips
    sources, layout, shapes = [], [], []
    for out, group in enumerate(groups):
        at = 0
        for shard in group:
            width = shard.shape[1] // 2
            layout.append((out, at, width))
            sources.append(shard)
            at += width
        rows = 2 * group[0].shape[0]
        shapes.append(jax.ShapeDtypeStruct(((chips,) if out < ringed else ()) + (rows, at), BF))
    dma = pltpu.SemaphoreType.DMA
    hops = (ringed, chips // 2)
    anywhere = pl.BlockSpec(memory_space=pltpu.HBM)
    near = pl.BlockSpec(memory_space=pltpu.VMEM)
    own = jax.ShapeDtypeStruct(tokens.shape, BF)
    rows = jax.ShapeDtypeStruct((2, 2) + tokens.shape, BF)
    return pl.pallas_call(
        partial(spread_kernel, chips, layout, ringed),
        out_shape=shapes + [own, own, rows, rows],
        in_specs=[anywhere] * len(sources) + [near] * 3,
        out_specs=[anywhere] * len(shapes) + [near] * 2 + [anywhere] * 2,
        scratch_shapes=[pltpu.VMEM(tokens.shape, BF)]
        + [dma((len(sources),))] * 3
        + [dma(hops)] * 4
        + [dma((2,))] * 5,
        compiler_params=pltpu.CompilerParams(
            collective_id=0, has_side_effects=True, vmem_limit_bytes=32 << 20
        ),
        name="spread",
    )(*sources, tokens, cot, gain)


PARTS = 2


def trade_kernel(compute, extras, results, *refs):
    part, inputs = refs[0], refs[1 : 1 + extras]
    rows_out, outputs = refs[1 + extras], refs[2 + extras : 2 + extras + results]
    got_core, sent_half, got_half, own = refs[2 + extras + results : 6 + extras + results]
    sems = refs[6 + extras + results :]
    me, member = lax.axis_index("dp"), lax.axis_index("tensor")
    peer = (me + 1 - 2 * (me % 2), member)
    across = (me, 1 - member)
    signal_all((peer, across))
    count = part.shape[2] // PARTS

    def chunk(k):
        return pl.ds(k * count, count)

    def copy(kind, k, source, target, device):
        return send(source, target, sems[2 * kind].at[k], sems[2 * kind + 1].at[k], device)

    first = [copy(0, k, part.at[1, :, chunk(k)], got_core.at[:, chunk(k)], peer) for k in range(PARTS)]
    second = [copy(1, k, sent_half.at[chunk(k)], got_half.at[chunk(k)], across) for k in range(PARTS)]
    third = [
        copy(2, k, own.at[chunk(k)], rows_out.at[0, member, chunk(k)], across) for k in range(PARTS)
    ]
    fourth = [
        copy(3, k, own.at[chunk(k)], rows_out.at[1, member, chunk(k)], peer) for k in range(PARTS)
    ]
    fifth = [
        copy(4, k, rows_out.at[0, 1 - member, chunk(k)], rows_out.at[1, 1 - member, chunk(k)], peer)
        for k in range(PARTS)
    ]
    for k in range(PARTS):
        first[k].start()
    for k in range(PARTS):
        first[k].wait_recv()
        total = part[0, 1 - member, chunk(k)] + got_core[1 - member, chunk(k)]
        sent_half[chunk(k)] = total.astype(BF)
        second[k].start()
    for k in range(PARTS):
        second[k].wait_recv()
        total = part[0, member, chunk(k)] + got_core[member, chunk(k)] + got_half[chunk(k)].astype(F32)
        value = compute(k, chunk(k), total, inputs, outputs).astype(BF)
        own[chunk(k)] = value
        third[k].start()
        fourth[k].start()
        rows_out[0, member, chunk(k)] = value
    for k in range(PARTS):
        third[k].wait_recv()
        fifth[k].start()
    for k in range(PARTS):
        fourth[k].wait_recv()
        fifth[k].wait_recv()
    for copies in (first, second, third, fourth, fifth):
        for one in copies:
            one.wait_send()


def trade(compute, part, inputs, results, name, number):
    rows, width = part.shape[0] // 4, part.shape[1]
    near = pl.BlockSpec(memory_space=pltpu.VMEM)
    dma = pltpu.SemaphoreType.DMA
    gathered, *rest = pl.pallas_call(
        partial(trade_kernel, compute, len(inputs), len(results)),
        out_shape=[jax.ShapeDtypeStruct((2, 2, rows, width), BF)] + results,
        in_specs=[near] * (1 + len(inputs)),
        out_specs=[near] * (1 + len(results)),
        scratch_shapes=[
            pltpu.VMEM((2, rows, width), F32),
            pltpu.VMEM((rows, width), BF),
            pltpu.VMEM((rows, width), BF),
            pltpu.VMEM((rows, width), BF),
        ]
        + [dma((PARTS,))] * 10,
        compiler_params=pltpu.CompilerParams(
            collective_id=number, has_side_effects=True, vmem_limit_bytes=32 << 20
        ),
        cost_estimate=pl.CostEstimate(flops=0, bytes_accessed=80_000_000, transcendentals=0),
        name=name,
    )(part.reshape(2, 2, rows, width), *inputs)
    return gathered.reshape(4 * rows, width), *rest


def middle_rows(k, rows, mixed, inputs, outputs):
    stream, gain = inputs
    middle = stream[rows].astype(F32) + mixed
    outputs[0][rows] = middle
    return middle * lax.rsqrt(jnp.mean(middle * middle, axis=1, keepdims=True) + 1e-06) * gain[...]


def middle_grad(k, rows, grad, inputs, outputs):
    cot, middle, gain = inputs
    value = middle[rows]
    scale = lax.rsqrt(jnp.mean(value * value, axis=1, keepdims=True) + 1e-06)
    unit = value * scale
    gained = jnp.sum(grad * unit, axis=0, keepdims=True)
    outputs[1][...] = gained if k == 0 else outputs[1][...] + gained
    grad = grad * gain[...]
    grad = scale * (grad - unit * jnp.mean(grad * unit, axis=1, keepdims=True))
    grad = grad + cot[rows].astype(F32)
    outputs[0][rows] = grad
    return grad


def collect_kernel(chips, steps, groups, fields, counts, *refs):
    n_left, n_right, n_out = counts
    refs = list(refs)

    def take(count):
        taken, refs[:] = refs[:count], refs[count:]
        return taken

    lefts, rights = take(n_left), take(n_right)
    back, ahead, stream, gain, middle, grad_middle, mlp_grad, small = take(8)
    outs = take(n_out)
    out_tokens, grad_tokens, small_out = take(3)
    begin, arrived, final, got_core, sent_half, got_half, small_in = take(7)
    send_ring, recv_ring, own_sem, send_core, recv_core = take(5)
    send_first, recv_first, send_second, recv_second, send_small, recv_small = take(6)
    me, member = lax.axis_index("dp"), lax.axis_index("tensor")
    core, chip = me % 2, me // 2
    spot = ring_spot(chip, chips)
    ways = (
        (2 * ring_chip((spot + 1) % chips, chips) + core, member),
        (2 * ring_chip((spot + chips - 1) % chips, chips) + core, member),
    )
    peer = (2 * chip + 1 - core, member)
    across = (me, 1 - member)
    partners = [across] + [
        (me + (1 << k) - 2 * (1 << k) * ((me // (1 << k)) % 2), member) for k in range(steps - 1)
    ]
    signal_all(list(ways) + partners)

    half = chips // 2
    width = lefts[0].shape[1] // chips
    mid = width // 2
    starts = []
    at = 0
    for _, right in groups:
        starts.append(at)
        at += rights[right].shape[1]

    def columns(group):
        return pl.ds(starts[group], rights[groups[group][1]].shape[1])

    def piece(group, place, lo=0, hi=width):
        left, right = lefts[groups[group][0]], rights[groups[group][1]]
        at = (place % chips) * width
        return lax.dot_general(
            left[:, at + lo : at + hi], right[...], (COLS_ROWS, ((), ())), preferred_element_type=F32
        )

    def rows_of(way):
        return pl.ds(mid * way, mid)

    def hop(way, step, group):
        if step:
            source, target = arrived.at[way, step - 1], arrived.at[way, step]
            source, target = source.at[:, columns(group)], target.at[:, columns(group)]
        else:
            source = begin.at[way, :, columns(group)]
            target = arrived.at[way, 0, rows_of(way), columns(group)]
        sems = (way, step, group)
        return send(source, target, send_ring.at[sems], recv_ring.at[sems], ways[way])

    sides = (back, ahead)
    first = [send(sides[i].at[1], got_core.at[i], send_first.at[i], recv_first.at[i], peer) for i in range(2)]
    second = [
        send(sent_half.at[i], got_half.at[i], send_second.at[i], recv_second.at[i], across) for i in range(2)
    ]

    def fold_small(step):
        source = small_out if step == 0 else small_in.at[steps + step - 1]
        return send(source, small_in.at[step], send_small.at[step], recv_small.at[step], partners[step])

    def put(ref, value):
        if width % 128:
            ref[...] = value
            return
        for place in range(chips):
            at = pl.multiple_of(ring_chip((spot + place) % chips, chips) * width, 128)
            ref[:, pl.ds(at, width)] = value[:, place * width : (place + 1) * width]

    def side_work():
        for i in range(2):
            first[i].wait_recv()
            total = sides[i][0, 1 - member].astype(F32) + got_core[i, 1 - member].astype(F32)
            sent_half[i] = total.astype(BF)
            second[i].start()
        yield
        total = []
        for i in range(2):
            second[i].wait_recv()
            value = sides[i][0, member].astype(F32) + got_core[i, member].astype(F32)
            total.append(value + got_half[i].astype(F32))
        put(out_tokens, middle[...] + total[1])
        value = stream[...].astype(F32)
        scale = lax.rsqrt(jnp.mean(value * value, axis=1, keepdims=True) + 1e-06)
        value = value * scale
        gained = jnp.sum(total[0] * value, axis=0, keepdims=True)
        grad = total[0] * gain[...]
        grad = scale * (grad - value * jnp.mean(grad * value, axis=1, keepdims=True))
        put(grad_tokens, grad_middle[...] + grad)
        small_out[...] = small[...]
        lanes = min(width, 128)
        each = width // lanes
        for i, vector in enumerate((gained, mlp_grad[...])):
            for place in range(chips):
                row = (i * chips + ring_chip((spot + place) % chips, chips)) * each
                for part in range(each):
                    at = place * width + part * lanes
                    small_out[pl.ds(row + part, 1), 0:lanes] = vector[:, at : at + lanes]
        fold_small(0).start()
        yield
        for step in range(steps):
            fold_small(step).wait_recv()
            before = small_out if step == 0 else small_in.at[steps + step - 1]
            small_in[steps + step] = before[...] + small_in[step]
            if step + 1 < steps:
                fold_small(step + 1).start()
            yield

    work = side_work()
    for copy in first:
        copy.start()
    for group in range(len(groups)):
        for way in range(2):
            begin[way, :, columns(group)] = piece(group, half, mid * way, mid * way + mid).astype(BF)
            hop(way, 0, group).start()
    for step in range(half - 1):
        place = half - 1 - step
        for group in range(len(groups)):
            next(work, None)
            for way in range(2):
                hop(way, step, group).wait_recv()
                value = piece(group, place if way == 0 else -place)
                if step:
                    value = value + arrived[way, step, :, columns(group)].astype(F32)
                    arrived[way, step, :, columns(group)] = value.astype(BF)
                else:
                    lo = mid * way
                    here = value[lo : lo + mid] + arrived[way, 0, rows_of(way), columns(group)].astype(F32)
                    arrived[way, 0, rows_of(way), columns(group)] = here.astype(BF)
                    arrived[way, 0, rows_of(1 - way), columns(group)] = value[
                        mid - lo : width - lo
                    ].astype(BF)
                hop(way, step + 1, group).start()
    for _ in work:
        pass
    for step in range(steps):
        fold_small(step).wait_send()
    small_out[...] = small_in[2 * steps - 1]

    rows = width // 2
    finals, used = [], {}
    for group in range(len(groups)):
        slot = group % 2
        for copy in used.get(slot, ()):
            copy()
        value = piece(group, 0)
        for way in range(2):
            hop(way, half - 1, group).wait_recv()
            value = value + arrived[way, half - 1, :, columns(group)].astype(F32)
        final[slot, :, 0 : value.shape[1]] = value
        used[slot] = []
        for number, (owner, at, size, out) in enumerate(fields):
            if owner == group:
                own = pl.ds(pl.multiple_of(core * rows, rows), rows)
                theirs = pl.ds(pl.multiple_of((1 - core) * rows, rows), rows)
                target = outs[out].at[:, pl.ds(pl.multiple_of(core * size, 128), size)]
                copy = pltpu.make_async_copy(final.at[slot, own, pl.ds(at, size)], target, own_sem.at[number])
                far = send(
                    final.at[slot, theirs, pl.ds(at, size)],
                    target,
                    send_core.at[number],
                    recv_core.at[number],
                    peer,
                )
                copy.start()
                far.start()
                finals.append(far)
                used[slot] += [copy.wait, far.wait_send]
    for slot in used:
        for copy in used[slot]:
            copy()
    for far in finals:
        far.wait_recv()
    for copy in first + second:
        copy.wait_send()
    for step in range(half):
        for group in range(len(groups)):
            for way in range(2):
                hop(way, step, group).wait_send()


def collect(grid, lefts, rights, groups, fields, sides, tokens_in, small):
    chips = grid.chips
    rows, width = sides[0].shape[0] // 4, sides[0].shape[1]
    steps = grid.devices.bit_length()
    sides = [side.reshape(2, 2, rows, width) for side in sides]
    n = sum(rights[right].shape[1] for _, right in groups)
    widest = max(rights[right].shape[1] for _, right in groups)
    block = width // chips
    half = chips // 2
    inputs = [*lefts, *rights, *sides, *tokens_in, small]
    fields = [(group, at, size, number) for number, (group, at, size) in enumerate(fields)]
    outs = [jax.ShapeDtypeStruct((block // 2, 2 * size), F32) for _, _, size, _ in fields]
    tokens = jax.ShapeDtypeStruct((rows, width), F32)
    near = pl.BlockSpec(memory_space=pltpu.VMEM)
    dma = pltpu.SemaphoreType.DMA
    ring = (2, half, len(groups))
    counts = (len(lefts), len(rights), len(outs))
    return pl.pallas_call(
        partial(collect_kernel, chips, steps, groups, fields, counts),
        out_shape=outs + [tokens, tokens, jax.ShapeDtypeStruct(small.shape, F32)],
        in_specs=[near] * len(inputs),
        out_specs=[pl.BlockSpec(memory_space=pltpu.HBM)] * len(outs) + [near] * 3,
        scratch_shapes=[
            pltpu.VMEM((2, block // 2, n), BF),
            pltpu.VMEM((2, half, block, n), BF),
            pltpu.VMEM((2, block, widest), F32),
            pltpu.VMEM((2, 2, rows, width), BF),
            pltpu.VMEM((2, rows, width), BF),
            pltpu.VMEM((2, rows, width), BF),
            pltpu.VMEM((2 * steps,) + small.shape, F32),
            dma(ring),
            dma(ring),
        ]
        + [dma((len(fields),))] * 3
        + [dma((2,))] * 4
        + [dma((steps,))] * 2,
        compiler_params=pltpu.CompilerParams(
            collective_id=3, has_side_effects=True, vmem_limit_bytes=62 << 20
        ),
        name="collect",
    )(*inputs)


def whole_rows(stack):
    return stack.reshape(-1, stack.shape[-1])


def per_device(
    tokens,
    segment_ids,
    norm_gain,
    w_query,
    w_key,
    w_value,
    w_outgate,
    w_beta,
    w_decay,
    conv_query,
    conv_key,
    conv_value,
    decay_log,
    decay_bias,
    out_gain,
    w_output,
    mlp_gain,
    w_gate,
    w_up,
    w_down,
    cotangent,
    *,
    devices,
):
    grid = Grid(devices)
    heads = w_beta.shape[1] // 2
    keyw = w_query.shape[1] // 2
    valw = w_value.shape[1] // 2
    ffw = w_gate.shape[1] // 2
    small = -(-2 * heads // 128) * 128

    filler = jnp.zeros((w_beta.shape[0], small - 2 * heads), BF)
    rates = []
    for at in (0, heads):
        rates += [w_beta[:, at : at + heads], w_decay[:, at : at + heads], filler]
    rates = jnp.concatenate(rates, axis=1)
    groups = [[w_query, w_key, rates], [w_value, w_outgate], [w_output.T], [w_gate, w_up, w_down.T]]
    norm_gain = grid.into(norm_gain)
    mlp_gain = grid.into(mlp_gain)
    shown, shown_cot = tokens[0], cotangent[0]
    if shown.shape[1] // grid.chips % 128:
        shown, shown_cot = grid.into(shown), grid.into(shown_cot)
    *gathered, stream, cot_own, rows_mix, cot_rows = spread(
        grid, groups, 3, shown, shown_cot, norm_gain[None]
    )
    wqk, wvg, wout = [whole_rows(stack) for stack in gathered[:3]]
    rows_mix, cot_rows = [rows.reshape(-1, rows.shape[-1]) for rows in (rows_mix, cot_rows)]
    segments = jnp.concatenate([segment_ids, grid.over_core(segment_ids)], axis=0)

    conv_parts = [
        part_of(conv_query, grid.quarter, keyw, 1),
        part_of(conv_key, grid.quarter, keyw, 1),
        part_of(conv_value, grid.quarter, valw, 1),
        part_of(decay_log, grid.quarter, heads, 0),
        part_of(decay_bias, grid.quarter, heads, 0),
    ]
    pre_qk = dot(rows_mix, wqk)
    pre_vg = dot(rows_mix, wvg)
    lanes = [jnp.pad(part[None], ((0, 0), (0, small - heads))) for part in conv_parts[3:]]
    mixer_in = (pre_qk, pre_vg, segments[:, :, None], segments[:, None, :], *conv_parts[:3], *lanes, out_gain[None])
    heads_out, kept = mixer(heads, mixer_in)
    own_rows = jax.ShapeDtypeStruct(stream.shape, F32)
    mix_part = cols_product(heads_out, wout)
    rows_mlp, middle = trade(
        middle_rows, mix_part, (stream, mlp_gain[None]), [own_rows], "middle", 1
    )
    mlp_full = grid.gather(gathered[3], [(), heads_out, rows_mlp])
    gate_full, up_full, down_full = [mlp_full[:, at : at + ffw] for at in (0, ffw, 2 * ffw)]
    gate = dot(rows_mlp, gate_full)
    upper = dot(rows_mlp, up_full)
    sigmoid_gate = jax.nn.sigmoid(gate)
    hidden = (gate * sigmoid_gate * upper).astype(BF)
    grad_hidden = dot(cot_rows, down_full)
    grad_gate = (grad_hidden * upper * sigmoid_gate * (1.0 + gate * (1.0 - sigmoid_gate))).astype(BF)
    grad_upper = (grad_hidden * gate * sigmoid_gate).astype(BF)
    grad_down, sent = grid.scatter(((cot_rows, hidden),), ())
    back_part = cols_product(grad_gate, gate_full) + cols_product(grad_upper, up_full)
    gain_row = jax.ShapeDtypeStruct((1, stream.shape[1]), F32)
    grad_mixed, grad_middle, grad_mlp_gain = trade(
        middle_grad,
        tied(back_part, sent[0]),
        (cot_own, middle, mlp_gain[None]),
        [own_rows, gain_row],
        "middle_back",
        2,
    )
    grad_heads = tied(dot(grad_mixed, wout), sent[1])
    grad_qk, grad_vg, *core_grads = mixer_back(heads, grad_heads, mixer_in, kept)
    grad_qk, grad_vg = tied((grad_qk, grad_vg), sent[2:3])
    ahead = cols_product(hidden, down_full).astype(BF)
    back = (cols_product(grad_vg, wvg) + cols_product(grad_qk, wqk)).astype(BF)

    def placed(piece, whole):
        start = grid.quarter * piece.shape[-1]
        return lax.dynamic_update_slice_in_dim(jnp.zeros(whole.shape, F32), piece, start, -1)

    grad_cq, grad_ck, grad_cv, grad_rate, grad_gain = core_grads
    grad_rate = grad_rate[:, heads : 2 * heads]
    width = norm_gain.shape[0]
    lanes = min(width // grid.chips, 128)
    gain_rows = width // lanes
    wholes = (conv_query, conv_key, conv_value, decay_log, decay_bias)
    pieces = [placed(piece, whole) for piece, whole in zip((grad_cq, grad_ck, grad_cv, *grad_rate), wholes)]
    pieces.append(grad_gain)
    packed = jnp.concatenate([piece.reshape(-1) for piece in pieces])
    packed = jnp.pad(packed, (0, (-packed.size) % 1024)).reshape(-1, 128)
    packed = jnp.pad(packed, ((2 * gain_rows, 0), (0, 0)))
    at = 2 * keyw
    *weight_grads, out_tokens, grad_tokens, packed = collect(
        grid,
        [rows_mlp, grad_mixed, rows_mix],
        [grad_gate, grad_upper, grad_vg, heads_out, grad_qk],
        [(0, 0), (0, 1), (2, 2), (1, 3), (2, 4)],
        [(0, 0, ffw), (1, 0, ffw), (2, 0, valw), (2, valw, valw), (3, 0, valw), (4, 0, keyw), (4, keyw, keyw), (4, at, small)],
        [back, ahead],
        [stream, norm_gain[None], middle, grad_middle, grad_mlp_gain],
        packed,
    )
    whole_gate, whole_up, whole_value, whole_outgate, whole_out, whole_query, whole_key, whole_small = weight_grads
    if out_tokens.shape[1] // grid.chips % 128:
        out_tokens, grad_tokens = grid.out_of(out_tokens), grid.out_of(grad_tokens)
    whole_beta = jnp.concatenate([whole_small[:, i : i + heads] for i in (0, small)], axis=1)
    whole_decay = jnp.concatenate([whole_small[:, i + heads : i + 2 * heads] for i in (0, small)], axis=1)
    whole_down = grid.join(*grid.own_block(grad_down))
    gains = packed[: 2 * gain_rows, :lanes].reshape(2, width)
    packed = packed[2 * gain_rows :].reshape(-1)
    sums = []
    at = 0
    for piece, whole in zip(pieces, wholes + (out_gain,)):
        sums.append(packed[at : at + piece.size].reshape(whole.shape))
        at += piece.size
    return (
        out_tokens[None],
        grad_tokens[None],
        gains[0],
        whole_query,
        whole_key,
        whole_value,
        whole_outgate,
        whole_beta,
        whole_decay,
        *sums,
        whole_out.T,
        gains[1],
        whole_gate,
        whole_up,
        whole_down.T,
    )


def solution(mesh):
    rows = P("dp", "tensor")
    cols = P("tensor", "dp")
    tokens = P("dp", "tensor", None)
    placed = (tokens, P("dp", None), P()) + (rows,) * 6 + (P(),) * 6
    placed = placed + (cols, P(), rows, rows, cols, tokens)
    given = (tokens, tokens, P()) + (rows,) * 6 + (P(),) * 6 + (cols, P(), rows, rows, cols)
    return jax.shard_map(
        partial(per_device, devices=mesh.shape["dp"]),
        mesh=mesh,
        in_specs=placed,
        out_specs=given,
        check_vma=False,
    )
```

```python
from functools import partial
import math

import jax
import jax.numpy as jnp
from jax import lax
from jax.experimental import pallas as pl
from jax.experimental.pallas import tpu as pltpu
from jax.sharding import PartitionSpec as P

HIGH = lax.Precision.HIGH
HIGHEST = lax.Precision.HIGHEST
BF = jnp.bfloat16
F32 = jnp.float32


def scale_rows(values, factor):
    return values * lax.rsqrt(jnp.mean(values * values, axis=-1, keepdims=True) + 1e-06) * factor


def split3(value):
    high = value.astype(BF)
    return high, (value - high.astype(F32)).astype(BF)


def product(left, right, dims):
    dims = (dims, ((), ()))
    total = lax.dot_general(left[0], right[0], dims, preferred_element_type=F32)
    total = total + lax.dot_general(left[0], right[1], dims, preferred_element_type=F32)
    return total + lax.dot_general(left[1], right[0], dims, preferred_element_type=F32)


ROWS_COLS = ((1,), (0,))
ROWS_ROWS = ((1,), (1,))
COLS_ROWS = ((0,), (0,))


def exact_sum(mask, value, dims):
    high, low = split3(value)
    last = (value - high.astype(F32) - low.astype(F32)).astype(BF)
    dims = (dims, ((), ()))
    total = lax.dot_general(mask, last, dims, preferred_element_type=F32)
    total = total + lax.dot_general(mask, low, dims, preferred_element_type=F32)
    return total + lax.dot_general(mask, high, dims, preferred_element_type=F32)


def conv_parts(values, taps, keeping):
    moved = [values] + [pltpu.roll(values, j, 0) * keeping[j] for j in range(1, 4)]
    total = moved[0] * taps[0:1]
    for j in range(1, 4):
        total = total + moved[j] * taps[j : j + 1]
    return moved, total


def conv_back(grad, moved, taps, keeping):
    rows = grad.shape[0]
    total = grad * taps[0:1]
    for j in range(1, 4):
        total = total + pltpu.roll(grad * keeping[j], rows - j, 0) * taps[j : j + 1]
    parts = [jnp.sum(grad * moved[j], axis=0, keepdims=True) for j in range(4)]
    return total, jnp.concatenate(parts, axis=0)


def silu_back(total, gate):
    return gate * (1.0 + total * (1.0 - gate))


def softplus(value):
    return jnp.maximum(value, 0.0) + jnp.log1p(jnp.exp(-jnp.abs(value)))


def block_masks(seg_col, seg_row):
    size = seg_col.shape[0]
    row = lax.broadcasted_iota(jnp.int32, (size, size), 0)
    col = lax.broadcasted_iota(jnp.int32, (size, size), 1)
    masking = ((seg_col == seg_row) & (col <= row)).astype(F32)
    spot = lax.broadcasted_iota(jnp.int32, (size, 1), 0)
    keeping = [None]
    for j in range(1, 4):
        keeping.append(((pltpu.roll(seg_col, j, 0) == seg_col) & (spot >= j)).astype(F32))
    return row, col, masking, keeping


def head_rates(small, log, bias, masking, heads):
    decay_in = pltpu.roll(small, small.shape[1] - heads, 1) + bias
    factor = -jnp.exp(log)
    rates = factor * softplus(decay_in)
    betas = jax.nn.sigmoid(small)
    summed = exact_sum(masking.astype(BF), rates, ROWS_COLS)
    return decay_in, factor, rates, betas, summed


def invert(mixing, row, col):
    size = mixing.shape[0]
    result = jnp.where(row == col, 1.0, 0.0) - jnp.where((row >> 1) == (col >> 1), mixing, 0.0)
    level = 1
    while (1 << level) < size:
        picked = ((row >> (level + 1)) == (col >> (level + 1))) & ((row >> level) != (col >> level))
        part = split3(jnp.where(picked, mixing, 0.0))
        halves = split3(result)
        step = product(halves, part, ROWS_COLS)
        result = result - product(split3(step), halves, ROWS_COLS)
        level += 1
    return result


def unit(values):
    return lax.rsqrt(jnp.sum(values * values, axis=1, keepdims=True) + 1e-06)


def mixer_kernel(heads, qk, vg, seg_col, seg_row, cq, ck, cv, log, bias, gain, *outs):
    heads_out, inverses, all_errors, all_kk, all_qk, all_raw = outs
    keyw, valw = cq.shape[1] // heads, cv.shape[1] // heads
    row, col, masking, keeping = block_masks(seg_col[0], seg_row[0])
    small = qk[:, 2 * heads * keyw :]
    _, _, _, betas, summed = head_rates(small, log[...], bias[...], masking, heads)
    betas_t, summed_t = betas.T, summed.T
    strict = (col < row).astype(F32)
    for h in range(heads):
        at = pl.ds(h * keyw, keyw)
        query = jax.nn.silu(conv_parts(qk[:, at], cq[:, at], keeping)[1])
        query = query * (unit(query) * (1.0 / math.sqrt(keyw)))
        key = jax.nn.silu(
            conv_parts(qk[:, pl.ds((heads + h) * keyw, keyw)], ck[:, at], keeping)[1]
        )
        key = key * unit(key)
        at = pl.ds(h * valw, valw)
        value = jax.nn.silu(conv_parts(vg[:, at], cv[:, at], keeping)[1])
        spread = summed[:, h : h + 1] - summed_t[h : h + 1]
        decays = jnp.exp(spread * masking) * masking * betas_t[h : h + 1]
        keys = split3(key)
        key_key = product(keys, keys, ROWS_ROWS)
        query_key = product(split3(query), keys, ROWS_ROWS)
        inverse = invert(decays * key_key * strict, row, col)
        errors = product(split3(inverse), split3(value), ROWS_COLS)
        raw = product(split3(decays * query_key), split3(errors), ROWS_COLS)
        inverses[0, h] = inverse
        all_errors[0, h] = errors
        all_kk[0, h] = key_key
        all_qk[0, h] = query_key
        all_raw[:, at] = raw
        scaled = raw * lax.rsqrt(jnp.mean(raw * raw, axis=1, keepdims=True) + 1e-05) * gain[...]
        gate = vg[:, pl.ds((heads + h) * valw, valw)]
        heads_out[:, at] = (scaled * jax.nn.silu(gate)).astype(BF)


def mixer_back_kernel(heads, grad, qk, vg, seg_col, seg_row, cq, ck, cv, log, bias, gain, *refs):
    inverses, all_errors, all_kk, all_qk, all_raw = refs[:5]
    grad_qk, grad_vg, grad_cq, grad_ck, grad_cv, grad_rate, grad_gain = refs[5:]
    keyw, valw = cq.shape[1] // heads, cv.shape[1] // heads
    size = qk.shape[0]

    @pl.when(pl.program_id(0) == 0)
    def _():
        for ref in (grad_cq, grad_ck, grad_cv, grad_rate, grad_gain):
            ref[...] = jnp.zeros_like(ref)

    row, col, masking, keeping = block_masks(seg_col[0], seg_row[0])
    small = qk[:, 2 * heads * keyw :]
    decay_in, factor, rates, betas, summed = head_rates(small, log[...], bias[...], masking, heads)
    betas_t, summed_t = betas.T, summed.T
    strict = (col < row).astype(F32)
    lanes = lax.broadcasted_iota(jnp.int32, (1, small.shape[1]), 1)
    spots = lax.broadcasted_iota(jnp.int32, (small.shape[1], 1), 0)
    grad_summed = jnp.zeros_like(small)
    from_cols = jnp.zeros((small.shape[1], size), F32)
    for h in range(heads):
        at = pl.ds(h * valw, valw)
        raw, gate_in = all_raw[:, at], vg[:, pl.ds((heads + h) * valw, valw)]
        gate = jax.nn.sigmoid(gate_in)
        scale = lax.rsqrt(jnp.mean(raw * raw, axis=1, keepdims=True) + 1e-05)
        above = grad[:, at]
        grad_vg[:, pl.ds((heads + h) * valw, valw)] = (
            above * (raw * scale * gain[...]) * silu_back(gate_in, gate)
        ).astype(BF)
        above = above * (gate_in * gate)
        grad_gain[...] += jnp.sum(above * raw * scale, axis=0, keepdims=True)
        above = above * gain[...]
        grad_raw = scale * (above - raw * (scale * scale * jnp.mean(above * raw, axis=1, keepdims=True)))

        spread = summed[:, h : h + 1] - summed_t[h : h + 1]
        plain = jnp.exp(spread * masking) * masking
        decays = plain * betas_t[h : h + 1]
        key_key, query_key = all_kk[0, h] * strict, all_qk[0, h]
        grad_raws, errors = split3(grad_raw), split3(all_errors[0, h])
        grad_reading = product(grad_raws, errors, ROWS_ROWS)
        grad_errors = product(split3(decays * query_key), grad_raws, COLS_ROWS)
        grad_value = product(split3(inverses[0, h]), split3(grad_errors), COLS_ROWS)
        grad_mixing = -product(split3(grad_value), errors, ROWS_ROWS)
        both = (grad_mixing * key_key + grad_reading * query_key) * plain
        grad_beta = jnp.sum(both, axis=0, keepdims=True)
        both = both * betas_t[h : h + 1]
        from_rows = jnp.sum(both, axis=1, keepdims=True)
        grad_summed = grad_summed + jnp.where(lanes == heads + h, from_rows, 0.0)
        from_cols = from_cols + jnp.where(spots == h, grad_beta, 0.0)
        from_cols = from_cols - jnp.where(spots == heads + h, jnp.sum(both, axis=0, keepdims=True), 0.0)

        at = pl.ds(h * keyw, keyw)
        query_moved, query_total = conv_parts(qk[:, at], cq[:, at], keeping)
        query_gate = jax.nn.sigmoid(query_total)
        query = query_total * query_gate
        query_scale = unit(query)
        query = query * query_scale
        key_at = pl.ds((heads + h) * keyw, keyw)
        key_moved, key_total = conv_parts(qk[:, key_at], ck[:, at], keeping)
        key_gate = jax.nn.sigmoid(key_total)
        key = key_total * key_gate
        key_scale = unit(key)
        key = key * key_scale
        keys = split3(key)
        grad_kk = split3(grad_mixing * decays * strict)
        grad_qk_product = split3(grad_reading * (decays * (1.0 / math.sqrt(keyw))))
        grad_query = product(grad_qk_product, keys, ROWS_COLS)
        grad_key = product(grad_qk_product, split3(query), COLS_ROWS)
        grad_key = grad_key + product(grad_kk, keys, ROWS_COLS) + product(grad_kk, keys, COLS_ROWS)

        grad_query = query_scale * (grad_query - query * jnp.sum(grad_query * query, axis=1, keepdims=True))
        grad_query = grad_query * silu_back(query_total, query_gate)
        grad_query, taps = conv_back(grad_query, query_moved, cq[:, at], keeping)
        grad_qk[:, at] = grad_query.astype(BF)
        grad_cq[:, at] += taps
        grad_key = key_scale * (grad_key - key * jnp.sum(grad_key * key, axis=1, keepdims=True))
        grad_key = grad_key * silu_back(key_total, key_gate)
        grad_key, taps = conv_back(grad_key, key_moved, ck[:, at], keeping)
        grad_qk[:, key_at] = grad_key.astype(BF)
        grad_ck[:, at] += taps

        at = pl.ds(h * valw, valw)
        moved, total = conv_parts(vg[:, at], cv[:, at], keeping)
        grad_value = grad_value * silu_back(total, jax.nn.sigmoid(total))
        grad_value, taps = conv_back(grad_value, moved, cv[:, at], keeping)
        grad_vg[:, at] = grad_value.astype(BF)
        grad_cv[:, at] += taps

    from_cols = from_cols.T
    grad_summed = grad_summed + jnp.where(lanes >= heads, from_cols, 0.0)
    grad_rates = exact_sum(masking.astype(BF), grad_summed, COLS_ROWS)
    decay_lanes = (lanes >= heads) & (lanes < 2 * heads)
    shifted = [pltpu.roll(value, heads, 1) for value in (decay_in, rates)]
    grad_decay = grad_rates * pltpu.roll(factor, heads, 1) * jax.nn.sigmoid(shifted[0])
    grad_rate[0:1] += jnp.sum(grad_rates * shifted[1], axis=0, keepdims=True)
    grad_rate[1:2] += jnp.sum(grad_decay, axis=0, keepdims=True)
    grad_small = jnp.where(decay_lanes, grad_decay, from_cols * betas * (1.0 - betas))
    grad_small = jnp.where(lanes < 2 * heads, grad_small, 0.0)
    grad_qk[:, 2 * heads * keyw :] = grad_small.astype(BF)


def mixer_specs(heads, qk, vg, cq, cv, small):
    length = qk.shape[0] // 2

    def by_rows(width):
        return pl.BlockSpec((length, width), lambda s: (s, 0))

    def fixed(*shape):
        return pl.BlockSpec(shape, lambda s: (0,) * len(shape))

    shared = [
        by_rows(qk.shape[1]),
        by_rows(vg.shape[1]),
        pl.BlockSpec((1, length, 1), lambda s: (s, 0, 0)),
        pl.BlockSpec((1, 1, length), lambda s: (s, 0, 0)),
        fixed(*cq.shape),
        fixed(*cq.shape),
        fixed(*cv.shape),
        fixed(1, small),
        fixed(1, small),
        fixed(1, cv.shape[1] // heads),
    ]
    valw = cv.shape[1] // heads
    square = (heads, length, length)
    kept = [square, (heads, length, valw), square, square]
    kept_specs = [pl.BlockSpec((1,) + shape, lambda s: (s, 0, 0, 0)) for shape in kept]
    kept_specs.append(by_rows(cv.shape[1]))
    kept_shapes = [jax.ShapeDtypeStruct((2,) + shape, F32) for shape in kept]
    kept_shapes.append(jax.ShapeDtypeStruct((2 * length, cv.shape[1]), F32))
    return by_rows, fixed, shared, kept_specs, kept_shapes


def mixer(heads, inputs):
    qk, vg, _, _, cq, _, cv, log, _, _ = inputs
    by_rows, _, shared, kept_specs, kept_shapes = mixer_specs(heads, qk, vg, cq, cv, log.shape[1])
    heads_out, *kept = pl.pallas_call(
        partial(mixer_kernel, heads),
        grid=(2,),
        out_shape=[jax.ShapeDtypeStruct((qk.shape[0], cv.shape[1]), BF)] + kept_shapes,
        in_specs=shared,
        out_specs=[by_rows(cv.shape[1])] + kept_specs,
        compiler_params=pltpu.CompilerParams(vmem_limit_bytes=48 << 20),
        name="mixer",
    )(*inputs)
    return heads_out, kept


def mixer_back(heads, grad, inputs, kept):
    qk, vg, _, _, cq, _, cv, log, _, gain = inputs
    by_rows, fixed, shared, kept_specs, _ = mixer_specs(heads, qk, vg, cq, cv, log.shape[1])
    sums = [cq.shape, cq.shape, cv.shape, (2, log.shape[1]), gain.shape]
    return pl.pallas_call(
        partial(mixer_back_kernel, heads),
        grid=(2,),
        out_shape=[jax.ShapeDtypeStruct(qk.shape, BF), jax.ShapeDtypeStruct(vg.shape, BF)]
        + [jax.ShapeDtypeStruct(shape, F32) for shape in sums],
        in_specs=[by_rows(cv.shape[1])] + shared + kept_specs,
        out_specs=[by_rows(qk.shape[1]), by_rows(vg.shape[1])] + [fixed(*shape) for shape in sums],
        compiler_params=pltpu.CompilerParams(vmem_limit_bytes=48 << 20),
        name="mixer_back",
    )(grad, *inputs, *kept)


def rows_product(left, right):
    return lax.dot_general(left, right, (((0,), (0,)), ((), ())), preferred_element_type=F32)


def cols_product(left, right):
    return lax.dot_general(left, right, (((1,), (1,)), ((), ())), preferred_element_type=F32)


def dot(left, right):
    return jnp.dot(left, right, preferred_element_type=F32)


def tied(value, after):
    return lax.optimization_barrier((value, after))[0]


def first_of(flag, own, peer, axis):
    return jnp.concatenate([jnp.where(flag, own, peer), jnp.where(flag, peer, own)], axis=axis)


def part_of(value, index, size, axis):
    return lax.dynamic_slice_in_dim(value, index * size, size, axis)


class Grid:
    def __init__(self, devices):
        self.devices = devices
        self.chips = devices // 2
        me = lax.axis_index("dp")
        self.core = me % 2
        self.spot = ring_spot(me // 2, self.chips)
        self.member = lax.axis_index("tensor")
        self.quarter = 2 * self.member + self.core

    def swap(self, value, offset):
        pairs = [(at, at ^ offset) for at in range(self.devices)]
        return lax.ppermute(value, "dp", pairs)

    def over_core(self, value):
        return self.swap(value, 1)

    def over_tensor(self, value):
        return lax.ppermute(value, "tensor", [(0, 1), (1, 0)])

    def shift(self, value, step):
        pairs = []
        for at in range(self.devices):
            spot = (ring_spot(at // 2, self.chips) + step) % self.chips
            pairs.append((at, 2 * ring_chip(spot, self.chips) + at % 2))
        return lax.ppermute(value, "dp", pairs)

    def into(self, value):
        width = value.shape[-1] // self.chips
        blocks = []
        for place in range(self.chips):
            chip = ring_chip((self.spot + place) % self.chips, self.chips)
            blocks.append(part_of(value, chip, width, -1))
        return jnp.concatenate(blocks, axis=-1)

    def out_of(self, value):
        width = value.shape[-1] // self.chips
        blocks = []
        for chip in range(self.chips):
            place = (ring_spot(chip, self.chips) - self.spot + self.chips) % self.chips
            blocks.append(part_of(value, place, width, -1))
        return jnp.concatenate(blocks, axis=-1)

    def gather_rows(self, own):
        whole = first_of(self.member == 0, own, self.over_tensor(own), 0)
        return jnp.concatenate([whole, self.over_core(whole)], axis=0)

    def scatter_rows(self, value):
        half = value.shape[0] // 2
        whole = value[:half] + self.over_core(value[half:])
        half //= 2
        theirs = part_of(whole, 1 - self.member, half, 0)
        peer = self.over_tensor(theirs.astype(BF)).astype(F32)
        return part_of(whole, self.member, half, 0) + peer

    def gather(self, chunk, gates):
        half = self.chips // 2
        mid = chunk.shape[0] // 2
        rights, lefts = [chunk], [chunk]
        for step in range(1, half):
            pair = tied((rights[-1], lefts[-1]), gates[step - 1 : step])
            rights.append(self.shift(pair[0], 1))
            lefts.append(self.shift(pair[1], -1))
        top, low = self.shift(rights[-1][:mid], 1), self.shift(lefts[-1][mid:], -1)
        return jnp.concatenate(lefts + [top, low] + rights[:0:-1], axis=0)

    def scatter(self, left, right):
        half = self.chips // 2
        width = left.shape[1] // self.chips

        def piece(place, lo=0, hi=width):
            at = (place % self.chips) * width
            return rows_product(left[:, at + lo : at + hi], right)

        mid = width // 2
        goes_right, goes_left = piece(half, 0, mid).astype(BF), piece(half, mid, width).astype(BF)
        hops = []
        for place in range(half - 1, 0, -1):
            from_left, from_right = self.shift(goes_right, 1), self.shift(goes_left, -1)
            hops.append((from_left, from_right))
            from_left, from_right = from_left.astype(F32), from_right.astype(F32)
            if place == half - 1:
                from_left = jnp.pad(from_left, ((0, width - mid), (0, 0)))
                from_right = jnp.pad(from_right, ((mid, 0), (0, 0)))
            goes_right = (piece(place) + from_left).astype(BF)
            goes_left = (piece(-place) + from_right).astype(BF)
        return goes_right, goes_left, hops


def ring_spot(chip, chips):
    line, pair = chip // 2, chip % 2
    return line * (1 - pair) + (chips - 1 - line) * pair


def ring_chip(spot, chips):
    pair = spot // (chips // 2)
    return 2 * (spot * (1 - pair) + (chips - 1 - spot) * pair) + pair


def signal_all(devices):
    barrier = pltpu.get_barrier_semaphore()
    for device in devices:
        pl.semaphore_signal(barrier, inc=1, device_id=device, device_id_type=pl.DeviceIdType.MESH)
    pl.semaphore_wait(barrier, len(devices))


def send(source, target, send_sem, recv_sem, device):
    return pltpu.make_async_remote_copy(
        src_ref=source,
        dst_ref=target,
        send_sem=send_sem,
        recv_sem=recv_sem,
        device_id=device,
        device_id_type=pl.DeviceIdType.MESH,
    )


def spread_kernel(chips, layout, ringed, *refs):
    count = len(layout)
    totals = 1 + max(out for out, _, _ in layout)
    sources, (tokens, cot, gain) = refs[:count], refs[count : count + 3]
    outs = refs[count + 3 : count + 3 + totals]
    stream, cot_own, rows_mix, rows_cot = refs[count + 3 + totals : count + 7 + totals]
    normed, near_sem, send_core, recv_core, send_right, recv_right, send_left, recv_left = refs[
        count + 7 + totals : count + 15 + totals
    ]
    own_sem, send_half, recv_half, send_whole, recv_whole = refs[count + 15 + totals :]
    me, member = lax.axis_index("dp"), lax.axis_index("tensor")
    core, chip = me % 2, me // 2
    spot = ring_spot(chip, chips)
    right = (2 * ring_chip((spot + 1) % chips, chips) + core, member)
    left = (2 * ring_chip((spot + chips - 1) % chips, chips) + core, member)
    peer = (2 * chip + 1 - core, member)
    across = (me, 1 - member)
    signal_all((right, left, peer, across))

    def home(out):
        return outs[out].at[0] if out < ringed else outs[out]

    near, far = [], []
    for i, (out, at, width) in enumerate(layout):
        rows = sources[i].shape[0]
        place = home(out).at[pl.ds(pl.multiple_of(core * rows, rows), rows), pl.ds(at, width)]
        mine = sources[i].at[:, pl.ds(pl.multiple_of(core * width, 128), width)]
        theirs = sources[i].at[:, pl.ds(pl.multiple_of((1 - core) * width, 128), width)]
        near.append(pltpu.make_async_copy(mine, place, near_sem.at[i]))
        far.append(send(theirs, place, send_core.at[i], recv_core.at[i], peer))
        far[-1].start()
        near[-1].start()

    def hop(out, step, way):
        last = step == chips // 2
        ref = outs[out]
        mid = ref.shape[1] // 2
        if way > 0:
            at, to, device, sends, receives = -(step - 1) % chips, chips - step, right, send_right, recv_right
            rows = pl.ds(0, mid)
        else:
            at, to, device, sends, receives = step - 1, step, left, send_left, recv_left
            rows = pl.ds(mid, mid)
        source, target = ref.at[at], ref.at[to]
        if last:
            source, target = source.at[rows], target.at[rows]
        return send(source, target, sends.at[out, step - 1], receives.at[out, step - 1], device)

    started, own = [], []
    pairs = ((normed, rows_mix), (cot_own, rows_cot))
    halves = [
        send(value, rows.at[0, member], send_half.at[i], recv_half.at[i], across)
        for i, (value, rows) in enumerate(pairs)
    ]
    wholes = [
        send(rows.at[0], rows.at[1], send_whole.at[i], recv_whole.at[i], peer)
        for i, (_, rows) in enumerate(pairs)
    ]
    for step in range(1, chips // 2 + 1):
        for out in range(ringed):
            if step == 1:
                for i, item in enumerate(layout):
                    if item[0] == out:
                        near[i].wait()
                        far[i].wait()
            for way in (1, -1):
                if step > 1:
                    hop(out, step - 1, way).wait_recv()
                copy = hop(out, step, way)
                copy.start()
                started.append(copy)
        if step == 1:
            width = tokens.shape[1] // chips
            aligned = width % 128 == 0
            squares = jnp.zeros((tokens.shape[0], 1), F32)
            for place in range(chips):
                to = pl.ds(place * width, width)
                at = to
                if aligned:
                    at = ring_chip((spot + place) % chips, chips) * width
                    at = pl.ds(pl.multiple_of(at, 128), width)
                stream[:, to] = tokens[:, at]
                cot_own[:, to] = cot[:, at]
                block = stream[:, to].astype(F32)
                squares = squares + jnp.sum(block * block, axis=1, keepdims=True)
            scale = lax.rsqrt(squares / tokens.shape[1] + 1e-06)
            normed[...] = (stream[...].astype(F32) * scale * gain[...]).astype(BF)
            for i, (value, rows) in enumerate(pairs):
                own.append(pltpu.make_async_copy(value, rows.at[0, member], own_sem.at[i]))
                own[-1].start()
                halves[i].start()
        if step == 2:
            for i in range(2):
                own[i].wait()
                halves[i].wait()
                wholes[i].start()
    for i, item in enumerate(layout):
        if item[0] >= ringed:
            near[i].wait()
            far[i].wait()
    for copy in wholes:
        copy.wait()
    for out in range(ringed):
        for way in (1, -1):
            hop(out, chips // 2, way).wait_recv()
    for copy in started:
        copy.wait_send()


def spread(grid, groups, ringed, tokens, cot, gain):
    chips = grid.chips
    sources, layout, shapes = [], [], []
    for out, group in enumerate(groups):
        at = 0
        for shard in group:
            width = shard.shape[1] // 2
            layout.append((out, at, width))
            sources.append(shard)
            at += width
        rows = 2 * group[0].shape[0]
        shapes.append(jax.ShapeDtypeStruct(((chips,) if out < ringed else ()) + (rows, at), BF))
    dma = pltpu.SemaphoreType.DMA
    hops = (ringed, chips // 2)
    anywhere = pl.BlockSpec(memory_space=pltpu.HBM)
    near = pl.BlockSpec(memory_space=pltpu.VMEM)
    own = jax.ShapeDtypeStruct(tokens.shape, BF)
    rows = jax.ShapeDtypeStruct((2, 2) + tokens.shape, BF)
    return pl.pallas_call(
        partial(spread_kernel, chips, layout, ringed),
        out_shape=shapes + [own, own, rows, rows],
        in_specs=[anywhere] * len(sources) + [near] * 3,
        out_specs=[anywhere] * len(shapes) + [near] * 2 + [anywhere] * 2,
        scratch_shapes=[pltpu.VMEM(tokens.shape, BF)]
        + [dma((len(sources),))] * 3
        + [dma(hops)] * 4
        + [dma((2,))] * 5,
        compiler_params=pltpu.CompilerParams(
            collective_id=0, has_side_effects=True, vmem_limit_bytes=62 << 20
        ),
        name="spread",
    )(*sources, tokens, cot, gain)


PARTS = 2


def trade_kernel(compute, extras, results, *refs):
    part, inputs = refs[0], refs[1 : 1 + extras]
    rows_out, outputs = refs[1 + extras], refs[2 + extras : 2 + extras + results]
    got_core, sent_half, got_half, own = refs[2 + extras + results : 6 + extras + results]
    sems = refs[6 + extras + results :]
    me, member = lax.axis_index("dp"), lax.axis_index("tensor")
    peer = (me + 1 - 2 * (me % 2), member)
    across = (me, 1 - member)
    signal_all((peer, across))
    count = part.shape[2] // PARTS

    def chunk(k):
        return pl.ds(k * count, count)

    def copy(kind, k, source, target, device):
        return send(source, target, sems[2 * kind].at[k], sems[2 * kind + 1].at[k], device)

    first = [copy(0, k, part.at[1, :, chunk(k)], got_core.at[:, chunk(k)], peer) for k in range(PARTS)]
    second = [copy(1, k, sent_half.at[chunk(k)], got_half.at[chunk(k)], across) for k in range(PARTS)]
    third = [
        copy(2, k, own.at[chunk(k)], rows_out.at[0, member, chunk(k)], across) for k in range(PARTS)
    ]
    fourth = [
        copy(3, k, own.at[chunk(k)], rows_out.at[1, member, chunk(k)], peer) for k in range(PARTS)
    ]
    fifth = [
        copy(4, k, rows_out.at[0, 1 - member, chunk(k)], rows_out.at[1, 1 - member, chunk(k)], peer)
        for k in range(PARTS)
    ]
    for k in range(PARTS):
        first[k].start()
    for k in range(PARTS):
        first[k].wait_recv()
        total = part[0, 1 - member, chunk(k)] + got_core[1 - member, chunk(k)]
        sent_half[chunk(k)] = total.astype(BF)
        second[k].start()
    for k in range(PARTS):
        second[k].wait_recv()
        total = part[0, member, chunk(k)] + got_core[member, chunk(k)] + got_half[chunk(k)].astype(F32)
        value = compute(k, chunk(k), total, inputs, outputs).astype(BF)
        own[chunk(k)] = value
        third[k].start()
        fourth[k].start()
        rows_out[0, member, chunk(k)] = value
    for k in range(PARTS):
        third[k].wait_recv()
        fifth[k].start()
    for k in range(PARTS):
        fourth[k].wait_recv()
        fifth[k].wait_recv()
    for copies in (first, second, third, fourth, fifth):
        for one in copies:
            one.wait_send()


def trade(compute, part, inputs, results, name, number):
    rows, width = part.shape[0] // 4, part.shape[1]
    near = pl.BlockSpec(memory_space=pltpu.VMEM)
    dma = pltpu.SemaphoreType.DMA
    gathered, *rest = pl.pallas_call(
        partial(trade_kernel, compute, len(inputs), len(results)),
        out_shape=[jax.ShapeDtypeStruct((2, 2, rows, width), BF)] + results,
        in_specs=[near] * (1 + len(inputs)),
        out_specs=[near] * (1 + len(results)),
        scratch_shapes=[
            pltpu.VMEM((2, rows, width), F32),
            pltpu.VMEM((rows, width), BF),
            pltpu.VMEM((rows, width), BF),
            pltpu.VMEM((rows, width), BF),
        ]
        + [dma((PARTS,))] * 10,
        compiler_params=pltpu.CompilerParams(
            collective_id=number, has_side_effects=True, vmem_limit_bytes=32 << 20
        ),
        cost_estimate=pl.CostEstimate(flops=0, bytes_accessed=80_000_000, transcendentals=0),
        name=name,
    )(part.reshape(2, 2, rows, width), *inputs)
    return gathered.reshape(4 * rows, width), *rest


def middle_rows(k, rows, mixed, inputs, outputs):
    stream, gain = inputs
    middle = stream[rows].astype(F32) + mixed
    outputs[0][rows] = middle
    return middle * lax.rsqrt(jnp.mean(middle * middle, axis=1, keepdims=True) + 1e-06) * gain[...]


def middle_grad(k, rows, grad, inputs, outputs):
    cot, middle, gain = inputs
    value = middle[rows]
    scale = lax.rsqrt(jnp.mean(value * value, axis=1, keepdims=True) + 1e-06)
    unit = value * scale
    gained = jnp.sum(grad * unit, axis=0, keepdims=True)
    outputs[1][...] = gained if k == 0 else outputs[1][...] + gained
    grad = grad * gain[...]
    grad = scale * (grad - unit * jnp.mean(grad * unit, axis=1, keepdims=True))
    grad = grad + cot[rows].astype(F32)
    outputs[0][rows] = grad
    return grad


def collect_kernel(chips, steps, groups, late_right, fields, side_of, counts, *refs):
    n_left, n_right, n_out, n_side = counts
    refs = list(refs)

    def take(count):
        taken, refs[:] = refs[:count], refs[count:]
        return taken

    lefts, rights = take(n_left), take(n_right)
    late_out, late_left = take(2), take(1)[0]
    weights = take(n_side)
    stream, gain, middle, grad_middle, mlp_grad, small = take(6)
    outs = take(n_out)
    out_tokens, grad_tokens, small_out = take(3)
    begin, arrived, late_in, final, sides, got_core, sent_half, got_half, small_in = take(9)
    buffers = take(n_side)
    send_ring, recv_ring, own_sem, send_core, recv_core, send_late, recv_late = take(7)
    send_first, recv_first, send_second, recv_second, send_small, recv_small, weight_sem, free = take(8)
    me, member = lax.axis_index("dp"), lax.axis_index("tensor")
    core, chip = me % 2, me // 2
    spot = ring_spot(chip, chips)
    ways = (
        (2 * ring_chip((spot + 1) % chips, chips) + core, member),
        (2 * ring_chip((spot + chips - 1) % chips, chips) + core, member),
    )
    peer = (2 * chip + 1 - core, member)
    across = (me, 1 - member)
    partners = [across] + [
        (me + (1 << k) - 2 * (1 << k) * ((me // (1 << k)) % 2), member) for k in range(steps - 1)
    ]
    signal_all(list(ways) + partners)

    half = chips // 2
    width = lefts[0].shape[1] // chips
    mid = width // 2
    starts = []
    at = 0
    for _, right in groups:
        starts.append(at)
        at += rights[right].shape[1]

    def columns(group):
        return pl.ds(starts[group], rights[groups[group][1]].shape[1])

    def piece(group, place, lo=0, hi=width):
        left, right = lefts[groups[group][0]], rights[groups[group][1]]
        at = (place % chips) * width
        return lax.dot_general(
            left[:, at + lo : at + hi], right[...], (COLS_ROWS, ((), ())), preferred_element_type=F32
        )

    def rows_of(way):
        return pl.ds(mid * way, mid)

    def hop(way, step, group):
        if step:
            source, target = arrived.at[way, step - 1], arrived.at[way, step % (half - 1)]
            source, target = source.at[:, columns(group)], target.at[:, columns(group)]
        else:
            source = begin.at[way, :, columns(group)]
            target = arrived.at[way, 0, rows_of(way), columns(group)]
        sems = (way, step, group)
        return send(source, target, send_ring.at[sems], recv_ring.at[sems], ways[way])

    late = [send(late_out[way], late_in.at[way], send_late.at[way], recv_late.at[way], ways[way]) for way in range(2)]
    first = [send(sides.at[i, 1], got_core.at[i], send_first.at[i], recv_first.at[i], peer) for i in range(2)]
    second = [
        send(sent_half.at[i], got_half.at[i], send_second.at[i], recv_second.at[i], across) for i in range(2)
    ]

    def fold_small(step):
        source = small_out if step == 0 else small_in.at[steps + step - 1]
        return send(source, small_in.at[step], send_small.at[step], recv_small.at[step], partners[step])

    def put(ref, value):
        if width % 128:
            ref[...] = value
            return
        for place in range(chips):
            at = pl.multiple_of(ring_chip((spot + place) % chips, chips) * width, 128)
            ref[:, pl.ds(at, width)] = value[:, place * width : (place + 1) * width]

    def fetch(place):
        return [
            pltpu.make_async_copy(
                weight.at[pl.ds(place * width, width), pl.ds(at, buffer.shape[2])],
                buffer.at[place % 2],
                weight_sem.at[number, place % 2],
            )
            for number, (weight, (_, at, _), buffer) in enumerate(zip(weights, side_of, buffers))
        ]

    def side_work():
        for place in range(chips):
            if place + 1 < chips:
                for copy in fetch(place + 1):
                    copy.start()
            for copy in fetch(place):
                copy.wait()
            total = [0.0, 0.0]
            for (side, _, right), buffer in zip(side_of, buffers):
                total[side] = total[side] + lax.dot_general(
                    rights[right][...],
                    buffer[place % 2],
                    (ROWS_ROWS, ((), ())),
                    preferred_element_type=F32,
                )
            for i in range(2):
                sides[i, :, :, :, place * width : (place + 1) * width] = (
                    total[i].astype(BF).reshape(2, 2, middle.shape[0], width)
                )
            yield
        for copy in first:
            copy.start()
        yield
        for i in range(2):
            first[i].wait_recv()
            total = sides[i, 0, 1 - member].astype(F32) + got_core[i, 1 - member].astype(F32)
            sent_half[i] = total.astype(BF)
            second[i].start()
        yield
        total = []
        for i in range(2):
            second[i].wait_recv()
            value = sides[i, 0, member].astype(F32) + got_core[i, member].astype(F32)
            total.append(value + got_half[i].astype(F32))
        put(out_tokens, middle[...] + total[1])
        value = stream[...].astype(F32)
        scale = lax.rsqrt(jnp.mean(value * value, axis=1, keepdims=True) + 1e-06)
        value = value * scale
        gained = jnp.sum(total[0] * value, axis=0, keepdims=True)
        grad = total[0] * gain[...]
        grad = scale * (grad - value * jnp.mean(grad * value, axis=1, keepdims=True))
        put(grad_tokens, grad_middle[...] + grad)
        small_out[...] = small[...]
        lanes = min(width, 128)
        each = width // lanes
        for i, vector in enumerate((gained, mlp_grad[...])):
            for place in range(chips):
                row = (i * chips + ring_chip((spot + place) % chips, chips)) * each
                for part in range(each):
                    at = place * width + part * lanes
                    small_out[pl.ds(row + part, 1), 0:lanes] = vector[:, at : at + lanes]
        fold_small(0).start()
        yield
        for step in range(steps):
            fold_small(step).wait_recv()
            before = small_out if step == 0 else small_in.at[steps + step - 1]
            small_in[steps + step] = before[...] + small_in[step]
            if step + 1 < steps:
                fold_small(step + 1).start()
            yield

    work = side_work()
    for copy in late + fetch(0):
        copy.start()
    for group in range(len(groups)):
        for way in range(2):
            begin[way, :, columns(group)] = piece(group, half, mid * way, mid * way + mid).astype(BF)
            hop(way, 0, group).start()
    for step in range(half - 1):
        place = half - 1 - step
        for group in range(len(groups)):
            next(work, None)
            next(work, None)
            for way in range(2):
                hop(way, step, group).wait_recv()
                value = piece(group, place if way == 0 else -place)
                if step:
                    value = value + arrived[way, step, :, columns(group)].astype(F32)
                    arrived[way, step, :, columns(group)] = value.astype(BF)
                else:
                    lo = mid * way
                    here = value[lo : lo + mid] + arrived[way, 0, rows_of(way), columns(group)].astype(F32)
                    arrived[way, 0, rows_of(way), columns(group)] = here.astype(BF)
                    arrived[way, 0, rows_of(1 - way), columns(group)] = value[
                        mid - lo : width - lo
                    ].astype(BF)
                if step == half - 2 and group == 0:
                    pl.semaphore_wait(free.at[way], 1)
                hop(way, step + 1, group).start()
        if step == min(1, half - 3):
            for way in range(2):
                for group in range(len(groups)):
                    hop(way, 1, group).wait_send()
                pl.semaphore_signal(
                    free.at[way], inc=1, device_id=ways[1 - way], device_id_type=pl.DeviceIdType.MESH
                )
    for _ in work:
        pass
    for step in range(steps):
        fold_small(step).wait_send()
    small_out[...] = small_in[2 * steps - 1]

    rows = width // 2
    finals, used = [], {}
    for group in [len(groups)] + list(range(len(groups))):
        slot = group % 2
        for copy in used.get(slot, ()):
            copy()
        if group == len(groups):
            value = lax.dot_general(
                late_left[...], rights[late_right][...], (COLS_ROWS, ((), ())), preferred_element_type=F32
            )
        else:
            value = piece(group, 0)
        for way in range(2):
            if group == len(groups):
                late[way].wait_recv()
                value = value + late_in[way].astype(F32)
            else:
                hop(way, half - 1, group).wait_recv()
                value = value + arrived[way, 0, :, columns(group)].astype(F32)
        final[slot, :, 0 : value.shape[1]] = value
        used[slot] = []
        for number, (owner, at, size, out) in enumerate(fields):
            if owner == group:
                own = pl.ds(pl.multiple_of(core * rows, rows), rows)
                theirs = pl.ds(pl.multiple_of((1 - core) * rows, rows), rows)
                target = outs[out].at[:, pl.ds(pl.multiple_of(core * size, 128), size)]
                copy = pltpu.make_async_copy(final.at[slot, own, pl.ds(at, size)], target, own_sem.at[number])
                far = send(
                    final.at[slot, theirs, pl.ds(at, size)],
                    target,
                    send_core.at[number],
                    recv_core.at[number],
                    peer,
                )
                copy.start()
                far.start()
                finals.append(far)
                used[slot] += [copy.wait, far.wait_send]
    for slot in used:
        for copy in used[slot]:
            copy()
    for far in finals:
        far.wait_recv()
    for copy in first + second + late:
        copy.wait_send()
    for step in range(half):
        for group in range(len(groups)):
            for way in range(2):
                if step != 1:
                    hop(way, step, group).wait_send()


def collect(grid, lefts, rights, groups, late, fields, sides, tokens_in, small):
    chips = grid.chips
    rows, width = tokens_in[2].shape
    steps = grid.devices.bit_length()
    n = sum(rights[right].shape[1] for _, right in groups)
    widest = max(right.shape[1] for right in rights)
    block = width // chips
    half = chips // 2
    *late, late_right = late
    weights = [weight for _, weight, _, _ in sides]
    side_of = [(side, at, right) for side, _, at, right in sides]
    inputs = [*lefts, *rights, *late, *weights, *tokens_in, small]
    fields = [(group, at, size, number) for number, (group, at, size) in enumerate(fields)]
    outs = [jax.ShapeDtypeStruct((block // 2, 2 * size), F32) for _, _, size, _ in fields]
    tokens = jax.ShapeDtypeStruct((rows, width), F32)
    near = pl.BlockSpec(memory_space=pltpu.VMEM)
    far = pl.BlockSpec(memory_space=pltpu.HBM)
    dma = pltpu.SemaphoreType.DMA
    ring = (2, half, len(groups))
    counts = (len(lefts), len(rights), len(outs), len(sides))
    before = len(lefts) + len(rights) + len(late)
    return pl.pallas_call(
        partial(collect_kernel, chips, steps, groups, late_right, fields, side_of, counts),
        out_shape=outs + [tokens, tokens, jax.ShapeDtypeStruct(small.shape, F32)],
        in_specs=[near] * before + [far] * len(sides) + [near] * (len(tokens_in) + 1),
        out_specs=[far] * len(outs) + [near] * 3,
        scratch_shapes=[
            pltpu.VMEM((2, block // 2, n), BF),
            pltpu.VMEM((2, half - 1, block, n), BF),
            pltpu.VMEM((2,) + late[0].shape, BF),
            pltpu.VMEM((2, block, widest), F32),
            pltpu.VMEM((2, 2, 2, rows, width), BF),
            pltpu.VMEM((2, 2, rows, width), BF),
            pltpu.VMEM((2, rows, width), BF),
            pltpu.VMEM((2, rows, width), BF),
            pltpu.VMEM((2 * steps,) + small.shape, F32),
        ]
        + [pltpu.VMEM((2, block, rights[right].shape[1]), BF) for _, _, right in side_of]
        + [dma(ring), dma(ring)]
        + [dma((len(fields),))] * 3
        + [dma((2,))] * 6
        + [dma((steps,))] * 2
        + [dma((len(sides), 2)), pltpu.SemaphoreType.REGULAR((2,))],
        compiler_params=pltpu.CompilerParams(
            collective_id=3, has_side_effects=True, vmem_limit_bytes=63 << 20
        ),
        name="collect",
    )(*inputs)


def whole_rows(stack):
    return stack.reshape(-1, stack.shape[-1])


def per_device(
    tokens,
    segment_ids,
    norm_gain,
    w_query,
    w_key,
    w_value,
    w_outgate,
    w_beta,
    w_decay,
    conv_query,
    conv_key,
    conv_value,
    decay_log,
    decay_bias,
    out_gain,
    w_output,
    mlp_gain,
    w_gate,
    w_up,
    w_down,
    cotangent,
    *,
    devices,
):
    grid = Grid(devices)
    heads = w_beta.shape[1] // 2
    keyw = w_query.shape[1] // 2
    valw = w_value.shape[1] // 2
    ffw = w_gate.shape[1] // 2
    small = -(-2 * heads // 128) * 128

    filler = jnp.zeros((w_beta.shape[0], small - 2 * heads), BF)
    rates = []
    for at in (0, heads):
        rates += [w_beta[:, at : at + heads], w_decay[:, at : at + heads], filler]
    rates = jnp.concatenate(rates, axis=1)
    groups = [[w_query, w_key, rates], [w_value, w_outgate], [w_output.T], [w_gate, w_up, w_down.T]]
    norm_gain = grid.into(norm_gain)
    mlp_gain = grid.into(mlp_gain)
    shown, shown_cot = tokens[0], cotangent[0]
    if shown.shape[1] // grid.chips % 128:
        shown, shown_cot = grid.into(shown), grid.into(shown_cot)
    *gathered, stream, cot_own, rows_mix, cot_rows = spread(
        grid, groups, 3, shown, shown_cot, norm_gain[None]
    )
    wqk, wvg, wout = [whole_rows(stack) for stack in gathered[:3]]
    rows_mix, cot_rows = [rows.reshape(-1, rows.shape[-1]) for rows in (rows_mix, cot_rows)]
    segments = jnp.concatenate([segment_ids, grid.over_core(segment_ids)], axis=0)

    conv_parts = [
        part_of(conv_query, grid.quarter, keyw, 1),
        part_of(conv_key, grid.quarter, keyw, 1),
        part_of(conv_value, grid.quarter, valw, 1),
        part_of(decay_log, grid.quarter, heads, 0),
        part_of(decay_bias, grid.quarter, heads, 0),
    ]
    pre_qk = dot(rows_mix, wqk)
    pre_vg = dot(rows_mix, wvg)
    lanes = [jnp.pad(part[None], ((0, 0), (0, small - heads))) for part in conv_parts[3:]]
    mixer_in = (pre_qk, pre_vg, segments[:, :, None], segments[:, None, :], *conv_parts[:3], *lanes, out_gain[None])
    heads_out, kept = mixer(heads, mixer_in)
    own_rows = jax.ShapeDtypeStruct(stream.shape, F32)
    mix_part = cols_product(heads_out, wout)
    rows_mlp, middle = trade(
        middle_rows, mix_part, (stream, mlp_gain[None]), [own_rows], "middle", 1
    )
    mlp_full = grid.gather(gathered[3], [(), heads_out, rows_mlp])
    gate_full, up_full, down_full = [mlp_full[:, at : at + ffw] for at in (0, ffw, 2 * ffw)]
    gate = dot(rows_mlp, gate_full)
    upper = dot(rows_mlp, up_full)
    sigmoid_gate = jax.nn.sigmoid(gate)
    hidden = (gate * sigmoid_gate * upper).astype(BF)
    grad_hidden = dot(cot_rows, down_full)
    grad_gate = (grad_hidden * upper * sigmoid_gate * (1.0 + gate * (1.0 - sigmoid_gate))).astype(BF)
    grad_upper = (grad_hidden * gate * sigmoid_gate).astype(BF)
    *late, sent = grid.scatter(cot_rows, hidden)
    back_part = cols_product(grad_gate, gate_full) + cols_product(grad_upper, up_full)
    gain_row = jax.ShapeDtypeStruct((1, stream.shape[1]), F32)
    grad_mixed, grad_middle, grad_mlp_gain = trade(
        middle_grad,
        tied(back_part, sent[0]),
        (cot_own, middle, mlp_gain[None]),
        [own_rows, gain_row],
        "middle_back",
        2,
    )
    grad_heads = tied(dot(grad_mixed, wout), sent[1])
    grad_qk, grad_vg, *core_grads = mixer_back(heads, grad_heads, mixer_in, kept)

    def placed(piece, whole):
        start = grid.quarter * piece.shape[-1]
        return lax.dynamic_update_slice_in_dim(jnp.zeros(whole.shape, F32), piece, start, -1)

    grad_cq, grad_ck, grad_cv, grad_rate, grad_gain = core_grads
    grad_rate = grad_rate[:, heads : 2 * heads]
    width = norm_gain.shape[0]
    lanes = min(width // grid.chips, 128)
    gain_rows = width // lanes
    wholes = (conv_query, conv_key, conv_value, decay_log, decay_bias)
    pieces = [placed(piece, whole) for piece, whole in zip((grad_cq, grad_ck, grad_cv, *grad_rate), wholes)]
    pieces.append(grad_gain)
    packed = jnp.concatenate([piece.reshape(-1) for piece in pieces])
    packed = jnp.pad(packed, (0, (-packed.size) % 1024)).reshape(-1, 128)
    packed = jnp.pad(packed, ((2 * gain_rows, 0), (0, 0)))
    at = 2 * keyw
    *weight_grads, out_tokens, grad_tokens, packed = collect(
        grid,
        [rows_mlp, grad_mixed, rows_mix],
        [grad_gate, grad_upper, grad_vg, heads_out, grad_qk, hidden],
        [(0, 0), (0, 1), (2, 2), (1, 3), (2, 4)],
        [*late, cot_rows[:, : cot_rows.shape[1] // grid.chips], 5],
        [(0, 0, ffw), (1, 0, ffw), (2, 0, valw), (2, valw, valw), (3, 0, valw)]
        + [(4, 0, keyw), (4, keyw, keyw), (4, at, small), (5, 0, ffw)],
        [(0, wvg, 0, 2), (0, wqk, 0, 4), (1, mlp_full, 2 * ffw, 5)],
        [stream, norm_gain[None], middle, grad_middle, grad_mlp_gain],
        packed,
    )
    whole_gate, whole_up, whole_value, whole_outgate, whole_out, whole_query, whole_key, whole_small, whole_down = weight_grads
    if out_tokens.shape[1] // grid.chips % 128:
        out_tokens, grad_tokens = grid.out_of(out_tokens), grid.out_of(grad_tokens)
    whole_beta = jnp.concatenate([whole_small[:, i : i + heads] for i in (0, small)], axis=1)
    whole_decay = jnp.concatenate([whole_small[:, i + heads : i + 2 * heads] for i in (0, small)], axis=1)
    gains = packed[: 2 * gain_rows, :lanes].reshape(2, width)
    packed = packed[2 * gain_rows :].reshape(-1)
    sums = []
    at = 0
    for piece, whole in zip(pieces, wholes + (out_gain,)):
        sums.append(packed[at : at + piece.size].reshape(whole.shape))
        at += piece.size
    return (
        out_tokens[None],
        grad_tokens[None],
        gains[0],
        whole_query,
        whole_key,
        whole_value,
        whole_outgate,
        whole_beta,
        whole_decay,
        *sums,
        whole_out.T,
        gains[1],
        whole_gate,
        whole_up,
        whole_down.T,
    )


def solution(mesh):
    rows = P("dp", "tensor")
    cols = P("tensor", "dp")
    tokens = P("dp", "tensor", None)
    placed = (tokens, P("dp", None), P()) + (rows,) * 6 + (P(),) * 6
    placed = placed + (cols, P(), rows, rows, cols, tokens)
    given = (tokens, tokens, P()) + (rows,) * 6 + (P(),) * 6 + (cols, P(), rows, rows, cols)
    return jax.shard_map(
        partial(per_device, devices=mesh.shape["dp"]),
        mesh=mesh,
        in_specs=placed,
        out_specs=given,
        check_vma=False,
    )
```

```python
from functools import partial
import math

import jax
import jax.numpy as jnp
from jax import lax
from jax.experimental import pallas as pl
from jax.experimental.pallas import tpu as pltpu
from jax.sharding import PartitionSpec as P

HIGH = lax.Precision.HIGH
HIGHEST = lax.Precision.HIGHEST
BF = jnp.bfloat16
F32 = jnp.float32


def scale_rows(values, factor):
    return values * lax.rsqrt(jnp.mean(values * values, axis=-1, keepdims=True) + 1e-06) * factor


def split3(value):
    high = value.astype(BF)
    return high, (value - high.astype(F32)).astype(BF)


def product(left, right, dims):
    dims = (dims, ((), ()))
    total = lax.dot_general(left[0], right[0], dims, preferred_element_type=F32)
    total = total + lax.dot_general(left[0], right[1], dims, preferred_element_type=F32)
    return total + lax.dot_general(left[1], right[0], dims, preferred_element_type=F32)


ROWS_COLS = ((1,), (0,))
ROWS_ROWS = ((1,), (1,))
COLS_ROWS = ((0,), (0,))


def exact_sum(mask, value, dims):
    high, low = split3(value)
    last = (value - high.astype(F32) - low.astype(F32)).astype(BF)
    dims = (dims, ((), ()))
    total = lax.dot_general(mask, last, dims, preferred_element_type=F32)
    total = total + lax.dot_general(mask, low, dims, preferred_element_type=F32)
    return total + lax.dot_general(mask, high, dims, preferred_element_type=F32)


def conv_parts(values, taps, keeping):
    moved = [values] + [pltpu.roll(values, j, 0) * keeping[j] for j in range(1, 4)]
    total = moved[0] * taps[0:1]
    for j in range(1, 4):
        total = total + moved[j] * taps[j : j + 1]
    return moved, total


def conv_back(grad, moved, taps, keeping):
    rows = grad.shape[0]
    total = grad * taps[0:1]
    for j in range(1, 4):
        total = total + pltpu.roll(grad * keeping[j], rows - j, 0) * taps[j : j + 1]
    parts = [jnp.sum(grad * moved[j], axis=0, keepdims=True) for j in range(4)]
    return total, jnp.concatenate(parts, axis=0)


def silu_back(total, gate):
    return gate * (1.0 + total * (1.0 - gate))


def softplus(value):
    return jnp.maximum(value, 0.0) + jnp.log1p(jnp.exp(-jnp.abs(value)))


def block_masks(seg_col, seg_row):
    size = seg_col.shape[0]
    row = lax.broadcasted_iota(jnp.int32, (size, size), 0)
    col = lax.broadcasted_iota(jnp.int32, (size, size), 1)
    masking = ((seg_col == seg_row) & (col <= row)).astype(F32)
    spot = lax.broadcasted_iota(jnp.int32, (size, 1), 0)
    keeping = [None]
    for j in range(1, 4):
        keeping.append(((pltpu.roll(seg_col, j, 0) == seg_col) & (spot >= j)).astype(F32))
    return row, col, masking, keeping


def head_rates(small, log, bias, masking, heads):
    decay_in = pltpu.roll(small, small.shape[1] - heads, 1) + bias
    factor = -jnp.exp(log)
    rates = factor * softplus(decay_in)
    betas = jax.nn.sigmoid(small)
    summed = exact_sum(masking.astype(BF), rates, ROWS_COLS)
    return decay_in, factor, rates, betas, summed


def invert(mixing, row, col):
    size = mixing.shape[0]
    result = jnp.where(row == col, 1.0, 0.0) - jnp.where((row >> 1) == (col >> 1), mixing, 0.0)
    level = 1
    while (1 << level) < size:
        picked = ((row >> (level + 1)) == (col >> (level + 1))) & ((row >> level) != (col >> level))
        part = split3(jnp.where(picked, mixing, 0.0))
        halves = split3(result)
        step = product(halves, part, ROWS_COLS)
        result = result - product(split3(step), halves, ROWS_COLS)
        level += 1
    return result


def unit(values):
    return lax.rsqrt(jnp.sum(values * values, axis=1, keepdims=True) + 1e-06)


def mixer_kernel(heads, qk, vg, seg_col, seg_row, cq, ck, cv, log, bias, gain, *outs):
    heads_out, inverses, all_errors, all_kk, all_qk, all_raw = outs
    keyw, valw = cq.shape[1] // heads, cv.shape[1] // heads
    row, col, masking, keeping = block_masks(seg_col[0], seg_row[0])
    small = qk[:, 2 * heads * keyw :]
    _, _, _, betas, summed = head_rates(small, log[...], bias[...], masking, heads)
    betas_t, summed_t = betas.T, summed.T
    strict = (col < row).astype(F32)
    for h in range(heads):
        at = pl.ds(h * keyw, keyw)
        query = jax.nn.silu(conv_parts(qk[:, at], cq[:, at], keeping)[1])
        query = query * (unit(query) * (1.0 / math.sqrt(keyw)))
        key = jax.nn.silu(
            conv_parts(qk[:, pl.ds((heads + h) * keyw, keyw)], ck[:, at], keeping)[1]
        )
        key = key * unit(key)
        at = pl.ds(h * valw, valw)
        value = jax.nn.silu(conv_parts(vg[:, at], cv[:, at], keeping)[1])
        spread = summed[:, h : h + 1] - summed_t[h : h + 1]
        decays = jnp.exp(spread * masking) * masking * betas_t[h : h + 1]
        keys = split3(key)
        key_key = product(keys, keys, ROWS_ROWS)
        query_key = product(split3(query), keys, ROWS_ROWS)
        inverse = invert(decays * key_key * strict, row, col)
        errors = product(split3(inverse), split3(value), ROWS_COLS)
        raw = product(split3(decays * query_key), split3(errors), ROWS_COLS)
        inverses[0, h] = inverse
        all_errors[0, h] = errors
        all_kk[0, h] = key_key
        all_qk[0, h] = query_key
        all_raw[:, at] = raw
        scaled = raw * lax.rsqrt(jnp.mean(raw * raw, axis=1, keepdims=True) + 1e-05) * gain[...]
        gate = vg[:, pl.ds((heads + h) * valw, valw)]
        heads_out[:, at] = (scaled * jax.nn.silu(gate)).astype(BF)


def mixer_back(heads, grad, inputs, kept, results):
    qk, vg, seg_col, seg_row, cq, ck, cv, log, bias, gain = inputs
    inverses, all_errors, all_kk, all_qk, all_raw = kept
    grad_qk, grad_vg, grad_cq, grad_ck, grad_cv, grad_rate, grad_gain = results
    keyw, valw = cq.shape[1] // heads, cv.shape[1] // heads
    size = qk.shape[0]
    row, col, masking, keeping = block_masks(seg_col[0], seg_row[0])
    small = qk[:, 2 * heads * keyw :]
    decay_in, factor, rates, betas, summed = head_rates(small, log[...], bias[...], masking, heads)
    betas_t, summed_t = betas.T, summed.T
    strict = (col < row).astype(F32)
    lanes = lax.broadcasted_iota(jnp.int32, (1, small.shape[1]), 1)
    spots = lax.broadcasted_iota(jnp.int32, (small.shape[1], 1), 0)
    grad_summed = jnp.zeros_like(small)
    from_cols = jnp.zeros((small.shape[1], size), F32)
    for h in range(heads):
        at = pl.ds(h * valw, valw)
        raw, gate_in = all_raw[:, at], vg[:, pl.ds((heads + h) * valw, valw)]
        gate = jax.nn.sigmoid(gate_in)
        scale = lax.rsqrt(jnp.mean(raw * raw, axis=1, keepdims=True) + 1e-05)
        above = grad[:, at]
        grad_vg[:, pl.ds((heads + h) * valw, valw)] = (
            above * (raw * scale * gain[...]) * silu_back(gate_in, gate)
        ).astype(BF)
        above = above * (gate_in * gate)
        grad_gain[...] += jnp.sum(above * raw * scale, axis=0, keepdims=True)
        above = above * gain[...]
        grad_raw = scale * (above - raw * (scale * scale * jnp.mean(above * raw, axis=1, keepdims=True)))

        spread = summed[:, h : h + 1] - summed_t[h : h + 1]
        plain = jnp.exp(spread * masking) * masking
        decays = plain * betas_t[h : h + 1]
        key_key, query_key = all_kk[0, h] * strict, all_qk[0, h]
        grad_raws, errors = split3(grad_raw), split3(all_errors[0, h])
        grad_reading = product(grad_raws, errors, ROWS_ROWS)
        grad_errors = product(split3(decays * query_key), grad_raws, COLS_ROWS)
        grad_value = product(split3(inverses[0, h]), split3(grad_errors), COLS_ROWS)
        grad_mixing = -product(split3(grad_value), errors, ROWS_ROWS)
        both = (grad_mixing * key_key + grad_reading * query_key) * plain
        grad_beta = jnp.sum(both, axis=0, keepdims=True)
        both = both * betas_t[h : h + 1]
        from_rows = jnp.sum(both, axis=1, keepdims=True)
        grad_summed = grad_summed + jnp.where(lanes == heads + h, from_rows, 0.0)
        from_cols = from_cols + jnp.where(spots == h, grad_beta, 0.0)
        from_cols = from_cols - jnp.where(spots == heads + h, jnp.sum(both, axis=0, keepdims=True), 0.0)

        at = pl.ds(h * keyw, keyw)
        query_moved, query_total = conv_parts(qk[:, at], cq[:, at], keeping)
        query_gate = jax.nn.sigmoid(query_total)
        query = query_total * query_gate
        query_scale = unit(query)
        query = query * query_scale
        key_at = pl.ds((heads + h) * keyw, keyw)
        key_moved, key_total = conv_parts(qk[:, key_at], ck[:, at], keeping)
        key_gate = jax.nn.sigmoid(key_total)
        key = key_total * key_gate
        key_scale = unit(key)
        key = key * key_scale
        keys = split3(key)
        grad_kk = split3(grad_mixing * decays * strict)
        grad_qk_product = split3(grad_reading * (decays * (1.0 / math.sqrt(keyw))))
        grad_query = product(grad_qk_product, keys, ROWS_COLS)
        grad_key = product(grad_qk_product, split3(query), COLS_ROWS)
        grad_key = grad_key + product(grad_kk, keys, ROWS_COLS) + product(grad_kk, keys, COLS_ROWS)

        grad_query = query_scale * (grad_query - query * jnp.sum(grad_query * query, axis=1, keepdims=True))
        grad_query = grad_query * silu_back(query_total, query_gate)
        grad_query, taps = conv_back(grad_query, query_moved, cq[:, at], keeping)
        grad_qk[:, at] = grad_query.astype(BF)
        grad_cq[:, at] += taps
        grad_key = key_scale * (grad_key - key * jnp.sum(grad_key * key, axis=1, keepdims=True))
        grad_key = grad_key * silu_back(key_total, key_gate)
        grad_key, taps = conv_back(grad_key, key_moved, ck[:, at], keeping)
        grad_qk[:, key_at] = grad_key.astype(BF)
        grad_ck[:, at] += taps

        at = pl.ds(h * valw, valw)
        moved, total = conv_parts(vg[:, at], cv[:, at], keeping)
        grad_value = grad_value * silu_back(total, jax.nn.sigmoid(total))
        grad_value, taps = conv_back(grad_value, moved, cv[:, at], keeping)
        grad_vg[:, at] = grad_value.astype(BF)
        grad_cv[:, at] += taps

    from_cols = from_cols.T
    grad_summed = grad_summed + jnp.where(lanes >= heads, from_cols, 0.0)
    grad_rates = exact_sum(masking.astype(BF), grad_summed, COLS_ROWS)
    decay_lanes = (lanes >= heads) & (lanes < 2 * heads)
    shifted = [pltpu.roll(value, heads, 1) for value in (decay_in, rates)]
    grad_decay = grad_rates * pltpu.roll(factor, heads, 1) * jax.nn.sigmoid(shifted[0])
    grad_rate[0:1] += jnp.sum(grad_rates * shifted[1], axis=0, keepdims=True)
    grad_rate[1:2] += jnp.sum(grad_decay, axis=0, keepdims=True)
    grad_small = jnp.where(decay_lanes, grad_decay, from_cols * betas * (1.0 - betas))
    grad_small = jnp.where(lanes < 2 * heads, grad_small, 0.0)
    grad_qk[:, 2 * heads * keyw :] = grad_small.astype(BF)


def mixer_specs(heads, qk, vg, cq, cv, small):
    length = qk.shape[0] // 2

    def by_rows(width):
        return pl.BlockSpec((length, width), lambda s: (s, 0))

    def fixed(*shape):
        return pl.BlockSpec(shape, lambda s: (0,) * len(shape))

    shared = [
        by_rows(qk.shape[1]),
        by_rows(vg.shape[1]),
        pl.BlockSpec((1, length, 1), lambda s: (s, 0, 0)),
        pl.BlockSpec((1, 1, length), lambda s: (s, 0, 0)),
        fixed(*cq.shape),
        fixed(*cq.shape),
        fixed(*cv.shape),
        fixed(1, small),
        fixed(1, small),
        fixed(1, cv.shape[1] // heads),
    ]
    valw = cv.shape[1] // heads
    square = (heads, length, length)
    kept = [square, (heads, length, valw), square, square]
    kept_specs = [pl.BlockSpec((1,) + shape, lambda s: (s, 0, 0, 0)) for shape in kept]
    kept_specs.append(by_rows(cv.shape[1]))
    kept_shapes = [jax.ShapeDtypeStruct((2,) + shape, F32) for shape in kept]
    kept_shapes.append(jax.ShapeDtypeStruct((2 * length, cv.shape[1]), F32))
    return by_rows, fixed, shared, kept_specs, kept_shapes


def mixer(heads, inputs):
    qk, vg, _, _, cq, _, cv, log, _, _ = inputs
    by_rows, _, shared, kept_specs, kept_shapes = mixer_specs(heads, qk, vg, cq, cv, log.shape[1])
    heads_out, *kept = pl.pallas_call(
        partial(mixer_kernel, heads),
        grid=(2,),
        out_shape=[jax.ShapeDtypeStruct((qk.shape[0], cv.shape[1]), BF)] + kept_shapes,
        in_specs=shared,
        out_specs=[by_rows(cv.shape[1])] + kept_specs,
        compiler_params=pltpu.CompilerParams(vmem_limit_bytes=48 << 20),
        name="mixer",
    )(*inputs)
    return heads_out, kept


def rows_product(left, right):
    return lax.dot_general(left, right, (((0,), (0,)), ((), ())), preferred_element_type=F32)


def cols_product(left, right):
    return lax.dot_general(left, right, (((1,), (1,)), ((), ())), preferred_element_type=F32)


def dot(left, right):
    return jnp.dot(left, right, preferred_element_type=F32)


def tied(value, after):
    return lax.optimization_barrier((value, after))[0]


def first_of(flag, own, peer, axis):
    return jnp.concatenate([jnp.where(flag, own, peer), jnp.where(flag, peer, own)], axis=axis)


def part_of(value, index, size, axis):
    return lax.dynamic_slice_in_dim(value, index * size, size, axis)


class Grid:
    def __init__(self, devices):
        self.devices = devices
        self.chips = devices // 2
        me = lax.axis_index("dp")
        self.core = me % 2
        self.spot = ring_spot(me // 2, self.chips)
        self.member = lax.axis_index("tensor")
        self.quarter = 2 * self.member + self.core

    def swap(self, value, offset):
        pairs = [(at, at ^ offset) for at in range(self.devices)]
        return lax.ppermute(value, "dp", pairs)

    def over_core(self, value):
        return self.swap(value, 1)

    def over_tensor(self, value):
        return lax.ppermute(value, "tensor", [(0, 1), (1, 0)])

    def shift(self, value, step):
        pairs = []
        for at in range(self.devices):
            spot = (ring_spot(at // 2, self.chips) + step) % self.chips
            pairs.append((at, 2 * ring_chip(spot, self.chips) + at % 2))
        return lax.ppermute(value, "dp", pairs)

    def into(self, value):
        width = value.shape[-1] // self.chips
        blocks = []
        for place in range(self.chips):
            chip = ring_chip((self.spot + place) % self.chips, self.chips)
            blocks.append(part_of(value, chip, width, -1))
        return jnp.concatenate(blocks, axis=-1)

    def out_of(self, value):
        width = value.shape[-1] // self.chips
        blocks = []
        for chip in range(self.chips):
            place = (ring_spot(chip, self.chips) - self.spot + self.chips) % self.chips
            blocks.append(part_of(value, place, width, -1))
        return jnp.concatenate(blocks, axis=-1)

    def gather_rows(self, own):
        whole = first_of(self.member == 0, own, self.over_tensor(own), 0)
        return jnp.concatenate([whole, self.over_core(whole)], axis=0)

    def scatter_rows(self, value):
        half = value.shape[0] // 2
        whole = value[:half] + self.over_core(value[half:])
        half //= 2
        theirs = part_of(whole, 1 - self.member, half, 0)
        peer = self.over_tensor(theirs.astype(BF)).astype(F32)
        return part_of(whole, self.member, half, 0) + peer


def ring_spot(chip, chips):
    line, pair = chip // 2, chip % 2
    return line * (1 - pair) + (chips - 1 - line) * pair


def ring_chip(spot, chips):
    pair = spot // (chips // 2)
    return 2 * (spot * (1 - pair) + (chips - 1 - spot) * pair) + pair


def signal_all(devices):
    barrier = pltpu.get_barrier_semaphore()
    for device in devices:
        pl.semaphore_signal(barrier, inc=1, device_id=device, device_id_type=pl.DeviceIdType.MESH)
    pl.semaphore_wait(barrier, len(devices))


def send(source, target, send_sem, recv_sem, device):
    return pltpu.make_async_remote_copy(
        src_ref=source,
        dst_ref=target,
        send_sem=send_sem,
        recv_sem=recv_sem,
        device_id=device,
        device_id_type=pl.DeviceIdType.MESH,
    )


def staged(sources, targets, sem):
    copies = [pltpu.make_async_copy(*pair, sem.at[i]) for i, pair in enumerate(zip(sources, targets))]
    pending = set(range(len(copies)))
    for copy in copies:
        copy.start()

    def ready(*numbers):
        for i in sorted(pending.intersection(numbers)):
            copies[i].wait()
            pending.remove(i)

    return ready


def spread_kernel(chips, layout, ringed, *refs):
    count = len(layout)
    totals = 1 + max(out for out, _, _ in layout)
    sources, (tokens, cot, gain) = refs[:count], refs[count : count + 3]
    outs = refs[count + 3 : count + 3 + totals]
    stream, cot_own, rows_mix, rows_cot = refs[count + 3 + totals : count + 7 + totals]
    normed, near_sem, send_core, recv_core, send_right, recv_right, send_left, recv_left = refs[
        count + 7 + totals : count + 15 + totals
    ]
    own_sem, send_half, recv_half, send_whole, recv_whole = refs[count + 15 + totals :]
    me, member = lax.axis_index("dp"), lax.axis_index("tensor")
    core, chip = me % 2, me // 2
    spot = ring_spot(chip, chips)
    right = (2 * ring_chip((spot + 1) % chips, chips) + core, member)
    left = (2 * ring_chip((spot + chips - 1) % chips, chips) + core, member)
    peer = (2 * chip + 1 - core, member)
    across = (me, 1 - member)
    signal_all((right, left, peer, across))

    def home(out):
        return outs[out].at[0] if out < ringed else outs[out]

    near, far = [], []
    for i, (out, at, width) in enumerate(layout):
        rows = sources[i].shape[0]
        place = home(out).at[pl.ds(pl.multiple_of(core * rows, rows), rows), pl.ds(at, width)]
        mine = sources[i].at[:, pl.ds(pl.multiple_of(core * width, 128), width)]
        theirs = sources[i].at[:, pl.ds(pl.multiple_of((1 - core) * width, 128), width)]
        near.append(pltpu.make_async_copy(mine, place, near_sem.at[i]))
        far.append(send(theirs, place, send_core.at[i], recv_core.at[i], peer))

    def trade_halves(outs_now):
        for i, item in enumerate(layout):
            if item[0] in outs_now:
                far[i].start()
                near[i].start()

    trade_halves(range(2))

    def hop(out, step, way):
        last = step == chips // 2
        ref = outs[out]
        mid = ref.shape[1] // 2
        if way > 0:
            at, to, device, sends, receives = -(step - 1) % chips, chips - step, right, send_right, recv_right
            rows = pl.ds(0, mid)
        else:
            at, to, device, sends, receives = step - 1, step, left, send_left, recv_left
            rows = pl.ds(mid, mid)
        source, target = ref.at[at], ref.at[to]
        if last:
            source, target = source.at[rows], target.at[rows]
        return send(source, target, sends.at[out, step - 1], receives.at[out, step - 1], device)

    started, own = [], []
    pairs = ((normed, rows_mix), (cot_own, rows_cot))
    halves = [
        send(value, rows.at[0, member], send_half.at[i], recv_half.at[i], across)
        for i, (value, rows) in enumerate(pairs)
    ]
    wholes = [
        send(rows.at[0], rows.at[1], send_whole.at[i], recv_whole.at[i], peer)
        for i, (_, rows) in enumerate(pairs)
    ]
    for step in range(1, chips // 2 + 1):
        for out in range(ringed):
            if step == 1:
                for i, item in enumerate(layout):
                    if item[0] == out:
                        near[i].wait()
                        far[i].wait()
            for way in (1, -1):
                if step > 1:
                    hop(out, step - 1, way).wait_recv()
                copy = hop(out, step, way)
                copy.start()
                started.append(copy)
            if step == 1:
                trade_halves((out + 2,) if out + 2 < ringed else ())
        if step == 1:
            trade_halves(range(ringed, totals))
            width = tokens.shape[1] // chips
            aligned = width % 128 == 0
            squares = jnp.zeros((tokens.shape[0], 1), F32)
            for place in range(chips):
                to = pl.ds(place * width, width)
                at = to
                if aligned:
                    at = ring_chip((spot + place) % chips, chips) * width
                    at = pl.ds(pl.multiple_of(at, 128), width)
                stream[:, to] = tokens[:, at]
                cot_own[:, to] = cot[:, at]
                block = stream[:, to].astype(F32)
                squares = squares + jnp.sum(block * block, axis=1, keepdims=True)
            scale = lax.rsqrt(squares / tokens.shape[1] + 1e-06)
            normed[...] = (stream[...].astype(F32) * scale * gain[...]).astype(BF)
            for i, (value, rows) in enumerate(pairs):
                own.append(pltpu.make_async_copy(value, rows.at[0, member], own_sem.at[i]))
                own[-1].start()
                halves[i].start()
        if step == 2:
            for i in range(2):
                own[i].wait()
                halves[i].wait()
                wholes[i].start()
    for i, item in enumerate(layout):
        if item[0] >= ringed:
            near[i].wait()
            far[i].wait()
    for copy in wholes:
        copy.wait()
    for out in range(ringed):
        for way in (1, -1):
            hop(out, chips // 2, way).wait_recv()
    for copy in started:
        copy.wait_send()


def spread(grid, groups, ringed, tokens, cot, gain):
    chips = grid.chips
    sources, layout, shapes = [], [], []
    for out, group in enumerate(groups):
        at = 0
        for shard in group:
            width = shard.shape[1] // 2
            layout.append((out, at, width))
            sources.append(shard)
            at += width
        rows = 2 * group[0].shape[0]
        shapes.append(jax.ShapeDtypeStruct(((chips,) if out < ringed else ()) + (rows, at), BF))
    dma = pltpu.SemaphoreType.DMA
    hops = (ringed, chips // 2)
    anywhere = pl.BlockSpec(memory_space=pltpu.HBM)
    near = pl.BlockSpec(memory_space=pltpu.VMEM)
    own = jax.ShapeDtypeStruct(tokens.shape, BF)
    rows = jax.ShapeDtypeStruct((2, 2) + tokens.shape, BF)
    return pl.pallas_call(
        partial(spread_kernel, chips, layout, ringed),
        out_shape=shapes + [own, own, rows, rows],
        in_specs=[anywhere] * len(sources) + [near] * 3,
        out_specs=[anywhere] * len(shapes) + [near] * 2 + [anywhere] * 2,
        scratch_shapes=[pltpu.VMEM(tokens.shape, BF)]
        + [dma((len(sources),))] * 3
        + [dma(hops)] * 4
        + [dma((2,))] * 5,
        compiler_params=pltpu.CompilerParams(
            collective_id=0, has_side_effects=True, vmem_limit_bytes=62 << 20
        ),
        name="spread",
    )(*sources, tokens, cot, gain)


PARTS = 2


def exchange(part, rows_out, buffers, sems, compute):
    got_core, sent_half, got_half, own = buffers
    me, member = lax.axis_index("dp"), lax.axis_index("tensor")
    peer = (me + 1 - 2 * (me % 2), member)
    across = (me, 1 - member)
    count = part.shape[2] // PARTS

    def chunk(k):
        return pl.ds(k * count, count)

    def copy(kind, k, source, target, device):
        return send(source, target, sems[2 * kind].at[k], sems[2 * kind + 1].at[k], device)

    first = [copy(0, k, part.at[1, :, chunk(k)], got_core.at[:, chunk(k)], peer) for k in range(PARTS)]
    second = [copy(1, k, sent_half.at[chunk(k)], got_half.at[chunk(k)], across) for k in range(PARTS)]
    third = [
        copy(2, k, own.at[chunk(k)], rows_out.at[0, member, chunk(k)], across) for k in range(PARTS)
    ]
    fourth = [
        copy(3, k, own.at[chunk(k)], rows_out.at[1, member, chunk(k)], peer) for k in range(PARTS)
    ]
    fifth = [
        copy(4, k, rows_out.at[0, 1 - member, chunk(k)], rows_out.at[1, 1 - member, chunk(k)], peer)
        for k in range(PARTS)
    ]
    for k in range(PARTS):
        first[k].start()
    for k in range(PARTS):
        first[k].wait_recv()
        total = part[0, 1 - member, chunk(k)] + got_core[1 - member, chunk(k)]
        sent_half[chunk(k)] = total.astype(BF)
        second[k].start()
    for k in range(PARTS):
        second[k].wait_recv()
        total = part[0, member, chunk(k)] + got_core[member, chunk(k)] + got_half[chunk(k)].astype(F32)
        value = compute(k, chunk(k), total).astype(BF)
        own[chunk(k)] = value
        third[k].start()
        fourth[k].start()
        rows_out[0, member, chunk(k)] = value
    for k in range(PARTS):
        third[k].wait_recv()
        fifth[k].start()
    for k in range(PARTS):
        fourth[k].wait_recv()
        fifth[k].wait_recv()
    for copies in (first, second, third, fourth, fifth):
        for one in copies:
            one.wait_send()


def exchange_scratch(rows, width):
    return [
        pltpu.VMEM((2, rows, width), F32),
        pltpu.VMEM((rows, width), BF),
        pltpu.VMEM((rows, width), BF),
        pltpu.VMEM((rows, width), BF),
    ] + [pltpu.SemaphoreType.DMA((PARTS,))] * 10


def middle_kernel(part, stream, gain, rows_out, middle, *scratch):
    me, member = lax.axis_index("dp"), lax.axis_index("tensor")
    signal_all(((me + 1 - 2 * (me % 2), member), (me, 1 - member)))

    def compute(k, rows, mixed):
        value = stream[rows].astype(F32) + mixed
        middle[rows] = value
        return value * lax.rsqrt(jnp.mean(value * value, axis=1, keepdims=True) + 1e-06) * gain[...]

    exchange(part, rows_out, scratch[:4], scratch[4:], compute)


def middle_rows(part, stream, gain):
    rows, width = stream.shape
    near = pl.BlockSpec(memory_space=pltpu.VMEM)
    gathered, middle = pl.pallas_call(
        middle_kernel,
        out_shape=[
            jax.ShapeDtypeStruct((2, 2, rows, width), BF),
            jax.ShapeDtypeStruct((rows, width), F32),
        ],
        in_specs=[near] * 3,
        out_specs=[near] * 2,
        scratch_shapes=exchange_scratch(rows, width),
        compiler_params=pltpu.CompilerParams(
            collective_id=1, has_side_effects=True, vmem_limit_bytes=32 << 20
        ),
        name="middle",
    )(part.reshape(2, 2, rows, width), stream, gain)
    return gathered.reshape(4 * rows, width), middle


def turn_kernel(chips, heads, ffw, early, *refs):
    refs = list(refs)

    def take(count):
        taken, refs[:] = refs[:count], refs[count:]
        return taken

    part, cot, middle, gain, rows_cot, rows_mlp, hidden, grad_gate, begun = take(9)
    small_inputs, later = take(8), take(8)
    rows_out, grad_middle, grad_gain, late = take(4)
    results = take(7)
    grad_heads, going, arrived = take(3)
    here_now, (later_sem,) = take(8), take(1)
    send_ring, recv_ring = take(2)
    me, member = lax.axis_index("dp"), lax.axis_index("tensor")
    core, chip = me % 2, me // 2
    spot = ring_spot(chip, chips)
    ways = (
        (2 * ring_chip((spot + 1) % chips, chips) + core, member),
        (2 * ring_chip((spot + chips - 1) % chips, chips) + core, member),
    )
    signal_all((*ways, (me + 1 - 2 * core, member), (me, 1 - member)))
    half = chips // 2
    width = rows_cot.shape[1] // chips
    mid = width // 2

    def total(way, place, step):
        at = (place if way == 0 else -place) % chips * width
        value = []
        for left, right, size in ((rows_cot, hidden, ffw), (rows_mlp, grad_gate, early)):
            value.append(
                lax.dot_general(
                    left[:, at : at + width],
                    right[:, 0:size],
                    (COLS_ROWS, ((), ())),
                    preferred_element_type=F32,
                )
            )
        value = jnp.concatenate(value, axis=1)
        if step:
            return (value + arrived[way, step - 1].astype(F32)).astype(BF)
        lo = mid * way
        here = value[lo : lo + mid] + begun[way].astype(F32)
        rest = value[mid - lo : width - lo]
        return jnp.concatenate([here, rest] if way == 0 else [rest, here], axis=0).astype(BF)

    def hop(way, step):
        sems = (way, step)
        source = arrived.at[way, step - 1] if step else going.at[way]
        return send(source, arrived.at[sems], send_ring.at[sems], recv_ring.at[sems], ways[way])

    def next_hop(step):
        for way in range(2):
            if step:
                hop(way, step - 1).wait_recv()
            value = total(way, half - 1 - step, step)
            if step == half - 2:
                late[way] = value
                continue
            if step:
                arrived[way, step - 1] = value
            else:
                going[way] = value
            hop(way, step).start()

    def compute(k, rows, grad):
        value = middle[rows]
        scale = lax.rsqrt(jnp.mean(value * value, axis=1, keepdims=True) + 1e-06)
        unit_value = value * scale
        gained = jnp.sum(grad * unit_value, axis=0, keepdims=True)
        grad_gain[...] = gained if k == 0 else grad_gain[...] + gained
        grad = grad * gain[...]
        grad = scale * (grad - unit_value * jnp.mean(grad * unit_value, axis=1, keepdims=True))
        grad = grad + cot[rows].astype(F32)
        grad_middle[rows] = grad
        return grad

    ready = staged(later, here_now, later_sem)
    wout, *kept = here_now[:6]
    inputs = here_now[6:] + small_inputs
    next_hop(0)
    exchange(part, rows_out, refs[:4], refs[4:], compute)
    ready(*range(8))
    for step in range(1, half - 2):
        next_hop(step)
    for ref in results[2:]:
        ref[...] = jnp.zeros_like(ref)
    length = inputs[0].shape[0] // 2

    @pl.loop(0, 2)
    def _(s):
        at = pl.multiple_of(s * length, length)
        here = pl.ds(at, length)
        for m in range(2):
            grad_heads[pl.ds(at + m * (length // 2), length // 2)] = jnp.dot(
                rows_out[s, m], wout[...], preferred_element_type=F32
            )
        mixer_back(
            heads,
            grad_heads.at[here],
            [ref.at[here] for ref in inputs[:2]] + [ref.at[pl.ds(s, 1)] for ref in inputs[2:4]] + inputs[4:],
            [ref.at[pl.ds(s, 1)] for ref in kept[:4]] + [kept[4].at[here]],
            [ref.at[here] for ref in results[:2]] + results[2:],
        )

    next_hop(half - 2)
    for step in range(half - 2):
        for way in range(2):
            hop(way, step).wait_send()


def turn(grid, heads, early, part, cot, middle, gain, wout, rows_cot, rows_mlp, hidden, grad_gate, begun, inputs, kept):
    chips = grid.chips
    rows, width = middle.shape
    block, half = width // chips, chips // 2
    ffw = hidden.shape[1]
    n = ffw + early
    qk, vg, _, _, cq, ck, cv, log, _, out_gain = inputs
    near = pl.BlockSpec(memory_space=pltpu.VMEM)
    dma = pltpu.SemaphoreType.DMA
    sums = [cq.shape, ck.shape, cv.shape, (2, log.shape[1]), out_gain.shape]
    operands = (part.reshape(2, 2, rows, width), cot, middle, gain, rows_cot, rows_mlp, hidden, grad_gate, begun)
    operands = (*operands, *inputs[2:])
    later = (wout, *kept, *inputs[:2])
    gathered, *rest = pl.pallas_call(
        partial(turn_kernel, chips, heads, ffw, early),
        out_shape=[
            jax.ShapeDtypeStruct((2, 2, rows, width), BF),
            jax.ShapeDtypeStruct((rows, width), F32),
            jax.ShapeDtypeStruct((1, width), F32),
            jax.ShapeDtypeStruct((2, block, n), BF),
            jax.ShapeDtypeStruct(qk.shape, BF),
            jax.ShapeDtypeStruct(vg.shape, BF),
        ]
        + [jax.ShapeDtypeStruct(shape, F32) for shape in sums],
        in_specs=[near] * len(operands) + [pl.BlockSpec(memory_space=pltpu.HBM)] * len(later),
        out_specs=[near] * (6 + len(sums)),
        scratch_shapes=[
            pltpu.VMEM((4 * rows, cv.shape[1]), F32),
            pltpu.VMEM((2, block, n), BF),
            pltpu.VMEM((2, half - 2, block, n), BF),
            *[pltpu.VMEM(value.shape, value.dtype) for value in later],
            dma((len(later),)),
            dma((2, half - 2)),
            dma((2, half - 2)),
        ]
        + exchange_scratch(rows, width),
        compiler_params=pltpu.CompilerParams(
            collective_id=2, has_side_effects=True, vmem_limit_bytes=62 << 20
        ),
        name="turn",
    )(*operands, *later)
    return gathered.reshape(4 * rows, width), *rest


def mlp_kernel(chips, ffw, early, *refs):
    rows, cot, own, right_1, left_1, right_2, left_2 = refs[:7]
    hidden, grad_gate, grad_upper, back, ahead, begun = refs[7:13]
    weights, sums, begin, load_sem, send_ring, recv_ring, send_begin, recv_begin = refs[13:]
    me, member = lax.axis_index("dp"), lax.axis_index("tensor")
    core, chip = me % 2, me // 2
    spot = ring_spot(chip, chips)
    ways = (
        (2 * ring_chip((spot + 1) % chips, chips) + core, member),
        (2 * ring_chip((spot + chips - 1) % chips, chips) + core, member),
    )
    signal_all(ways)
    half = chips // 2
    block = own.shape[0]
    mid = block // 2

    def spots(place, lo=0, hi=block):
        return pl.ds((place % chips) * block + lo, hi - lo)

    def hop(way, step):
        place, to = (1 - step, -step) if way == 0 else (step - 1, step)
        lo, hi = (0, block) if step < half else (mid * way, mid * way + mid)
        if step == 3:
            source = (right_2, left_2)[way].at[pl.ds(lo, hi - lo)]
        else:
            source = weights.at[spots(place, lo, hi)]
        sems = (way, step - 3)
        return send(source, weights.at[spots(to, lo, hi)], send_ring.at[sems], recv_ring.at[sems], ways[way])

    for way in range(2):
        hop(way, 3).start()
    loads = []
    for number, (place, source) in enumerate(((0, own), (1, left_1), (2, left_2), (-2, right_2), (-1, right_1))):
        loads.append(pltpu.make_async_copy(source, weights.at[spots(place)], load_sem.at[number]))
        loads[-1].start()

    tile = ffw // 2

    def add(lo, hi, first):
        inner = slice((lo % chips) * block, (lo % chips + hi - lo) * block)
        for at in range(0, 3 * ffw, tile):
            left = rows if at < 2 * ffw else cot
            value = jnp.dot(left[:, inner], weights[inner, at : at + tile], preferred_element_type=F32)
            sums[:, at : at + tile] = value if first else sums[:, at : at + tile] + value

    for copy in loads[:3]:
        copy.wait()
    add(0, 3, True)
    for copy in loads[3:]:
        copy.wait()
    add(-2, 0, False)
    for step in range(3, half):
        for way in range(2):
            hop(way, step).wait_recv()
            hop(way, step + 1).start()
        add(step, step + 1, False)
        add(-step, 1 - step, False)
    for way in range(2):
        hop(way, half).wait_recv()
    add(half, half + 1, False)

    for at in range(0, ffw, 128):
        gate, upper = sums[:, at : at + 128], sums[:, ffw + at : ffw + at + 128]
        grad = sums[:, 2 * ffw + at : 2 * ffw + at + 128]
        open_gate = jax.nn.sigmoid(gate)
        passed = gate * open_gate
        hidden[:, at : at + 128] = (passed * upper).astype(BF)
        grad_gate[:, at : at + 128] = (grad * upper * silu_back(gate, open_gate)).astype(BF)
        grad_upper[:, at : at + 128] = (grad * passed).astype(BF)

    starts = []
    for way in range(2):
        lo = half * block + mid * way
        for left, right, at, size in ((cot, hidden, 0, ffw), (rows, grad_gate, ffw, early)):
            begin[way, :, at : at + size] = lax.dot_general(
                left[:, lo : lo + mid],
                right[:, 0:size],
                (COLS_ROWS, ((), ())),
                preferred_element_type=F32,
            ).astype(BF)
        starts.append(send(begin.at[way], begun.at[way], send_begin.at[way], recv_begin.at[way], ways[way]))
        starts[-1].start()
    for place in range(chips):
        inner = slice(place * block, (place + 1) * block)
        value = lax.dot_general(
            grad_gate[...], weights[inner, 0:ffw], (ROWS_ROWS, ((), ())), preferred_element_type=F32
        )
        back[:, inner] = value + lax.dot_general(
            grad_upper[...], weights[inner, ffw : 2 * ffw], (ROWS_ROWS, ((), ())), preferred_element_type=F32
        )
        ahead[:, inner] = lax.dot_general(
            hidden[...], weights[inner, 2 * ffw :], (ROWS_ROWS, ((), ())), preferred_element_type=F32
        ).astype(BF)
    for copy in starts:
        copy.wait()
    for step in range(3, half + 1):
        for way in range(2):
            hop(way, step).wait_send()


def mlp(grid, rows, cot, chunks, ffw, early):
    chips = grid.chips
    count, width = rows.shape
    block, n = chunks[0].shape
    half = chips // 2
    near = pl.BlockSpec(memory_space=pltpu.VMEM)
    far = pl.BlockSpec(memory_space=pltpu.HBM)
    dma = pltpu.SemaphoreType.DMA
    inner = jax.ShapeDtypeStruct((count, ffw), BF)
    return pl.pallas_call(
        partial(mlp_kernel, chips, ffw, early),
        out_shape=[
            inner,
            inner,
            inner,
            jax.ShapeDtypeStruct((count, width), F32),
            jax.ShapeDtypeStruct((count, width), BF),
            jax.ShapeDtypeStruct((2, block // 2, ffw + early), BF),
        ],
        in_specs=[near] * 2 + [far] * 5,
        out_specs=[near] * 6,
        scratch_shapes=[
            pltpu.VMEM((chips * block, n), BF),
            pltpu.VMEM((count, n), F32),
            pltpu.VMEM((2, block // 2, ffw + early), BF),
            dma((5,)),
            dma((2, half - 2)),
            dma((2, half - 2)),
            dma((2,)),
            dma((2,)),
        ],
        compiler_params=pltpu.CompilerParams(
            collective_id=4, has_side_effects=True, vmem_limit_bytes=56 << 20
        ),
        name="mlp",
    )(rows, cot, *chunks)


def collect_kernel(chips, steps, groups, late_parts, fields, side_of, counts, *refs):
    n_left, n_right, n_out, n_side = counts
    refs = list(refs)

    def take(count):
        taken, refs[:] = refs[:count], refs[count:]
        return taken

    far = take(n_left + n_right)
    late_out, late_left = take(2)
    weights = take(n_side)
    ahead_far, *far_tokens = take(4)
    gain, mlp_grad, small = take(3)
    outs = take(n_out)
    out_tokens, grad_tokens, small_out = take(3)
    begin, arrived, late_in, final, back, got_core, sent_half, got_half, small_in = take(9)
    buffers = take(n_side)
    near, near_tokens = take(n_left + n_right), take(4)
    lefts, rights = near[:n_left], near[n_left:]
    ahead, stream, middle, grad_middle = near_tokens
    (far_sem,) = take(1)
    send_ring, recv_ring, own_sem, send_core, recv_core, send_late, recv_late = take(7)
    send_first, recv_first, send_second, recv_second, send_small, recv_small, weight_sem, free = take(8)
    me, member = lax.axis_index("dp"), lax.axis_index("tensor")
    core, chip = me % 2, me // 2
    spot = ring_spot(chip, chips)
    ways = (
        (2 * ring_chip((spot + 1) % chips, chips) + core, member),
        (2 * ring_chip((spot + chips - 1) % chips, chips) + core, member),
    )
    peer = (2 * chip + 1 - core, member)
    across = (me, 1 - member)
    partners = [across] + [
        (me + (1 << k) - 2 * (1 << k) * ((me // (1 << k)) % 2), member) for k in range(steps - 1)
    ]
    signal_all(list(ways) + partners)

    half = chips // 2
    width = lefts[0].shape[1] // chips
    mid = width // 2
    starts = []
    at = 0
    for _, right in groups:
        starts.append(at)
        at += rights[right].shape[1]

    def columns(group):
        return pl.ds(starts[group], rights[groups[group][1]].shape[1])

    def piece(group, place, lo=0, hi=width):
        left, right = lefts[groups[group][0]], rights[groups[group][1]]
        at = (place % chips) * width
        return lax.dot_general(
            left[:, at + lo : at + hi], right[...], (COLS_ROWS, ((), ())), preferred_element_type=F32
        )

    def rows_of(way):
        return pl.ds(mid * way, mid)

    def hop(way, step, group):
        if step:
            source, target = arrived.at[way, step - 1], arrived.at[way, step % (half - 1)]
            source, target = source.at[:, columns(group)], target.at[:, columns(group)]
        else:
            source = begin.at[way, :, columns(group)]
            target = arrived.at[way, 0, rows_of(way), columns(group)]
        sems = (way, step, group)
        return send(source, target, send_ring.at[sems], recv_ring.at[sems], ways[way])

    late = [send(late_out.at[way], late_in.at[way], send_late.at[way], recv_late.at[way], ways[way]) for way in range(2)]
    sides = (back, ahead)
    first = [
        send(value.at[1], got_core.at[i], send_first.at[i], recv_first.at[i], peer)
        for i, value in enumerate((back, ahead_far))
    ]
    second = [
        send(sent_half.at[i], got_half.at[i], send_second.at[i], recv_second.at[i], across) for i in range(2)
    ]

    def fold_small(step):
        source = small_out if step == 0 else small_in.at[steps + step - 1]
        return send(source, small_in.at[step], send_small.at[step], recv_small.at[step], partners[step])

    def put(ref, value):
        if width % 128:
            ref[...] = value
            return
        for place in range(chips):
            at = pl.multiple_of(ring_chip((spot + place) % chips, chips) * width, 128)
            ref[:, pl.ds(at, width)] = value[:, place * width : (place + 1) * width]

    def fetch(place):
        return [
            pltpu.make_async_copy(
                weight.at[pl.ds(place * width, width), pl.ds(at, buffer.shape[2])],
                buffer.at[place % 2],
                weight_sem.at[number, place % 2],
            )
            for number, (weight, (at, _), buffer) in enumerate(zip(weights, side_of, buffers))
        ]

    def side_work():
        for place in range(chips):
            if place + 1 < chips:
                for copy in fetch(place + 1):
                    copy.start()
            for copy in fetch(place):
                copy.wait()
            total = 0.0
            for (_, right), buffer in zip(side_of, buffers):
                total = total + lax.dot_general(
                    rights[right][...],
                    buffer[place % 2],
                    (ROWS_ROWS, ((), ())),
                    preferred_element_type=F32,
                )
            back[:, :, :, place * width : (place + 1) * width] = (
                total.astype(BF).reshape(2, 2, middle.shape[0], width)
            )
            yield
        for copy in first:
            copy.start()
        yield
        ready(*range(n_left + n_right, n_left + n_right + 4))
        for i in range(2):
            first[i].wait_recv()
            total = sides[i][0, 1 - member].astype(F32) + got_core[i, 1 - member].astype(F32)
            sent_half[i] = total.astype(BF)
            second[i].start()
        yield
        total = []
        for i in range(2):
            second[i].wait_recv()
            value = sides[i][0, member].astype(F32) + got_core[i, member].astype(F32)
            total.append(value + got_half[i].astype(F32))
        put(out_tokens, middle[...] + total[1])
        value = stream[...].astype(F32)
        scale = lax.rsqrt(jnp.mean(value * value, axis=1, keepdims=True) + 1e-06)
        value = value * scale
        gained = jnp.sum(total[0] * value, axis=0, keepdims=True)
        grad = total[0] * gain[...]
        grad = scale * (grad - value * jnp.mean(grad * value, axis=1, keepdims=True))
        put(grad_tokens, grad_middle[...] + grad)
        small_out[...] = small[...]
        lanes = min(width, 128)
        each = width // lanes
        for i, vector in enumerate((gained, mlp_grad[...])):
            for place in range(chips):
                row = (i * chips + ring_chip((spot + place) % chips, chips)) * each
                for part in range(each):
                    at = place * width + part * lanes
                    small_out[pl.ds(row + part, 1), 0:lanes] = vector[:, at : at + lanes]
        fold_small(0).start()
        yield
        for step in range(steps):
            fold_small(step).wait_recv()
            before = small_out if step == 0 else small_in.at[steps + step - 1]
            small_in[steps + step] = before[...] + small_in[step]
            if step + 1 < steps:
                fold_small(step + 1).start()
            yield

    work = side_work()
    ready = staged([*far, ahead_far.at[pl.ds(0, 1)], *far_tokens], near + near_tokens, far_sem)
    for copy in late + fetch(0):
        copy.start()
    for group in range(len(groups)):
        ready(groups[group][0], n_left + groups[group][1])
        for way in range(2):
            begin[way, :, columns(group)] = piece(group, half, mid * way, mid * way + mid).astype(BF)
            hop(way, 0, group).start()
    ready(*range(n_left + n_right))
    for step in range(half - 1):
        place = half - 1 - step
        for group in range(len(groups)):
            next(work, None)
            next(work, None)
            for way in range(2):
                hop(way, step, group).wait_recv()
                value = piece(group, place if way == 0 else -place)
                if step:
                    value = value + arrived[way, step, :, columns(group)].astype(F32)
                    arrived[way, step, :, columns(group)] = value.astype(BF)
                else:
                    lo = mid * way
                    here = value[lo : lo + mid] + arrived[way, 0, rows_of(way), columns(group)].astype(F32)
                    arrived[way, 0, rows_of(way), columns(group)] = here.astype(BF)
                    arrived[way, 0, rows_of(1 - way), columns(group)] = value[
                        mid - lo : width - lo
                    ].astype(BF)
                if step == half - 2 and group == 0:
                    pl.semaphore_wait(free.at[way], 1)
                hop(way, step + 1, group).start()
        if step == min(1, half - 3):
            for way in range(2):
                for group in range(len(groups)):
                    hop(way, 1, group).wait_send()
                pl.semaphore_signal(
                    free.at[way], inc=1, device_id=ways[1 - way], device_id_type=pl.DeviceIdType.MESH
                )
    for _ in work:
        pass
    for step in range(steps):
        fold_small(step).wait_send()
    small_out[...] = small_in[2 * steps - 1]

    rows = width // 2
    finals, used = [], {}
    for group in [len(groups)] + list(range(len(groups))):
        slot = group % 2
        for copy in used.get(slot, ()):
            copy()
        if group == len(groups):
            value = []
            for left, right in late_parts:
                left = late_left if left is None else lefts[left]
                value.append(
                    lax.dot_general(
                        left[:, 0:width],
                        rights[right][...],
                        (COLS_ROWS, ((), ())),
                        preferred_element_type=F32,
                    )
                )
            value = jnp.concatenate(value, axis=1)
        else:
            value = piece(group, 0)
        for way in range(2):
            if group == len(groups):
                late[way].wait_recv()
                value = value + late_in[way].astype(F32)
            else:
                hop(way, half - 1, group).wait_recv()
                value = value + arrived[way, 0, :, columns(group)].astype(F32)
        final[slot, :, 0 : value.shape[1]] = value
        used[slot] = []
        for number, (owner, at, out, to, whole, size) in enumerate(fields):
            if owner == group:
                own = pl.ds(pl.multiple_of(core * rows, rows), rows)
                theirs = pl.ds(pl.multiple_of((1 - core) * rows, rows), rows)
                target = outs[out].at[:, pl.ds(pl.multiple_of(core * whole + to, 128), size)]
                copy = pltpu.make_async_copy(final.at[slot, own, pl.ds(at, size)], target, own_sem.at[number])
                far = send(
                    final.at[slot, theirs, pl.ds(at, size)],
                    target,
                    send_core.at[number],
                    recv_core.at[number],
                    peer,
                )
                copy.start()
                far.start()
                finals.append(far)
                used[slot] += [copy.wait, far.wait_send]
    for slot in used:
        for copy in used[slot]:
            copy()
    for far in finals:
        far.wait_recv()
    for copy in first + second + late:
        copy.wait_send()
    for step in range(half):
        for group in range(len(groups)):
            for way in range(2):
                if step != 1:
                    hop(way, step, group).wait_send()


def collect(grid, lefts, rights, groups, late, fields, sides, ahead, tokens_in, small):
    chips = grid.chips
    rows, width = tokens_in[2].shape
    steps = grid.devices.bit_length()
    n = sum(rights[right].shape[1] for _, right in groups)
    widest = max([rights[right].shape[1] for _, right in groups] + [late[0].shape[2]])
    block = width // chips
    half = chips // 2
    *late, late_parts = late
    weights = [weight for weight, _, _ in sides]
    side_of = [(at, right) for _, at, right in sides]
    stream, gain, middle, grad_middle, mlp_grad = tokens_in
    tokens_in = [ahead.reshape(2, 2, rows, width), stream, middle, grad_middle]
    inputs = [*lefts, *rights, *late, *weights, *tokens_in, gain, mlp_grad, small]
    wholes = {}
    for _, _, out, _, whole in fields:
        wholes[out] = whole
    outs = [jax.ShapeDtypeStruct((block // 2, 2 * wholes[out]), F32) for out in range(len(wholes))]
    ends = [sum(rights[right].shape[1] for _, right in late_parts)]
    ends = [rights[right].shape[1] for _, right in groups] + ends
    sized = []
    for i, (group, at, out, to, whole) in enumerate(fields):
        starts = [other[1] for other in fields if other[0] == group and other[1] > at]
        sized.append((group, at, out, to, whole, min(starts + [ends[group]]) - at))
    fields = sized
    tokens = jax.ShapeDtypeStruct((rows, width), F32)
    near = pl.BlockSpec(memory_space=pltpu.VMEM)
    far = pl.BlockSpec(memory_space=pltpu.HBM)
    dma = pltpu.SemaphoreType.DMA
    ring = (2, half, len(groups))
    counts = (len(lefts), len(rights), len(outs), len(sides))
    held = [value.shape for value in (*lefts, *rights)]
    return pl.pallas_call(
        partial(collect_kernel, chips, steps, groups, late_parts, fields, side_of, counts),
        out_shape=outs + [tokens, tokens, jax.ShapeDtypeStruct(small.shape, F32)],
        in_specs=[far] * (len(held) + 1) + [near] + [far] * (len(sides) + 4) + [near] * 3,
        out_specs=[far] * len(outs) + [near] * 3,
        scratch_shapes=[
            pltpu.VMEM((2, block // 2, n), BF),
            pltpu.VMEM((2, half - 1, block, n), BF),
            pltpu.VMEM(late[0].shape, BF),
            pltpu.VMEM((2, block, widest), F32),
            pltpu.VMEM((2, 2, rows, width), BF),
            pltpu.VMEM((2, 2, rows, width), BF),
            pltpu.VMEM((2, rows, width), BF),
            pltpu.VMEM((2, rows, width), BF),
            pltpu.VMEM((2 * steps,) + small.shape, F32),
        ]
        + [pltpu.VMEM((2, block, rights[right].shape[1]), BF) for _, right in side_of]
        + [pltpu.VMEM(shape, BF) for shape in held]
        + [
            pltpu.VMEM((1, 2, rows, width), BF),
            pltpu.VMEM((rows, width), BF),
            pltpu.VMEM((rows, width), F32),
            pltpu.VMEM((rows, width), F32),
            dma((len(held) + 4,)),
        ]
        + [dma(ring), dma(ring)]
        + [dma((len(fields),))] * 3
        + [dma((2,))] * 6
        + [dma((steps,))] * 2
        + [dma((len(sides), 2)), pltpu.SemaphoreType.REGULAR((2,))],
        compiler_params=pltpu.CompilerParams(
            collective_id=3, has_side_effects=True, vmem_limit_bytes=63 << 20
        ),
        name="collect",
    )(*inputs)


def whole_rows(stack):
    return stack.reshape(-1, stack.shape[-1])


def per_device(
    tokens,
    segment_ids,
    norm_gain,
    w_query,
    w_key,
    w_value,
    w_outgate,
    w_beta,
    w_decay,
    conv_query,
    conv_key,
    conv_value,
    decay_log,
    decay_bias,
    out_gain,
    w_output,
    mlp_gain,
    w_gate,
    w_up,
    w_down,
    cotangent,
    *,
    devices,
):
    grid = Grid(devices)
    heads = w_beta.shape[1] // 2
    keyw = w_query.shape[1] // 2
    valw = w_value.shape[1] // 2
    ffw = w_gate.shape[1] // 2
    small = -(-2 * heads // 128) * 128

    filler = jnp.zeros((w_beta.shape[0], small - 2 * heads), BF)
    rates = []
    for at in (0, heads):
        rates += [w_beta[:, at : at + heads], w_decay[:, at : at + heads], filler]
    rates = jnp.concatenate(rates, axis=1)
    groups = [[w_query, w_key, rates], [w_value, w_outgate], [w_output.T], [w_gate, w_up, w_down.T]]
    norm_gain = grid.into(norm_gain)
    mlp_gain = grid.into(mlp_gain)
    shown, shown_cot = tokens[0], cotangent[0]
    if shown.shape[1] // grid.chips % 128:
        shown, shown_cot = grid.into(shown), grid.into(shown_cot)
    *gathered, stream, cot_own, rows_mix, cot_rows = spread(
        grid, groups, 3, shown, shown_cot, norm_gain[None]
    )
    wqk, wvg, wout = [whole_rows(stack) for stack in gathered[:3]]
    rows_mix, cot_rows = [rows.reshape(-1, rows.shape[-1]) for rows in (rows_mix, cot_rows)]
    segments = jnp.concatenate([segment_ids, grid.over_core(segment_ids)], axis=0)

    conv_parts = [
        part_of(conv_query, grid.quarter, keyw, 1),
        part_of(conv_key, grid.quarter, keyw, 1),
        part_of(conv_value, grid.quarter, valw, 1),
        part_of(decay_log, grid.quarter, heads, 0),
        part_of(decay_bias, grid.quarter, heads, 0),
    ]
    pre_qk = dot(rows_mix, wqk)
    pre_vg = dot(rows_mix, wvg)
    lanes = [jnp.pad(part[None], ((0, 0), (0, small - heads))) for part in conv_parts[3:]]
    mixer_in = (pre_qk, pre_vg, segments[:, :, None], segments[:, None, :], *conv_parts[:3], *lanes, out_gain[None])
    heads_out, kept = mixer(heads, mixer_in)
    rows_mlp, middle = middle_rows(cols_product(heads_out, wout), stream, mlp_gain[None])
    chunk = gathered[3]
    chunks = [chunk, grid.shift(chunk, 1), grid.shift(chunk, -1)]
    pair = tied((chunks[1], chunks[2]), heads_out)
    chunks += [grid.shift(pair[0], 1), grid.shift(pair[1], -1)]
    early = ffw // 256 * 128
    hidden, grad_gate, grad_upper, back_part, ahead, begun = mlp(grid, rows_mlp, cot_rows, chunks, ffw, early)
    gate_parts = [grad_gate[:, :early], grad_gate[:, early:]]
    grad_mixed, grad_middle, grad_mlp_gain, late, grad_qk, grad_vg, *core_grads = turn(
        grid,
        heads,
        early,
        back_part,
        cot_own,
        middle,
        mlp_gain[None],
        wout,
        cot_rows,
        rows_mlp,
        hidden,
        grad_gate,
        begun,
        mixer_in,
        kept,
    )

    def placed(piece, whole):
        start = grid.quarter * piece.shape[-1]
        return lax.dynamic_update_slice_in_dim(jnp.zeros(whole.shape, F32), piece, start, -1)

    grad_cq, grad_ck, grad_cv, grad_rate, grad_gain = core_grads
    grad_rate = grad_rate[:, heads : 2 * heads]
    width = norm_gain.shape[0]
    lanes = min(width // grid.chips, 128)
    gain_rows = width // lanes
    wholes = (conv_query, conv_key, conv_value, decay_log, decay_bias)
    pieces = [placed(piece, whole) for piece, whole in zip((grad_cq, grad_ck, grad_cv, *grad_rate), wholes)]
    pieces.append(grad_gain)
    packed = jnp.concatenate([piece.reshape(-1) for piece in pieces])
    packed = jnp.pad(packed, (0, (-packed.size) % 1024)).reshape(-1, 128)
    packed = jnp.pad(packed, ((2 * gain_rows, 0), (0, 0)))
    at = 2 * keyw
    *weight_grads, out_tokens, grad_tokens, packed = collect(
        grid,
        [rows_mlp, grad_mixed, rows_mix],
        [gate_parts[1], grad_upper, grad_vg, heads_out, grad_qk, hidden, gate_parts[0]],
        [(0, 1), (2, 2), (0, 0), (1, 3), (2, 4)],
        [late, cot_rows[:, : cot_rows.shape[1] // grid.chips], [(None, 5), (0, 6)]],
        [
            (2, 0, 0, early, ffw),
            (5, ffw, 0, 0, ffw),
            (0, 0, 1, 0, ffw),
            (1, 0, 2, 0, valw),
            (1, valw, 3, 0, valw),
            (3, 0, 4, 0, valw),
            (4, 0, 5, 0, keyw),
            (4, keyw, 6, 0, keyw),
            (4, at, 7, 0, small),
            (5, 0, 8, 0, ffw),
        ],
        [(wvg, 0, 2), (wqk, 0, 4)],
        ahead,
        [stream, norm_gain[None], middle, grad_middle, grad_mlp_gain],
        packed,
    )
    whole_gate, whole_up, whole_value, whole_outgate, whole_out, whole_query, whole_key, whole_small, whole_down = weight_grads
    if out_tokens.shape[1] // grid.chips % 128:
        out_tokens, grad_tokens = grid.out_of(out_tokens), grid.out_of(grad_tokens)
    whole_beta = jnp.concatenate([whole_small[:, i : i + heads] for i in (0, small)], axis=1)
    whole_decay = jnp.concatenate([whole_small[:, i + heads : i + 2 * heads] for i in (0, small)], axis=1)
    gains = packed[: 2 * gain_rows, :lanes].reshape(2, width)
    packed = packed[2 * gain_rows :].reshape(-1)
    sums = []
    at = 0
    for piece, whole in zip(pieces, wholes + (out_gain,)):
        sums.append(packed[at : at + piece.size].reshape(whole.shape))
        at += piece.size
    return (
        out_tokens[None],
        grad_tokens[None],
        gains[0],
        whole_query,
        whole_key,
        whole_value,
        whole_outgate,
        whole_beta,
        whole_decay,
        *sums,
        whole_out.T,
        gains[1],
        whole_gate,
        whole_up,
        whole_down.T,
    )


def solution(mesh):
    rows = P("dp", "tensor")
    cols = P("tensor", "dp")
    tokens = P("dp", "tensor", None)
    placed = (tokens, P("dp", None), P()) + (rows,) * 6 + (P(),) * 6
    placed = placed + (cols, P(), rows, rows, cols, tokens)
    given = (tokens, tokens, P()) + (rows,) * 6 + (P(),) * 6 + (cols, P(), rows, rows, cols)
    return jax.shard_map(
        partial(per_device, devices=mesh.shape["dp"]),
        mesh=mesh,
        in_specs=placed,
        out_specs=given,
        check_vma=False,
    )
```

```python
from functools import partial
import math

import jax
import jax.numpy as jnp
from jax import lax
from jax.experimental import pallas as pl
from jax.experimental.pallas import tpu as pltpu
from jax.sharding import PartitionSpec as P

HIGH = lax.Precision.HIGH
HIGHEST = lax.Precision.HIGHEST
BF = jnp.bfloat16
F32 = jnp.float32


def scale_rows(values, factor):
    return values * lax.rsqrt(jnp.mean(values * values, axis=-1, keepdims=True) + 1e-06) * factor


def split3(value):
    high = value.astype(BF)
    return high, (value - high.astype(F32)).astype(BF)


def product(left, right, dims):
    dims = (dims, ((), ()))
    total = lax.dot_general(left[0], right[0], dims, preferred_element_type=F32)
    total = total + lax.dot_general(left[0], right[1], dims, preferred_element_type=F32)
    return total + lax.dot_general(left[1], right[0], dims, preferred_element_type=F32)


ROWS_COLS = ((1,), (0,))
ROWS_ROWS = ((1,), (1,))
COLS_ROWS = ((0,), (0,))


def exact_sum(mask, value, dims):
    high, low = split3(value)
    last = (value - high.astype(F32) - low.astype(F32)).astype(BF)
    dims = (dims, ((), ()))
    total = lax.dot_general(mask, last, dims, preferred_element_type=F32)
    total = total + lax.dot_general(mask, low, dims, preferred_element_type=F32)
    return total + lax.dot_general(mask, high, dims, preferred_element_type=F32)


def conv_parts(values, taps, keeping):
    moved = [values] + [pltpu.roll(values, j, 0) * keeping[j] for j in range(1, 4)]
    total = moved[0] * taps[0:1]
    for j in range(1, 4):
        total = total + moved[j] * taps[j : j + 1]
    return moved, total


def conv_back(grad, moved, taps, keeping):
    rows = grad.shape[0]
    total = grad * taps[0:1]
    for j in range(1, 4):
        total = total + pltpu.roll(grad * keeping[j], rows - j, 0) * taps[j : j + 1]
    parts = [jnp.sum(grad * moved[j], axis=0, keepdims=True) for j in range(4)]
    return total, jnp.concatenate(parts, axis=0)


def silu_back(total, gate):
    return gate * (1.0 + total * (1.0 - gate))


def softplus(value):
    return jnp.maximum(value, 0.0) + jnp.log1p(jnp.exp(-jnp.abs(value)))


def block_masks(seg_col, seg_row):
    size = seg_col.shape[0]
    row = lax.broadcasted_iota(jnp.int32, (size, size), 0)
    col = lax.broadcasted_iota(jnp.int32, (size, size), 1)
    masking = ((seg_col == seg_row) & (col <= row)).astype(F32)
    spot = lax.broadcasted_iota(jnp.int32, (size, 1), 0)
    keeping = [None]
    for j in range(1, 4):
        keeping.append(((pltpu.roll(seg_col, j, 0) == seg_col) & (spot >= j)).astype(F32))
    return row, col, masking, keeping


def head_rates(small, log, bias, masking, heads):
    decay_in = pltpu.roll(small, small.shape[1] - heads, 1) + bias
    factor = -jnp.exp(log)
    rates = factor * softplus(decay_in)
    betas = jax.nn.sigmoid(small)
    summed = exact_sum(masking.astype(BF), rates, ROWS_COLS)
    return decay_in, factor, rates, betas, summed


def invert(mixing, row, col):
    size = mixing.shape[0]
    result = jnp.where(row == col, 1.0, 0.0) - jnp.where((row >> 1) == (col >> 1), mixing, 0.0)
    level = 1
    while (1 << level) < size:
        picked = ((row >> (level + 1)) == (col >> (level + 1))) & ((row >> level) != (col >> level))
        part = split3(jnp.where(picked, mixing, 0.0))
        halves = split3(result)
        step = product(halves, part, ROWS_COLS)
        result = result - product(split3(step), halves, ROWS_COLS)
        level += 1
    return result


def unit(values):
    return lax.rsqrt(jnp.sum(values * values, axis=1, keepdims=True) + 1e-06)


def mixer_kernel(heads, qk, vg, seg_col, seg_row, cq, ck, cv, log, bias, gain, *outs):
    heads_out, inverses, all_errors, all_kk, all_qk, all_raw = outs
    keyw, valw = cq.shape[1] // heads, cv.shape[1] // heads
    row, col, masking, keeping = block_masks(seg_col[0], seg_row[0])
    small = qk[:, 2 * heads * keyw :]
    _, _, _, betas, summed = head_rates(small, log[...], bias[...], masking, heads)
    betas_t, summed_t = betas.T, summed.T
    strict = (col < row).astype(F32)
    for h in range(heads):
        at = pl.ds(h * keyw, keyw)
        query = jax.nn.silu(conv_parts(qk[:, at], cq[:, at], keeping)[1])
        query = query * (unit(query) * (1.0 / math.sqrt(keyw)))
        key = jax.nn.silu(
            conv_parts(qk[:, pl.ds((heads + h) * keyw, keyw)], ck[:, at], keeping)[1]
        )
        key = key * unit(key)
        at = pl.ds(h * valw, valw)
        value = jax.nn.silu(conv_parts(vg[:, at], cv[:, at], keeping)[1])
        spread = summed[:, h : h + 1] - summed_t[h : h + 1]
        decays = jnp.exp(spread * masking) * masking * betas_t[h : h + 1]
        keys = split3(key)
        key_key = product(keys, keys, ROWS_ROWS)
        query_key = product(split3(query), keys, ROWS_ROWS)
        inverse = invert(decays * key_key * strict, row, col)
        errors = product(split3(inverse), split3(value), ROWS_COLS)
        raw = product(split3(decays * query_key), split3(errors), ROWS_COLS)
        inverses[0, h] = inverse
        all_errors[0, h] = errors
        all_kk[0, h] = key_key
        all_qk[0, h] = query_key
        all_raw[:, at] = raw
        scaled = raw * lax.rsqrt(jnp.mean(raw * raw, axis=1, keepdims=True) + 1e-05) * gain[...]
        gate = vg[:, pl.ds((heads + h) * valw, valw)]
        heads_out[:, at] = (scaled * jax.nn.silu(gate)).astype(BF)


def mixer_back(heads, grad, inputs, kept, results):
    qk, vg, seg_col, seg_row, cq, ck, cv, log, bias, gain = inputs
    inverses, all_errors, all_kk, all_qk, all_raw = kept
    grad_qk, grad_vg, grad_cq, grad_ck, grad_cv, grad_rate, grad_gain = results
    keyw, valw = cq.shape[1] // heads, cv.shape[1] // heads
    size = qk.shape[0]
    row, col, masking, keeping = block_masks(seg_col[0], seg_row[0])
    small = qk[:, 2 * heads * keyw :]
    decay_in, factor, rates, betas, summed = head_rates(small, log[...], bias[...], masking, heads)
    betas_t, summed_t = betas.T, summed.T
    strict = (col < row).astype(F32)
    lanes = lax.broadcasted_iota(jnp.int32, (1, small.shape[1]), 1)
    spots = lax.broadcasted_iota(jnp.int32, (small.shape[1], 1), 0)
    grad_summed = jnp.zeros_like(small)
    from_cols = jnp.zeros((small.shape[1], size), F32)
    for h in range(heads):
        at = pl.ds(h * valw, valw)
        raw, gate_in = all_raw[:, at], vg[:, pl.ds((heads + h) * valw, valw)]
        gate = jax.nn.sigmoid(gate_in)
        scale = lax.rsqrt(jnp.mean(raw * raw, axis=1, keepdims=True) + 1e-05)
        above = grad[:, at]
        grad_vg[:, pl.ds((heads + h) * valw, valw)] = (
            above * (raw * scale * gain[...]) * silu_back(gate_in, gate)
        ).astype(BF)
        above = above * (gate_in * gate)
        grad_gain[...] += jnp.sum(above * raw * scale, axis=0, keepdims=True)
        above = above * gain[...]
        grad_raw = scale * (above - raw * (scale * scale * jnp.mean(above * raw, axis=1, keepdims=True)))

        spread = summed[:, h : h + 1] - summed_t[h : h + 1]
        plain = jnp.exp(spread * masking) * masking
        decays = plain * betas_t[h : h + 1]
        key_key, query_key = all_kk[0, h] * strict, all_qk[0, h]
        grad_raws, errors = split3(grad_raw), split3(all_errors[0, h])
        grad_reading = product(grad_raws, errors, ROWS_ROWS)
        grad_errors = product(split3(decays * query_key), grad_raws, COLS_ROWS)
        grad_value = product(split3(inverses[0, h]), split3(grad_errors), COLS_ROWS)
        grad_mixing = -product(split3(grad_value), errors, ROWS_ROWS)
        both = (grad_mixing * key_key + grad_reading * query_key) * plain
        grad_beta = jnp.sum(both, axis=0, keepdims=True)
        both = both * betas_t[h : h + 1]
        from_rows = jnp.sum(both, axis=1, keepdims=True)
        grad_summed = grad_summed + jnp.where(lanes == heads + h, from_rows, 0.0)
        from_cols = from_cols + jnp.where(spots == h, grad_beta, 0.0)
        from_cols = from_cols - jnp.where(spots == heads + h, jnp.sum(both, axis=0, keepdims=True), 0.0)

        at = pl.ds(h * keyw, keyw)
        query_moved, query_total = conv_parts(qk[:, at], cq[:, at], keeping)
        query_gate = jax.nn.sigmoid(query_total)
        query = query_total * query_gate
        query_scale = unit(query)
        query = query * query_scale
        key_at = pl.ds((heads + h) * keyw, keyw)
        key_moved, key_total = conv_parts(qk[:, key_at], ck[:, at], keeping)
        key_gate = jax.nn.sigmoid(key_total)
        key = key_total * key_gate
        key_scale = unit(key)
        key = key * key_scale
        keys = split3(key)
        grad_kk = split3(grad_mixing * decays * strict)
        grad_qk_product = split3(grad_reading * (decays * (1.0 / math.sqrt(keyw))))
        grad_query = product(grad_qk_product, keys, ROWS_COLS)
        grad_key = product(grad_qk_product, split3(query), COLS_ROWS)
        grad_key = grad_key + product(grad_kk, keys, ROWS_COLS) + product(grad_kk, keys, COLS_ROWS)

        grad_query = query_scale * (grad_query - query * jnp.sum(grad_query * query, axis=1, keepdims=True))
        grad_query = grad_query * silu_back(query_total, query_gate)
        grad_query, taps = conv_back(grad_query, query_moved, cq[:, at], keeping)
        grad_qk[:, at] = grad_query.astype(BF)
        grad_cq[:, at] += taps
        grad_key = key_scale * (grad_key - key * jnp.sum(grad_key * key, axis=1, keepdims=True))
        grad_key = grad_key * silu_back(key_total, key_gate)
        grad_key, taps = conv_back(grad_key, key_moved, ck[:, at], keeping)
        grad_qk[:, key_at] = grad_key.astype(BF)
        grad_ck[:, at] += taps

        at = pl.ds(h * valw, valw)
        moved, total = conv_parts(vg[:, at], cv[:, at], keeping)
        grad_value = grad_value * silu_back(total, jax.nn.sigmoid(total))
        grad_value, taps = conv_back(grad_value, moved, cv[:, at], keeping)
        grad_vg[:, at] = grad_value.astype(BF)
        grad_cv[:, at] += taps

    from_cols = from_cols.T
    grad_summed = grad_summed + jnp.where(lanes >= heads, from_cols, 0.0)
    grad_rates = exact_sum(masking.astype(BF), grad_summed, COLS_ROWS)
    decay_lanes = (lanes >= heads) & (lanes < 2 * heads)
    shifted = [pltpu.roll(value, heads, 1) for value in (decay_in, rates)]
    grad_decay = grad_rates * pltpu.roll(factor, heads, 1) * jax.nn.sigmoid(shifted[0])
    grad_rate[0:1] += jnp.sum(grad_rates * shifted[1], axis=0, keepdims=True)
    grad_rate[1:2] += jnp.sum(grad_decay, axis=0, keepdims=True)
    grad_small = jnp.where(decay_lanes, grad_decay, from_cols * betas * (1.0 - betas))
    grad_small = jnp.where(lanes < 2 * heads, grad_small, 0.0)
    grad_qk[:, 2 * heads * keyw :] = grad_small.astype(BF)


def mixer_specs(heads, qk, vg, cq, cv, small):
    length = qk.shape[0] // 2

    def by_rows(width):
        return pl.BlockSpec((length, width), lambda s: (s, 0))

    def fixed(*shape):
        return pl.BlockSpec(shape, lambda s: (0,) * len(shape))

    shared = [
        by_rows(qk.shape[1]),
        by_rows(vg.shape[1]),
        pl.BlockSpec((1, length, 1), lambda s: (s, 0, 0)),
        pl.BlockSpec((1, 1, length), lambda s: (s, 0, 0)),
        fixed(*cq.shape),
        fixed(*cq.shape),
        fixed(*cv.shape),
        fixed(1, small),
        fixed(1, small),
        fixed(1, cv.shape[1] // heads),
    ]
    valw = cv.shape[1] // heads
    square = (heads, length, length)
    kept = [square, (heads, length, valw), square, square]
    kept_specs = [pl.BlockSpec((1,) + shape, lambda s: (s, 0, 0, 0)) for shape in kept]
    kept_specs.append(by_rows(cv.shape[1]))
    kept_shapes = [jax.ShapeDtypeStruct((2,) + shape, F32) for shape in kept]
    kept_shapes.append(jax.ShapeDtypeStruct((2 * length, cv.shape[1]), F32))
    return by_rows, fixed, shared, kept_specs, kept_shapes


def mixer(heads, inputs):
    qk, vg, _, _, cq, _, cv, log, _, _ = inputs
    by_rows, _, shared, kept_specs, kept_shapes = mixer_specs(heads, qk, vg, cq, cv, log.shape[1])
    heads_out, *kept = pl.pallas_call(
        partial(mixer_kernel, heads),
        grid=(2,),
        out_shape=[jax.ShapeDtypeStruct((qk.shape[0], cv.shape[1]), BF)] + kept_shapes,
        in_specs=shared,
        out_specs=[by_rows(cv.shape[1])] + kept_specs,
        compiler_params=pltpu.CompilerParams(vmem_limit_bytes=48 << 20),
        name="mixer",
    )(*inputs)
    return heads_out, kept


def rows_product(left, right):
    return lax.dot_general(left, right, (((0,), (0,)), ((), ())), preferred_element_type=F32)


def cols_product(left, right):
    return lax.dot_general(left, right, (((1,), (1,)), ((), ())), preferred_element_type=F32)


def dot(left, right):
    return jnp.dot(left, right, preferred_element_type=F32)


def tied(value, after):
    return lax.optimization_barrier((value, after))[0]


def first_of(flag, own, peer, axis):
    return jnp.concatenate([jnp.where(flag, own, peer), jnp.where(flag, peer, own)], axis=axis)


def part_of(value, index, size, axis):
    return lax.dynamic_slice_in_dim(value, index * size, size, axis)


class Grid:
    def __init__(self, devices):
        self.devices = devices
        self.chips = devices // 2
        me = lax.axis_index("dp")
        self.core = me % 2
        self.spot = ring_spot(me // 2, self.chips)
        self.member = lax.axis_index("tensor")
        self.quarter = 2 * self.member + self.core

    def swap(self, value, offset):
        pairs = [(at, at ^ offset) for at in range(self.devices)]
        return lax.ppermute(value, "dp", pairs)

    def over_core(self, value):
        return self.swap(value, 1)

    def over_tensor(self, value):
        return lax.ppermute(value, "tensor", [(0, 1), (1, 0)])

    def shift(self, value, step):
        pairs = []
        for at in range(self.devices):
            spot = (ring_spot(at // 2, self.chips) + step) % self.chips
            pairs.append((at, 2 * ring_chip(spot, self.chips) + at % 2))
        return lax.ppermute(value, "dp", pairs)

    def into(self, value):
        width = value.shape[-1] // self.chips
        blocks = []
        for place in range(self.chips):
            chip = ring_chip((self.spot + place) % self.chips, self.chips)
            blocks.append(part_of(value, chip, width, -1))
        return jnp.concatenate(blocks, axis=-1)

    def out_of(self, value):
        width = value.shape[-1] // self.chips
        blocks = []
        for chip in range(self.chips):
            place = (ring_spot(chip, self.chips) - self.spot + self.chips) % self.chips
            blocks.append(part_of(value, place, width, -1))
        return jnp.concatenate(blocks, axis=-1)

    def gather_rows(self, own):
        whole = first_of(self.member == 0, own, self.over_tensor(own), 0)
        return jnp.concatenate([whole, self.over_core(whole)], axis=0)

    def scatter_rows(self, value):
        half = value.shape[0] // 2
        whole = value[:half] + self.over_core(value[half:])
        half //= 2
        theirs = part_of(whole, 1 - self.member, half, 0)
        peer = self.over_tensor(theirs.astype(BF)).astype(F32)
        return part_of(whole, self.member, half, 0) + peer


def ring_spot(chip, chips):
    line, pair = chip // 2, chip % 2
    return line * (1 - pair) + (chips - 1 - line) * pair


def ring_chip(spot, chips):
    pair = spot // (chips // 2)
    return 2 * (spot * (1 - pair) + (chips - 1 - spot) * pair) + pair


def signal_all(devices):
    barrier = pltpu.get_barrier_semaphore()
    for device in devices:
        pl.semaphore_signal(barrier, inc=1, device_id=device, device_id_type=pl.DeviceIdType.MESH)
    pl.semaphore_wait(barrier, len(devices))


def send(source, target, send_sem, recv_sem, device):
    return pltpu.make_async_remote_copy(
        src_ref=source,
        dst_ref=target,
        send_sem=send_sem,
        recv_sem=recv_sem,
        device_id=device,
        device_id_type=pl.DeviceIdType.MESH,
    )


def staged(sources, targets, sem):
    copies = [pltpu.make_async_copy(*pair, sem.at[i]) for i, pair in enumerate(zip(sources, targets))]
    pending = set(range(len(copies)))
    for copy in copies:
        copy.start()

    def ready(*numbers):
        for i in sorted(pending.intersection(numbers)):
            copies[i].wait()
            pending.remove(i)

    return ready


def spread_kernel(chips, layout, ringed, *refs):
    count = len(layout)
    totals = 1 + max(item[0] for item in layout)
    sources, (tokens, cot, gain, gain_mlp) = refs[:count], refs[count : count + 4]
    refs = refs[count + 4 :]
    outs = refs[:totals]
    stream, cot_own, own_gain, own_gain_mlp, rows_mix, rows_cot = refs[totals : totals + 6]
    refs = refs[totals + 6 :]
    normed, near_sem, send_core, recv_core, send_right, recv_right, send_left, recv_left = refs[:8]
    own_sem, send_half, recv_half, send_whole, recv_whole, *turned = refs[8:]
    me, member = lax.axis_index("dp"), lax.axis_index("tensor")
    core, chip = me % 2, me // 2
    spot = ring_spot(chip, chips)
    right = (2 * ring_chip((spot + 1) % chips, chips) + core, member)
    left = (2 * ring_chip((spot + chips - 1) % chips, chips) + core, member)
    peer = (2 * chip + 1 - core, member)
    across = (me, 1 - member)
    signal_all((right, left, peer, across))

    def home(out):
        return outs[out].at[0] if out < ringed else outs[out]

    near, far = [], []
    given = list(sources)
    turned = [(i, target) for i, target in zip([i for i, item in enumerate(layout) if item[3]], turned)]
    sources = list(sources)
    for i, target in turned:
        sources[i] = target
    for i, (out, at, width, _) in enumerate(layout):
        rows = sources[i].shape[0]
        place = home(out).at[pl.ds(pl.multiple_of(core * rows, rows), rows), pl.ds(at, width)]
        mine = sources[i].at[:, pl.ds(pl.multiple_of(core * width, 128), width)]
        theirs = sources[i].at[:, pl.ds(pl.multiple_of((1 - core) * width, 128), width)]
        near.append(pltpu.make_async_copy(mine, place, near_sem.at[i]))
        far.append(send(theirs, place, send_core.at[i], recv_core.at[i], peer))

    def trade_halves(outs_now):
        for i, target in turned:
            if layout[i][0] in outs_now:
                target[...] = given[i][...].T
        for i, item in enumerate(layout):
            if item[0] in outs_now:
                far[i].start()
                near[i].start()

    trade_halves(range(2))

    def hop(out, step, way):
        last = step == chips // 2
        ref = outs[out]
        mid = ref.shape[1] // 2
        if way > 0:
            at, to, device, sends, receives = -(step - 1) % chips, chips - step, right, send_right, recv_right
            rows = pl.ds(0, mid)
        else:
            at, to, device, sends, receives = step - 1, step, left, send_left, recv_left
            rows = pl.ds(mid, mid)
        source, target = ref.at[at], ref.at[to]
        if last:
            source, target = source.at[rows], target.at[rows]
        return send(source, target, sends.at[out, step - 1], receives.at[out, step - 1], device)

    started, own = [], []
    pairs = ((normed, rows_mix), (cot_own, rows_cot))
    halves = [
        send(value, rows.at[0, member], send_half.at[i], recv_half.at[i], across)
        for i, (value, rows) in enumerate(pairs)
    ]
    wholes = [
        send(rows.at[0], rows.at[1], send_whole.at[i], recv_whole.at[i], peer)
        for i, (_, rows) in enumerate(pairs)
    ]
    for step in range(1, chips // 2 + 1):
        for out in range(ringed):
            if step == 1:
                for i, item in enumerate(layout):
                    if item[0] == out:
                        near[i].wait()
                        far[i].wait()
            for way in (1, -1):
                if step > 1:
                    hop(out, step - 1, way).wait_recv()
                copy = hop(out, step, way)
                copy.start()
                started.append(copy)
            if step == 1:
                trade_halves((out + 2,) if out + 2 < ringed else ())
        if step == 1:
            trade_halves(range(ringed, totals))
            width = tokens.shape[1] // chips
            aligned = width % 128 == 0
            squares = jnp.zeros((tokens.shape[0], 1), F32)
            for place in range(chips):
                to = pl.ds(place * width, width)
                at = to
                if aligned:
                    at = ring_chip((spot + place) % chips, chips) * width
                    at = pl.ds(pl.multiple_of(at, 128), width)
                stream[:, to] = tokens[:, at]
                cot_own[:, to] = cot[:, at]
                own_gain[:, to] = gain[:, at]
                own_gain_mlp[:, to] = gain_mlp[:, at]
                block = stream[:, to].astype(F32)
                squares = squares + jnp.sum(block * block, axis=1, keepdims=True)
            scale = lax.rsqrt(squares / tokens.shape[1] + 1e-06)
            normed[...] = (stream[...].astype(F32) * scale * own_gain[...]).astype(BF)
            for i, (value, rows) in enumerate(pairs):
                own.append(pltpu.make_async_copy(value, rows.at[0, member], own_sem.at[i]))
                own[-1].start()
                halves[i].start()
        if step == 2:
            for i in range(2):
                own[i].wait()
                halves[i].wait()
                wholes[i].start()
    for i, item in enumerate(layout):
        if item[0] >= ringed:
            near[i].wait()
            far[i].wait()
    for copy in wholes:
        copy.wait()
    for out in range(ringed):
        for way in (1, -1):
            hop(out, chips // 2, way).wait_recv()
    for copy in started:
        copy.wait_send()


def spread(grid, groups, ringed, tokens, cot, gains):
    chips = grid.chips
    sources, layout, shapes, turned_shapes = [], [], [], []
    for out, group in enumerate(groups):
        at = 0
        for shard in group:
            turned = isinstance(shard, tuple)
            if turned:
                (shard,) = shard
                turned_shapes.append(pltpu.VMEM(shard.shape[::-1], BF))
            width = shard.shape[0 if turned else 1] // 2
            layout.append((out, at, width, turned))
            sources.append(shard)
            at += width
        rows = 2 * tokens.shape[1] // grid.devices
        shapes.append(jax.ShapeDtypeStruct(((chips,) if out < ringed else ()) + (rows, at), BF))
    dma = pltpu.SemaphoreType.DMA
    hops = (ringed, chips // 2)
    anywhere = pl.BlockSpec(memory_space=pltpu.HBM)
    near = pl.BlockSpec(memory_space=pltpu.VMEM)
    own = jax.ShapeDtypeStruct(tokens.shape, BF)
    rows = jax.ShapeDtypeStruct((2, 2) + tokens.shape, BF)
    return pl.pallas_call(
        partial(spread_kernel, chips, layout, ringed),
        out_shape=shapes + [own, own] + [jax.ShapeDtypeStruct(gains[0].shape, F32)] * 2 + [rows, rows],
        in_specs=[near if item[3] else anywhere for item in layout] + [near] * 4,
        out_specs=[near] * ringed + [anywhere] * (len(shapes) - ringed) + [near] * 4 + [anywhere] * 2,
        scratch_shapes=[pltpu.VMEM(tokens.shape, BF)]
        + [dma((len(sources),))] * 3
        + [dma(hops)] * 4
        + [dma((2,))] * 5
        + turned_shapes,
        compiler_params=pltpu.CompilerParams(
            collective_id=0, has_side_effects=True, vmem_limit_bytes=62 << 20
        ),
        name="spread",
    )(*sources, tokens, cot, *gains)


PARTS = 2


def exchange(part, rows_out, buffers, sems, compute, early=None, late=None):
    got_core, sent_half, got_half, own = buffers
    me, member = lax.axis_index("dp"), lax.axis_index("tensor")
    peer = (me + 1 - 2 * (me % 2), member)
    across = (me, 1 - member)
    count = part.shape[2] // PARTS

    def chunk(k):
        return pl.ds(k * count, count)

    def copy(kind, k, source, target, device):
        return send(source, target, sems[2 * kind].at[k], sems[2 * kind + 1].at[k], device)

    first = [copy(0, k, part.at[1, :, chunk(k)], got_core.at[:, chunk(k)], peer) for k in range(PARTS)]
    second = [copy(1, k, sent_half.at[chunk(k)], got_half.at[chunk(k)], across) for k in range(PARTS)]
    third = [
        copy(2, k, own.at[chunk(k)], rows_out.at[0, member, chunk(k)], across) for k in range(PARTS)
    ]
    fourth = [
        copy(3, k, own.at[chunk(k)], rows_out.at[1, member, chunk(k)], peer) for k in range(PARTS)
    ]
    fifth = [
        copy(4, k, rows_out.at[0, 1 - member, chunk(k)], rows_out.at[1, 1 - member, chunk(k)], peer)
        for k in range(PARTS)
    ]
    for k in range(PARTS):
        first[k].start()
    if early:
        early()
    for k in range(PARTS):
        first[k].wait_recv()
        total = part[0, 1 - member, chunk(k)] + got_core[1 - member, chunk(k)]
        sent_half[chunk(k)] = total.astype(BF)
        second[k].start()
    for k in range(PARTS):
        second[k].wait_recv()
        total = part[0, member, chunk(k)] + got_core[member, chunk(k)] + got_half[chunk(k)].astype(F32)
        value = compute(k, chunk(k), total).astype(BF)
        own[chunk(k)] = value
        third[k].start()
        fourth[k].start()
        rows_out[0, member, chunk(k)] = value
    for k in range(PARTS):
        third[k].wait_recv()
        fifth[k].start()
    if late:
        late()
    for k in range(PARTS):
        fourth[k].wait_recv()
        fifth[k].wait_recv()
    for copies in (first, second, third, fourth, fifth):
        for one in copies:
            one.wait_send()


def exchange_scratch(rows, width):
    return [
        pltpu.VMEM((2, rows, width), F32),
        pltpu.VMEM((rows, width), BF),
        pltpu.VMEM((rows, width), BF),
        pltpu.VMEM((rows, width), BF),
    ] + [pltpu.SemaphoreType.DMA((PARTS,))] * 10


def middle_kernel(part, stream, gain, rows_out, middle, *scratch):
    me, member = lax.axis_index("dp"), lax.axis_index("tensor")
    signal_all(((me + 1 - 2 * (me % 2), member), (me, 1 - member)))

    def compute(k, rows, mixed):
        value = stream[rows].astype(F32) + mixed
        middle[rows] = value
        return value * lax.rsqrt(jnp.mean(value * value, axis=1, keepdims=True) + 1e-06) * gain[...]

    exchange(part, rows_out, scratch[:4], scratch[4:], compute)


def middle_rows(part, stream, gain):
    rows, width = stream.shape
    near = pl.BlockSpec(memory_space=pltpu.VMEM)
    gathered, middle = pl.pallas_call(
        middle_kernel,
        out_shape=[
            jax.ShapeDtypeStruct((2, 2, rows, width), BF),
            jax.ShapeDtypeStruct((rows, width), F32),
        ],
        in_specs=[near] * 3,
        out_specs=[near] * 2,
        scratch_shapes=exchange_scratch(rows, width),
        compiler_params=pltpu.CompilerParams(
            collective_id=1, has_side_effects=True, vmem_limit_bytes=32 << 20
        ),
        name="middle",
    )(part.reshape(2, 2, rows, width), stream, gain)
    return gathered.reshape(4 * rows, width), middle


def turn_kernel(chips, heads, ffw, early, *refs):
    refs = list(refs)

    def take(count):
        taken, refs[:] = refs[:count], refs[count:]
        return taken

    part, cot, middle, gain, rows_cot, rows_mlp, hidden, grad_gate, begun = take(9)
    small_inputs, later = take(8), take(8)
    rows_out, grad_middle, grad_gain, late = take(4)
    results = take(7)
    grad_heads, going, arrived = take(3)
    here_now, (later_sem,) = take(8), take(1)
    send_ring, recv_ring = take(2)
    me, member = lax.axis_index("dp"), lax.axis_index("tensor")
    core, chip = me % 2, me // 2
    spot = ring_spot(chip, chips)
    ways = (
        (2 * ring_chip((spot + 1) % chips, chips) + core, member),
        (2 * ring_chip((spot + chips - 1) % chips, chips) + core, member),
    )
    signal_all((*ways, (me + 1 - 2 * core, member), (me, 1 - member)))
    half = chips // 2
    width = rows_cot.shape[1] // chips
    mid = width // 2

    def total(way, place, step):
        at = (place if way == 0 else -place) % chips * width
        value = []
        for left, right, size in ((rows_cot, hidden, ffw), (rows_mlp, grad_gate, early)):
            value.append(
                lax.dot_general(
                    left[:, at : at + width],
                    right[:, 0:size],
                    (COLS_ROWS, ((), ())),
                    preferred_element_type=F32,
                )
            )
        value = jnp.concatenate(value, axis=1)
        if step:
            return (value + arrived[way, step - 1].astype(F32)).astype(BF)
        lo = mid * way
        here = value[lo : lo + mid] + begun[way].astype(F32)
        rest = value[mid - lo : width - lo]
        return jnp.concatenate([here, rest] if way == 0 else [rest, here], axis=0).astype(BF)

    def hop(way, step):
        sems = (way, step)
        source = arrived.at[way, step - 1] if step else going.at[way]
        return send(source, arrived.at[sems], send_ring.at[sems], recv_ring.at[sems], ways[way])

    def next_hop(step):
        for way in range(2):
            if step:
                hop(way, step - 1).wait_recv()
            value = total(way, half - 1 - step, step)
            if step == half - 2:
                late[way] = value
                continue
            if step:
                arrived[way, step - 1] = value
            else:
                going[way] = value
            hop(way, step).start()

    def compute(k, rows, grad):
        value = middle[rows]
        scale = lax.rsqrt(jnp.mean(value * value, axis=1, keepdims=True) + 1e-06)
        unit_value = value * scale
        gained = jnp.sum(grad * unit_value, axis=0, keepdims=True)
        grad_gain[...] = gained if k == 0 else grad_gain[...] + gained
        grad = grad * gain[...]
        grad = scale * (grad - unit_value * jnp.mean(grad * unit_value, axis=1, keepdims=True))
        grad = grad + cot[rows].astype(F32)
        grad_middle[rows] = grad
        return grad

    ready = staged(later, here_now, later_sem)
    wout, *kept = here_now[:6]
    inputs = here_now[6:] + small_inputs
    exchange(
        part, rows_out, refs[:4], refs[4:], compute, lambda: next_hop(0), lambda: next_hop(1) if half > 3 else None
    )
    ready(*range(8))
    for step in range(2, half - 2):
        next_hop(step)
    for ref in results[2:]:
        ref[...] = jnp.zeros_like(ref)
    length = inputs[0].shape[0] // 2

    @pl.loop(0, 2)
    def _(s):
        at = pl.multiple_of(s * length, length)
        here = pl.ds(at, length)
        for m in range(2):
            grad_heads[pl.ds(at + m * (length // 2), length // 2)] = jnp.dot(
                rows_out[s, m], wout[...], preferred_element_type=F32
            )
        mixer_back(
            heads,
            grad_heads.at[here],
            [ref.at[here] for ref in inputs[:2]] + [ref.at[pl.ds(s, 1)] for ref in inputs[2:4]] + inputs[4:],
            [ref.at[pl.ds(s, 1)] for ref in kept[:4]] + [kept[4].at[here]],
            [ref.at[here] for ref in results[:2]] + results[2:],
        )

    next_hop(half - 2)
    for step in range(half - 2):
        for way in range(2):
            hop(way, step).wait_send()


def turn(grid, heads, early, part, cot, middle, gain, wout, rows_cot, rows_mlp, hidden, grad_gate, begun, inputs, kept):
    chips = grid.chips
    rows, width = middle.shape
    block, half = width // chips, chips // 2
    ffw = hidden.shape[1]
    n = ffw + early
    qk, vg, _, _, cq, ck, cv, log, _, out_gain = inputs
    near = pl.BlockSpec(memory_space=pltpu.VMEM)
    dma = pltpu.SemaphoreType.DMA
    sums = [cq.shape, ck.shape, cv.shape, (2, log.shape[1]), out_gain.shape]
    operands = (part.reshape(2, 2, rows, width), cot, middle, gain, rows_cot, rows_mlp, hidden, grad_gate, begun)
    operands = (*operands, *inputs[2:])
    later = (wout, *kept, *inputs[:2])
    gathered, *rest = pl.pallas_call(
        partial(turn_kernel, chips, heads, ffw, early),
        out_shape=[
            jax.ShapeDtypeStruct((2, 2, rows, width), BF),
            jax.ShapeDtypeStruct((rows, width), F32),
            jax.ShapeDtypeStruct((1, width), F32),
            jax.ShapeDtypeStruct((2, block, n), BF),
            jax.ShapeDtypeStruct(qk.shape, BF),
            jax.ShapeDtypeStruct(vg.shape, BF),
        ]
        + [jax.ShapeDtypeStruct(shape, F32) for shape in sums],
        in_specs=[near] * len(operands) + [pl.BlockSpec(memory_space=pltpu.HBM)] * len(later),
        out_specs=[near] * (6 + len(sums)),
        scratch_shapes=[
            pltpu.VMEM((4 * rows, cv.shape[1]), F32),
            pltpu.VMEM((2, block, n), BF),
            pltpu.VMEM((2, half - 2, block, n), BF),
            *[pltpu.VMEM(value.shape, value.dtype) for value in later],
            dma((len(later),)),
            dma((2, half - 2)),
            dma((2, half - 2)),
        ]
        + exchange_scratch(rows, width),
        compiler_params=pltpu.CompilerParams(
            collective_id=2, has_side_effects=True, vmem_limit_bytes=62 << 20
        ),
        name="turn",
    )(*operands, *later)
    return gathered.reshape(4 * rows, width), *rest


def mlp_kernel(chips, ffw, early, *refs):
    rows, cot, own, right_1, left_1, right_2, left_2 = refs[:7]
    hidden, gate_early, gate_rest, grad_upper, back, ahead, begun = refs[7:14]
    weights, sums, begin, load_sem, send_ring, recv_ring, send_begin, recv_begin = refs[14:]
    me, member = lax.axis_index("dp"), lax.axis_index("tensor")
    core, chip = me % 2, me // 2
    spot = ring_spot(chip, chips)
    ways = (
        (2 * ring_chip((spot + 1) % chips, chips) + core, member),
        (2 * ring_chip((spot + chips - 1) % chips, chips) + core, member),
    )
    signal_all(ways)
    half = chips // 2
    block = own.shape[0]
    mid = block // 2

    def spots(place, lo=0, hi=block):
        return pl.ds((place % chips) * block + lo, hi - lo)

    def hop(way, step):
        place, to = (1 - step, -step) if way == 0 else (step - 1, step)
        lo, hi = (0, block) if step < half else (mid * way, mid * way + mid)
        if step == 3:
            source = (right_2, left_2)[way].at[pl.ds(lo, hi - lo)]
        else:
            source = weights.at[spots(place, lo, hi)]
        sems = (way, step - 3)
        return send(source, weights.at[spots(to, lo, hi)], send_ring.at[sems], recv_ring.at[sems], ways[way])

    for way in range(2):
        hop(way, 3).start()
    loads = []
    for number, (place, source) in enumerate(((0, own), (1, left_1), (2, left_2), (-2, right_2), (-1, right_1))):
        loads.append(pltpu.make_async_copy(source, weights.at[spots(place)], load_sem.at[number]))
        loads[-1].start()

    tile = ffw // 2

    def add(lo, hi, first):
        inner = slice((lo % chips) * block, (lo % chips + hi - lo) * block)
        for at in range(0, 3 * ffw, tile):
            left = rows if at < 2 * ffw else cot
            value = jnp.dot(left[:, inner], weights[inner, at : at + tile], preferred_element_type=F32)
            sums[:, at : at + tile] = value if first else sums[:, at : at + tile] + value

    for copy in loads[:3]:
        copy.wait()
    add(0, 3, True)
    for copy in loads[3:]:
        copy.wait()
    add(-2, 0, False)
    for step in range(3, half):
        for way in range(2):
            hop(way, step).wait_recv()
            hop(way, step + 1).start()
        add(step, step + 1, False)
        add(-step, 1 - step, False)
    for way in range(2):
        hop(way, half).wait_recv()
    add(half, half + 1, False)

    for at in range(0, ffw, 128):
        gate, upper = sums[:, at : at + 128], sums[:, ffw + at : ffw + at + 128]
        grad = sums[:, 2 * ffw + at : 2 * ffw + at + 128]
        open_gate = jax.nn.sigmoid(gate)
        passed = gate * open_gate
        hidden[:, at : at + 128] = (passed * upper).astype(BF)
        part, to = (gate_early, at) if at < early else (gate_rest, at - early)
        part[:, to : to + 128] = (grad * upper * silu_back(gate, open_gate)).astype(BF)
        grad_upper[:, at : at + 128] = (grad * passed).astype(BF)

    starts = []
    for way in range(2):
        lo = half * block + mid * way
        for left, right, at, size in ((cot, hidden, 0, ffw), (rows, gate_early, ffw, early)):
            begin[way, :, at : at + size] = lax.dot_general(
                left[:, lo : lo + mid],
                right[:, 0:size],
                (COLS_ROWS, ((), ())),
                preferred_element_type=F32,
            ).astype(BF)
        starts.append(send(begin.at[way], begun.at[way], send_begin.at[way], recv_begin.at[way], ways[way]))
        starts[-1].start()
    for place in range(chips):
        inner = slice(place * block, (place + 1) * block)
        value, at = 0.0, 0
        for part in (gate_early, gate_rest, grad_upper):
            cols = slice(at, at + part.shape[1])
            value = value + lax.dot_general(
                part[...], weights[inner, cols], (ROWS_ROWS, ((), ())), preferred_element_type=F32
            )
            at += part.shape[1]
        back[:, inner] = value
        ahead[:, inner] = lax.dot_general(
            hidden[...], weights[inner, 2 * ffw :], (ROWS_ROWS, ((), ())), preferred_element_type=F32
        ).astype(BF)
    for copy in starts:
        copy.wait()
    for step in range(3, half + 1):
        for way in range(2):
            hop(way, step).wait_send()


def mlp(grid, rows, cot, chunks, ffw, early):
    chips = grid.chips
    count, width = rows.shape
    block, n = chunks[0].shape
    half = chips // 2
    near = pl.BlockSpec(memory_space=pltpu.VMEM)
    far = pl.BlockSpec(memory_space=pltpu.HBM)
    dma = pltpu.SemaphoreType.DMA
    inner = jax.ShapeDtypeStruct((count, ffw), BF)
    return pl.pallas_call(
        partial(mlp_kernel, chips, ffw, early),
        out_shape=[
            inner,
            jax.ShapeDtypeStruct((count, early), BF),
            jax.ShapeDtypeStruct((count, ffw - early), BF),
            inner,
            jax.ShapeDtypeStruct((count, width), F32),
            jax.ShapeDtypeStruct((count, width), BF),
            jax.ShapeDtypeStruct((2, block // 2, ffw + early), BF),
        ],
        in_specs=[near] * 2 + [far] * 5,
        out_specs=[near] * 7,
        scratch_shapes=[
            pltpu.VMEM((chips * block, n), BF),
            pltpu.VMEM((count, n), F32),
            pltpu.VMEM((2, block // 2, ffw + early), BF),
            dma((5,)),
            dma((2, half - 2)),
            dma((2, half - 2)),
            dma((2,)),
            dma((2,)),
        ],
        compiler_params=pltpu.CompilerParams(
            collective_id=4, has_side_effects=True, vmem_limit_bytes=56 << 20
        ),
        name="mlp",
    )(rows, cot, *chunks)


def collect_kernel(chips, steps, groups, late_parts, fields, side_of, counts, *refs):
    n_left, n_right, n_out, n_side = counts
    refs = list(refs)

    def take(count):
        taken, refs[:] = refs[:count], refs[count:]
        return taken

    far = take(n_left + n_right)
    late_out, late_left = take(2)
    weights = take(n_side)
    ahead_far, *far_tokens = take(4)
    gain, mlp_grad = take(2)
    grad_cq, grad_ck, grad_cv, grad_rate, grad_gain = take(5)
    outs = take(n_out)
    out_tokens, grad_tokens, *small_outs = take(4)
    begin, arrived, late_in, final, back, got_core, sent_half, got_half, *small_ins = take(10)
    buffers = take(n_side)
    near, near_tokens = take(n_left + n_right), take(4)
    lefts, rights = near[:n_left], near[n_left:]
    ahead, stream, middle, grad_middle = near_tokens
    (far_sem,) = take(1)
    send_ring, recv_ring, own_sem, send_core, recv_core, send_late, recv_late = take(7)
    send_first, recv_first, send_second, recv_second, send_small, recv_small, weight_sem, free = take(8)
    me, member = lax.axis_index("dp"), lax.axis_index("tensor")
    core, chip = me % 2, me // 2
    spot = ring_spot(chip, chips)
    ways = (
        (2 * ring_chip((spot + 1) % chips, chips) + core, member),
        (2 * ring_chip((spot + chips - 1) % chips, chips) + core, member),
    )
    peer = (2 * chip + 1 - core, member)
    across = (me, 1 - member)
    partners = [across] + [
        (me + (1 << k) - 2 * (1 << k) * ((me // (1 << k)) % 2), member) for k in range(steps - 1)
    ]
    signal_all(list(ways) + partners)

    half = chips // 2
    width = lefts[0].shape[1] // chips
    mid = width // 2
    starts = []
    at = 0
    for _, right in groups:
        starts.append(at)
        at += rights[right].shape[1]

    def columns(group):
        return pl.ds(starts[group], rights[groups[group][1]].shape[1])

    def piece(group, place, lo=0, hi=width):
        left, right = lefts[groups[group][0]], rights[groups[group][1]]
        at = (place % chips) * width
        return lax.dot_general(
            left[:, at + lo : at + hi], right[...], (COLS_ROWS, ((), ())), preferred_element_type=F32
        )

    def rows_of(way):
        return pl.ds(mid * way, mid)

    def hop(way, step, group):
        if step:
            source, target = arrived.at[way, step - 1], arrived.at[way, step % (half - 1)]
            source, target = source.at[:, columns(group)], target.at[:, columns(group)]
        else:
            source = begin.at[way, :, columns(group)]
            target = arrived.at[way, 0, rows_of(way), columns(group)]
        sems = (way, step, group)
        return send(source, target, send_ring.at[sems], recv_ring.at[sems], ways[way])

    late = [send(late_out.at[way], late_in.at[way], send_late.at[way], recv_late.at[way], ways[way]) for way in range(2)]
    sides = (back, ahead)
    first = [
        send(value.at[1], got_core.at[i], send_first.at[i], recv_first.at[i], peer)
        for i, value in enumerate((back, ahead_far))
    ]
    second = [
        send(sent_half.at[i], got_half.at[i], send_second.at[i], recv_second.at[i], across) for i in range(2)
    ]

    def fold_small(step):
        copies = []
        for i, (out, arrivals) in enumerate(zip(small_outs, small_ins)):
            source = arrivals.at[steps + step - 1] if step else out
            sems = (step, i)
            copies.append(send(source, arrivals.at[step], send_small.at[sems], recv_small.at[sems], partners[step]))
        return copies

    def put(ref, value):
        if width % 128:
            ref[...] = value
            return
        for place in range(chips):
            at = pl.multiple_of(ring_chip((spot + place) % chips, chips) * width, 128)
            ref[:, pl.ds(at, width)] = value[:, place * width : (place + 1) * width]

    def fetch(place):
        return [
            pltpu.make_async_copy(
                weight.at[pl.ds(place * width, width), pl.ds(at, buffer.shape[2])],
                buffer.at[place % 2],
                weight_sem.at[number, place % 2],
            )
            for number, (weight, (at, _), buffer) in enumerate(zip(weights, side_of, buffers))
        ]

    def side_work():
        for place in range(chips):
            if place + 1 < chips:
                for copy in fetch(place + 1):
                    copy.start()
            for copy in fetch(place):
                copy.wait()
            total = 0.0
            for (_, right), buffer in zip(side_of, buffers):
                total = total + lax.dot_general(
                    rights[right][...],
                    buffer[place % 2],
                    (ROWS_ROWS, ((), ())),
                    preferred_element_type=F32,
                )
            back[:, :, :, place * width : (place + 1) * width] = (
                total.astype(BF).reshape(2, 2, middle.shape[0], width)
            )
            yield
        for copy in first:
            copy.start()
        yield
        ready(*range(n_left + n_right, n_left + n_right + 4))
        for i in range(2):
            first[i].wait_recv()
            total = sides[i][0, 1 - member].astype(F32) + got_core[i, 1 - member].astype(F32)
            sent_half[i] = total.astype(BF)
            second[i].start()
        yield
        total = []
        for i in range(2):
            second[i].wait_recv()
            value = sides[i][0, member].astype(F32) + got_core[i, member].astype(F32)
            total.append(value + got_half[i].astype(F32))
        put(out_tokens, middle[...] + total[1])
        value = stream[...].astype(F32)
        scale = lax.rsqrt(jnp.mean(value * value, axis=1, keepdims=True) + 1e-06)
        value = value * scale
        gained = jnp.sum(total[0] * value, axis=0, keepdims=True)
        grad = total[0] * gain[...]
        grad = scale * (grad - value * jnp.mean(grad * value, axis=1, keepdims=True))
        put(grad_tokens, grad_middle[...] + grad)
        small_out, wide = small_outs
        small_out[...] = jnp.zeros_like(small_out)
        wide[...] = jnp.zeros_like(wide)
        quarter = 2 * member + core
        taps, keyw = grad_cq.shape
        valw = grad_cv.shape[1]
        after = max(8 * keyw, 4 * valw)

        def part(at, size):
            return pl.ds(pl.multiple_of(at + quarter * size, 128), size)

        wide[0:taps, part(0, keyw)] = grad_cq[...]
        wide[0:taps, part(4 * keyw, keyw)] = grad_ck[...]
        wide[taps : 2 * taps, part(0, valw)] = grad_cv[...]
        wide[0:1, after : after + grad_gain.shape[1]] = grad_gain[...]
        wide[0:2, part(after + grad_gain.shape[1], grad_rate.shape[1])] = grad_rate[...]
        lanes = min(width, 128)
        each = width // lanes
        for i, vector in enumerate((gained, mlp_grad[...])):
            for place in range(chips):
                row = (i * chips + ring_chip((spot + place) % chips, chips)) * each
                for k in range(each):
                    at = place * width + k * lanes
                    small_out[pl.ds(row + k, 1), 0:lanes] = vector[:, at : at + lanes]
        for copy in fold_small(0):
            copy.start()
        yield
        for step in range(steps):
            for copy in fold_small(step):
                copy.wait_recv()
            for out, arrivals in zip(small_outs, small_ins):
                before = arrivals.at[steps + step - 1] if step else out
                arrivals[steps + step] = before[...] + arrivals[step]
            if step + 1 < steps:
                for copy in fold_small(step + 1):
                    copy.start()
            yield

    work = side_work()
    ready = staged([*far, ahead_far.at[pl.ds(0, 1)], *far_tokens], near + near_tokens, far_sem)
    for copy in late + fetch(0):
        copy.start()
    for group in range(len(groups)):
        ready(groups[group][0], n_left + groups[group][1])
        for way in range(2):
            begin[way, :, columns(group)] = piece(group, half, mid * way, mid * way + mid).astype(BF)
            hop(way, 0, group).start()
    ready(*range(n_left + n_right))
    for step in range(half - 1):
        place = half - 1 - step
        for group in range(len(groups)):
            next(work, None)
            next(work, None)
            for way in range(2):
                hop(way, step, group).wait_recv()
                value = piece(group, place if way == 0 else -place)
                if step:
                    value = value + arrived[way, step, :, columns(group)].astype(F32)
                    arrived[way, step, :, columns(group)] = value.astype(BF)
                else:
                    lo = mid * way
                    here = value[lo : lo + mid] + arrived[way, 0, rows_of(way), columns(group)].astype(F32)
                    arrived[way, 0, rows_of(way), columns(group)] = here.astype(BF)
                    arrived[way, 0, rows_of(1 - way), columns(group)] = value[
                        mid - lo : width - lo
                    ].astype(BF)
                if step == half - 2 and group == 0:
                    pl.semaphore_wait(free.at[way], 1)
                hop(way, step + 1, group).start()
        if step == min(1, half - 3):
            for way in range(2):
                for group in range(len(groups)):
                    hop(way, 1, group).wait_send()
                pl.semaphore_signal(
                    free.at[way], inc=1, device_id=ways[1 - way], device_id_type=pl.DeviceIdType.MESH
                )
    for _ in work:
        pass
    for step in range(steps):
        for copy in fold_small(step):
            copy.wait_send()
    for out, arrivals in zip(small_outs, small_ins):
        out[...] = arrivals[2 * steps - 1]

    rows = width // 2
    finals, used = [], {}
    for group in [len(groups)] + list(range(len(groups))):
        slot = group % 2
        for copy in used.get(slot, ()):
            copy()
        if group == len(groups):
            value = []
            for left, right in late_parts:
                left = late_left if left is None else lefts[left]
                value.append(
                    lax.dot_general(
                        left[:, 0:width],
                        rights[right][...],
                        (COLS_ROWS, ((), ())),
                        preferred_element_type=F32,
                    )
                )
            value = jnp.concatenate(value, axis=1)
        else:
            value = piece(group, 0)
        for way in range(2):
            if group == len(groups):
                late[way].wait_recv()
                value = value + late_in[way].astype(F32)
            else:
                hop(way, half - 1, group).wait_recv()
                value = value + arrived[way, 0, :, columns(group)].astype(F32)
        final[slot, :, 0 : value.shape[1]] = value
        used[slot] = []
        for number, (owner, at, out, to, whole, size) in enumerate(fields):
            if owner == group:
                own = pl.ds(pl.multiple_of(core * rows, rows), rows)
                theirs = pl.ds(pl.multiple_of((1 - core) * rows, rows), rows)
                target = outs[out].at[:, pl.ds(pl.multiple_of(core * whole + to, 128), size)]
                copy = pltpu.make_async_copy(final.at[slot, own, pl.ds(at, size)], target, own_sem.at[number])
                far = send(
                    final.at[slot, theirs, pl.ds(at, size)],
                    target,
                    send_core.at[number],
                    recv_core.at[number],
                    peer,
                )
                copy.start()
                far.start()
                finals.append(far)
                used[slot] += [copy.wait, far.wait_send]
    for slot in used:
        for copy in used[slot]:
            copy()
    for far in finals:
        far.wait_recv()
    for copy in first + second + late:
        copy.wait_send()
    for step in range(half):
        for group in range(len(groups)):
            for way in range(2):
                if step != 1:
                    hop(way, step, group).wait_send()


def collect(grid, lefts, rights, groups, late, fields, sides, ahead, tokens_in, small, small_shapes):
    chips = grid.chips
    rows, width = tokens_in[2].shape
    steps = grid.devices.bit_length()
    n = sum(rights[right].shape[1] for _, right in groups)
    widest = max([rights[right].shape[1] for _, right in groups] + [late[0].shape[2]])
    block = width // chips
    half = chips // 2
    *late, late_parts = late
    weights = [weight for weight, _, _ in sides]
    side_of = [(at, right) for _, at, right in sides]
    stream, gain, middle, grad_middle, mlp_grad = tokens_in
    tokens_in = [ahead.reshape(2, 2, rows, width), stream, middle, grad_middle]
    inputs = [*lefts, *rights, *late, *weights, *tokens_in, gain, mlp_grad, *small]
    wholes = {}
    for _, _, out, _, whole in fields:
        wholes[out] = whole
    outs = [jax.ShapeDtypeStruct((block // 2, 2 * wholes[out]), F32) for out in range(len(wholes))]
    ends = [sum(rights[right].shape[1] for _, right in late_parts)]
    ends = [rights[right].shape[1] for _, right in groups] + ends
    sized = []
    for i, (group, at, out, to, whole) in enumerate(fields):
        starts = [other[1] for other in fields if other[0] == group and other[1] > at]
        sized.append((group, at, out, to, whole, min(starts + [ends[group]]) - at))
    fields = sized
    tokens = jax.ShapeDtypeStruct((rows, width), F32)
    near = pl.BlockSpec(memory_space=pltpu.VMEM)
    far = pl.BlockSpec(memory_space=pltpu.HBM)
    dma = pltpu.SemaphoreType.DMA
    ring = (2, half, len(groups))
    counts = (len(lefts), len(rights), len(outs), len(sides))
    held = [value.shape for value in (*lefts, *rights)]
    return pl.pallas_call(
        partial(collect_kernel, chips, steps, groups, late_parts, fields, side_of, counts),
        out_shape=outs + [tokens, tokens] + [jax.ShapeDtypeStruct(shape, F32) for shape in small_shapes],
        in_specs=[far] * (len(held) + 1) + [near] + [far] * (len(sides) + 4) + [near] * 7,
        out_specs=[far] * len(outs) + [near] * 4,
        scratch_shapes=[
            pltpu.VMEM((2, block // 2, n), BF),
            pltpu.VMEM((2, half - 1, block, n), BF),
            pltpu.VMEM(late[0].shape, BF),
            pltpu.VMEM((2, block, widest), F32),
            pltpu.VMEM((2, 2, rows, width), BF),
            pltpu.VMEM((2, 2, rows, width), BF),
            pltpu.VMEM((2, rows, width), BF),
            pltpu.VMEM((2, rows, width), BF),
            *[pltpu.VMEM((2 * steps,) + shape, F32) for shape in small_shapes],
        ]
        + [pltpu.VMEM((2, block, rights[right].shape[1]), BF) for _, right in side_of]
        + [pltpu.VMEM(shape, BF) for shape in held]
        + [
            pltpu.VMEM((1, 2, rows, width), BF),
            pltpu.VMEM((rows, width), BF),
            pltpu.VMEM((rows, width), F32),
            pltpu.VMEM((rows, width), F32),
            dma((len(held) + 4,)),
        ]
        + [dma(ring), dma(ring)]
        + [dma((len(fields),))] * 3
        + [dma((2,))] * 6
        + [dma((steps, 2))] * 2
        + [dma((len(sides), 2)), pltpu.SemaphoreType.REGULAR((2,))],
        compiler_params=pltpu.CompilerParams(
            collective_id=3, has_side_effects=True, vmem_limit_bytes=63 << 20
        ),
        name="collect",
    )(*inputs)


def finish_kernel(chips, heads, counts, *refs):
    moved, turned = counts
    refs = list(refs)

    def take(count):
        taken, refs[:] = refs[:count], refs[count:]
        return taken

    sources, turning, (rates, gains, wide) = take(moved), take(turned), take(3)
    targets, turned_out = take(moved), take(turned)
    beta, decay, norm_gain, mlp_gain, cq, ck, cv, log, bias, out_gain = take(10)
    held = take(moved)
    sem_in, sem_out = take(2)
    ready = staged(sources, held, sem_in)
    copies = []
    for i, (source, target) in enumerate(zip(held, targets)):
        if len(target.shape) > len(source.shape):
            target = target.at[0]
        ready(i)
        copies.append(pltpu.make_async_copy(source, target, sem_out.at[i]))
        copies[-1].start()
    for source, target in zip(turning, turned_out):
        target[...] = source[...].T
    small = rates.shape[1] // 2
    by_head = rates[...].T
    for core in range(2):
        to = slice(core * heads, (core + 1) * heads)
        beta[to] = by_head[core * small : core * small + heads]
        decay[to] = by_head[core * small + heads : core * small + 2 * heads]
    lanes = min(norm_gain.shape[1] // chips, 128)
    count = norm_gain.shape[1] // lanes
    for i, vector in enumerate((norm_gain, mlp_gain)):
        for row in range(count):
            vector[:, row * lanes : (row + 1) * lanes] = gains[i * count + row : i * count + row + 1, 0:lanes]
    taps, keyw = cq.shape
    valw = cv.shape[1]
    after = max(2 * keyw, valw)
    cq[...] = wide[0:taps, 0:keyw]
    ck[...] = wide[0:taps, keyw : 2 * keyw]
    cv[...] = wide[taps : 2 * taps, 0:valw]
    out_gain[...] = wide[0:1, after : after + out_gain.shape[1]]
    after += out_gain.shape[1]
    for quarter in range(4):
        at = after + quarter * small + heads
        to = slice(quarter * heads, (quarter + 1) * heads)
        log[:, to] = wide[0:1, at : at + heads]
        bias[:, to] = wide[1:2, at : at + heads]
    for copy in copies:
        copy.wait()


def finish(grid, heads, moved, turning, rates, gains, wide, vectors, convs):
    near = pl.BlockSpec(memory_space=pltpu.VMEM)
    far = pl.BlockSpec(memory_space=pltpu.HBM)
    out_shape = [jax.ShapeDtypeStruct(shape, F32) for _, shape in moved]
    out_shape += [jax.ShapeDtypeStruct(value.shape[::-1], F32) for value in turning]
    rate = jax.ShapeDtypeStruct((2 * heads, rates.shape[0]), F32)
    vectors = [jax.ShapeDtypeStruct((1, size), F32) for size in vectors]
    convs = [jax.ShapeDtypeStruct(value.shape, F32) for value in convs]
    small = [rate, rate, *vectors[:2], *convs, *vectors[2:]]
    return pl.pallas_call(
        partial(finish_kernel, grid.chips, heads, (len(moved), len(turning))),
        out_shape=out_shape + small,
        in_specs=[far] * len(moved) + [near] * (len(turning) + 3),
        out_specs=[far] * len(moved) + [near] * (len(turning) + len(small)),
        scratch_shapes=[pltpu.VMEM(value.shape, F32) for value, _ in moved]
        + [pltpu.SemaphoreType.DMA((len(moved),))] * 2,
        compiler_params=pltpu.CompilerParams(vmem_limit_bytes=63 << 20),
        name="finish",
    )(*[value for value, _ in moved], *turning, rates, gains, wide)


def whole_rows(stack):
    return stack.reshape(-1, stack.shape[-1])


def per_device(
    tokens,
    segment_ids,
    norm_gain,
    w_query,
    w_key,
    w_value,
    w_outgate,
    w_beta,
    w_decay,
    conv_query,
    conv_key,
    conv_value,
    decay_log,
    decay_bias,
    out_gain,
    w_output,
    mlp_gain,
    w_gate,
    w_up,
    w_down,
    cotangent,
    *,
    devices,
):
    grid = Grid(devices)
    heads = w_beta.shape[1] // 2
    keyw = w_query.shape[1] // 2
    valw = w_value.shape[1] // 2
    ffw = w_gate.shape[1] // 2
    small = -(-2 * heads // 128) * 128

    filler = jnp.zeros((w_beta.shape[0], small - 2 * heads), BF)
    rates = []
    for at in (0, heads):
        rates += [w_beta[:, at : at + heads], w_decay[:, at : at + heads], filler]
    rates = jnp.concatenate(rates, axis=1)
    groups = [[w_query, w_key, rates], [w_value, w_outgate], [(w_output,)], [w_gate, w_up, (w_down,)]]
    shown = (tokens[0], cotangent[0], norm_gain[None], mlp_gain[None])
    if norm_gain.shape[0] // grid.chips % 128:
        shown = [grid.into(value) for value in shown]
    *gathered, stream, cot_own, norm_row, mlp_row, rows_mix, cot_rows = spread(
        grid, groups, 3, *shown[:2], shown[2:]
    )
    wqk, wvg, wout = [whole_rows(stack) for stack in gathered[:3]]
    rows_mix, cot_rows = [rows.reshape(-1, rows.shape[-1]) for rows in (rows_mix, cot_rows)]
    segments = jnp.concatenate([segment_ids, grid.over_core(segment_ids)], axis=0)

    conv_parts = [
        part_of(conv_query, grid.quarter, keyw, 1),
        part_of(conv_key, grid.quarter, keyw, 1),
        part_of(conv_value, grid.quarter, valw, 1),
        part_of(decay_log, grid.quarter, heads, 0),
        part_of(decay_bias, grid.quarter, heads, 0),
    ]
    pre_qk = dot(rows_mix, wqk)
    pre_vg = dot(rows_mix, wvg)
    lanes = [jnp.pad(part[None], ((0, 0), (0, small - heads))) for part in conv_parts[3:]]
    mixer_in = (pre_qk, pre_vg, segments[:, :, None], segments[:, None, :], *conv_parts[:3], *lanes, out_gain[None])
    heads_out, kept = mixer(heads, mixer_in)
    rows_mlp, middle = middle_rows(cols_product(heads_out, wout), stream, mlp_row)
    chunk = gathered[3]
    chunks = [chunk, grid.shift(chunk, 1), grid.shift(chunk, -1)]
    pair = tied((chunks[1], chunks[2]), heads_out)
    chunks += [grid.shift(pair[0], 1), grid.shift(pair[1], -1)]
    early = ffw // 256 * 128
    hidden, *gate_parts, grad_upper, back_part, ahead, begun = mlp(grid, rows_mlp, cot_rows, chunks, ffw, early)
    grad_mixed, grad_middle, grad_mlp_gain, late, grad_qk, grad_vg, *core_grads = turn(
        grid,
        heads,
        early,
        back_part,
        cot_own,
        middle,
        mlp_row,
        wout,
        cot_rows,
        rows_mlp,
        hidden,
        gate_parts[0],
        begun,
        mixer_in,
        kept,
    )

    width = norm_gain.shape[0]
    gain_rows = width // min(width // grid.chips, 128)
    wide = max(8 * keyw, 4 * valw) + out_gain.shape[0] + 4 * small
    at = 2 * keyw
    *weight_grads, out_tokens, grad_tokens, gains, wide = collect(
        grid,
        [rows_mlp, grad_mixed, rows_mix],
        [gate_parts[1], grad_upper, grad_vg, heads_out, grad_qk, hidden, gate_parts[0]],
        [(0, 1), (2, 2), (0, 0), (1, 3), (2, 4)],
        [late, cot_rows[:, : cot_rows.shape[1] // grid.chips], [(None, 5), (0, 6)]],
        [
            (2, 0, 0, early, ffw),
            (5, ffw, 0, 0, ffw),
            (0, 0, 1, 0, ffw),
            (1, 0, 2, 0, valw),
            (1, valw, 3, 0, valw),
            (3, 0, 4, 0, valw),
            (4, 0, 5, 0, keyw),
            (4, keyw, 6, 0, keyw),
            (4, at, 7, 0, small),
            (5, 0, 8, 0, ffw),
        ],
        [(wvg, 0, 2), (wqk, 0, 4)],
        ahead,
        [stream, norm_row, middle, grad_middle, grad_mlp_gain],
        core_grads,
        [(2 * gain_rows, 128), (2 * conv_query.shape[0], wide)],
    )
    whole_gate, whole_up, whole_value, whole_outgate, whole_out, whole_query, whole_key, whole_small, whole_down = weight_grads
    if out_tokens.shape[1] // grid.chips % 128:
        out_tokens, grad_tokens = grid.out_of(out_tokens), grid.out_of(grad_tokens)
    moved = [out_tokens, grad_tokens, whole_query, whole_key, whole_value, whole_outgate, whole_gate, whole_up]
    shapes = [(1,) + value.shape if i < 2 else value.shape for i, value in enumerate(moved)]
    sizes = [width, width, decay_log.shape[0], decay_bias.shape[0], out_gain.shape[0]]
    *moved, whole_out, whole_down, whole_beta, whole_decay, norm_row, mlp_row, cq, ck, cv, log, bias, gain = finish(
        grid,
        heads,
        list(zip(moved, shapes)),
        [whole_out, whole_down],
        whole_small,
        gains,
        wide,
        sizes,
        [conv_query, conv_key, conv_value],
    )
    out_tokens, grad_tokens, *moved = moved
    whole_query, whole_key, whole_value, whole_outgate, whole_gate, whole_up = moved
    return (
        out_tokens,
        grad_tokens,
        norm_row[0],
        whole_query,
        whole_key,
        whole_value,
        whole_outgate,
        whole_beta.T,
        whole_decay.T,
        cq,
        ck,
        cv,
        log[0],
        bias[0],
        gain[0],
        whole_out,
        mlp_row[0],
        whole_gate,
        whole_up,
        whole_down,
    )


def solution(mesh):
    rows = P("dp", "tensor")
    cols = P("tensor", "dp")
    tokens = P("dp", "tensor", None)
    placed = (tokens, P("dp", None), P()) + (rows,) * 6 + (P(),) * 6
    placed = placed + (cols, P(), rows, rows, cols, tokens)
    given = (tokens, tokens, P()) + (rows,) * 6 + (P(),) * 6 + (cols, P(), rows, rows, cols)
    return jax.shard_map(
        partial(per_device, devices=mesh.shape["dp"]),
        mesh=mesh,
        in_specs=placed,
        out_specs=given,
        check_vma=False,
    )
```

```python
from functools import partial
import math

import jax
import jax.numpy as jnp
from jax import lax
from jax.experimental import pallas as pl
from jax.experimental.pallas import tpu as pltpu
from jax.sharding import PartitionSpec as P

HIGH = lax.Precision.HIGH
HIGHEST = lax.Precision.HIGHEST
BF = jnp.bfloat16
F32 = jnp.float32


def scale_rows(values, factor):
    return values * lax.rsqrt(jnp.mean(values * values, axis=-1, keepdims=True) + 1e-06) * factor


def split3(value):
    high = value.astype(BF)
    return high, (value - high.astype(F32)).astype(BF)


def product(left, right, dims):
    dims = (dims, ((), ()))
    total = lax.dot_general(left[0], right[0], dims, preferred_element_type=F32)
    total = total + lax.dot_general(left[0], right[1], dims, preferred_element_type=F32)
    return total + lax.dot_general(left[1], right[0], dims, preferred_element_type=F32)


ROWS_COLS = ((1,), (0,))
ROWS_ROWS = ((1,), (1,))
COLS_ROWS = ((0,), (0,))


def exact_sum(mask, value, dims):
    high, low = split3(value)
    last = (value - high.astype(F32) - low.astype(F32)).astype(BF)
    dims = (dims, ((), ()))
    total = lax.dot_general(mask, last, dims, preferred_element_type=F32)
    total = total + lax.dot_general(mask, low, dims, preferred_element_type=F32)
    return total + lax.dot_general(mask, high, dims, preferred_element_type=F32)


def conv_parts(values, taps, keeping):
    moved = [values] + [pltpu.roll(values, j, 0) * keeping[j] for j in range(1, 4)]
    total = moved[0] * taps[0:1]
    for j in range(1, 4):
        total = total + moved[j] * taps[j : j + 1]
    return moved, total


def conv_back(grad, moved, taps, keeping):
    rows = grad.shape[0]
    total = grad * taps[0:1]
    for j in range(1, 4):
        total = total + pltpu.roll(grad * keeping[j], rows - j, 0) * taps[j : j + 1]
    parts = [jnp.sum(grad * moved[j], axis=0, keepdims=True) for j in range(4)]
    return total, jnp.concatenate(parts, axis=0)


def silu_back(total, gate):
    return gate * (1.0 + total * (1.0 - gate))


def softplus(value):
    return jnp.maximum(value, 0.0) + jnp.log1p(jnp.exp(-jnp.abs(value)))


def block_masks(seg_col, seg_row):
    size = seg_col.shape[0]
    row = lax.broadcasted_iota(jnp.int32, (size, size), 0)
    col = lax.broadcasted_iota(jnp.int32, (size, size), 1)
    masking = ((seg_col == seg_row) & (col <= row)).astype(F32)
    spot = lax.broadcasted_iota(jnp.int32, (size, 1), 0)
    keeping = [None]
    for j in range(1, 4):
        keeping.append(((pltpu.roll(seg_col, j, 0) == seg_col) & (spot >= j)).astype(F32))
    return row, col, masking, keeping


def head_rates(small, log, bias, masking, heads):
    decay_in = pltpu.roll(small, small.shape[1] - heads, 1) + bias
    factor = -jnp.exp(log)
    rates = factor * softplus(decay_in)
    betas = jax.nn.sigmoid(small)
    summed = exact_sum(masking.astype(BF), rates, ROWS_COLS)
    return decay_in, factor, rates, betas, summed


def invert(mixing, row, col):
    size = mixing.shape[0]
    result = jnp.where(row == col, 1.0, 0.0) - jnp.where((row >> 1) == (col >> 1), mixing, 0.0)
    level = 1
    while (1 << level) < size:
        picked = ((row >> (level + 1)) == (col >> (level + 1))) & ((row >> level) != (col >> level))
        part = split3(jnp.where(picked, mixing, 0.0))
        halves = split3(result)
        step = product(halves, part, ROWS_COLS)
        result = result - product(split3(step), halves, ROWS_COLS)
        level += 1
    return result


def unit(values):
    return lax.rsqrt(jnp.sum(values * values, axis=1, keepdims=True) + 1e-06)


def mixer_kernel(heads, qk, rates_in, vg, seg_col, seg_row, cq, ck, cv, log, bias, gain, *outs):
    heads_out, inverses, all_errors, all_kk, all_qk, all_raw = outs
    keyw, valw = cq.shape[1] // heads, cv.shape[1] // heads
    row, col, masking, keeping = block_masks(seg_col[0], seg_row[0])
    small = rates_in[...]
    _, _, _, betas, summed = head_rates(small, log[...], bias[...], masking, heads)
    betas_t, summed_t = betas.T, summed.T
    strict = (col < row).astype(F32)
    for h in range(heads):
        at = pl.ds(h * keyw, keyw)
        query = jax.nn.silu(conv_parts(qk[:, at], cq[:, at], keeping)[1])
        query = query * (unit(query) * (1.0 / math.sqrt(keyw)))
        key = jax.nn.silu(
            conv_parts(qk[:, pl.ds((heads + h) * keyw, keyw)], ck[:, at], keeping)[1]
        )
        key = key * unit(key)
        at = pl.ds(h * valw, valw)
        value = jax.nn.silu(conv_parts(vg[:, at], cv[:, at], keeping)[1])
        spread = summed[:, h : h + 1] - summed_t[h : h + 1]
        decays = jnp.exp(spread * masking) * masking * betas_t[h : h + 1]
        keys = split3(key)
        key_key = product(keys, keys, ROWS_ROWS)
        query_key = product(split3(query), keys, ROWS_ROWS)
        inverse = invert(decays * key_key * strict, row, col)
        errors = product(split3(inverse), split3(value), ROWS_COLS)
        raw = product(split3(decays * query_key), split3(errors), ROWS_COLS)
        inverses[0, h] = inverse
        all_errors[0, h] = errors
        all_kk[0, h] = key_key
        all_qk[0, h] = query_key
        all_raw[:, at] = raw
        scaled = raw * lax.rsqrt(jnp.mean(raw * raw, axis=1, keepdims=True) + 1e-05) * gain[...]
        gate = vg[:, pl.ds((heads + h) * valw, valw)]
        heads_out[:, at] = (scaled * jax.nn.silu(gate)).astype(BF)


def mixer_back(heads, grad, inputs, kept, results):
    qk, rates_in, vg, seg_col, seg_row, cq, ck, cv, log, bias, gain = inputs
    inverses, all_errors, all_kk, all_qk, all_raw = kept
    grad_qk, grad_small_out, grad_vg, grad_cq, grad_ck, grad_cv, grad_rate, grad_gain = results
    keyw, valw = cq.shape[1] // heads, cv.shape[1] // heads
    size = qk.shape[0]
    row, col, masking, keeping = block_masks(seg_col[0], seg_row[0])
    small = rates_in[...]
    decay_in, factor, rates, betas, summed = head_rates(small, log[...], bias[...], masking, heads)
    betas_t, summed_t = betas.T, summed.T
    strict = (col < row).astype(F32)
    lanes = lax.broadcasted_iota(jnp.int32, (1, small.shape[1]), 1)
    spots = lax.broadcasted_iota(jnp.int32, (small.shape[1], 1), 0)
    grad_summed = jnp.zeros_like(small)
    from_cols = jnp.zeros((small.shape[1], size), F32)
    for h in range(heads):
        at = pl.ds(h * valw, valw)
        raw, gate_in = all_raw[:, at], vg[:, pl.ds((heads + h) * valw, valw)]
        gate = jax.nn.sigmoid(gate_in)
        scale = lax.rsqrt(jnp.mean(raw * raw, axis=1, keepdims=True) + 1e-05)
        above = grad[:, at]
        grad_vg[:, pl.ds((heads + h) * valw, valw)] = (
            above * (raw * scale * gain[...]) * silu_back(gate_in, gate)
        ).astype(BF)
        above = above * (gate_in * gate)
        grad_gain[...] += jnp.sum(above * raw * scale, axis=0, keepdims=True)
        above = above * gain[...]
        grad_raw = scale * (above - raw * (scale * scale * jnp.mean(above * raw, axis=1, keepdims=True)))

        spread = summed[:, h : h + 1] - summed_t[h : h + 1]
        plain = jnp.exp(spread * masking) * masking
        decays = plain * betas_t[h : h + 1]
        key_key, query_key = all_kk[0, h] * strict, all_qk[0, h]
        grad_raws, errors = split3(grad_raw), split3(all_errors[0, h])
        grad_reading = product(grad_raws, errors, ROWS_ROWS)
        grad_errors = product(split3(decays * query_key), grad_raws, COLS_ROWS)
        grad_value = product(split3(inverses[0, h]), split3(grad_errors), COLS_ROWS)
        grad_mixing = -product(split3(grad_value), errors, ROWS_ROWS)
        both = (grad_mixing * key_key + grad_reading * query_key) * plain
        grad_beta = jnp.sum(both, axis=0, keepdims=True)
        both = both * betas_t[h : h + 1]
        from_rows = jnp.sum(both, axis=1, keepdims=True)
        grad_summed = grad_summed + jnp.where(lanes == heads + h, from_rows, 0.0)
        from_cols = from_cols + jnp.where(spots == h, grad_beta, 0.0)
        from_cols = from_cols - jnp.where(spots == heads + h, jnp.sum(both, axis=0, keepdims=True), 0.0)

        at = pl.ds(h * keyw, keyw)
        query_moved, query_total = conv_parts(qk[:, at], cq[:, at], keeping)
        query_gate = jax.nn.sigmoid(query_total)
        query = query_total * query_gate
        query_scale = unit(query)
        query = query * query_scale
        key_at = pl.ds((heads + h) * keyw, keyw)
        key_moved, key_total = conv_parts(qk[:, key_at], ck[:, at], keeping)
        key_gate = jax.nn.sigmoid(key_total)
        key = key_total * key_gate
        key_scale = unit(key)
        key = key * key_scale
        keys = split3(key)
        grad_kk = split3(grad_mixing * decays * strict)
        grad_qk_product = split3(grad_reading * (decays * (1.0 / math.sqrt(keyw))))
        grad_query = product(grad_qk_product, keys, ROWS_COLS)
        grad_key = product(grad_qk_product, split3(query), COLS_ROWS)
        grad_key = grad_key + product(grad_kk, keys, ROWS_COLS) + product(grad_kk, keys, COLS_ROWS)

        grad_query = query_scale * (grad_query - query * jnp.sum(grad_query * query, axis=1, keepdims=True))
        grad_query = grad_query * silu_back(query_total, query_gate)
        grad_query, taps = conv_back(grad_query, query_moved, cq[:, at], keeping)
        grad_qk[:, at] = grad_query.astype(BF)
        grad_cq[:, at] += taps
        grad_key = key_scale * (grad_key - key * jnp.sum(grad_key * key, axis=1, keepdims=True))
        grad_key = grad_key * silu_back(key_total, key_gate)
        grad_key, taps = conv_back(grad_key, key_moved, ck[:, at], keeping)
        grad_qk[:, key_at] = grad_key.astype(BF)
        grad_ck[:, at] += taps

        at = pl.ds(h * valw, valw)
        moved, total = conv_parts(vg[:, at], cv[:, at], keeping)
        grad_value = grad_value * silu_back(total, jax.nn.sigmoid(total))
        grad_value, taps = conv_back(grad_value, moved, cv[:, at], keeping)
        grad_vg[:, at] = grad_value.astype(BF)
        grad_cv[:, at] += taps

    from_cols = from_cols.T
    grad_summed = grad_summed + jnp.where(lanes >= heads, from_cols, 0.0)
    grad_rates = exact_sum(masking.astype(BF), grad_summed, COLS_ROWS)
    decay_lanes = (lanes >= heads) & (lanes < 2 * heads)
    shifted = [pltpu.roll(value, heads, 1) for value in (decay_in, rates)]
    grad_decay = grad_rates * pltpu.roll(factor, heads, 1) * jax.nn.sigmoid(shifted[0])
    grad_rate[0:1] += jnp.sum(grad_rates * shifted[1], axis=0, keepdims=True)
    grad_rate[1:2] += jnp.sum(grad_decay, axis=0, keepdims=True)
    grad_small = jnp.where(decay_lanes, grad_decay, from_cols * betas * (1.0 - betas))
    grad_small = jnp.where(lanes < 2 * heads, grad_small, 0.0)
    grad_small_out[...] = grad_small.astype(BF)


def mixer_specs(heads, qk, vg, cq, cv, small):
    length = qk.shape[0] // 2

    def by_rows(width):
        return pl.BlockSpec((length, width), lambda s: (s, 0))

    def fixed(*shape):
        return pl.BlockSpec(shape, lambda s: (0,) * len(shape))

    shared = [
        by_rows(qk.shape[1]),
        by_rows(small),
        by_rows(vg.shape[1]),
        pl.BlockSpec((1, length, 1), lambda s: (s, 0, 0)),
        pl.BlockSpec((1, 1, length), lambda s: (s, 0, 0)),
        fixed(*cq.shape),
        fixed(*cq.shape),
        fixed(*cv.shape),
        fixed(1, small),
        fixed(1, small),
        fixed(1, cv.shape[1] // heads),
    ]
    valw = cv.shape[1] // heads
    square = (heads, length, length)
    kept = [square, (heads, length, valw), square, square]
    kept_specs = [pl.BlockSpec((1,) + shape, lambda s: (s, 0, 0, 0)) for shape in kept]
    kept_specs.append(by_rows(cv.shape[1]))
    kept_shapes = [jax.ShapeDtypeStruct((2,) + shape, F32) for shape in kept]
    kept_shapes.append(jax.ShapeDtypeStruct((2 * length, cv.shape[1]), F32))
    return by_rows, fixed, shared, kept_specs, kept_shapes


def mixer(heads, inputs):
    qk, _, vg, _, _, cq, _, cv, log, _, _ = inputs
    by_rows, _, shared, kept_specs, kept_shapes = mixer_specs(heads, qk, vg, cq, cv, log.shape[1])
    heads_out, *kept = pl.pallas_call(
        partial(mixer_kernel, heads),
        grid=(2,),
        out_shape=[jax.ShapeDtypeStruct((qk.shape[0], cv.shape[1]), BF)] + kept_shapes,
        in_specs=shared,
        out_specs=[by_rows(cv.shape[1])] + kept_specs,
        compiler_params=pltpu.CompilerParams(vmem_limit_bytes=48 << 20),
        name="mixer",
    )(*inputs)
    return heads_out, kept


def rows_product(left, right):
    return lax.dot_general(left, right, (((0,), (0,)), ((), ())), preferred_element_type=F32)


def cols_product(left, right):
    return lax.dot_general(left, right, (((1,), (1,)), ((), ())), preferred_element_type=F32)


def dot(left, right):
    return jnp.dot(left, right, preferred_element_type=F32)


def tied(value, after):
    return lax.optimization_barrier((value, after))[0]


def first_of(flag, own, peer, axis):
    return jnp.concatenate([jnp.where(flag, own, peer), jnp.where(flag, peer, own)], axis=axis)


def part_of(value, index, size, axis):
    return lax.dynamic_slice_in_dim(value, index * size, size, axis)


class Grid:
    def __init__(self, devices):
        self.devices = devices
        self.chips = devices // 2
        me = lax.axis_index("dp")
        self.core = me % 2
        self.spot = ring_spot(me // 2, self.chips)
        self.member = lax.axis_index("tensor")
        self.quarter = 2 * self.member + self.core

    def swap(self, value, offset):
        pairs = [(at, at ^ offset) for at in range(self.devices)]
        return lax.ppermute(value, "dp", pairs)

    def over_core(self, value):
        return self.swap(value, 1)

    def over_tensor(self, value):
        return lax.ppermute(value, "tensor", [(0, 1), (1, 0)])

    def shift(self, value, step):
        pairs = []
        for at in range(self.devices):
            spot = (ring_spot(at // 2, self.chips) + step) % self.chips
            pairs.append((at, 2 * ring_chip(spot, self.chips) + at % 2))
        return lax.ppermute(value, "dp", pairs)

    def into(self, value):
        width = value.shape[-1] // self.chips
        blocks = []
        for place in range(self.chips):
            chip = ring_chip((self.spot + place) % self.chips, self.chips)
            blocks.append(part_of(value, chip, width, -1))
        return jnp.concatenate(blocks, axis=-1)

    def out_of(self, value):
        width = value.shape[-1] // self.chips
        blocks = []
        for chip in range(self.chips):
            place = (ring_spot(chip, self.chips) - self.spot + self.chips) % self.chips
            blocks.append(part_of(value, place, width, -1))
        return jnp.concatenate(blocks, axis=-1)

    def gather_rows(self, own):
        whole = first_of(self.member == 0, own, self.over_tensor(own), 0)
        return jnp.concatenate([whole, self.over_core(whole)], axis=0)

    def scatter_rows(self, value):
        half = value.shape[0] // 2
        whole = value[:half] + self.over_core(value[half:])
        half //= 2
        theirs = part_of(whole, 1 - self.member, half, 0)
        peer = self.over_tensor(theirs.astype(BF)).astype(F32)
        return part_of(whole, self.member, half, 0) + peer


def ring_spot(chip, chips):
    line, pair = chip // 2, chip % 2
    return line * (1 - pair) + (chips - 1 - line) * pair


def ring_chip(spot, chips):
    pair = spot // (chips // 2)
    return 2 * (spot * (1 - pair) + (chips - 1 - spot) * pair) + pair


def signal_all(devices):
    barrier = pltpu.get_barrier_semaphore()
    for device in devices:
        pl.semaphore_signal(barrier, inc=1, device_id=device, device_id_type=pl.DeviceIdType.MESH)
    pl.semaphore_wait(barrier, len(devices))


def send(source, target, send_sem, recv_sem, device):
    return pltpu.make_async_remote_copy(
        src_ref=source,
        dst_ref=target,
        send_sem=send_sem,
        recv_sem=recv_sem,
        device_id=device,
        device_id_type=pl.DeviceIdType.MESH,
    )


def staged(sources, targets, sem):
    copies = [pltpu.make_async_copy(*pair, sem.at[i]) for i, pair in enumerate(zip(sources, targets))]
    pending = set(range(len(copies)))
    for copy in copies:
        copy.start()

    def ready(*numbers):
        for i in sorted(pending.intersection(numbers)):
            copies[i].wait()
            pending.remove(i)

    return ready


def spread_kernel(chips, layout, ringed, *refs):
    count = len(layout)
    totals = 1 + max(item[0] for item in layout)
    sources, (tokens, cot, gain, gain_mlp, w_decay) = refs[:count], refs[count : count + 5]
    refs = refs[count + 5 :]
    outs = refs[:totals]
    stream, cot_own, own_gain, own_gain_mlp, rows_mix, rows_cot = refs[totals : totals + 6]
    refs = refs[totals + 6 :]
    normed, near_sem, send_core, recv_core, send_right, recv_right, send_left, recv_left = refs[:8]
    own_sem, send_half, recv_half, send_whole, recv_whole, rate_sum, rate_own, *turned = refs[8:]
    me, member = lax.axis_index("dp"), lax.axis_index("tensor")
    core, chip = me % 2, me // 2
    spot = ring_spot(chip, chips)
    right = (2 * ring_chip((spot + 1) % chips, chips) + core, member)
    left = (2 * ring_chip((spot + chips - 1) % chips, chips) + core, member)
    peer = (2 * chip + 1 - core, member)
    across = (me, 1 - member)
    signal_all((right, left, peer, across))

    def home(out):
        return outs[out].at[0] if out < ringed else outs[out]

    near, far = [], []
    given = list(sources)
    turned = [(i, target) for i, target in zip([i for i, item in enumerate(layout) if item[3]], turned)]
    sources = list(sources)
    for i, target in turned:
        sources[i] = target
    for i, (out, at, width, _) in enumerate(layout):
        if width is None:
            place = home(out).at[core]
            near.append(pltpu.make_async_copy(rate_own.at[core], place, near_sem.at[i]))
            far.append(send(rate_own.at[1 - core], place, send_core.at[i], recv_core.at[i], peer))
            heads = w_decay.shape[0] // 2
            rate_sum[...] = jnp.zeros_like(rate_sum)
            for at, part in ((0, sources[i][...].astype(F32)), (heads, w_decay[...].astype(F32))):
                for c in range(2):
                    rate_sum[c, at : at + heads] = part[c * heads : (c + 1) * heads]
            rate_own[...] = rate_sum[...].astype(BF)
            continue
        rows = sources[i].shape[0]
        place = home(out).at[pl.ds(pl.multiple_of(core * rows, rows), rows), pl.ds(at, width)]
        mine = sources[i].at[:, pl.ds(pl.multiple_of(core * width, 128), width)]
        theirs = sources[i].at[:, pl.ds(pl.multiple_of((1 - core) * width, 128), width)]
        near.append(pltpu.make_async_copy(mine, place, near_sem.at[i]))
        far.append(send(theirs, place, send_core.at[i], recv_core.at[i], peer))

    def trade_halves(outs_now):
        for i, target in turned:
            if layout[i][0] in outs_now:
                target[...] = given[i][...].T
        for i, item in enumerate(layout):
            if item[0] in outs_now:
                far[i].start()
                near[i].start()

    trade_halves(range(2))

    def hop(out, step, way):
        last = step == chips // 2
        ref = outs[out]
        mid = ref.shape[1] // 2
        if way > 0:
            at, to, device, sends, receives = -(step - 1) % chips, chips - step, right, send_right, recv_right
            rows = pl.ds(0, mid)
        else:
            at, to, device, sends, receives = step - 1, step, left, send_left, recv_left
            rows = pl.ds(mid, mid)
        source, target = ref.at[at], ref.at[to]
        if last:
            source, target = source.at[rows], target.at[rows]
        return send(source, target, sends.at[out, step - 1], receives.at[out, step - 1], device)

    started, own = [], []
    pairs = ((normed, rows_mix), (cot_own, rows_cot))
    halves = [
        send(value, rows.at[0, member], send_half.at[i], recv_half.at[i], across)
        for i, (value, rows) in enumerate(pairs)
    ]
    wholes = [
        send(rows.at[0], rows.at[1], send_whole.at[i], recv_whole.at[i], peer)
        for i, (_, rows) in enumerate(pairs)
    ]
    for step in range(1, chips // 2 + 1):
        for out in range(ringed):
            if step == 1:
                for i, item in enumerate(layout):
                    if item[0] == out:
                        near[i].wait()
                        far[i].wait()
            for way in (1, -1):
                if step > 1:
                    hop(out, step - 1, way).wait_recv()
                copy = hop(out, step, way)
                copy.start()
                started.append(copy)
            if step == 1:
                trade_halves((out + 2,) if out + 2 < ringed else ())
        if step == 1:
            trade_halves(range(ringed, totals))
            width = tokens.shape[1] // chips
            aligned = width % 128 == 0
            squares = jnp.zeros((tokens.shape[0], 1), F32)
            for place in range(chips):
                to = pl.ds(place * width, width)
                at = to
                if aligned:
                    at = ring_chip((spot + place) % chips, chips) * width
                    at = pl.ds(pl.multiple_of(at, 128), width)
                stream[:, to] = tokens[:, at]
                cot_own[:, to] = cot[:, at]
                own_gain[:, to] = gain[:, at]
                own_gain_mlp[:, to] = gain_mlp[:, at]
                block = stream[:, to].astype(F32)
                squares = squares + jnp.sum(block * block, axis=1, keepdims=True)
            scale = lax.rsqrt(squares / tokens.shape[1] + 1e-06)
            normed[...] = (stream[...].astype(F32) * scale * own_gain[...]).astype(BF)
            for i, (value, rows) in enumerate(pairs):
                own.append(pltpu.make_async_copy(value, rows.at[0, member], own_sem.at[i]))
                own[-1].start()
                halves[i].start()
        if step == 2:
            for i in range(2):
                own[i].wait()
                halves[i].wait()
                wholes[i].start()
    for i, item in enumerate(layout):
        if item[0] >= ringed:
            near[i].wait()
            far[i].wait()
    for copy in wholes:
        copy.wait()
    for out in range(ringed):
        for way in (1, -1):
            hop(out, chips // 2, way).wait_recv()
    for copy in started:
        copy.wait_send()


def spread(grid, groups, ringed, tokens, cot, gains, rates):
    chips = grid.chips
    sources, layout, shapes, turned_shapes = [], [], [], []
    for out, group in enumerate(groups):
        if not isinstance(group, list):
            rate = (2, group, rates[0].shape[1])
            layout.append((out, 0, None, False))
            sources.append(rates[0])
            shapes.append(jax.ShapeDtypeStruct((chips,) + rate, BF))
            continue
        at = 0
        for shard in group:
            turned = isinstance(shard, tuple)
            if turned:
                (shard,) = shard
                turned_shapes.append(pltpu.VMEM(shard.shape[::-1], BF))
            width = shard.shape[0 if turned else 1] // 2
            layout.append((out, at, width, turned))
            sources.append(shard)
            at += width
        rows = 2 * tokens.shape[1] // grid.devices
        shapes.append(jax.ShapeDtypeStruct(((chips,) if out < ringed else ()) + (rows, at), BF))
    dma = pltpu.SemaphoreType.DMA
    hops = (ringed, chips // 2)
    anywhere = pl.BlockSpec(memory_space=pltpu.HBM)
    near = pl.BlockSpec(memory_space=pltpu.VMEM)
    own = jax.ShapeDtypeStruct(tokens.shape, BF)
    rows = jax.ShapeDtypeStruct((2, 2) + tokens.shape, BF)
    return pl.pallas_call(
        partial(spread_kernel, chips, layout, ringed),
        out_shape=shapes + [own, own] + [jax.ShapeDtypeStruct(gains[0].shape, F32)] * 2 + [rows, rows],
        in_specs=[near if item[3] or item[2] is None else anywhere for item in layout] + [near] * 5,
        out_specs=[near] * ringed + [anywhere] * (len(shapes) - ringed) + [near] * 4 + [anywhere] * 2,
        scratch_shapes=[pltpu.VMEM(tokens.shape, BF)]
        + [dma((len(sources),))] * 3
        + [dma(hops)] * 4
        + [dma((2,))] * 5
        + [pltpu.VMEM(rate, F32), pltpu.VMEM(rate, BF)]
        + turned_shapes,
        compiler_params=pltpu.CompilerParams(
            collective_id=0, has_side_effects=True, vmem_limit_bytes=62 << 20
        ),
        name="spread",
    )(*sources, tokens, cot, *gains, rates[1])


PARTS = 2


def exchange(part, own_part, rows_out, buffers, sems, compute, early=None, late=None):
    got_core, sent_half, got_half, own = buffers
    me, member = lax.axis_index("dp"), lax.axis_index("tensor")
    peer = (me + 1 - 2 * (me % 2), member)
    across = (me, 1 - member)
    count = part.shape[2] // PARTS

    def chunk(k):
        return pl.ds(k * count, count)

    def copy(kind, k, source, target, device):
        return send(source, target, sems[2 * kind].at[k], sems[2 * kind + 1].at[k], device)

    first = [copy(0, k, part.at[1, :, chunk(k)], got_core.at[:, chunk(k)], peer) for k in range(PARTS)]
    second = [copy(1, k, sent_half.at[chunk(k)], got_half.at[chunk(k)], across) for k in range(PARTS)]
    third = [
        copy(2, k, own.at[chunk(k)], rows_out.at[0, member, chunk(k)], across) for k in range(PARTS)
    ]
    fourth = [
        copy(3, k, own.at[chunk(k)], rows_out.at[1, member, chunk(k)], peer) for k in range(PARTS)
    ]
    fifth = [
        copy(4, k, rows_out.at[0, 1 - member, chunk(k)], rows_out.at[1, 1 - member, chunk(k)], peer)
        for k in range(PARTS)
    ]
    for k in range(PARTS):
        first[k].start()
    if early:
        early()
    for k in range(PARTS):
        first[k].wait_recv()
        total = own_part[1 - member, chunk(k)] + got_core[1 - member, chunk(k)]
        sent_half[chunk(k)] = total.astype(BF)
        second[k].start()
    for k in range(PARTS):
        second[k].wait_recv()
        total = own_part[member, chunk(k)] + got_core[member, chunk(k)] + got_half[chunk(k)].astype(F32)
        value = compute(k, chunk(k), total).astype(BF)
        own[chunk(k)] = value
        third[k].start()
        fourth[k].start()
        rows_out[0, member, chunk(k)] = value
    for k in range(PARTS):
        third[k].wait_recv()
        fifth[k].start()
    if late:
        late()
    for k in range(PARTS):
        fourth[k].wait_recv()
        fifth[k].wait_recv()
    for copies in (first, second, third, fourth, fifth):
        for one in copies:
            one.wait_send()


def exchange_scratch(rows, width):
    return [
        pltpu.VMEM((2, rows, width), F32),
        pltpu.VMEM((rows, width), BF),
        pltpu.VMEM((rows, width), BF),
        pltpu.VMEM((rows, width), BF),
    ] + [pltpu.SemaphoreType.DMA((PARTS,))] * 10


def middle_kernel(part, stream, gain, rows_out, middle, *scratch):
    me, member = lax.axis_index("dp"), lax.axis_index("tensor")
    signal_all(((me + 1 - 2 * (me % 2), member), (me, 1 - member)))

    def compute(k, rows, mixed):
        value = stream[rows].astype(F32) + mixed
        middle[rows] = value
        return value * lax.rsqrt(jnp.mean(value * value, axis=1, keepdims=True) + 1e-06) * gain[...]

    exchange(part, part.at[0], rows_out, scratch[:4], scratch[4:], compute)


def middle_rows(part, stream, gain):
    rows, width = stream.shape
    near = pl.BlockSpec(memory_space=pltpu.VMEM)
    gathered, middle = pl.pallas_call(
        middle_kernel,
        out_shape=[
            jax.ShapeDtypeStruct((2, 2, rows, width), BF),
            jax.ShapeDtypeStruct((rows, width), F32),
        ],
        in_specs=[near] * 3,
        out_specs=[near] * 2,
        scratch_shapes=exchange_scratch(rows, width),
        compiler_params=pltpu.CompilerParams(
            collective_id=1, has_side_effects=True, vmem_limit_bytes=32 << 20
        ),
        name="middle",
    )(part.reshape(2, 2, rows, width), stream, gain)
    return gathered.reshape(4 * rows, width), middle


def turn_kernel(chips, heads, ffw, early, *refs):
    refs = list(refs)

    def take(count):
        taken, refs[:] = refs[:count], refs[count:]
        return taken

    part, gain = take(2)
    small_inputs, later = take(8), take(17)
    rows_out, grad_middle, grad_gain, late = take(4)
    results = take(8)
    grad_heads, going, arrived = take(3)
    here_now, (later_sem,) = take(17), take(1)
    send_ring, recv_ring = take(2)
    me, member = lax.axis_index("dp"), lax.axis_index("tensor")
    core, chip = me % 2, me // 2
    spot = ring_spot(chip, chips)
    ways = (
        (2 * ring_chip((spot + 1) % chips, chips) + core, member),
        (2 * ring_chip((spot + chips - 1) % chips, chips) + core, member),
    )
    rows_cot, rows_mlp, hidden, grad_gate, begun, own_part, cot, middle, wout, *kept = here_now[:14]
    inputs = here_now[14:] + small_inputs
    later[5] = later[5].at[0]
    ready = staged(later, here_now, later_sem)
    signal_all((*ways, (me + 1 - 2 * core, member), (me, 1 - member)))
    half = chips // 2
    width = rows_cot.shape[1] // chips
    mid = width // 2

    def total(way, place, step):
        at = (place if way == 0 else -place) % chips * width
        value = []
        for left, right, size in ((rows_cot, hidden, ffw), (rows_mlp, grad_gate, early)):
            value.append(
                lax.dot_general(
                    left[:, at : at + width],
                    right[:, 0:size],
                    (COLS_ROWS, ((), ())),
                    preferred_element_type=F32,
                )
            )
        value = jnp.concatenate(value, axis=1)
        if step:
            return (value + arrived[way, step - 1].astype(F32)).astype(BF)
        lo = mid * way
        here = value[lo : lo + mid] + begun[way].astype(F32)
        rest = value[mid - lo : width - lo]
        return jnp.concatenate([here, rest] if way == 0 else [rest, here], axis=0).astype(BF)

    def hop(way, step):
        sems = (way, step)
        source = arrived.at[way, step - 1] if step else going.at[way]
        return send(source, arrived.at[sems], send_ring.at[sems], recv_ring.at[sems], ways[way])

    def next_hop(step):
        for way in range(2):
            if step:
                hop(way, step - 1).wait_recv()
            value = total(way, half - 1 - step, step)
            if step == half - 2:
                late[way] = value
                continue
            if step:
                arrived[way, step - 1] = value
            else:
                going[way] = value
            hop(way, step).start()

    def compute(k, rows, grad):
        value = middle[rows]
        scale = lax.rsqrt(jnp.mean(value * value, axis=1, keepdims=True) + 1e-06)
        unit_value = value * scale
        gained = jnp.sum(grad * unit_value, axis=0, keepdims=True)
        grad_gain[...] = gained if k == 0 else grad_gain[...] + gained
        grad = grad * gain[...]
        grad = scale * (grad - unit_value * jnp.mean(grad * unit_value, axis=1, keepdims=True))
        grad = grad + cot[rows].astype(F32)
        grad_middle[rows] = grad
        return grad


    def early_work():
        ready(*range(5))
        next_hop(0)
        ready(5, 6, 7)

    def late_work():
        if half > 3:
            next_hop(1)

    exchange(part, own_part, rows_out, refs[:4], refs[4:], compute, early_work, late_work)
    ready(*range(17))
    for step in range(2, half - 2):
        next_hop(step)
    for ref in results[3:]:
        ref[...] = jnp.zeros_like(ref)
    length = inputs[0].shape[0] // 2

    @pl.loop(0, 2)
    def _(s):
        at = pl.multiple_of(s * length, length)
        here = pl.ds(at, length)
        for m in range(2):
            grad_heads[pl.ds(at + m * (length // 2), length // 2)] = jnp.dot(
                rows_out[s, m], wout[...], preferred_element_type=F32
            )
        mixer_back(
            heads,
            grad_heads.at[here],
            [ref.at[here] for ref in inputs[:3]] + [ref.at[pl.ds(s, 1)] for ref in inputs[3:5]] + inputs[5:],
            [ref.at[pl.ds(s, 1)] for ref in kept[:4]] + [kept[4].at[here]],
            [ref.at[here] for ref in results[:3]] + results[3:],
        )

    next_hop(half - 2)
    for step in range(half - 2):
        for way in range(2):
            hop(way, step).wait_send()


def turn(grid, heads, early, part, cot, middle, gain, wout, rows_cot, rows_mlp, hidden, grad_gate, begun, inputs, kept):
    chips = grid.chips
    rows, width = middle.shape
    block, half = width // chips, chips // 2
    ffw = hidden.shape[1]
    n = ffw + early
    qk, rates_in, vg, _, _, cq, ck, cv, log, _, out_gain = inputs
    near = pl.BlockSpec(memory_space=pltpu.VMEM)
    far = pl.BlockSpec(memory_space=pltpu.HBM)
    dma = pltpu.SemaphoreType.DMA
    sums = [cq.shape, ck.shape, cv.shape, (2, log.shape[1]), out_gain.shape]
    part = part.reshape(2, 2, rows, width)
    near_in = (gain, *inputs[3:])
    later = (rows_cot, rows_mlp, hidden, grad_gate, begun, part, cot, middle, wout, *kept, *inputs[:3])
    held = [value.shape[1:] if value is part else value.shape for value in later]
    gathered, *rest = pl.pallas_call(
        partial(turn_kernel, chips, heads, ffw, early),
        out_shape=[
            jax.ShapeDtypeStruct((2, 2, rows, width), BF),
            jax.ShapeDtypeStruct((rows, width), F32),
            jax.ShapeDtypeStruct((1, width), F32),
            jax.ShapeDtypeStruct((2, block, n), BF),
            jax.ShapeDtypeStruct(qk.shape, BF),
            jax.ShapeDtypeStruct(rates_in.shape, BF),
            jax.ShapeDtypeStruct(vg.shape, BF),
        ]
        + [jax.ShapeDtypeStruct(shape, F32) for shape in sums],
        in_specs=[far] + [near] * len(near_in) + [far] * len(later),
        out_specs=[near] * (7 + len(sums)),
        scratch_shapes=[
            pltpu.VMEM((4 * rows, cv.shape[1]), F32),
            pltpu.VMEM((2, block, n), BF),
            pltpu.VMEM((2, half - 2, block, n), BF),
            *[pltpu.VMEM(shape, value.dtype) for shape, value in zip(held, later)],
            dma((len(later),)),
            dma((2, half - 2)),
            dma((2, half - 2)),
        ]
        + exchange_scratch(rows, width),
        compiler_params=pltpu.CompilerParams(
            collective_id=2, has_side_effects=True, vmem_limit_bytes=62 << 20
        ),
        name="turn",
    )(part, *near_in, *later)
    return gathered.reshape(4 * rows, width), *rest


def mlp_kernel(chips, ffw, early, *refs):
    rows_far, cot_far, own, right_1, left_1, right_2, left_2 = refs[:7]
    hidden, gate_early, gate_rest, grad_upper, back, ahead, begun = refs[7:14]
    rows, cot, rows_sem, weights, sums, begin, load_sem, send_ring, recv_ring, send_begin, recv_begin = refs[14:]
    me, member = lax.axis_index("dp"), lax.axis_index("tensor")
    core, chip = me % 2, me // 2
    spot = ring_spot(chip, chips)
    ways = (
        (2 * ring_chip((spot + 1) % chips, chips) + core, member),
        (2 * ring_chip((spot + chips - 1) % chips, chips) + core, member),
    )
    signal_all(ways)
    half = chips // 2
    block = own.shape[0]
    mid = block // 2

    def spots(place, lo=0, hi=block):
        return pl.ds((place % chips) * block + lo, hi - lo)

    def hop(way, step):
        place, to = (1 - step, -step) if way == 0 else (step - 1, step)
        lo, hi = (0, block) if step < half else (mid * way, mid * way + mid)
        if step == 3:
            source = (right_2, left_2)[way].at[pl.ds(lo, hi - lo)]
        else:
            source = weights.at[spots(place, lo, hi)]
        sems = (way, step - 3)
        return send(source, weights.at[spots(to, lo, hi)], send_ring.at[sems], recv_ring.at[sems], ways[way])

    for way in range(2):
        hop(way, 3).start()
    loads = []
    for number, (place, source) in enumerate(((0, own), (1, left_1), (2, left_2), (-2, right_2), (-1, right_1))):
        loads.append(pltpu.make_async_copy(source, weights.at[spots(place)], load_sem.at[number]))
        loads[-1].start()

    ready = staged((rows_far, cot_far), (rows, cot), rows_sem)
    tile = ffw // 2

    def add(lo, hi, first):
        inner = slice((lo % chips) * block, (lo % chips + hi - lo) * block)
        for at in range(0, 3 * ffw, tile):
            left = rows if at < 2 * ffw else cot
            value = jnp.dot(left[:, inner], weights[inner, at : at + tile], preferred_element_type=F32)
            sums[:, at : at + tile] = value if first else sums[:, at : at + tile] + value

    ready(0, 1)
    for copy in loads[:3]:
        copy.wait()
    add(0, 3, True)
    for copy in loads[3:]:
        copy.wait()
    add(-2, 0, False)
    for step in range(3, half):
        for way in range(2):
            hop(way, step).wait_recv()
            hop(way, step + 1).start()
        add(step, step + 1, False)
        add(-step, 1 - step, False)
    for way in range(2):
        hop(way, half).wait_recv()
    add(half, half + 1, False)

    for at in range(0, ffw, 128):
        gate, upper = sums[:, at : at + 128], sums[:, ffw + at : ffw + at + 128]
        grad = sums[:, 2 * ffw + at : 2 * ffw + at + 128]
        open_gate = jax.nn.sigmoid(gate)
        passed = gate * open_gate
        hidden[:, at : at + 128] = (passed * upper).astype(BF)
        part, to = (gate_early, at) if at < early else (gate_rest, at - early)
        part[:, to : to + 128] = (grad * upper * silu_back(gate, open_gate)).astype(BF)
        grad_upper[:, at : at + 128] = (grad * passed).astype(BF)

    starts = []
    for way in range(2):
        lo = half * block + mid * way
        for left, right, at, size in ((cot, hidden, 0, ffw), (rows, gate_early, ffw, early)):
            begin[way, :, at : at + size] = lax.dot_general(
                left[:, lo : lo + mid],
                right[:, 0:size],
                (COLS_ROWS, ((), ())),
                preferred_element_type=F32,
            ).astype(BF)
        starts.append(send(begin.at[way], begun.at[way], send_begin.at[way], recv_begin.at[way], ways[way]))
        starts[-1].start()
    for place in range(chips):
        inner = slice(place * block, (place + 1) * block)
        value, at = 0.0, 0
        for part in (gate_early, gate_rest, grad_upper):
            cols = slice(at, at + part.shape[1])
            value = value + lax.dot_general(
                part[...], weights[inner, cols], (ROWS_ROWS, ((), ())), preferred_element_type=F32
            )
            at += part.shape[1]
        back[:, inner] = value
        ahead[:, inner] = lax.dot_general(
            hidden[...], weights[inner, 2 * ffw :], (ROWS_ROWS, ((), ())), preferred_element_type=F32
        ).astype(BF)
    for copy in starts:
        copy.wait()
    for step in range(3, half + 1):
        for way in range(2):
            hop(way, step).wait_send()


def mlp(grid, rows, cot, chunks, ffw, early):
    chips = grid.chips
    count, width = rows.shape
    block, n = chunks[0].shape
    half = chips // 2
    near = pl.BlockSpec(memory_space=pltpu.VMEM)
    far = pl.BlockSpec(memory_space=pltpu.HBM)
    dma = pltpu.SemaphoreType.DMA
    inner = jax.ShapeDtypeStruct((count, ffw), BF)
    return pl.pallas_call(
        partial(mlp_kernel, chips, ffw, early),
        out_shape=[
            inner,
            jax.ShapeDtypeStruct((count, early), BF),
            jax.ShapeDtypeStruct((count, ffw - early), BF),
            inner,
            jax.ShapeDtypeStruct((count, width), F32),
            jax.ShapeDtypeStruct((count, width), BF),
            jax.ShapeDtypeStruct((2, block // 2, ffw + early), BF),
        ],
        in_specs=[far] * 7,
        out_specs=[near] * 7,
        scratch_shapes=[
            pltpu.VMEM(rows.shape, BF),
            pltpu.VMEM(rows.shape, BF),
            dma((2,)),
            pltpu.VMEM((chips * block, n), BF),
            pltpu.VMEM((count, n), F32),
            pltpu.VMEM((2, block // 2, ffw + early), BF),
            dma((5,)),
            dma((2, half - 2)),
            dma((2, half - 2)),
            dma((2,)),
            dma((2,)),
        ],
        compiler_params=pltpu.CompilerParams(
            collective_id=4, has_side_effects=True, vmem_limit_bytes=56 << 20
        ),
        name="mlp",
    )(rows, cot, *chunks)


def collect_kernel(chips, steps, groups, late_parts, fields, side_of, counts, *refs):
    n_left, n_right, n_out, n_side = counts
    refs = list(refs)

    def take(count):
        taken, refs[:] = refs[:count], refs[count:]
        return taken

    far = take(n_left + n_right)
    late_out, late_left = take(2)
    weights = take(n_side)
    ahead_far, *far_tokens = take(4)
    gain, mlp_grad, rate_weights = take(3)
    grad_cq, grad_ck, grad_cv, grad_rate, grad_gain = take(5)
    outs = take(n_out)
    rates_out, out_tokens, grad_tokens, *small_outs = take(5)
    begin, arrived, late_in, final, back, got_core, sent_half, got_half, *small_ins = take(10)
    buffers = take(n_side)
    near, near_tokens = take(n_left + n_right), take(4)
    lefts, rights = near[:n_left], near[n_left:]
    ahead, stream, middle, grad_middle = near_tokens
    (far_sem,) = take(1)
    send_ring, recv_ring, own_sem, send_core, recv_core, send_late, recv_late = take(7)
    send_first, recv_first, send_second, recv_second, send_small, recv_small, weight_sem, free = take(8)
    rate_begin, rate_arrived, rate_final, send_rate, recv_rate, rate_sems = take(6)
    me, member = lax.axis_index("dp"), lax.axis_index("tensor")
    core, chip = me % 2, me // 2
    spot = ring_spot(chip, chips)
    ways = (
        (2 * ring_chip((spot + 1) % chips, chips) + core, member),
        (2 * ring_chip((spot + chips - 1) % chips, chips) + core, member),
    )
    peer = (2 * chip + 1 - core, member)
    across = (me, 1 - member)
    partners = [across] + [
        (me + (1 << k) - 2 * (1 << k) * ((me // (1 << k)) % 2), member) for k in range(steps - 1)
    ]
    signal_all(list(ways) + partners)

    half = chips // 2
    width = lefts[0].shape[1] // chips
    mid = width // 2
    starts = []
    at = 0
    for _, right in groups:
        starts.append(at)
        at += rights[right].shape[1]

    def columns(group):
        return pl.ds(starts[group], rights[groups[group][1]].shape[1])

    def piece(group, place, lo=0, hi=width):
        left, right = lefts[groups[group][0]], rights[groups[group][1]]
        at = (place % chips) * width
        return lax.dot_general(
            left[:, at + lo : at + hi], right[...], (COLS_ROWS, ((), ())), preferred_element_type=F32
        )

    def rows_of(way):
        return pl.ds(mid * way, mid)

    def hop(way, step, group):
        if step:
            source, target = arrived.at[way, step - 1], arrived.at[way, step % (half - 1)]
            source, target = source.at[:, columns(group)], target.at[:, columns(group)]
        else:
            source = begin.at[way, :, columns(group)]
            target = arrived.at[way, 0, rows_of(way), columns(group)]
        sems = (way, step, group)
        return send(source, target, send_ring.at[sems], recv_ring.at[sems], ways[way])

    rate_rows = rate_begin.shape[1]

    def rate_piece(place):
        at = (place % chips) * width
        value = lax.dot_general(
            rights[-1][:, 0:rate_rows], lefts[-1][:, at : at + width], (COLS_ROWS, ((), ())), preferred_element_type=F32
        )
        return value[:, 0:mid], value[:, mid:width]

    def rate_hop(way, step):
        source = rate_arrived.at[way, step - 1] if step else rate_begin.at[way]
        target = rate_arrived.at[way, step % (half - 1)] if step else rate_arrived.at[way, 0, way]
        sems = (way, step)
        return send(source, target, send_rate.at[sems], recv_rate.at[sems], ways[way])

    def rate_step(step, place):
        for way in range(2):
            rate_hop(way, step).wait_recv()
            for c, value in enumerate(rate_piece(place if way == 0 else -place)):
                if step or c == way:
                    value = value + rate_arrived[way, step, c].astype(F32)
                rate_arrived[way, step, c] = value.astype(BF)
            rate_hop(way, step + 1).start()

    late = [send(late_out.at[way], late_in.at[way], send_late.at[way], recv_late.at[way], ways[way]) for way in range(2)]
    sides = (back, ahead)
    first = [
        send(value.at[1], got_core.at[i], send_first.at[i], recv_first.at[i], peer)
        for i, value in enumerate((back, ahead_far))
    ]
    second = [
        send(sent_half.at[i], got_half.at[i], send_second.at[i], recv_second.at[i], across) for i in range(2)
    ]

    def fold_small(step):
        copies = []
        for i, (out, arrivals) in enumerate(zip(small_outs, small_ins)):
            source = arrivals.at[steps + step - 1] if step else out
            sems = (step, i)
            copies.append(send(source, arrivals.at[step], send_small.at[sems], recv_small.at[sems], partners[step]))
        return copies

    def put(ref, value):
        if width % 128:
            ref[...] = value
            return
        for place in range(chips):
            at = pl.multiple_of(ring_chip((spot + place) % chips, chips) * width, 128)
            ref[:, pl.ds(at, width)] = value[:, place * width : (place + 1) * width]

    def fetch(place):
        return [
            pltpu.make_async_copy(
                weight.at[pl.ds(place * width, width), pl.ds(at, buffer.shape[2])],
                buffer.at[place % 2],
                weight_sem.at[number, place % 2],
            )
            for number, (weight, (at, _), buffer) in enumerate(zip(weights, side_of, buffers))
        ]

    def side_work():
        for place in range(chips):
            if place + 1 < chips:
                for copy in fetch(place + 1):
                    copy.start()
            for copy in fetch(place):
                copy.wait()
            total = jnp.dot(
                rights[-1][:, 0:rate_rows],
                rate_weights[:, place * width : (place + 1) * width],
                preferred_element_type=F32,
            )
            for (_, right), buffer in zip(side_of, buffers):
                total = total + lax.dot_general(
                    rights[right][...],
                    buffer[place % 2],
                    (ROWS_ROWS, ((), ())),
                    preferred_element_type=F32,
                )
            back[:, :, :, place * width : (place + 1) * width] = (
                total.astype(BF).reshape(2, 2, middle.shape[0], width)
            )
            yield
        for copy in first:
            copy.start()
        yield
        ready(*range(n_left + n_right, n_left + n_right + 4))
        for i in range(2):
            first[i].wait_recv()
            total = sides[i][0, 1 - member].astype(F32) + got_core[i, 1 - member].astype(F32)
            sent_half[i] = total.astype(BF)
            second[i].start()
        yield
        total = []
        for i in range(2):
            second[i].wait_recv()
            value = sides[i][0, member].astype(F32) + got_core[i, member].astype(F32)
            total.append(value + got_half[i].astype(F32))
        put(out_tokens, middle[...] + total[1])
        value = stream[...].astype(F32)
        scale = lax.rsqrt(jnp.mean(value * value, axis=1, keepdims=True) + 1e-06)
        value = value * scale
        gained = jnp.sum(total[0] * value, axis=0, keepdims=True)
        grad = total[0] * gain[...]
        grad = scale * (grad - value * jnp.mean(grad * value, axis=1, keepdims=True))
        put(grad_tokens, grad_middle[...] + grad)
        small_out, wide = small_outs
        small_out[...] = jnp.zeros_like(small_out)
        wide[...] = jnp.zeros_like(wide)
        quarter = 2 * member + core
        taps, keyw = grad_cq.shape
        valw = grad_cv.shape[1]
        after = max(8 * keyw, 4 * valw)

        def part(at, size):
            return pl.ds(pl.multiple_of(at + quarter * size, 128), size)

        wide[0:taps, part(0, keyw)] = grad_cq[...]
        wide[0:taps, part(4 * keyw, keyw)] = grad_ck[...]
        wide[taps : 2 * taps, part(0, valw)] = grad_cv[...]
        wide[0:1, after : after + grad_gain.shape[1]] = grad_gain[...]
        wide[0:2, part(after + grad_gain.shape[1], grad_rate.shape[1])] = grad_rate[...]
        lanes = min(width, 128)
        each = width // lanes
        for i, vector in enumerate((gained, mlp_grad[...])):
            for place in range(chips):
                row = (i * chips + ring_chip((spot + place) % chips, chips)) * each
                for k in range(each):
                    at = place * width + k * lanes
                    small_out[pl.ds(row + k, 1), 0:lanes] = vector[:, at : at + lanes]
        for copy in fold_small(0):
            copy.start()
        yield
        for step in range(steps):
            for copy in fold_small(step):
                copy.wait_recv()
            for out, arrivals in zip(small_outs, small_ins):
                before = arrivals.at[steps + step - 1] if step else out
                arrivals[steps + step] = before[...] + arrivals[step]
            if step + 1 < steps:
                for copy in fold_small(step + 1):
                    copy.start()
            yield

    work = side_work()
    ready = staged([*far, ahead_far.at[pl.ds(0, 1)], *far_tokens], near + near_tokens, far_sem)
    for copy in late + fetch(0):
        copy.start()
    for group in range(len(groups)):
        ready(groups[group][0], n_left + groups[group][1])
        for way in range(2):
            begin[way, :, columns(group)] = piece(group, half, mid * way, mid * way + mid).astype(BF)
            hop(way, 0, group).start()
    ready(*range(n_left + n_right))
    for way in range(2):
        rate_begin[way] = rate_piece(half)[way].astype(BF)
        rate_hop(way, 0).start()
    for step in range(half - 1):
        place = half - 1 - step
        for group in range(len(groups)):
            next(work, None)
            next(work, None)
            for way in range(2):
                hop(way, step, group).wait_recv()
                value = piece(group, place if way == 0 else -place)
                if step:
                    value = value + arrived[way, step, :, columns(group)].astype(F32)
                    arrived[way, step, :, columns(group)] = value.astype(BF)
                else:
                    lo = mid * way
                    here = value[lo : lo + mid] + arrived[way, 0, rows_of(way), columns(group)].astype(F32)
                    arrived[way, 0, rows_of(way), columns(group)] = here.astype(BF)
                    arrived[way, 0, rows_of(1 - way), columns(group)] = value[
                        mid - lo : width - lo
                    ].astype(BF)
                if step == half - 2 and group == 0:
                    pl.semaphore_wait(free.at[way], 1)
                hop(way, step + 1, group).start()
            if group == 0:
                rate_step(step, place)
        if step == min(1, half - 3):
            for way in range(2):
                rate_hop(way, 1).wait_send()
                for group in range(len(groups)):
                    hop(way, 1, group).wait_send()
                pl.semaphore_signal(
                    free.at[way], inc=1, device_id=ways[1 - way], device_id_type=pl.DeviceIdType.MESH
                )
    for _ in work:
        pass
    for step in range(steps):
        for copy in fold_small(step):
            copy.wait_send()
    for out, arrivals in zip(small_outs, small_ins):
        out[...] = arrivals[2 * steps - 1]

    rows = width // 2
    finals, used = [], {}
    values = rate_piece(0)
    for way in range(2):
        rate_hop(way, half - 1).wait_recv()
        values = [value + rate_arrived[way, 0, c].astype(F32) for c, value in enumerate(values)]
    for c in range(2):
        rate_final[c] = values[c]
    rate_own = pltpu.make_async_copy(rate_final.at[core], rates_out.at[core], rate_sems.at[0])
    rate_far = send(rate_final.at[1 - core], rates_out.at[core], rate_sems.at[1], rate_sems.at[2], peer)
    rate_own.start()
    rate_far.start()
    for group in [len(groups)] + list(range(len(groups))):
        slot = group % 2
        for copy in used.get(slot, ()):
            copy()
        if group == len(groups):
            value = []
            for left, right in late_parts:
                left = late_left if left is None else lefts[left]
                value.append(
                    lax.dot_general(
                        left[:, 0:width],
                        rights[right][...],
                        (COLS_ROWS, ((), ())),
                        preferred_element_type=F32,
                    )
                )
            value = jnp.concatenate(value, axis=1)
        else:
            value = piece(group, 0)
        for way in range(2):
            if group == len(groups):
                late[way].wait_recv()
                value = value + late_in[way].astype(F32)
            else:
                hop(way, half - 1, group).wait_recv()
                value = value + arrived[way, 0, :, columns(group)].astype(F32)
        final[slot, :, 0 : value.shape[1]] = value
        used[slot] = []
        for number, (owner, at, out, to, whole, size) in enumerate(fields):
            if owner == group:
                own = pl.ds(pl.multiple_of(core * rows, rows), rows)
                theirs = pl.ds(pl.multiple_of((1 - core) * rows, rows), rows)
                target = outs[out].at[:, pl.ds(pl.multiple_of(core * whole + to, 128), size)]
                copy = pltpu.make_async_copy(final.at[slot, own, pl.ds(at, size)], target, own_sem.at[number])
                far = send(
                    final.at[slot, theirs, pl.ds(at, size)],
                    target,
                    send_core.at[number],
                    recv_core.at[number],
                    peer,
                )
                copy.start()
                far.start()
                finals.append(far)
                used[slot] += [copy.wait, far.wait_send]
    for slot in used:
        for copy in used[slot]:
            copy()
    for far in finals:
        far.wait_recv()
    rate_own.wait()
    rate_far.wait()
    for way in range(2):
        for step in range(half):
            if step != 1:
                rate_hop(way, step).wait_send()
    for copy in first + second + late:
        copy.wait_send()
    for step in range(half):
        for group in range(len(groups)):
            for way in range(2):
                if step != 1:
                    hop(way, step, group).wait_send()


def collect(grid, lefts, rights, groups, late, fields, sides, ahead, tokens_in, small, small_shapes, rate_weights):
    chips = grid.chips
    rows, width = tokens_in[2].shape
    steps = grid.devices.bit_length()
    n = sum(rights[right].shape[1] for _, right in groups)
    widest = max([rights[right].shape[1] for _, right in groups] + [late[0].shape[2]])
    block = width // chips
    half = chips // 2
    *late, late_parts = late
    weights = [weight for weight, _, _ in sides]
    side_of = [(at, right) for _, at, right in sides]
    stream, gain, middle, grad_middle, mlp_grad = tokens_in
    tokens_in = [ahead.reshape(2, 2, rows, width), stream, middle, grad_middle]
    inputs = [*lefts, *rights, *late, *weights, *tokens_in, gain, mlp_grad, rate_weights, *small]
    wholes = {}
    for _, _, out, _, whole in fields:
        wholes[out] = whole
    outs = [jax.ShapeDtypeStruct((block // 2, 2 * wholes[out]), F32) for out in range(len(wholes))]
    ends = [sum(rights[right].shape[1] for _, right in late_parts)]
    ends = [rights[right].shape[1] for _, right in groups] + ends
    sized = []
    for i, (group, at, out, to, whole) in enumerate(fields):
        starts = [other[1] for other in fields if other[0] == group and other[1] > at]
        sized.append((group, at, out, to, whole, min(starts + [ends[group]]) - at))
    fields = sized
    tokens = jax.ShapeDtypeStruct((rows, width), F32)
    near = pl.BlockSpec(memory_space=pltpu.VMEM)
    far = pl.BlockSpec(memory_space=pltpu.HBM)
    dma = pltpu.SemaphoreType.DMA
    ring = (2, half, len(groups))
    counts = (len(lefts), len(rights), len(outs), len(sides))
    held = [value.shape for value in (*lefts, *rights)]
    rate = (rate_weights.shape[0], block // 2)
    rates = jax.ShapeDtypeStruct((2,) + rate, F32)
    return pl.pallas_call(
        partial(collect_kernel, chips, steps, groups, late_parts, fields, side_of, counts),
        out_shape=outs + [rates, tokens, tokens] + [jax.ShapeDtypeStruct(shape, F32) for shape in small_shapes],
        in_specs=[far] * (len(held) + 1) + [near] + [far] * (len(sides) + 4) + [near] * 8,
        out_specs=[far] * (len(outs) + 1) + [near] * 4,
        scratch_shapes=[
            pltpu.VMEM((2, block // 2, n), BF),
            pltpu.VMEM((2, half - 1, block, n), BF),
            pltpu.VMEM(late[0].shape, BF),
            pltpu.VMEM((2, block, widest), F32),
            pltpu.VMEM((2, 2, rows, width), BF),
            pltpu.VMEM((2, 2, rows, width), BF),
            pltpu.VMEM((2, rows, width), BF),
            pltpu.VMEM((2, rows, width), BF),
            *[pltpu.VMEM((2 * steps,) + shape, F32) for shape in small_shapes],
        ]
        + [pltpu.VMEM((2, block, rights[right].shape[1]), BF) for _, right in side_of]
        + [pltpu.VMEM(shape, BF) for shape in held]
        + [
            pltpu.VMEM((1, 2, rows, width), BF),
            pltpu.VMEM((rows, width), BF),
            pltpu.VMEM((rows, width), F32),
            pltpu.VMEM((rows, width), F32),
            dma((len(held) + 4,)),
        ]
        + [dma(ring), dma(ring)]
        + [dma((len(fields),))] * 3
        + [dma((2,))] * 6
        + [dma((steps, 2))] * 2
        + [dma((len(sides), 2)), pltpu.SemaphoreType.REGULAR((2,))]
        + [
            pltpu.VMEM((2,) + rate, BF),
            pltpu.VMEM((2, half - 1, 2) + rate, BF),
            pltpu.VMEM((2,) + rate, F32),
            dma((2, half)),
            dma((2, half)),
            dma((3,)),
        ],
        compiler_params=pltpu.CompilerParams(
            collective_id=3, has_side_effects=True, vmem_limit_bytes=63 << 20
        ),
        name="collect",
    )(*inputs)


def finish_kernel(chips, heads, counts, *refs):
    moved, turned = counts
    refs = list(refs)

    def take(count):
        taken, refs[:] = refs[:count], refs[count:]
        return taken

    sources, turning, (rates, gains, wide) = take(moved), take(turned), take(3)
    targets, turned_out = take(moved), take(turned)
    beta, decay, norm_gain, mlp_gain, cq, ck, cv, log, bias, out_gain = take(10)
    held = take(moved)
    sem_in, sem_out = take(2)
    ready = staged(sources, held, sem_in)
    copies = []
    for i, (source, target) in enumerate(zip(held, targets)):
        if len(target.shape) > len(source.shape):
            target = target.at[0]
        ready(i)
        copies.append(pltpu.make_async_copy(source, target, sem_out.at[i]))
        copies[-1].start()
    for source, target in zip(turning, turned_out):
        target[...] = source[...].T
    for core in range(2):
        to = slice(core * heads, (core + 1) * heads)
        beta[to] = rates[core, 0:heads]
        decay[to] = rates[core, heads : 2 * heads]
    lanes = min(norm_gain.shape[1] // chips, 128)
    count = norm_gain.shape[1] // lanes
    for i, vector in enumerate((norm_gain, mlp_gain)):
        for row in range(count):
            vector[:, row * lanes : (row + 1) * lanes] = gains[i * count + row : i * count + row + 1, 0:lanes]
    taps, keyw = cq.shape
    valw = cv.shape[1]
    after = max(2 * keyw, valw)
    cq[...] = wide[0:taps, 0:keyw]
    ck[...] = wide[0:taps, keyw : 2 * keyw]
    cv[...] = wide[taps : 2 * taps, 0:valw]
    out_gain[...] = wide[0:1, after : after + out_gain.shape[1]]
    after += out_gain.shape[1]
    small = (wide.shape[1] - after) // 4
    for quarter in range(4):
        at = after + quarter * small + heads
        to = slice(quarter * heads, (quarter + 1) * heads)
        log[:, to] = wide[0:1, at : at + heads]
        bias[:, to] = wide[1:2, at : at + heads]
    for copy in copies:
        copy.wait()


def finish(grid, heads, moved, turning, rates, gains, wide, vectors, convs):
    near = pl.BlockSpec(memory_space=pltpu.VMEM)
    far = pl.BlockSpec(memory_space=pltpu.HBM)
    out_shape = [jax.ShapeDtypeStruct(shape, F32) for _, shape in moved]
    out_shape += [jax.ShapeDtypeStruct(value.shape[::-1], F32) for value in turning]
    rate = jax.ShapeDtypeStruct((2 * heads, rates.shape[2]), F32)
    vectors = [jax.ShapeDtypeStruct((1, size), F32) for size in vectors]
    convs = [jax.ShapeDtypeStruct(value.shape, F32) for value in convs]
    small = [rate, rate, *vectors[:2], *convs, *vectors[2:]]
    return pl.pallas_call(
        partial(finish_kernel, grid.chips, heads, (len(moved), len(turning))),
        out_shape=out_shape + small,
        in_specs=[far] * len(moved) + [near] * (len(turning) + 3),
        out_specs=[far] * len(moved) + [near] * (len(turning) + len(small)),
        scratch_shapes=[pltpu.VMEM(value.shape, F32) for value, _ in moved]
        + [pltpu.SemaphoreType.DMA((len(moved),))] * 2,
        compiler_params=pltpu.CompilerParams(vmem_limit_bytes=63 << 20),
        name="finish",
    )(*[value for value, _ in moved], *turning, rates, gains, wide)


def whole_rows(stack):
    return stack.reshape(-1, stack.shape[-1])


def per_device(
    tokens,
    segment_ids,
    norm_gain,
    w_query,
    w_key,
    w_value,
    w_outgate,
    w_beta,
    w_decay,
    conv_query,
    conv_key,
    conv_value,
    decay_log,
    decay_bias,
    out_gain,
    w_output,
    mlp_gain,
    w_gate,
    w_up,
    w_down,
    cotangent,
    *,
    devices,
):
    grid = Grid(devices)
    heads = w_beta.shape[1] // 2
    keyw = w_query.shape[1] // 2
    valw = w_value.shape[1] // 2
    ffw = w_gate.shape[1] // 2
    small = -(-2 * heads // 128) * 128

    rate_rows = -(-2 * heads // 16) * 16
    groups = [[w_query, w_key], [w_value, w_outgate], [(w_output,)], rate_rows, [w_gate, w_up, (w_down,)]]
    shown = (tokens[0], cotangent[0], norm_gain[None], mlp_gain[None])
    if norm_gain.shape[0] // grid.chips % 128:
        shown = [grid.into(value) for value in shown]
    *gathered, stream, cot_own, norm_row, mlp_row, rows_mix, cot_rows = spread(
        grid, groups, 4, *shown[:2], shown[2:], (w_beta.T, w_decay.T)
    )
    wqk, wvg, wout = [whole_rows(stack) for stack in gathered[:3]]
    rows_mix, cot_rows = [rows.reshape(-1, rows.shape[-1]) for rows in (rows_mix, cot_rows)]
    segments = jnp.concatenate([segment_ids, grid.over_core(segment_ids)], axis=0)

    conv_parts = [
        part_of(conv_query, grid.quarter, keyw, 1),
        part_of(conv_key, grid.quarter, keyw, 1),
        part_of(conv_value, grid.quarter, valw, 1),
        part_of(decay_log, grid.quarter, heads, 0),
        part_of(decay_bias, grid.quarter, heads, 0),
    ]
    rate_weights = gathered[3].transpose(2, 0, 1, 3).reshape(rate_rows, -1)
    pre_qk = dot(rows_mix, wqk)
    pre_rates = jnp.pad(cols_product(rows_mix, rate_weights), ((0, 0), (0, small - rate_rows)))
    pre_vg = dot(rows_mix, wvg)
    lanes = [jnp.pad(part[None], ((0, 0), (0, small - heads))) for part in conv_parts[3:]]
    mixer_in = (pre_qk, pre_rates, pre_vg, segments[:, :, None], segments[:, None, :], *conv_parts[:3], *lanes, out_gain[None])
    heads_out, kept = mixer(heads, mixer_in)
    rows_mlp, middle = middle_rows(cols_product(heads_out, wout), stream, mlp_row)
    chunk = gathered[4]
    chunks = [chunk, grid.shift(chunk, 1), grid.shift(chunk, -1)]
    pair = tied((chunks[1], chunks[2]), heads_out)
    chunks += [grid.shift(pair[0], 1), grid.shift(pair[1], -1)]
    early = ffw // 256 * 128
    hidden, *gate_parts, grad_upper, back_part, ahead, begun = mlp(grid, rows_mlp, cot_rows, chunks, ffw, early)
    grad_mixed, grad_middle, grad_mlp_gain, late, grad_qk, grad_rates, grad_vg, *core_grads = turn(
        grid,
        heads,
        early,
        back_part,
        cot_own,
        middle,
        mlp_row,
        wout,
        cot_rows,
        rows_mlp,
        hidden,
        gate_parts[0],
        begun,
        mixer_in,
        kept,
    )

    width = norm_gain.shape[0]
    gain_rows = width // min(width // grid.chips, 128)
    wide = max(8 * keyw, 4 * valw) + out_gain.shape[0] + 4 * small
    *weight_grads, rates, out_tokens, grad_tokens, gains, wide = collect(
        grid,
        [rows_mlp, grad_mixed, rows_mix],
        [gate_parts[1], grad_upper, grad_vg, heads_out, grad_qk, hidden, gate_parts[0], grad_rates],
        [(0, 1), (2, 2), (0, 0), (1, 3), (2, 4)],
        [late, cot_rows[:, : cot_rows.shape[1] // grid.chips], [(None, 5), (0, 6)]],
        [
            (2, 0, 0, early, ffw),
            (5, ffw, 0, 0, ffw),
            (0, 0, 1, 0, ffw),
            (1, 0, 2, 0, valw),
            (1, valw, 3, 0, valw),
            (3, 0, 4, 0, valw),
            (4, 0, 5, 0, keyw),
            (4, keyw, 6, 0, keyw),
            (5, 0, 7, 0, ffw),
        ],
        [(wvg, 0, 2), (wqk, 0, 4)],
        ahead,
        [stream, norm_row, middle, grad_middle, grad_mlp_gain],
        core_grads,
        [(2 * gain_rows, 128), (2 * conv_query.shape[0], wide)],
        rate_weights,
    )
    whole_gate, whole_up, whole_value, whole_outgate, whole_out, whole_query, whole_key, whole_down = weight_grads
    if out_tokens.shape[1] // grid.chips % 128:
        out_tokens, grad_tokens = grid.out_of(out_tokens), grid.out_of(grad_tokens)
    moved = [out_tokens, grad_tokens, whole_query, whole_key, whole_value, whole_outgate, whole_gate, whole_up]
    shapes = [(1,) + value.shape if i < 2 else value.shape for i, value in enumerate(moved)]
    sizes = [width, width, decay_log.shape[0], decay_bias.shape[0], out_gain.shape[0]]
    *moved, whole_out, whole_down, whole_beta, whole_decay, norm_row, mlp_row, cq, ck, cv, log, bias, gain = finish(
        grid,
        heads,
        list(zip(moved, shapes)),
        [whole_out, whole_down],
        rates,
        gains,
        wide,
        sizes,
        [conv_query, conv_key, conv_value],
    )
    out_tokens, grad_tokens, *moved = moved
    whole_query, whole_key, whole_value, whole_outgate, whole_gate, whole_up = moved
    return (
        out_tokens,
        grad_tokens,
        norm_row[0],
        whole_query,
        whole_key,
        whole_value,
        whole_outgate,
        whole_beta.T,
        whole_decay.T,
        cq,
        ck,
        cv,
        log[0],
        bias[0],
        gain[0],
        whole_out,
        mlp_row[0],
        whole_gate,
        whole_up,
        whole_down,
    )


def solution(mesh):
    rows = P("dp", "tensor")
    cols = P("tensor", "dp")
    tokens = P("dp", "tensor", None)
    placed = (tokens, P("dp", None), P()) + (rows,) * 6 + (P(),) * 6
    placed = placed + (cols, P(), rows, rows, cols, tokens)
    given = (tokens, tokens, P()) + (rows,) * 6 + (P(),) * 6 + (cols, P(), rows, rows, cols)
    return jax.shard_map(
        partial(per_device, devices=mesh.shape["dp"]),
        mesh=mesh,
        in_specs=placed,
        out_specs=given,
        check_vma=False,
    )
```

```python
from functools import partial
import math

import jax
import jax.numpy as jnp
from jax import lax
from jax.experimental import pallas as pl
from jax.experimental.pallas import tpu as pltpu
from jax.sharding import PartitionSpec as P

HIGH = lax.Precision.HIGH
HIGHEST = lax.Precision.HIGHEST
BF = jnp.bfloat16
F32 = jnp.float32


def scale_rows(values, factor):
    return values * lax.rsqrt(jnp.mean(values * values, axis=-1, keepdims=True) + 1e-06) * factor


def split3(value):
    high = value.astype(BF)
    return high, (value - high.astype(F32)).astype(BF)


def product(left, right, dims):
    dims = (dims, ((), ()))
    total = lax.dot_general(left[0], right[0], dims, preferred_element_type=F32)
    total = total + lax.dot_general(left[0], right[1], dims, preferred_element_type=F32)
    return total + lax.dot_general(left[1], right[0], dims, preferred_element_type=F32)


ROWS_COLS = ((1,), (0,))
ROWS_ROWS = ((1,), (1,))
COLS_ROWS = ((0,), (0,))


def exact_sum(mask, value, dims):
    high, low = split3(value)
    last = (value - high.astype(F32) - low.astype(F32)).astype(BF)
    dims = (dims, ((), ()))
    total = lax.dot_general(mask, last, dims, preferred_element_type=F32)
    total = total + lax.dot_general(mask, low, dims, preferred_element_type=F32)
    return total + lax.dot_general(mask, high, dims, preferred_element_type=F32)


def conv_parts(values, taps, keeping):
    moved = [values] + [pltpu.roll(values, j, 0) * keeping[j] for j in range(1, 4)]
    total = moved[0] * taps[0:1]
    for j in range(1, 4):
        total = total + moved[j] * taps[j : j + 1]
    return moved, total


def conv_back(grad, moved, taps, keeping):
    rows = grad.shape[0]
    total = grad * taps[0:1]
    for j in range(1, 4):
        total = total + pltpu.roll(grad * keeping[j], rows - j, 0) * taps[j : j + 1]
    parts = [jnp.sum(grad * moved[j], axis=0, keepdims=True) for j in range(4)]
    return total, jnp.concatenate(parts, axis=0)


def silu_back(total, gate):
    return gate * (1.0 + total * (1.0 - gate))


def softplus(value):
    return jnp.maximum(value, 0.0) + jnp.log1p(jnp.exp(-jnp.abs(value)))


def block_masks(seg_col, seg_row):
    size = seg_col.shape[0]
    row = lax.broadcasted_iota(jnp.int32, (size, size), 0)
    col = lax.broadcasted_iota(jnp.int32, (size, size), 1)
    masking = ((seg_col == seg_row) & (col <= row)).astype(F32)
    spot = lax.broadcasted_iota(jnp.int32, (size, 1), 0)
    keeping = [None]
    for j in range(1, 4):
        keeping.append(((pltpu.roll(seg_col, j, 0) == seg_col) & (spot >= j)).astype(F32))
    return row, col, masking, keeping


def head_rates(small, log, bias, masking, heads):
    decay_in = pltpu.roll(small, small.shape[1] - heads, 1) + bias
    factor = -jnp.exp(log)
    rates = factor * softplus(decay_in)
    betas = jax.nn.sigmoid(small)
    summed = exact_sum(masking.astype(BF), rates, ROWS_COLS)
    return decay_in, factor, rates, betas, summed


def invert(mixing, row, col):
    size = mixing.shape[0]
    result = jnp.where(row == col, 1.0, 0.0) - jnp.where((row >> 1) == (col >> 1), mixing, 0.0)
    level = 1
    while (1 << level) < size:
        picked = ((row >> (level + 1)) == (col >> (level + 1))) & ((row >> level) != (col >> level))
        part = split3(jnp.where(picked, mixing, 0.0))
        halves = split3(result)
        step = product(halves, part, ROWS_COLS)
        result = result - product(split3(step), halves, ROWS_COLS)
        level += 1
    return result


def unit(values):
    return lax.rsqrt(jnp.sum(values * values, axis=1, keepdims=True) + 1e-06)


def mixer_kernel(heads, qk, rates_in, vg, seg_col, seg_row, cq, ck, cv, log, bias, gain, *outs):
    heads_out, inverses, all_errors, all_kk, all_qk, all_raw = outs
    keyw, valw = cq.shape[1] // heads, cv.shape[1] // heads
    row, col, masking, keeping = block_masks(seg_col[0], seg_row[0])
    small = rates_in[...]
    _, _, _, betas, summed = head_rates(small, log[...], bias[...], masking, heads)
    betas_t, summed_t = betas.T, summed.T
    strict = (col < row).astype(F32)
    for h in range(heads):
        at = pl.ds(h * keyw, keyw)
        query = jax.nn.silu(conv_parts(qk[:, at], cq[:, at], keeping)[1])
        query = query * (unit(query) * (1.0 / math.sqrt(keyw)))
        key = jax.nn.silu(
            conv_parts(qk[:, pl.ds((heads + h) * keyw, keyw)], ck[:, at], keeping)[1]
        )
        key = key * unit(key)
        at = pl.ds(h * valw, valw)
        value = jax.nn.silu(conv_parts(vg[:, at], cv[:, at], keeping)[1])
        spread = summed[:, h : h + 1] - summed_t[h : h + 1]
        decays = jnp.exp(spread * masking) * masking * betas_t[h : h + 1]
        keys = split3(key)
        key_key = product(keys, keys, ROWS_ROWS)
        query_key = product(split3(query), keys, ROWS_ROWS)
        inverse = invert(decays * key_key * strict, row, col)
        errors = product(split3(inverse), split3(value), ROWS_COLS)
        raw = product(split3(decays * query_key), split3(errors), ROWS_COLS)
        inverses[0, h] = inverse
        all_errors[0, h] = errors
        all_kk[0, h] = key_key
        all_qk[0, h] = query_key
        all_raw[:, at] = raw
        scaled = raw * lax.rsqrt(jnp.mean(raw * raw, axis=1, keepdims=True) + 1e-05) * gain[...]
        gate = vg[:, pl.ds((heads + h) * valw, valw)]
        heads_out[:, at] = (scaled * jax.nn.silu(gate)).astype(BF)


def mixer_back(heads, grad, inputs, kept, results):
    qk, rates_in, vg, seg_col, seg_row, cq, ck, cv, log, bias, gain = inputs
    inverses, all_errors, all_kk, all_qk, all_raw = kept
    grad_qk, grad_small_out, grad_vg, grad_cq, grad_ck, grad_cv, grad_rate, grad_gain = results
    keyw, valw = cq.shape[1] // heads, cv.shape[1] // heads
    size = qk.shape[0]
    row, col, masking, keeping = block_masks(seg_col[0], seg_row[0])
    small = rates_in[...]
    decay_in, factor, rates, betas, summed = head_rates(small, log[...], bias[...], masking, heads)
    betas_t, summed_t = betas.T, summed.T
    strict = (col < row).astype(F32)
    lanes = lax.broadcasted_iota(jnp.int32, (1, small.shape[1]), 1)
    spots = lax.broadcasted_iota(jnp.int32, (small.shape[1], 1), 0)
    grad_summed = jnp.zeros_like(small)
    from_cols = jnp.zeros((small.shape[1], size), F32)
    for h in range(heads):
        at = pl.ds(h * valw, valw)
        raw, gate_in = all_raw[:, at], vg[:, pl.ds((heads + h) * valw, valw)]
        gate = jax.nn.sigmoid(gate_in)
        scale = lax.rsqrt(jnp.mean(raw * raw, axis=1, keepdims=True) + 1e-05)
        above = grad[:, at]
        grad_vg[:, pl.ds((heads + h) * valw, valw)] = (
            above * (raw * scale * gain[...]) * silu_back(gate_in, gate)
        ).astype(BF)
        above = above * (gate_in * gate)
        grad_gain[...] += jnp.sum(above * raw * scale, axis=0, keepdims=True)
        above = above * gain[...]
        grad_raw = scale * (above - raw * (scale * scale * jnp.mean(above * raw, axis=1, keepdims=True)))

        spread = summed[:, h : h + 1] - summed_t[h : h + 1]
        plain = jnp.exp(spread * masking) * masking
        decays = plain * betas_t[h : h + 1]
        key_key, query_key = all_kk[0, h] * strict, all_qk[0, h]
        grad_raws, errors = split3(grad_raw), split3(all_errors[0, h])
        grad_reading = product(grad_raws, errors, ROWS_ROWS)
        grad_errors = product(split3(decays * query_key), grad_raws, COLS_ROWS)
        grad_value = product(split3(inverses[0, h]), split3(grad_errors), COLS_ROWS)
        grad_mixing = -product(split3(grad_value), errors, ROWS_ROWS)
        both = (grad_mixing * key_key + grad_reading * query_key) * plain
        grad_beta = jnp.sum(both, axis=0, keepdims=True)
        both = both * betas_t[h : h + 1]
        from_rows = jnp.sum(both, axis=1, keepdims=True)
        grad_summed = grad_summed + jnp.where(lanes == heads + h, from_rows, 0.0)
        from_cols = from_cols + jnp.where(spots == h, grad_beta, 0.0)
        from_cols = from_cols - jnp.where(spots == heads + h, jnp.sum(both, axis=0, keepdims=True), 0.0)

        at = pl.ds(h * keyw, keyw)
        query_moved, query_total = conv_parts(qk[:, at], cq[:, at], keeping)
        query_gate = jax.nn.sigmoid(query_total)
        query = query_total * query_gate
        query_scale = unit(query)
        query = query * query_scale
        key_at = pl.ds((heads + h) * keyw, keyw)
        key_moved, key_total = conv_parts(qk[:, key_at], ck[:, at], keeping)
        key_gate = jax.nn.sigmoid(key_total)
        key = key_total * key_gate
        key_scale = unit(key)
        key = key * key_scale
        keys = split3(key)
        grad_kk = split3(grad_mixing * decays * strict)
        grad_qk_product = split3(grad_reading * (decays * (1.0 / math.sqrt(keyw))))
        grad_query = product(grad_qk_product, keys, ROWS_COLS)
        grad_key = product(grad_qk_product, split3(query), COLS_ROWS)
        grad_key = grad_key + product(grad_kk, keys, ROWS_COLS) + product(grad_kk, keys, COLS_ROWS)

        grad_query = query_scale * (grad_query - query * jnp.sum(grad_query * query, axis=1, keepdims=True))
        grad_query = grad_query * silu_back(query_total, query_gate)
        grad_query, taps = conv_back(grad_query, query_moved, cq[:, at], keeping)
        grad_qk[:, at] = grad_query.astype(BF)
        grad_cq[:, at] += taps
        grad_key = key_scale * (grad_key - key * jnp.sum(grad_key * key, axis=1, keepdims=True))
        grad_key = grad_key * silu_back(key_total, key_gate)
        grad_key, taps = conv_back(grad_key, key_moved, ck[:, at], keeping)
        grad_qk[:, key_at] = grad_key.astype(BF)
        grad_ck[:, at] += taps

        at = pl.ds(h * valw, valw)
        moved, total = conv_parts(vg[:, at], cv[:, at], keeping)
        grad_value = grad_value * silu_back(total, jax.nn.sigmoid(total))
        grad_value, taps = conv_back(grad_value, moved, cv[:, at], keeping)
        grad_vg[:, at] = grad_value.astype(BF)
        grad_cv[:, at] += taps

    from_cols = from_cols.T
    grad_summed = grad_summed + jnp.where(lanes >= heads, from_cols, 0.0)
    grad_rates = exact_sum(masking.astype(BF), grad_summed, COLS_ROWS)
    decay_lanes = (lanes >= heads) & (lanes < 2 * heads)
    shifted = [pltpu.roll(value, heads, 1) for value in (decay_in, rates)]
    grad_decay = grad_rates * pltpu.roll(factor, heads, 1) * jax.nn.sigmoid(shifted[0])
    grad_rate[0:1] += jnp.sum(grad_rates * shifted[1], axis=0, keepdims=True)
    grad_rate[1:2] += jnp.sum(grad_decay, axis=0, keepdims=True)
    grad_small = jnp.where(decay_lanes, grad_decay, from_cols * betas * (1.0 - betas))
    grad_small = jnp.where(lanes < 2 * heads, grad_small, 0.0)
    grad_small_out[...] = grad_small.astype(BF)


def mixer_specs(heads, qk, vg, cq, cv, small):
    length = qk.shape[0] // 2

    def by_rows(width):
        return pl.BlockSpec((length, width), lambda s: (s, 0))

    def fixed(*shape):
        return pl.BlockSpec(shape, lambda s: (0,) * len(shape))

    shared = [
        by_rows(qk.shape[1]),
        by_rows(small),
        by_rows(vg.shape[1]),
        pl.BlockSpec((1, length, 1), lambda s: (s, 0, 0)),
        pl.BlockSpec((1, 1, length), lambda s: (s, 0, 0)),
        fixed(*cq.shape),
        fixed(*cq.shape),
        fixed(*cv.shape),
        fixed(1, small),
        fixed(1, small),
        fixed(1, cv.shape[1] // heads),
    ]
    valw = cv.shape[1] // heads
    square = (heads, length, length)
    kept = [square, (heads, length, valw), square, square]
    kept_specs = [pl.BlockSpec((1,) + shape, lambda s: (s, 0, 0, 0)) for shape in kept]
    kept_specs.append(by_rows(cv.shape[1]))
    kept_shapes = [jax.ShapeDtypeStruct((2,) + shape, F32) for shape in kept]
    kept_shapes.append(jax.ShapeDtypeStruct((2 * length, cv.shape[1]), F32))
    return by_rows, fixed, shared, kept_specs, kept_shapes


def mixer(heads, inputs):
    qk, _, vg, _, _, cq, _, cv, log, _, _ = inputs
    by_rows, _, shared, kept_specs, kept_shapes = mixer_specs(heads, qk, vg, cq, cv, log.shape[1])
    heads_out, *kept = pl.pallas_call(
        partial(mixer_kernel, heads),
        grid=(2,),
        out_shape=[jax.ShapeDtypeStruct((qk.shape[0], cv.shape[1]), BF)] + kept_shapes,
        in_specs=shared,
        out_specs=[by_rows(cv.shape[1])] + kept_specs,
        compiler_params=pltpu.CompilerParams(vmem_limit_bytes=48 << 20),
        name="mixer",
    )(*inputs)
    return heads_out, kept


def rows_product(left, right):
    return lax.dot_general(left, right, (((0,), (0,)), ((), ())), preferred_element_type=F32)


def cols_product(left, right):
    return lax.dot_general(left, right, (((1,), (1,)), ((), ())), preferred_element_type=F32)


def dot(left, right):
    return jnp.dot(left, right, preferred_element_type=F32)


def tied(value, after):
    return lax.optimization_barrier((value, after))[0]


def first_of(flag, own, peer, axis):
    return jnp.concatenate([jnp.where(flag, own, peer), jnp.where(flag, peer, own)], axis=axis)


def part_of(value, index, size, axis):
    return lax.dynamic_slice_in_dim(value, index * size, size, axis)


class Grid:
    def __init__(self, devices):
        self.devices = devices
        self.chips = devices // 2
        me = lax.axis_index("dp")
        self.core = me % 2
        self.spot = ring_spot(me // 2, self.chips)
        self.member = lax.axis_index("tensor")
        self.quarter = 2 * self.member + self.core

    def swap(self, value, offset):
        pairs = [(at, at ^ offset) for at in range(self.devices)]
        return lax.ppermute(value, "dp", pairs)

    def over_core(self, value):
        return self.swap(value, 1)

    def over_tensor(self, value):
        return lax.ppermute(value, "tensor", [(0, 1), (1, 0)])

    def shift(self, value, step):
        pairs = []
        for at in range(self.devices):
            spot = (ring_spot(at // 2, self.chips) + step) % self.chips
            pairs.append((at, 2 * ring_chip(spot, self.chips) + at % 2))
        return lax.ppermute(value, "dp", pairs)

    def into(self, value):
        width = value.shape[-1] // self.chips
        blocks = []
        for place in range(self.chips):
            chip = ring_chip((self.spot + place) % self.chips, self.chips)
            blocks.append(part_of(value, chip, width, -1))
        return jnp.concatenate(blocks, axis=-1)

    def out_of(self, value):
        width = value.shape[-1] // self.chips
        blocks = []
        for chip in range(self.chips):
            place = (ring_spot(chip, self.chips) - self.spot + self.chips) % self.chips
            blocks.append(part_of(value, place, width, -1))
        return jnp.concatenate(blocks, axis=-1)

    def gather_rows(self, own):
        whole = first_of(self.member == 0, own, self.over_tensor(own), 0)
        return jnp.concatenate([whole, self.over_core(whole)], axis=0)

    def scatter_rows(self, value):
        half = value.shape[0] // 2
        whole = value[:half] + self.over_core(value[half:])
        half //= 2
        theirs = part_of(whole, 1 - self.member, half, 0)
        peer = self.over_tensor(theirs.astype(BF)).astype(F32)
        return part_of(whole, self.member, half, 0) + peer


def ring_spot(chip, chips):
    line, pair = chip // 2, chip % 2
    return line * (1 - pair) + (chips - 1 - line) * pair


def ring_chip(spot, chips):
    pair = spot // (chips // 2)
    return 2 * (spot * (1 - pair) + (chips - 1 - spot) * pair) + pair


def signal_all(devices):
    barrier = pltpu.get_barrier_semaphore()
    for device in devices:
        pl.semaphore_signal(barrier, inc=1, device_id=device, device_id_type=pl.DeviceIdType.MESH)
    pl.semaphore_wait(barrier, len(devices))


def send(source, target, send_sem, recv_sem, device):
    return pltpu.make_async_remote_copy(
        src_ref=source,
        dst_ref=target,
        send_sem=send_sem,
        recv_sem=recv_sem,
        device_id=device,
        device_id_type=pl.DeviceIdType.MESH,
    )


def staged(sources, targets, sem):
    copies = [pltpu.make_async_copy(*pair, sem.at[i]) for i, pair in enumerate(zip(sources, targets))]
    pending = set(range(len(copies)))
    for copy in copies:
        copy.start()

    def ready(*numbers):
        for i in sorted(pending.intersection(numbers)):
            copies[i].wait()
            pending.remove(i)

    return ready


def spread_kernel(chips, layout, ringed, *refs):
    count = len(layout)
    totals = 1 + max(item[0] for item in layout)
    sources, (tokens, cot, gain, gain_mlp, w_decay) = refs[:count], refs[count : count + 5]
    refs = refs[count + 5 :]
    given_out = refs[:totals]
    stream, cot_own, own_gain, own_gain_mlp, rows_mix, rows_cot = refs[totals : totals + 6]
    refs = refs[totals + 6 :]
    normed, near_sem, send_core, recv_core, send_right, recv_right, send_left, recv_left = refs[:8]
    own_sem, send_half, recv_half, send_whole, recv_whole, rate_sum, rate_own, store_sem, *turned = refs[8:]
    outs, turned = (*turned[:ringed], *given_out[ringed:]), turned[ringed:]
    me, member = lax.axis_index("dp"), lax.axis_index("tensor")
    core, chip = me % 2, me // 2
    spot = ring_spot(chip, chips)
    right = (2 * ring_chip((spot + 1) % chips, chips) + core, member)
    left = (2 * ring_chip((spot + chips - 1) % chips, chips) + core, member)
    peer = (2 * chip + 1 - core, member)
    across = (me, 1 - member)
    signal_all((right, left, peer, across))

    def home(out):
        return outs[out].at[0] if out < ringed else outs[out]

    near, far = [], []
    given = list(sources)
    turned = [(i, target) for i, target in zip([i for i, item in enumerate(layout) if item[3]], turned)]
    sources = list(sources)
    for i, target in turned:
        sources[i] = target
    for i, (out, at, width, _) in enumerate(layout):
        if width is None:
            place = home(out).at[core]
            near.append(pltpu.make_async_copy(rate_own.at[core], place, near_sem.at[i]))
            far.append(send(rate_own.at[1 - core], place, send_core.at[i], recv_core.at[i], peer))
            heads = w_decay.shape[0] // 2
            rate_sum[...] = jnp.zeros_like(rate_sum)
            for at, part in ((0, sources[i][...].astype(F32)), (heads, w_decay[...].astype(F32))):
                for c in range(2):
                    rate_sum[c, at : at + heads] = part[c * heads : (c + 1) * heads]
            rate_own[...] = rate_sum[...].astype(BF)
            continue
        rows = sources[i].shape[0]
        place = home(out).at[pl.ds(pl.multiple_of(core * rows, rows), rows), pl.ds(at, width)]
        mine = sources[i].at[:, pl.ds(pl.multiple_of(core * width, 128), width)]
        theirs = sources[i].at[:, pl.ds(pl.multiple_of((1 - core) * width, 128), width)]
        near.append(pltpu.make_async_copy(mine, place, near_sem.at[i]))
        far.append(send(theirs, place, send_core.at[i], recv_core.at[i], peer))

    def trade_halves(outs_now):
        for i, target in turned:
            if layout[i][0] in outs_now:
                target[...] = given[i][...].T
        for i, item in enumerate(layout):
            if item[0] in outs_now:
                far[i].start()
                near[i].start()

    trade_halves(range(2))

    def hop(out, step, way):
        last = step == chips // 2
        ref = outs[out]
        mid = ref.shape[1] // 2
        if way > 0:
            at, to, device, sends, receives = -(step - 1) % chips, chips - step, right, send_right, recv_right
            rows = pl.ds(0, mid)
        else:
            at, to, device, sends, receives = step - 1, step, left, send_left, recv_left
            rows = pl.ds(mid, mid)
        source, target = ref.at[at], ref.at[to]
        if last:
            source, target = source.at[rows], target.at[rows]
        return send(source, target, sends.at[out, step - 1], receives.at[out, step - 1], device)

    stored = []

    def store(out, slot):
        stored.append(pltpu.make_async_copy(outs[out].at[slot], given_out[out].at[slot], store_sem.at[out, slot]))
        stored[-1].start()

    started, own = [], []
    pairs = ((normed, rows_mix), (cot_own, rows_cot))
    halves = [
        send(value, rows.at[0, member], send_half.at[i], recv_half.at[i], across)
        for i, (value, rows) in enumerate(pairs)
    ]
    wholes = [
        send(rows.at[0], rows.at[1], send_whole.at[i], recv_whole.at[i], peer)
        for i, (_, rows) in enumerate(pairs)
    ]
    for step in range(1, chips // 2 + 1):
        for out in range(ringed):
            if step == 1:
                for i, item in enumerate(layout):
                    if item[0] == out:
                        near[i].wait()
                        far[i].wait()
            for way in (1, -1):
                if step > 1:
                    hop(out, step - 1, way).wait_recv()
                copy = hop(out, step, way)
                copy.start()
                started.append(copy)
                if step > 1:
                    store(out, chips - step + 1 if way > 0 else step - 1)
            if step == 1:
                store(out, 0)
                trade_halves((out + 2,) if out + 2 < ringed else ())
        if step == 1:
            trade_halves(range(ringed, totals))
            width = tokens.shape[1] // chips
            aligned = width % 128 == 0
            squares = jnp.zeros((tokens.shape[0], 1), F32)
            for place in range(chips):
                to = pl.ds(place * width, width)
                at = to
                if aligned:
                    at = ring_chip((spot + place) % chips, chips) * width
                    at = pl.ds(pl.multiple_of(at, 128), width)
                stream[:, to] = tokens[:, at]
                cot_own[:, to] = cot[:, at]
                own_gain[:, to] = gain[:, at]
                own_gain_mlp[:, to] = gain_mlp[:, at]
                block = stream[:, to].astype(F32)
                squares = squares + jnp.sum(block * block, axis=1, keepdims=True)
            scale = lax.rsqrt(squares / tokens.shape[1] + 1e-06)
            normed[...] = (stream[...].astype(F32) * scale * own_gain[...]).astype(BF)
            for i, (value, rows) in enumerate(pairs):
                own.append(pltpu.make_async_copy(value, rows.at[0, member], own_sem.at[i]))
                own[-1].start()
                halves[i].start()
        if step == 2:
            for i in range(2):
                own[i].wait()
                halves[i].wait()
                wholes[i].start()
    for i, item in enumerate(layout):
        if item[0] >= ringed:
            near[i].wait()
            far[i].wait()
    for copy in wholes:
        copy.wait()
    for out in range(ringed):
        for way in (1, -1):
            hop(out, chips // 2, way).wait_recv()
        store(out, chips // 2)
    for copy in stored:
        copy.wait()
    for copy in started:
        copy.wait_send()


def spread(grid, groups, ringed, tokens, cot, gains, rates):
    chips = grid.chips
    sources, layout, shapes, turned_shapes = [], [], [], []
    for out, group in enumerate(groups):
        if not isinstance(group, list):
            rate = (2, group, rates[0].shape[1])
            layout.append((out, 0, None, False))
            sources.append(rates[0])
            shapes.append(jax.ShapeDtypeStruct((chips,) + rate, BF))
            continue
        at = 0
        for shard in group:
            turned = isinstance(shard, tuple)
            if turned:
                (shard,) = shard
                turned_shapes.append(pltpu.VMEM(shard.shape[::-1], BF))
            width = shard.shape[0 if turned else 1] // 2
            layout.append((out, at, width, turned))
            sources.append(shard)
            at += width
        rows = 2 * tokens.shape[1] // grid.devices
        shapes.append(jax.ShapeDtypeStruct(((chips,) if out < ringed else ()) + (rows, at), BF))
    dma = pltpu.SemaphoreType.DMA
    hops = (ringed, chips // 2)
    anywhere = pl.BlockSpec(memory_space=pltpu.HBM)
    near = pl.BlockSpec(memory_space=pltpu.VMEM)
    own = jax.ShapeDtypeStruct(tokens.shape, BF)
    rows = jax.ShapeDtypeStruct((2, 2) + tokens.shape, BF)
    return pl.pallas_call(
        partial(spread_kernel, chips, layout, ringed),
        out_shape=shapes + [own, own] + [jax.ShapeDtypeStruct(gains[0].shape, F32)] * 2 + [rows, rows],
        in_specs=[near if item[3] or item[2] is None else anywhere for item in layout] + [near] * 5,
        out_specs=[anywhere] * len(shapes) + [near] * 4 + [anywhere] * 2,
        scratch_shapes=[pltpu.VMEM(tokens.shape, BF)]
        + [dma((len(sources),))] * 3
        + [dma(hops)] * 4
        + [dma((2,))] * 5
        + [pltpu.VMEM(rate, F32), pltpu.VMEM(rate, BF), dma((ringed, chips))]
        + [pltpu.VMEM(shape.shape, BF) for shape in shapes[:ringed]]
        + turned_shapes,
        compiler_params=pltpu.CompilerParams(
            collective_id=0, has_side_effects=True, vmem_limit_bytes=62 << 20
        ),
        name="spread",
    )(*sources, tokens, cot, *gains, rates[1])


PARTS = 2


def exchange(part, own_part, rows_out, buffers, sems, compute, early=None, late=None):
    got_core, sent_half, got_half, own = buffers
    me, member = lax.axis_index("dp"), lax.axis_index("tensor")
    peer = (me + 1 - 2 * (me % 2), member)
    across = (me, 1 - member)
    count = part.shape[2] // PARTS

    def chunk(k):
        return pl.ds(k * count, count)

    def copy(kind, k, source, target, device):
        return send(source, target, sems[2 * kind].at[k], sems[2 * kind + 1].at[k], device)

    first = [copy(0, k, part.at[1, :, chunk(k)], got_core.at[:, chunk(k)], peer) for k in range(PARTS)]
    second = [copy(1, k, sent_half.at[chunk(k)], got_half.at[chunk(k)], across) for k in range(PARTS)]
    third = [
        copy(2, k, own.at[chunk(k)], rows_out.at[0, member, chunk(k)], across) for k in range(PARTS)
    ]
    fourth = [
        copy(3, k, own.at[chunk(k)], rows_out.at[1, member, chunk(k)], peer) for k in range(PARTS)
    ]
    fifth = [
        copy(4, k, rows_out.at[0, 1 - member, chunk(k)], rows_out.at[1, 1 - member, chunk(k)], peer)
        for k in range(PARTS)
    ]
    for k in range(PARTS):
        first[k].start()
    if early:
        early()
    for k in range(PARTS):
        first[k].wait_recv()
        total = own_part[1 - member, chunk(k)] + got_core[1 - member, chunk(k)]
        sent_half[chunk(k)] = total.astype(BF)
        second[k].start()
    for k in range(PARTS):
        second[k].wait_recv()
        total = own_part[member, chunk(k)] + got_core[member, chunk(k)] + got_half[chunk(k)].astype(F32)
        value = compute(k, chunk(k), total).astype(BF)
        own[chunk(k)] = value
        third[k].start()
        fourth[k].start()
        rows_out[0, member, chunk(k)] = value
    for k in range(PARTS):
        third[k].wait_recv()
        fifth[k].start()
    if late:
        late()
    for k in range(PARTS):
        fourth[k].wait_recv()
        fifth[k].wait_recv()
    for copies in (first, second, third, fourth, fifth):
        for one in copies:
            one.wait_send()


def exchange_scratch(rows, width):
    return [
        pltpu.VMEM((2, rows, width), F32),
        pltpu.VMEM((rows, width), BF),
        pltpu.VMEM((rows, width), BF),
        pltpu.VMEM((rows, width), BF),
    ] + [pltpu.SemaphoreType.DMA((PARTS,))] * 10


def middle_kernel(part, stream, gain, rows_out, middle, *scratch):
    me, member = lax.axis_index("dp"), lax.axis_index("tensor")
    signal_all(((me + 1 - 2 * (me % 2), member), (me, 1 - member)))

    def compute(k, rows, mixed):
        value = stream[rows].astype(F32) + mixed
        middle[rows] = value
        return value * lax.rsqrt(jnp.mean(value * value, axis=1, keepdims=True) + 1e-06) * gain[...]

    exchange(part, part.at[0], rows_out, scratch[:4], scratch[4:], compute)


def middle_rows(part, stream, gain):
    rows, width = stream.shape
    near = pl.BlockSpec(memory_space=pltpu.VMEM)
    gathered, middle = pl.pallas_call(
        middle_kernel,
        out_shape=[
            jax.ShapeDtypeStruct((2, 2, rows, width), BF),
            jax.ShapeDtypeStruct((rows, width), F32),
        ],
        in_specs=[near] * 3,
        out_specs=[near] * 2,
        scratch_shapes=exchange_scratch(rows, width),
        compiler_params=pltpu.CompilerParams(
            collective_id=1, has_side_effects=True, vmem_limit_bytes=62 << 20
        ),
        name="middle",
    )(part.reshape(2, 2, rows, width), stream, gain)
    return gathered.reshape(4 * rows, width), middle


def turn_kernel(chips, heads, ffw, early, *refs):
    refs = list(refs)

    def take(count):
        taken, refs[:] = refs[:count], refs[count:]
        return taken

    part, gain = take(2)
    small_inputs, later = take(8), take(17)
    rows_out, grad_middle, grad_gain, late = take(4)
    results = take(8)
    grad_heads, going, arrived = take(3)
    here_now, (later_sem,) = take(17), take(1)
    send_ring, recv_ring = take(2)
    me, member = lax.axis_index("dp"), lax.axis_index("tensor")
    core, chip = me % 2, me // 2
    spot = ring_spot(chip, chips)
    ways = (
        (2 * ring_chip((spot + 1) % chips, chips) + core, member),
        (2 * ring_chip((spot + chips - 1) % chips, chips) + core, member),
    )
    rows_cot, rows_mlp, hidden, grad_gate, begun, own_part, cot, middle, wout, *kept = here_now[:14]
    inputs = here_now[14:] + small_inputs
    later[5] = later[5].at[0]
    ready = staged(later, here_now, later_sem)
    signal_all((*ways, (me + 1 - 2 * core, member), (me, 1 - member)))
    half = chips // 2
    width = rows_cot.shape[1] // chips
    mid = width // 2

    def total(way, place, step):
        at = (place if way == 0 else -place) % chips * width
        value = []
        for left, right, size in ((rows_cot, hidden, ffw), (rows_mlp, grad_gate, early)):
            value.append(
                lax.dot_general(
                    left[:, at : at + width],
                    right[:, 0:size],
                    (COLS_ROWS, ((), ())),
                    preferred_element_type=F32,
                )
            )
        value = jnp.concatenate(value, axis=1)
        if step:
            return (value + arrived[way, step - 1].astype(F32)).astype(BF)
        lo = mid * way
        here = value[lo : lo + mid] + begun[way].astype(F32)
        rest = value[mid - lo : width - lo]
        return jnp.concatenate([here, rest] if way == 0 else [rest, here], axis=0).astype(BF)

    def hop(way, step):
        sems = (way, step)
        source = arrived.at[way, step - 1] if step else going.at[way]
        return send(source, arrived.at[sems], send_ring.at[sems], recv_ring.at[sems], ways[way])

    def next_hop(step):
        for way in range(2):
            if step:
                hop(way, step - 1).wait_recv()
            value = total(way, half - 1 - step, step)
            if step == half - 2:
                late[way] = value
                continue
            if step:
                arrived[way, step - 1] = value
            else:
                going[way] = value
            hop(way, step).start()

    def compute(k, rows, grad):
        value = middle[rows]
        scale = lax.rsqrt(jnp.mean(value * value, axis=1, keepdims=True) + 1e-06)
        unit_value = value * scale
        gained = jnp.sum(grad * unit_value, axis=0, keepdims=True)
        grad_gain[...] = gained if k == 0 else grad_gain[...] + gained
        grad = grad * gain[...]
        grad = scale * (grad - unit_value * jnp.mean(grad * unit_value, axis=1, keepdims=True))
        grad = grad + cot[rows].astype(F32)
        grad_middle[rows] = grad
        return grad


    def early_work():
        ready(*range(5))
        next_hop(0)
        ready(5, 6, 7)

    def late_work():
        if half > 3:
            next_hop(1)

    exchange(part, own_part, rows_out, refs[:4], refs[4:], compute, early_work, late_work)
    ready(*range(17))
    for step in range(2, half - 2):
        next_hop(step)
    for ref in results[3:]:
        ref[...] = jnp.zeros_like(ref)
    length = inputs[0].shape[0] // 2

    @pl.loop(0, 2)
    def _(s):
        at = pl.multiple_of(s * length, length)
        here = pl.ds(at, length)
        for m in range(2):
            grad_heads[pl.ds(at + m * (length // 2), length // 2)] = jnp.dot(
                rows_out[s, m], wout[...], preferred_element_type=F32
            )
        mixer_back(
            heads,
            grad_heads.at[here],
            [ref.at[here] for ref in inputs[:3]] + [ref.at[pl.ds(s, 1)] for ref in inputs[3:5]] + inputs[5:],
            [ref.at[pl.ds(s, 1)] for ref in kept[:4]] + [kept[4].at[here]],
            [ref.at[here] for ref in results[:3]] + results[3:],
        )

    next_hop(half - 2)
    for step in range(half - 2):
        for way in range(2):
            hop(way, step).wait_send()


def turn(grid, heads, early, part, cot, middle, gain, wout, rows_cot, rows_mlp, hidden, grad_gate, begun, inputs, kept):
    chips = grid.chips
    rows, width = middle.shape
    block, half = width // chips, chips // 2
    ffw = hidden.shape[1]
    n = ffw + early
    qk, rates_in, vg, _, _, cq, ck, cv, log, _, out_gain = inputs
    near = pl.BlockSpec(memory_space=pltpu.VMEM)
    far = pl.BlockSpec(memory_space=pltpu.HBM)
    dma = pltpu.SemaphoreType.DMA
    sums = [cq.shape, ck.shape, cv.shape, (2, log.shape[1]), out_gain.shape]
    part = part.reshape(2, 2, rows, width)
    near_in = (gain, *inputs[3:])
    later = (rows_cot, rows_mlp, hidden, grad_gate, begun, part, cot, middle, wout, *kept, *inputs[:3])
    held = [value.shape[1:] if value is part else value.shape for value in later]
    gathered, *rest = pl.pallas_call(
        partial(turn_kernel, chips, heads, ffw, early),
        out_shape=[
            jax.ShapeDtypeStruct((2, 2, rows, width), BF),
            jax.ShapeDtypeStruct((rows, width), F32),
            jax.ShapeDtypeStruct((1, width), F32),
            jax.ShapeDtypeStruct((2, block, n), BF),
            jax.ShapeDtypeStruct(qk.shape, BF),
            jax.ShapeDtypeStruct(rates_in.shape, BF),
            jax.ShapeDtypeStruct(vg.shape, BF),
        ]
        + [jax.ShapeDtypeStruct(shape, F32) for shape in sums],
        in_specs=[far] + [near] * len(near_in) + [far] * len(later),
        out_specs=[near] * (7 + len(sums)),
        scratch_shapes=[
            pltpu.VMEM((4 * rows, cv.shape[1]), F32),
            pltpu.VMEM((2, block, n), BF),
            pltpu.VMEM((2, half - 2, block, n), BF),
            *[pltpu.VMEM(shape, value.dtype) for shape, value in zip(held, later)],
            dma((len(later),)),
            dma((2, half - 2)),
            dma((2, half - 2)),
        ]
        + exchange_scratch(rows, width),
        compiler_params=pltpu.CompilerParams(
            collective_id=2, has_side_effects=True, vmem_limit_bytes=62 << 20
        ),
        name="turn",
    )(part, *near_in, *later)
    return gathered.reshape(4 * rows, width), *rest


def mlp_kernel(chips, ffw, early, *refs):
    rows_far, cot_far, own, right_1, left_1, right_2, left_2 = refs[:7]
    hidden, gate_early, gate_rest, grad_upper, back, ahead, begun = refs[7:14]
    rows, cot, rows_sem, weights, sums, begin, load_sem, send_ring, recv_ring, send_begin, recv_begin = refs[14:]
    me, member = lax.axis_index("dp"), lax.axis_index("tensor")
    core, chip = me % 2, me // 2
    spot = ring_spot(chip, chips)
    ways = (
        (2 * ring_chip((spot + 1) % chips, chips) + core, member),
        (2 * ring_chip((spot + chips - 1) % chips, chips) + core, member),
    )
    signal_all(ways)
    half = chips // 2
    block = own.shape[0]
    mid = block // 2

    def spots(place, lo=0, hi=block):
        return pl.ds((place % chips) * block + lo, hi - lo)

    def hop(way, step):
        place, to = (1 - step, -step) if way == 0 else (step - 1, step)
        lo, hi = (0, block) if step < half else (mid * way, mid * way + mid)
        if step == 3:
            source = (right_2, left_2)[way].at[pl.ds(lo, hi - lo)]
        else:
            source = weights.at[spots(place, lo, hi)]
        sems = (way, step - 3)
        return send(source, weights.at[spots(to, lo, hi)], send_ring.at[sems], recv_ring.at[sems], ways[way])

    for way in range(2):
        hop(way, 3).start()
    loads = []
    for number, (place, source) in enumerate(((0, own), (1, left_1), (2, left_2), (-2, right_2), (-1, right_1))):
        loads.append(pltpu.make_async_copy(source, weights.at[spots(place)], load_sem.at[number]))
        loads[-1].start()

    ready = staged((rows_far, cot_far), (rows, cot), rows_sem)
    tile = ffw // 2

    def add(lo, hi, first):
        inner = slice((lo % chips) * block, (lo % chips + hi - lo) * block)
        for at in range(0, 3 * ffw, tile):
            left = rows if at < 2 * ffw else cot
            value = jnp.dot(left[:, inner], weights[inner, at : at + tile], preferred_element_type=F32)
            sums[:, at : at + tile] = value if first else sums[:, at : at + tile] + value

    ready(0, 1)
    for copy in loads[:3]:
        copy.wait()
    add(0, 3, True)
    for copy in loads[3:]:
        copy.wait()
    add(-2, 0, False)
    for step in range(3, half):
        for way in range(2):
            hop(way, step).wait_recv()
            hop(way, step + 1).start()
        add(step, step + 1, False)
        add(-step, 1 - step, False)
    for way in range(2):
        hop(way, half).wait_recv()
    add(half, half + 1, False)

    starts = []

    def first_hop(lo, hi):
        number = len(starts) // 2
        for way in range(2):
            row = half * block + mid * way
            for left, right, at, size in ((cot, hidden, 0, ffw), (rows, gate_early, ffw, early)):
                begins, ends = max(lo - at, 0), min(hi - at, size)
                if begins < ends:
                    begin[way, :, at + begins : at + ends] = lax.dot_general(
                        left[:, row : row + mid],
                        right[:, begins:ends],
                        (COLS_ROWS, ((), ())),
                        preferred_element_type=F32,
                    ).astype(BF)
            cols = pl.ds(lo, hi - lo)
            sems = (way, number)
            starts.append(
                send(
                    begin.at[way, :, cols], begun.at[way, :, cols], send_begin.at[sems], recv_begin.at[sems], ways[way]
                )
            )
            starts[-1].start()

    middle = ffw // 256 * 128
    for at in range(0, ffw, 128):
        gate, upper = sums[:, at : at + 128], sums[:, ffw + at : ffw + at + 128]
        grad = sums[:, 2 * ffw + at : 2 * ffw + at + 128]
        open_gate = jax.nn.sigmoid(gate)
        passed = gate * open_gate
        hidden[:, at : at + 128] = (passed * upper).astype(BF)
        part, to = (gate_early, at) if at < early else (gate_rest, at - early)
        part[:, to : to + 128] = (grad * upper * silu_back(gate, open_gate)).astype(BF)
        grad_upper[:, at : at + 128] = (grad * passed).astype(BF)
        if at + 128 == middle:
            first_hop(0, middle)
    first_hop(middle, ffw + early)
    for place in range(chips):
        inner = slice(place * block, (place + 1) * block)
        value, at = 0.0, 0
        for part in (gate_early, gate_rest, grad_upper):
            cols = slice(at, at + part.shape[1])
            value = value + lax.dot_general(
                part[...], weights[inner, cols], (ROWS_ROWS, ((), ())), preferred_element_type=F32
            )
            at += part.shape[1]
        back[:, inner] = value
        ahead[:, inner] = lax.dot_general(
            hidden[...], weights[inner, 2 * ffw :], (ROWS_ROWS, ((), ())), preferred_element_type=F32
        ).astype(BF)
    for copy in starts:
        copy.wait()
    for step in range(3, half + 1):
        for way in range(2):
            hop(way, step).wait_send()


def mlp(grid, rows, cot, chunks, ffw, early):
    chips = grid.chips
    count, width = rows.shape
    block, n = chunks[0].shape
    half = chips // 2
    near = pl.BlockSpec(memory_space=pltpu.VMEM)
    far = pl.BlockSpec(memory_space=pltpu.HBM)
    dma = pltpu.SemaphoreType.DMA
    inner = jax.ShapeDtypeStruct((count, ffw), BF)
    return pl.pallas_call(
        partial(mlp_kernel, chips, ffw, early),
        out_shape=[
            inner,
            jax.ShapeDtypeStruct((count, early), BF),
            jax.ShapeDtypeStruct((count, ffw - early), BF),
            inner,
            jax.ShapeDtypeStruct((count, width), F32),
            jax.ShapeDtypeStruct((count, width), BF),
            jax.ShapeDtypeStruct((2, block // 2, ffw + early), BF),
        ],
        in_specs=[far] * 7,
        out_specs=[near] * 7,
        scratch_shapes=[
            pltpu.VMEM(rows.shape, BF),
            pltpu.VMEM(rows.shape, BF),
            dma((2,)),
            pltpu.VMEM((chips * block, n), BF),
            pltpu.VMEM((count, n), F32),
            pltpu.VMEM((2, block // 2, ffw + early), BF),
            dma((5,)),
            dma((2, half - 2)),
            dma((2, half - 2)),
            dma((2, 2)),
            dma((2, 2)),
        ],
        compiler_params=pltpu.CompilerParams(
            collective_id=4, has_side_effects=True, vmem_limit_bytes=62 << 20
        ),
        name="mlp",
    )(rows, cot, *chunks)


def collect_kernel(chips, steps, groups, late_parts, fields, side_of, counts, *refs):
    n_left, n_right, n_out, n_side = counts
    refs = list(refs)

    def take(count):
        taken, refs[:] = refs[:count], refs[count:]
        return taken

    far = take(n_left + n_right)
    late_out, late_left = take(2)
    weights = take(n_side)
    ahead_far, *far_tokens = take(4)
    gain, mlp_grad, rate_weights = take(3)
    grad_cq, grad_ck, grad_cv, grad_rate, grad_gain = take(5)
    outs = take(n_out)
    rates_out, out_tokens, grad_tokens, *small_outs = take(5)
    begin, arrived, late_in, final, back, got_core, sent_half, got_half, *small_ins = take(10)
    buffers = take(n_side)
    near, near_tokens = take(n_left + n_right), take(4)
    lefts, rights = near[:n_left], near[n_left:]
    ahead, stream, middle, grad_middle = near_tokens
    (far_sem,) = take(1)
    send_ring, recv_ring, own_sem, send_core, recv_core, send_late, recv_late = take(7)
    send_first, recv_first, send_second, recv_second, send_small, recv_small, weight_sem, free = take(8)
    rate_begin, rate_arrived, rate_final, send_rate, recv_rate, rate_sems = take(6)
    me, member = lax.axis_index("dp"), lax.axis_index("tensor")
    core, chip = me % 2, me // 2
    spot = ring_spot(chip, chips)
    ways = (
        (2 * ring_chip((spot + 1) % chips, chips) + core, member),
        (2 * ring_chip((spot + chips - 1) % chips, chips) + core, member),
    )
    peer = (2 * chip + 1 - core, member)
    across = (me, 1 - member)
    partners = [across] + [
        (me + (1 << k) - 2 * (1 << k) * ((me // (1 << k)) % 2), member) for k in range(steps - 1)
    ]
    signal_all(list(ways) + partners)

    half = chips // 2
    width = lefts[0].shape[1] // chips
    mid = width // 2
    starts = []
    at = 0
    for _, right in groups:
        starts.append(at)
        at += rights[right].shape[1]

    def columns(group):
        return pl.ds(starts[group], rights[groups[group][1]].shape[1])

    def piece(group, place, lo=0, hi=width):
        left, right = lefts[groups[group][0]], rights[groups[group][1]]
        at = (place % chips) * width
        return lax.dot_general(
            left[:, at + lo : at + hi], right[...], (COLS_ROWS, ((), ())), preferred_element_type=F32
        )

    def rows_of(way):
        return pl.ds(mid * way, mid)

    def hop(way, step, group):
        if step:
            source, target = arrived.at[way, step - 1], arrived.at[way, step % (half - 1)]
            source, target = source.at[:, columns(group)], target.at[:, columns(group)]
        else:
            source = begin.at[way, :, columns(group)]
            target = arrived.at[way, 0, rows_of(way), columns(group)]
        sems = (way, step, group)
        return send(source, target, send_ring.at[sems], recv_ring.at[sems], ways[way])

    rate_rows = rate_begin.shape[1]

    def rate_piece(place):
        at = (place % chips) * width
        value = lax.dot_general(
            rights[-1][:, 0:rate_rows], lefts[-1][:, at : at + width], (COLS_ROWS, ((), ())), preferred_element_type=F32
        )
        return value[:, 0:mid], value[:, mid:width]

    def rate_hop(way, step):
        source = rate_arrived.at[way, step - 1] if step else rate_begin.at[way]
        target = rate_arrived.at[way, step % (half - 1)] if step else rate_arrived.at[way, 0, way]
        sems = (way, step)
        return send(source, target, send_rate.at[sems], recv_rate.at[sems], ways[way])

    def rate_step(step, place):
        for way in range(2):
            rate_hop(way, step).wait_recv()
            for c, value in enumerate(rate_piece(place if way == 0 else -place)):
                if step or c == way:
                    value = value + rate_arrived[way, step, c].astype(F32)
                rate_arrived[way, step, c] = value.astype(BF)
            rate_hop(way, step + 1).start()

    late = [send(late_out.at[way], late_in.at[way], send_late.at[way], recv_late.at[way], ways[way]) for way in range(2)]
    sides = (back, ahead)
    first = [
        send(value.at[1], got_core.at[i], send_first.at[i], recv_first.at[i], peer)
        for i, value in enumerate((back, ahead_far))
    ]
    second = [
        send(sent_half.at[i], got_half.at[i], send_second.at[i], recv_second.at[i], across) for i in range(2)
    ]

    def fold_small(step):
        copies = []
        for i, (out, arrivals) in enumerate(zip(small_outs, small_ins)):
            source = arrivals.at[steps + step - 1] if step else out
            sems = (step, i)
            copies.append(send(source, arrivals.at[step], send_small.at[sems], recv_small.at[sems], partners[step]))
        return copies

    def put(ref, value):
        if width % 128:
            ref[...] = value
            return
        for place in range(chips):
            at = pl.multiple_of(ring_chip((spot + place) % chips, chips) * width, 128)
            ref[:, pl.ds(at, width)] = value[:, place * width : (place + 1) * width]

    def fetch(place):
        return [
            pltpu.make_async_copy(
                weight.at[pl.ds(place * width, width), pl.ds(at, buffer.shape[2])],
                buffer.at[place % 2],
                weight_sem.at[number, place % 2],
            )
            for number, (weight, (at, _), buffer) in enumerate(zip(weights, side_of, buffers))
        ]

    def side_work():
        for place in range(chips):
            if place + 1 < chips:
                for copy in fetch(place + 1):
                    copy.start()
            for copy in fetch(place):
                copy.wait()
            total = jnp.dot(
                rights[-1][:, 0:rate_rows],
                rate_weights[:, place * width : (place + 1) * width],
                preferred_element_type=F32,
            )
            for (_, right), buffer in zip(side_of, buffers):
                total = total + lax.dot_general(
                    rights[right][...],
                    buffer[place % 2],
                    (ROWS_ROWS, ((), ())),
                    preferred_element_type=F32,
                )
            back[:, :, :, place * width : (place + 1) * width] = (
                total.astype(BF).reshape(2, 2, middle.shape[0], width)
            )
            yield
        for copy in first:
            copy.start()
        yield
        ready(*range(n_left + n_right, n_left + n_right + 4))
        for i in range(2):
            first[i].wait_recv()
            total = sides[i][0, 1 - member].astype(F32) + got_core[i, 1 - member].astype(F32)
            sent_half[i] = total.astype(BF)
            second[i].start()
        yield
        total = []
        for i in range(2):
            second[i].wait_recv()
            value = sides[i][0, member].astype(F32) + got_core[i, member].astype(F32)
            total.append(value + got_half[i].astype(F32))
        put(out_tokens, middle[...] + total[1])
        value = stream[...].astype(F32)
        scale = lax.rsqrt(jnp.mean(value * value, axis=1, keepdims=True) + 1e-06)
        value = value * scale
        gained = jnp.sum(total[0] * value, axis=0, keepdims=True)
        grad = total[0] * gain[...]
        grad = scale * (grad - value * jnp.mean(grad * value, axis=1, keepdims=True))
        put(grad_tokens, grad_middle[...] + grad)
        small_out, wide = small_outs
        small_out[...] = jnp.zeros_like(small_out)
        wide[...] = jnp.zeros_like(wide)
        quarter = 2 * member + core
        taps, keyw = grad_cq.shape
        valw = grad_cv.shape[1]
        after = max(8 * keyw, 4 * valw)

        def part(at, size):
            return pl.ds(pl.multiple_of(at + quarter * size, 128), size)

        wide[0:taps, part(0, keyw)] = grad_cq[...]
        wide[0:taps, part(4 * keyw, keyw)] = grad_ck[...]
        wide[taps : 2 * taps, part(0, valw)] = grad_cv[...]
        wide[0:1, after : after + grad_gain.shape[1]] = grad_gain[...]
        wide[0:2, part(after + grad_gain.shape[1], grad_rate.shape[1])] = grad_rate[...]
        lanes = min(width, 128)
        each = width // lanes
        for i, vector in enumerate((gained, mlp_grad[...])):
            for place in range(chips):
                row = (i * chips + ring_chip((spot + place) % chips, chips)) * each
                for k in range(each):
                    at = place * width + k * lanes
                    small_out[pl.ds(row + k, 1), 0:lanes] = vector[:, at : at + lanes]
        for copy in fold_small(0):
            copy.start()
        yield
        for step in range(steps):
            for copy in fold_small(step):
                copy.wait_recv()
            for out, arrivals in zip(small_outs, small_ins):
                before = arrivals.at[steps + step - 1] if step else out
                arrivals[steps + step] = before[...] + arrivals[step]
            if step + 1 < steps:
                for copy in fold_small(step + 1):
                    copy.start()
            yield

    work = side_work()
    ready = staged([*far, ahead_far.at[pl.ds(0, 1)], *far_tokens], near + near_tokens, far_sem)
    for copy in late + fetch(0):
        copy.start()
    for group in range(len(groups)):
        ready(groups[group][0], n_left + groups[group][1])
        for way in range(2):
            begin[way, :, columns(group)] = piece(group, half, mid * way, mid * way + mid).astype(BF)
            hop(way, 0, group).start()
    ready(*range(n_left + n_right))
    for way in range(2):
        rate_begin[way] = rate_piece(half)[way].astype(BF)
        rate_hop(way, 0).start()
    for step in range(half - 1):
        place = half - 1 - step
        for group in range(len(groups)):
            next(work, None)
            next(work, None)
            for way in range(2):
                hop(way, step, group).wait_recv()
                value = piece(group, place if way == 0 else -place)
                if step:
                    value = value + arrived[way, step, :, columns(group)].astype(F32)
                    arrived[way, step, :, columns(group)] = value.astype(BF)
                else:
                    lo = mid * way
                    here = value[lo : lo + mid] + arrived[way, 0, rows_of(way), columns(group)].astype(F32)
                    arrived[way, 0, rows_of(way), columns(group)] = here.astype(BF)
                    arrived[way, 0, rows_of(1 - way), columns(group)] = value[
                        mid - lo : width - lo
                    ].astype(BF)
                if step == half - 2 and group == 0:
                    pl.semaphore_wait(free.at[way], 1)
                hop(way, step + 1, group).start()
            if group == 0:
                rate_step(step, place)
        if step == min(1, half - 3):
            for way in range(2):
                rate_hop(way, 1).wait_send()
                for group in range(len(groups)):
                    hop(way, 1, group).wait_send()
                pl.semaphore_signal(
                    free.at[way], inc=1, device_id=ways[1 - way], device_id_type=pl.DeviceIdType.MESH
                )
    for _ in work:
        pass
    for step in range(steps):
        for copy in fold_small(step):
            copy.wait_send()
    for out, arrivals in zip(small_outs, small_ins):
        out[...] = arrivals[2 * steps - 1]

    rows = width // 2
    finals, used = [], {}
    values = rate_piece(0)
    for way in range(2):
        rate_hop(way, half - 1).wait_recv()
        values = [value + rate_arrived[way, 0, c].astype(F32) for c, value in enumerate(values)]
    for c in range(2):
        rate_final[c] = values[c]
    rate_own = pltpu.make_async_copy(rate_final.at[core], rates_out.at[core], rate_sems.at[0])
    rate_far = send(rate_final.at[1 - core], rates_out.at[core], rate_sems.at[1], rate_sems.at[2], peer)
    rate_own.start()
    rate_far.start()
    for group in [len(groups)] + list(range(len(groups))):
        slot = group % 2
        for copy in used.get(slot, ()):
            copy()
        if group == len(groups):
            value = []
            for left, right in late_parts:
                left = late_left if left is None else lefts[left]
                value.append(
                    lax.dot_general(
                        left[:, 0:width],
                        rights[right][...],
                        (COLS_ROWS, ((), ())),
                        preferred_element_type=F32,
                    )
                )
            value = jnp.concatenate(value, axis=1)
        else:
            value = piece(group, 0)
        for way in range(2):
            if group == len(groups):
                late[way].wait_recv()
                value = value + late_in[way].astype(F32)
            else:
                hop(way, half - 1, group).wait_recv()
                value = value + arrived[way, 0, :, columns(group)].astype(F32)
        final[slot, :, 0 : value.shape[1]] = value
        used[slot] = []
        for number, (owner, at, out, to, whole, size) in enumerate(fields):
            if owner == group:
                own = pl.ds(pl.multiple_of(core * rows, rows), rows)
                theirs = pl.ds(pl.multiple_of((1 - core) * rows, rows), rows)
                target = outs[out].at[:, pl.ds(pl.multiple_of(core * whole + to, 128), size)]
                copy = pltpu.make_async_copy(final.at[slot, own, pl.ds(at, size)], target, own_sem.at[number])
                far = send(
                    final.at[slot, theirs, pl.ds(at, size)],
                    target,
                    send_core.at[number],
                    recv_core.at[number],
                    peer,
                )
                copy.start()
                far.start()
                finals.append(far)
                used[slot] += [copy.wait, far.wait_send]
    for slot in used:
        for copy in used[slot]:
            copy()
    for far in finals:
        far.wait_recv()
    rate_own.wait()
    rate_far.wait()
    for way in range(2):
        for step in range(half):
            if step != 1:
                rate_hop(way, step).wait_send()
    for copy in first + second + late:
        copy.wait_send()
    for step in range(half):
        for group in range(len(groups)):
            for way in range(2):
                if step != 1:
                    hop(way, step, group).wait_send()


def collect(grid, lefts, rights, groups, late, fields, sides, ahead, tokens_in, small, small_shapes, rate_weights):
    chips = grid.chips
    rows, width = tokens_in[2].shape
    steps = grid.devices.bit_length()
    n = sum(rights[right].shape[1] for _, right in groups)
    widest = max([rights[right].shape[1] for _, right in groups] + [late[0].shape[2]])
    block = width // chips
    half = chips // 2
    *late, late_parts = late
    weights = [weight for weight, _, _ in sides]
    side_of = [(at, right) for _, at, right in sides]
    stream, gain, middle, grad_middle, mlp_grad = tokens_in
    tokens_in = [ahead.reshape(2, 2, rows, width), stream, middle, grad_middle]
    inputs = [*lefts, *rights, *late, *weights, *tokens_in, gain, mlp_grad, rate_weights, *small]
    wholes = {}
    for _, _, out, _, whole in fields:
        wholes[out] = whole
    outs = [jax.ShapeDtypeStruct((block // 2, 2 * wholes[out]), F32) for out in range(len(wholes))]
    ends = [sum(rights[right].shape[1] for _, right in late_parts)]
    ends = [rights[right].shape[1] for _, right in groups] + ends
    sized = []
    for i, (group, at, out, to, whole) in enumerate(fields):
        starts = [other[1] for other in fields if other[0] == group and other[1] > at]
        sized.append((group, at, out, to, whole, min(starts + [ends[group]]) - at))
    fields = sized
    tokens = jax.ShapeDtypeStruct((rows, width), F32)
    near = pl.BlockSpec(memory_space=pltpu.VMEM)
    far = pl.BlockSpec(memory_space=pltpu.HBM)
    dma = pltpu.SemaphoreType.DMA
    ring = (2, half, len(groups))
    counts = (len(lefts), len(rights), len(outs), len(sides))
    held = [value.shape for value in (*lefts, *rights)]
    rate = (rate_weights.shape[0], block // 2)
    rates = jax.ShapeDtypeStruct((2,) + rate, F32)
    return pl.pallas_call(
        partial(collect_kernel, chips, steps, groups, late_parts, fields, side_of, counts),
        out_shape=outs + [rates, tokens, tokens] + [jax.ShapeDtypeStruct(shape, F32) for shape in small_shapes],
        in_specs=[far] * (len(held) + 1) + [near] + [far] * (len(sides) + 4) + [near] * 8,
        out_specs=[far] * (len(outs) + 1) + [near] * 4,
        scratch_shapes=[
            pltpu.VMEM((2, block // 2, n), BF),
            pltpu.VMEM((2, half - 1, block, n), BF),
            pltpu.VMEM(late[0].shape, BF),
            pltpu.VMEM((2, block, widest), F32),
            pltpu.VMEM((2, 2, rows, width), BF),
            pltpu.VMEM((2, 2, rows, width), BF),
            pltpu.VMEM((2, rows, width), BF),
            pltpu.VMEM((2, rows, width), BF),
            *[pltpu.VMEM((2 * steps,) + shape, F32) for shape in small_shapes],
        ]
        + [pltpu.VMEM((2, block, rights[right].shape[1]), BF) for _, right in side_of]
        + [pltpu.VMEM(shape, BF) for shape in held]
        + [
            pltpu.VMEM((1, 2, rows, width), BF),
            pltpu.VMEM((rows, width), BF),
            pltpu.VMEM((rows, width), F32),
            pltpu.VMEM((rows, width), F32),
            dma((len(held) + 4,)),
        ]
        + [dma(ring), dma(ring)]
        + [dma((len(fields),))] * 3
        + [dma((2,))] * 6
        + [dma((steps, 2))] * 2
        + [dma((len(sides), 2)), pltpu.SemaphoreType.REGULAR((2,))]
        + [
            pltpu.VMEM((2,) + rate, BF),
            pltpu.VMEM((2, half - 1, 2) + rate, BF),
            pltpu.VMEM((2,) + rate, F32),
            dma((2, half)),
            dma((2, half)),
            dma((3,)),
        ],
        compiler_params=pltpu.CompilerParams(
            collective_id=3, has_side_effects=True, vmem_limit_bytes=63 << 20
        ),
        name="collect",
    )(*inputs)


def finish_kernel(chips, heads, counts, *refs):
    moved, turned = counts
    refs = list(refs)

    def take(count):
        taken, refs[:] = refs[:count], refs[count:]
        return taken

    sources, turning, (rates, gains, wide) = take(moved), take(turned), take(3)
    targets, turned_out = take(moved), take(turned)
    beta, decay, norm_gain, mlp_gain, cq, ck, cv, log, bias, out_gain = take(10)
    held = take(moved)
    sem_in, sem_out = take(2)
    ready = staged(sources, held, sem_in)
    copies = []
    for i, (source, target) in enumerate(zip(held, targets)):
        if len(target.shape) > len(source.shape):
            target = target.at[0]
        ready(i)
        copies.append(pltpu.make_async_copy(source, target, sem_out.at[i]))
        copies[-1].start()
    for source, target in zip(turning, turned_out):
        target[...] = source[...].T
    for core in range(2):
        to = slice(core * heads, (core + 1) * heads)
        beta[to] = rates[core, 0:heads]
        decay[to] = rates[core, heads : 2 * heads]
    lanes = min(norm_gain.shape[1] // chips, 128)
    count = norm_gain.shape[1] // lanes
    for i, vector in enumerate((norm_gain, mlp_gain)):
        for row in range(count):
            vector[:, row * lanes : (row + 1) * lanes] = gains[i * count + row : i * count + row + 1, 0:lanes]
    taps, keyw = cq.shape
    valw = cv.shape[1]
    after = max(2 * keyw, valw)
    cq[...] = wide[0:taps, 0:keyw]
    ck[...] = wide[0:taps, keyw : 2 * keyw]
    cv[...] = wide[taps : 2 * taps, 0:valw]
    out_gain[...] = wide[0:1, after : after + out_gain.shape[1]]
    after += out_gain.shape[1]
    small = (wide.shape[1] - after) // 4
    for quarter in range(4):
        at = after + quarter * small + heads
        to = slice(quarter * heads, (quarter + 1) * heads)
        log[:, to] = wide[0:1, at : at + heads]
        bias[:, to] = wide[1:2, at : at + heads]
    for copy in copies:
        copy.wait()


def finish(grid, heads, moved, turning, rates, gains, wide, vectors, convs):
    near = pl.BlockSpec(memory_space=pltpu.VMEM)
    far = pl.BlockSpec(memory_space=pltpu.HBM)
    out_shape = [jax.ShapeDtypeStruct(shape, F32) for _, shape in moved]
    out_shape += [jax.ShapeDtypeStruct(value.shape[::-1], F32) for value in turning]
    rate = jax.ShapeDtypeStruct((2 * heads, rates.shape[2]), F32)
    vectors = [jax.ShapeDtypeStruct((1, size), F32) for size in vectors]
    convs = [jax.ShapeDtypeStruct(value.shape, F32) for value in convs]
    small = [rate, rate, *vectors[:2], *convs, *vectors[2:]]
    return pl.pallas_call(
        partial(finish_kernel, grid.chips, heads, (len(moved), len(turning))),
        out_shape=out_shape + small,
        in_specs=[far] * len(moved) + [near] * (len(turning) + 3),
        out_specs=[far] * len(moved) + [near] * (len(turning) + len(small)),
        scratch_shapes=[pltpu.VMEM(value.shape, F32) for value, _ in moved]
        + [pltpu.SemaphoreType.DMA((len(moved),))] * 2,
        compiler_params=pltpu.CompilerParams(vmem_limit_bytes=63 << 20),
        name="finish",
    )(*[value for value, _ in moved], *turning, rates, gains, wide)


def whole_rows(stack):
    return stack.reshape(-1, stack.shape[-1])


def per_device(
    tokens,
    segment_ids,
    norm_gain,
    w_query,
    w_key,
    w_value,
    w_outgate,
    w_beta,
    w_decay,
    conv_query,
    conv_key,
    conv_value,
    decay_log,
    decay_bias,
    out_gain,
    w_output,
    mlp_gain,
    w_gate,
    w_up,
    w_down,
    cotangent,
    *,
    devices,
):
    grid = Grid(devices)
    heads = w_beta.shape[1] // 2
    keyw = w_query.shape[1] // 2
    valw = w_value.shape[1] // 2
    ffw = w_gate.shape[1] // 2
    small = -(-2 * heads // 128) * 128

    rate_rows = -(-2 * heads // 16) * 16
    groups = [[w_query, w_key], [w_value, w_outgate], [(w_output,)], rate_rows, [w_gate, w_up, (w_down,)]]
    shown = (tokens[0], cotangent[0], norm_gain[None], mlp_gain[None])
    if norm_gain.shape[0] // grid.chips % 128:
        shown = [grid.into(value) for value in shown]
    *gathered, stream, cot_own, norm_row, mlp_row, rows_mix, cot_rows = spread(
        grid, groups, 4, *shown[:2], shown[2:], (w_beta.T, w_decay.T)
    )
    wqk, wvg, wout = [whole_rows(stack) for stack in gathered[:3]]
    rows_mix, cot_rows = [rows.reshape(-1, rows.shape[-1]) for rows in (rows_mix, cot_rows)]
    segments = jnp.concatenate([segment_ids, grid.over_core(segment_ids)], axis=0)

    conv_parts = [
        part_of(conv_query, grid.quarter, keyw, 1),
        part_of(conv_key, grid.quarter, keyw, 1),
        part_of(conv_value, grid.quarter, valw, 1),
        part_of(decay_log, grid.quarter, heads, 0),
        part_of(decay_bias, grid.quarter, heads, 0),
    ]
    rate_weights = gathered[3].transpose(2, 0, 1, 3).reshape(rate_rows, -1)
    pre_qk = dot(rows_mix, wqk)
    pre_rates = jnp.pad(cols_product(rows_mix, rate_weights), ((0, 0), (0, small - rate_rows)))
    pre_vg = dot(rows_mix, wvg)
    lanes = [jnp.pad(part[None], ((0, 0), (0, small - heads))) for part in conv_parts[3:]]
    mixer_in = (pre_qk, pre_rates, pre_vg, segments[:, :, None], segments[:, None, :], *conv_parts[:3], *lanes, out_gain[None])
    heads_out, kept = mixer(heads, mixer_in)
    rows_mlp, middle = middle_rows(cols_product(heads_out, wout), stream, mlp_row)
    chunk = gathered[4]
    chunks = [chunk, grid.shift(chunk, 1), grid.shift(chunk, -1)]
    pair = tied((chunks[1], chunks[2]), heads_out)
    chunks += [grid.shift(pair[0], 1), grid.shift(pair[1], -1)]
    early = ffw * 1024 // 1408 // 128 * 128
    hidden, *gate_parts, grad_upper, back_part, ahead, begun = mlp(grid, rows_mlp, cot_rows, chunks, ffw, early)
    grad_mixed, grad_middle, grad_mlp_gain, late, grad_qk, grad_rates, grad_vg, *core_grads = turn(
        grid,
        heads,
        early,
        back_part,
        cot_own,
        middle,
        mlp_row,
        wout,
        cot_rows,
        rows_mlp,
        hidden,
        gate_parts[0],
        begun,
        mixer_in,
        kept,
    )

    width = norm_gain.shape[0]
    gain_rows = width // min(width // grid.chips, 128)
    wide = max(8 * keyw, 4 * valw) + out_gain.shape[0] + 4 * small
    *weight_grads, rates, out_tokens, grad_tokens, gains, wide = collect(
        grid,
        [rows_mlp, grad_mixed, rows_mix],
        [gate_parts[1], grad_upper, grad_vg, heads_out, grad_qk, hidden, gate_parts[0], grad_rates],
        [(0, 1), (2, 2), (1, 3), (2, 4), (0, 0)],
        [late, cot_rows[:, : cot_rows.shape[1] // grid.chips], [(None, 5), (0, 6)]],
        [
            (4, 0, 0, early, ffw),
            (5, ffw, 0, 0, ffw),
            (0, 0, 1, 0, ffw),
            (1, 0, 2, 0, valw),
            (1, valw, 3, 0, valw),
            (2, 0, 4, 0, valw),
            (3, 0, 5, 0, keyw),
            (3, keyw, 6, 0, keyw),
            (5, 0, 7, 0, ffw),
        ],
        [(wvg, 0, 2), (wqk, 0, 4)],
        ahead,
        [stream, norm_row, middle, grad_middle, grad_mlp_gain],
        core_grads,
        [(2 * gain_rows, 128), (2 * conv_query.shape[0], wide)],
        rate_weights,
    )
    whole_gate, whole_up, whole_value, whole_outgate, whole_out, whole_query, whole_key, whole_down = weight_grads
    if out_tokens.shape[1] // grid.chips % 128:
        out_tokens, grad_tokens = grid.out_of(out_tokens), grid.out_of(grad_tokens)
    moved = [out_tokens, grad_tokens, whole_query, whole_key, whole_value, whole_outgate, whole_gate, whole_up]
    shapes = [(1,) + value.shape if i < 2 else value.shape for i, value in enumerate(moved)]
    sizes = [width, width, decay_log.shape[0], decay_bias.shape[0], out_gain.shape[0]]
    *moved, whole_out, whole_down, whole_beta, whole_decay, norm_row, mlp_row, cq, ck, cv, log, bias, gain = finish(
        grid,
        heads,
        list(zip(moved, shapes)),
        [whole_out, whole_down],
        rates,
        gains,
        wide,
        sizes,
        [conv_query, conv_key, conv_value],
    )
    out_tokens, grad_tokens, *moved = moved
    whole_query, whole_key, whole_value, whole_outgate, whole_gate, whole_up = moved
    return (
        out_tokens,
        grad_tokens,
        norm_row[0],
        whole_query,
        whole_key,
        whole_value,
        whole_outgate,
        whole_beta.T,
        whole_decay.T,
        cq,
        ck,
        cv,
        log[0],
        bias[0],
        gain[0],
        whole_out,
        mlp_row[0],
        whole_gate,
        whole_up,
        whole_down,
    )


def solution(mesh):
    rows = P("dp", "tensor")
    cols = P("tensor", "dp")
    tokens = P("dp", "tensor", None)
    placed = (tokens, P("dp", None), P()) + (rows,) * 6 + (P(),) * 6
    placed = placed + (cols, P(), rows, rows, cols, tokens)
    given = (tokens, tokens, P()) + (rows,) * 6 + (P(),) * 6 + (cols, P(), rows, rows, cols)
    return jax.shard_map(
        partial(per_device, devices=mesh.shape["dp"]),
        mesh=mesh,
        in_specs=placed,
        out_specs=given,
        check_vma=False,
    )
```

```python
from functools import partial
import math

import jax
import jax.numpy as jnp
from jax import lax
from jax.experimental import pallas as pl
from jax.experimental.pallas import tpu as pltpu
from jax.sharding import PartitionSpec as P

HIGH = lax.Precision.HIGH
HIGHEST = lax.Precision.HIGHEST
BF = jnp.bfloat16
F32 = jnp.float32


def scale_rows(values, factor):
    return values * lax.rsqrt(jnp.mean(values * values, axis=-1, keepdims=True) + 1e-06) * factor


def split3(value):
    high = value.astype(BF)
    return high, (value - high.astype(F32)).astype(BF)


def product(left, right, dims):
    dims = (dims, ((), ()))
    total = lax.dot_general(left[0], right[0], dims, preferred_element_type=F32)
    total = total + lax.dot_general(left[0], right[1], dims, preferred_element_type=F32)
    return total + lax.dot_general(left[1], right[0], dims, preferred_element_type=F32)


ROWS_COLS = ((1,), (0,))
ROWS_ROWS = ((1,), (1,))
COLS_ROWS = ((0,), (0,))


def exact_sum(mask, value, dims):
    high, low = split3(value)
    last = (value - high.astype(F32) - low.astype(F32)).astype(BF)
    dims = (dims, ((), ()))
    total = lax.dot_general(mask, last, dims, preferred_element_type=F32)
    total = total + lax.dot_general(mask, low, dims, preferred_element_type=F32)
    return total + lax.dot_general(mask, high, dims, preferred_element_type=F32)


def conv_parts(values, taps, keeping):
    moved = [values] + [pltpu.roll(values, j, 0) * keeping[j] for j in range(1, 4)]
    total = moved[0] * taps[0:1]
    for j in range(1, 4):
        total = total + moved[j] * taps[j : j + 1]
    return moved, total


def conv_back(grad, moved, taps, keeping):
    rows = grad.shape[0]
    total = grad * taps[0:1]
    for j in range(1, 4):
        total = total + pltpu.roll(grad * keeping[j], rows - j, 0) * taps[j : j + 1]
    parts = [jnp.sum(grad * moved[j], axis=0, keepdims=True) for j in range(4)]
    return total, jnp.concatenate(parts, axis=0)


def silu_back(total, gate):
    return gate * (1.0 + total * (1.0 - gate))


def softplus(value):
    return jnp.maximum(value, 0.0) + jnp.log1p(jnp.exp(-jnp.abs(value)))


def block_masks(seg_col, seg_row):
    size = seg_col.shape[0]
    row = lax.broadcasted_iota(jnp.int32, (size, size), 0)
    col = lax.broadcasted_iota(jnp.int32, (size, size), 1)
    masking = ((seg_col == seg_row) & (col <= row)).astype(F32)
    spot = lax.broadcasted_iota(jnp.int32, (size, 1), 0)
    keeping = [None]
    for j in range(1, 4):
        keeping.append(((pltpu.roll(seg_col, j, 0) == seg_col) & (spot >= j)).astype(F32))
    return row, col, masking, keeping


def head_rates(small, log, bias, masking, heads):
    decay_in = pltpu.roll(small, small.shape[1] - heads, 1) + bias
    factor = -jnp.exp(log)
    rates = factor * softplus(decay_in)
    betas = jax.nn.sigmoid(small)
    summed = exact_sum(masking.astype(BF), rates, ROWS_COLS)
    return decay_in, factor, rates, betas, summed


def invert(mixing, row, col):
    size = mixing.shape[0]
    result = jnp.where(row == col, 1.0, 0.0) - jnp.where((row >> 1) == (col >> 1), mixing, 0.0)
    level = 1
    while (1 << level) < size:
        picked = ((row >> (level + 1)) == (col >> (level + 1))) & ((row >> level) != (col >> level))
        part = split3(jnp.where(picked, mixing, 0.0))
        halves = split3(result)
        step = product(halves, part, ROWS_COLS)
        result = result - product(split3(step), halves, ROWS_COLS)
        level += 1
    return result


def unit(values):
    return lax.rsqrt(jnp.sum(values * values, axis=1, keepdims=True) + 1e-06)


def mixer_kernel(heads, qk, rates_in, vg, seg_col, seg_row, cq, ck, cv, log, bias, gain, *outs):
    heads_out, inverses, all_errors, all_kk, all_qk, all_raw = outs
    keyw, valw = cq.shape[1] // heads, cv.shape[1] // heads
    row, col, masking, keeping = block_masks(seg_col[0], seg_row[0])
    small = rates_in[...]
    _, _, _, betas, summed = head_rates(small, log[...], bias[...], masking, heads)
    betas_t, summed_t = betas.T, summed.T
    strict = (col < row).astype(F32)
    for h in range(heads):
        at = pl.ds(h * keyw, keyw)
        query = jax.nn.silu(conv_parts(qk[:, at], cq[:, at], keeping)[1])
        query = query * (unit(query) * (1.0 / math.sqrt(keyw)))
        key = jax.nn.silu(
            conv_parts(qk[:, pl.ds((heads + h) * keyw, keyw)], ck[:, at], keeping)[1]
        )
        key = key * unit(key)
        at = pl.ds(h * valw, valw)
        value = jax.nn.silu(conv_parts(vg[:, at], cv[:, at], keeping)[1])
        spread = summed[:, h : h + 1] - summed_t[h : h + 1]
        decays = jnp.exp(spread * masking) * masking * betas_t[h : h + 1]
        keys = split3(key)
        key_key = product(keys, keys, ROWS_ROWS)
        query_key = product(split3(query), keys, ROWS_ROWS)
        inverse = invert(decays * key_key * strict, row, col)
        errors = product(split3(inverse), split3(value), ROWS_COLS)
        raw = product(split3(decays * query_key), split3(errors), ROWS_COLS)
        inverses[0, h] = inverse
        all_errors[0, h] = errors
        all_kk[0, h] = key_key
        all_qk[0, h] = query_key
        all_raw[:, at] = raw
        scaled = raw * lax.rsqrt(jnp.mean(raw * raw, axis=1, keepdims=True) + 1e-05) * gain[...]
        gate = vg[:, pl.ds((heads + h) * valw, valw)]
        heads_out[:, at] = (scaled * jax.nn.silu(gate)).astype(BF)


def mixer_back(heads, grad, inputs, kept, results):
    qk, rates_in, vg, seg_col, seg_row, cq, ck, cv, log, bias, gain = inputs
    inverses, all_errors, all_kk, all_qk, all_raw = kept
    grad_qk, grad_small_out, grad_vg, grad_cq, grad_ck, grad_cv, grad_rate, grad_gain = results
    keyw, valw = cq.shape[1] // heads, cv.shape[1] // heads
    size = qk.shape[0]
    row, col, masking, keeping = block_masks(seg_col[0], seg_row[0])
    small = rates_in[...]
    decay_in, factor, rates, betas, summed = head_rates(small, log[...], bias[...], masking, heads)
    betas_t, summed_t = betas.T, summed.T
    strict = (col < row).astype(F32)
    lanes = lax.broadcasted_iota(jnp.int32, (1, small.shape[1]), 1)
    spots = lax.broadcasted_iota(jnp.int32, (small.shape[1], 1), 0)
    grad_summed = jnp.zeros_like(small)
    from_cols = jnp.zeros((small.shape[1], size), F32)
    for h in range(heads):
        at = pl.ds(h * valw, valw)
        raw, gate_in = all_raw[:, at], vg[:, pl.ds((heads + h) * valw, valw)]
        gate = jax.nn.sigmoid(gate_in)
        scale = lax.rsqrt(jnp.mean(raw * raw, axis=1, keepdims=True) + 1e-05)
        above = grad[:, at]
        grad_vg[:, pl.ds((heads + h) * valw, valw)] = (
            above * (raw * scale * gain[...]) * silu_back(gate_in, gate)
        ).astype(BF)
        above = above * (gate_in * gate)
        grad_gain[...] += jnp.sum(above * raw * scale, axis=0, keepdims=True)
        above = above * gain[...]
        grad_raw = scale * (above - raw * (scale * scale * jnp.mean(above * raw, axis=1, keepdims=True)))

        spread = summed[:, h : h + 1] - summed_t[h : h + 1]
        plain = jnp.exp(spread * masking) * masking
        decays = plain * betas_t[h : h + 1]
        key_key, query_key = all_kk[0, h] * strict, all_qk[0, h]
        grad_raws, errors = split3(grad_raw), split3(all_errors[0, h])
        grad_reading = product(grad_raws, errors, ROWS_ROWS)
        grad_errors = product(split3(decays * query_key), grad_raws, COLS_ROWS)
        grad_value = product(split3(inverses[0, h]), split3(grad_errors), COLS_ROWS)
        grad_mixing = -product(split3(grad_value), errors, ROWS_ROWS)
        both = (grad_mixing * key_key + grad_reading * query_key) * plain
        grad_beta = jnp.sum(both, axis=0, keepdims=True)
        both = both * betas_t[h : h + 1]
        from_rows = jnp.sum(both, axis=1, keepdims=True)
        grad_summed = grad_summed + jnp.where(lanes == heads + h, from_rows, 0.0)
        from_cols = from_cols + jnp.where(spots == h, grad_beta, 0.0)
        from_cols = from_cols - jnp.where(spots == heads + h, jnp.sum(both, axis=0, keepdims=True), 0.0)

        at = pl.ds(h * keyw, keyw)
        query_moved, query_total = conv_parts(qk[:, at], cq[:, at], keeping)
        query_gate = jax.nn.sigmoid(query_total)
        query = query_total * query_gate
        query_scale = unit(query)
        query = query * query_scale
        key_at = pl.ds((heads + h) * keyw, keyw)
        key_moved, key_total = conv_parts(qk[:, key_at], ck[:, at], keeping)
        key_gate = jax.nn.sigmoid(key_total)
        key = key_total * key_gate
        key_scale = unit(key)
        key = key * key_scale
        keys = split3(key)
        grad_kk = split3(grad_mixing * decays * strict)
        grad_qk_product = split3(grad_reading * (decays * (1.0 / math.sqrt(keyw))))
        grad_query = product(grad_qk_product, keys, ROWS_COLS)
        grad_key = product(grad_qk_product, split3(query), COLS_ROWS)
        grad_key = grad_key + product(grad_kk, keys, ROWS_COLS) + product(grad_kk, keys, COLS_ROWS)

        grad_query = query_scale * (grad_query - query * jnp.sum(grad_query * query, axis=1, keepdims=True))
        grad_query = grad_query * silu_back(query_total, query_gate)
        grad_query, taps = conv_back(grad_query, query_moved, cq[:, at], keeping)
        grad_qk[:, at] = grad_query.astype(BF)
        grad_cq[:, at] += taps
        grad_key = key_scale * (grad_key - key * jnp.sum(grad_key * key, axis=1, keepdims=True))
        grad_key = grad_key * silu_back(key_total, key_gate)
        grad_key, taps = conv_back(grad_key, key_moved, ck[:, at], keeping)
        grad_qk[:, key_at] = grad_key.astype(BF)
        grad_ck[:, at] += taps

        at = pl.ds(h * valw, valw)
        moved, total = conv_parts(vg[:, at], cv[:, at], keeping)
        grad_value = grad_value * silu_back(total, jax.nn.sigmoid(total))
        grad_value, taps = conv_back(grad_value, moved, cv[:, at], keeping)
        grad_vg[:, at] = grad_value.astype(BF)
        grad_cv[:, at] += taps

    from_cols = from_cols.T
    grad_summed = grad_summed + jnp.where(lanes >= heads, from_cols, 0.0)
    grad_rates = exact_sum(masking.astype(BF), grad_summed, COLS_ROWS)
    decay_lanes = (lanes >= heads) & (lanes < 2 * heads)
    shifted = [pltpu.roll(value, heads, 1) for value in (decay_in, rates)]
    grad_decay = grad_rates * pltpu.roll(factor, heads, 1) * jax.nn.sigmoid(shifted[0])
    grad_rate[0:1] += jnp.sum(grad_rates * shifted[1], axis=0, keepdims=True)
    grad_rate[1:2] += jnp.sum(grad_decay, axis=0, keepdims=True)
    grad_small = jnp.where(decay_lanes, grad_decay, from_cols * betas * (1.0 - betas))
    grad_small = jnp.where(lanes < 2 * heads, grad_small, 0.0)
    grad_small_out[...] = grad_small.astype(BF)


def mixer_specs(heads, qk, vg, cq, cv, small):
    length = qk.shape[0] // 2

    def by_rows(width):
        return pl.BlockSpec((length, width), lambda s: (s, 0))

    def fixed(*shape):
        return pl.BlockSpec(shape, lambda s: (0,) * len(shape))

    shared = [
        by_rows(qk.shape[1]),
        by_rows(small),
        by_rows(vg.shape[1]),
        pl.BlockSpec((1, length, 1), lambda s: (s, 0, 0)),
        pl.BlockSpec((1, 1, length), lambda s: (s, 0, 0)),
        fixed(*cq.shape),
        fixed(*cq.shape),
        fixed(*cv.shape),
        fixed(1, small),
        fixed(1, small),
        fixed(1, cv.shape[1] // heads),
    ]
    valw = cv.shape[1] // heads
    square = (heads, length, length)
    kept = [square, (heads, length, valw), square, square]
    kept_specs = [pl.BlockSpec((1,) + shape, lambda s: (s, 0, 0, 0)) for shape in kept]
    kept_specs.append(by_rows(cv.shape[1]))
    kept_shapes = [jax.ShapeDtypeStruct((2,) + shape, F32) for shape in kept]
    kept_shapes.append(jax.ShapeDtypeStruct((2 * length, cv.shape[1]), F32))
    return by_rows, fixed, shared, kept_specs, kept_shapes


def mixer(heads, inputs):
    qk, _, vg, _, _, cq, _, cv, log, _, _ = inputs
    by_rows, _, shared, kept_specs, kept_shapes = mixer_specs(heads, qk, vg, cq, cv, log.shape[1])
    heads_out, *kept = pl.pallas_call(
        partial(mixer_kernel, heads),
        grid=(2,),
        out_shape=[jax.ShapeDtypeStruct((qk.shape[0], cv.shape[1]), BF)] + kept_shapes,
        in_specs=shared,
        out_specs=[by_rows(cv.shape[1])] + kept_specs,
        compiler_params=pltpu.CompilerParams(vmem_limit_bytes=48 << 20),
        name="mixer",
    )(*inputs)
    return heads_out, kept


def rows_product(left, right):
    return lax.dot_general(left, right, (((0,), (0,)), ((), ())), preferred_element_type=F32)


def cols_product(left, right):
    return lax.dot_general(left, right, (((1,), (1,)), ((), ())), preferred_element_type=F32)


def dot(left, right):
    return jnp.dot(left, right, preferred_element_type=F32)


def tied(value, after):
    return lax.optimization_barrier((value, after))[0]


def first_of(flag, own, peer, axis):
    return jnp.concatenate([jnp.where(flag, own, peer), jnp.where(flag, peer, own)], axis=axis)


def part_of(value, index, size, axis):
    return lax.dynamic_slice_in_dim(value, index * size, size, axis)


class Grid:
    def __init__(self, devices):
        self.devices = devices
        self.chips = devices // 2
        me = lax.axis_index("dp")
        self.core = me % 2
        self.spot = ring_spot(me // 2, self.chips)
        self.member = lax.axis_index("tensor")
        self.quarter = 2 * self.member + self.core

    def swap(self, value, offset):
        pairs = [(at, at ^ offset) for at in range(self.devices)]
        return lax.ppermute(value, "dp", pairs)

    def over_core(self, value):
        return self.swap(value, 1)

    def over_tensor(self, value):
        return lax.ppermute(value, "tensor", [(0, 1), (1, 0)])

    def shift(self, value, step):
        pairs = []
        for at in range(self.devices):
            spot = (ring_spot(at // 2, self.chips) + step) % self.chips
            pairs.append((at, 2 * ring_chip(spot, self.chips) + at % 2))
        return lax.ppermute(value, "dp", pairs)

    def into(self, value):
        width = value.shape[-1] // self.chips
        blocks = []
        for place in range(self.chips):
            chip = ring_chip((self.spot + place) % self.chips, self.chips)
            blocks.append(part_of(value, chip, width, -1))
        return jnp.concatenate(blocks, axis=-1)

    def out_of(self, value):
        width = value.shape[-1] // self.chips
        blocks = []
        for chip in range(self.chips):
            place = (ring_spot(chip, self.chips) - self.spot + self.chips) % self.chips
            blocks.append(part_of(value, place, width, -1))
        return jnp.concatenate(blocks, axis=-1)

    def gather_rows(self, own):
        whole = first_of(self.member == 0, own, self.over_tensor(own), 0)
        return jnp.concatenate([whole, self.over_core(whole)], axis=0)

    def scatter_rows(self, value):
        half = value.shape[0] // 2
        whole = value[:half] + self.over_core(value[half:])
        half //= 2
        theirs = part_of(whole, 1 - self.member, half, 0)
        peer = self.over_tensor(theirs.astype(BF)).astype(F32)
        return part_of(whole, self.member, half, 0) + peer


def ring_spot(chip, chips):
    line, pair = chip // 2, chip % 2
    return line * (1 - pair) + (chips - 1 - line) * pair


def ring_chip(spot, chips):
    pair = spot // (chips // 2)
    return 2 * (spot * (1 - pair) + (chips - 1 - spot) * pair) + pair


def signal_all(devices):
    barrier = pltpu.get_barrier_semaphore()
    for device in devices:
        pl.semaphore_signal(barrier, inc=1, device_id=device, device_id_type=pl.DeviceIdType.MESH)
    pl.semaphore_wait(barrier, len(devices))


def send(source, target, send_sem, recv_sem, device):
    return pltpu.make_async_remote_copy(
        src_ref=source,
        dst_ref=target,
        send_sem=send_sem,
        recv_sem=recv_sem,
        device_id=device,
        device_id_type=pl.DeviceIdType.MESH,
    )


def staged(sources, targets, sem):
    copies = [pltpu.make_async_copy(*pair, sem.at[i]) for i, pair in enumerate(zip(sources, targets))]
    pending = set(range(len(copies)))
    for copy in copies:
        copy.start()

    def ready(*numbers):
        for i in sorted(pending.intersection(numbers)):
            copies[i].wait()
            pending.remove(i)

    return ready


def spread_kernel(chips, layout, ringed, *refs):
    count = len(layout)
    totals = 1 + max(item[0] for item in layout)
    sources, (tokens, cot, gain, gain_mlp, w_decay) = refs[:count], refs[count : count + 5]
    refs = refs[count + 5 :]
    given_out = refs[:totals]
    stream, cot_own, own_gain, own_gain_mlp, rows_mix, rows_cot = refs[totals : totals + 6]
    refs = refs[totals + 6 :]
    normed, near_sem, send_core, recv_core, send_right, recv_right, send_left, recv_left = refs[:8]
    own_sem, send_half, recv_half, send_whole, recv_whole, rate_sum, rate_own, store_sem, *turned = refs[8:]
    outs, turned = (*turned[:ringed], *given_out[ringed:]), turned[ringed:]
    me, member = lax.axis_index("dp"), lax.axis_index("tensor")
    core, chip = me % 2, me // 2
    spot = ring_spot(chip, chips)
    right = (2 * ring_chip((spot + 1) % chips, chips) + core, member)
    left = (2 * ring_chip((spot + chips - 1) % chips, chips) + core, member)
    peer = (2 * chip + 1 - core, member)
    across = (me, 1 - member)
    signal_all((right, left, peer, across))

    def home(out):
        return outs[out].at[0] if out < ringed else outs[out]

    near, far = [], []
    given = list(sources)
    turned = [(i, target) for i, target in zip([i for i, item in enumerate(layout) if item[3]], turned)]
    sources = list(sources)
    for i, target in turned:
        sources[i] = target
    for i, (out, at, width, _) in enumerate(layout):
        if width is None:
            place = home(out).at[core]
            near.append(pltpu.make_async_copy(rate_own.at[core], place, near_sem.at[i]))
            far.append(send(rate_own.at[1 - core], place, send_core.at[i], recv_core.at[i], peer))
            heads = w_decay.shape[0] // 2
            rate_sum[...] = jnp.zeros_like(rate_sum)
            for at, part in ((0, sources[i][...].astype(F32)), (heads, w_decay[...].astype(F32))):
                for c in range(2):
                    rate_sum[c, at : at + heads] = part[c * heads : (c + 1) * heads]
            rate_own[...] = rate_sum[...].astype(BF)
            continue
        rows = sources[i].shape[0]
        place = home(out).at[pl.ds(pl.multiple_of(core * rows, rows), rows), pl.ds(at, width)]
        mine = sources[i].at[:, pl.ds(pl.multiple_of(core * width, 128), width)]
        theirs = sources[i].at[:, pl.ds(pl.multiple_of((1 - core) * width, 128), width)]
        near.append(pltpu.make_async_copy(mine, place, near_sem.at[i]))
        far.append(send(theirs, place, send_core.at[i], recv_core.at[i], peer))

    def trade_halves(outs_now):
        for i, target in turned:
            if layout[i][0] in outs_now:
                target[...] = given[i][...].T
        for i, item in enumerate(layout):
            if item[0] in outs_now:
                far[i].start()
                near[i].start()

    trade_halves(range(2))

    def hop(out, step, way):
        last = step == chips // 2
        ref = outs[out]
        mid = ref.shape[1] // 2
        if way > 0:
            at, to, device, sends, receives = -(step - 1) % chips, chips - step, right, send_right, recv_right
            rows = pl.ds(0, mid)
        else:
            at, to, device, sends, receives = step - 1, step, left, send_left, recv_left
            rows = pl.ds(mid, mid)
        source, target = ref.at[at], ref.at[to]
        if last:
            source, target = source.at[rows], target.at[rows]
        return send(source, target, sends.at[out, step - 1], receives.at[out, step - 1], device)

    stored = []

    def store(out, slot):
        stored.append(pltpu.make_async_copy(outs[out].at[slot], given_out[out].at[slot], store_sem.at[out, slot]))
        stored[-1].start()

    started, own = [], []
    pairs = ((normed, rows_mix), (cot_own, rows_cot))
    halves = [
        send(value, rows.at[0, member], send_half.at[i], recv_half.at[i], across)
        for i, (value, rows) in enumerate(pairs)
    ]
    wholes = [
        send(rows.at[0], rows.at[1], send_whole.at[i], recv_whole.at[i], peer)
        for i, (_, rows) in enumerate(pairs)
    ]
    for step in range(1, chips // 2 + 1):
        for out in range(ringed):
            if step == 1:
                for i, item in enumerate(layout):
                    if item[0] == out:
                        near[i].wait()
                        far[i].wait()
            for way in (1, -1):
                if step > 1:
                    hop(out, step - 1, way).wait_recv()
                copy = hop(out, step, way)
                copy.start()
                started.append(copy)
                if step > 1:
                    store(out, chips - step + 1 if way > 0 else step - 1)
            if step == 1:
                store(out, 0)
                trade_halves((out + 2,) if out + 2 < ringed else ())
        if step == 1:
            trade_halves(range(ringed, totals))
            width = tokens.shape[1] // chips
            aligned = width % 128 == 0
            squares = jnp.zeros((tokens.shape[0], 1), F32)
            for place in range(chips):
                to = pl.ds(place * width, width)
                at = to
                if aligned:
                    at = ring_chip((spot + place) % chips, chips) * width
                    at = pl.ds(pl.multiple_of(at, 128), width)
                stream[:, to] = tokens[:, at]
                cot_own[:, to] = cot[:, at]
                own_gain[:, to] = gain[:, at]
                own_gain_mlp[:, to] = gain_mlp[:, at]
                block = stream[:, to].astype(F32)
                squares = squares + jnp.sum(block * block, axis=1, keepdims=True)
            scale = lax.rsqrt(squares / tokens.shape[1] + 1e-06)
            normed[...] = (stream[...].astype(F32) * scale * own_gain[...]).astype(BF)
            for i, (value, rows) in enumerate(pairs):
                own.append(pltpu.make_async_copy(value, rows.at[0, member], own_sem.at[i]))
                own[-1].start()
                halves[i].start()
        if step == 2:
            for i in range(2):
                own[i].wait()
                halves[i].wait()
                wholes[i].start()
    for i, item in enumerate(layout):
        if item[0] >= ringed:
            near[i].wait()
            far[i].wait()
    for copy in wholes:
        copy.wait()
    for out in range(ringed):
        for way in (1, -1):
            hop(out, chips // 2, way).wait_recv()
        store(out, chips // 2)
    for copy in stored:
        copy.wait()
    for copy in started:
        copy.wait_send()


def spread(grid, groups, ringed, tokens, cot, gains, rates):
    chips = grid.chips
    sources, layout, shapes, turned_shapes = [], [], [], []
    for out, group in enumerate(groups):
        if not isinstance(group, list):
            rate = (2, group, rates[0].shape[1])
            layout.append((out, 0, None, False))
            sources.append(rates[0])
            shapes.append(jax.ShapeDtypeStruct((chips,) + rate, BF))
            continue
        at = 0
        for shard in group:
            turned = isinstance(shard, tuple)
            if turned:
                (shard,) = shard
                turned_shapes.append(pltpu.VMEM(shard.shape[::-1], BF))
            width = shard.shape[0 if turned else 1] // 2
            layout.append((out, at, width, turned))
            sources.append(shard)
            at += width
        rows = 2 * tokens.shape[1] // grid.devices
        shapes.append(jax.ShapeDtypeStruct(((chips,) if out < ringed else ()) + (rows, at), BF))
    dma = pltpu.SemaphoreType.DMA
    hops = (ringed, chips // 2)
    anywhere = pl.BlockSpec(memory_space=pltpu.HBM)
    near = pl.BlockSpec(memory_space=pltpu.VMEM)
    own = jax.ShapeDtypeStruct(tokens.shape, BF)
    rows = jax.ShapeDtypeStruct((2, 2) + tokens.shape, BF)
    return pl.pallas_call(
        partial(spread_kernel, chips, layout, ringed),
        out_shape=shapes + [own, own] + [jax.ShapeDtypeStruct(gains[0].shape, F32)] * 2 + [rows, rows],
        in_specs=[near if item[3] or item[2] is None else anywhere for item in layout] + [near] * 5,
        out_specs=[anywhere] * len(shapes) + [near] * 4 + [anywhere] * 2,
        scratch_shapes=[pltpu.VMEM(tokens.shape, BF)]
        + [dma((len(sources),))] * 3
        + [dma(hops)] * 4
        + [dma((2,))] * 5
        + [pltpu.VMEM(rate, F32), pltpu.VMEM(rate, BF), dma((ringed, chips))]
        + [pltpu.VMEM(shape.shape, BF) for shape in shapes[:ringed]]
        + turned_shapes,
        compiler_params=pltpu.CompilerParams(
            collective_id=0, has_side_effects=True, vmem_limit_bytes=62 << 20
        ),
        name="spread",
    )(*sources, tokens, cot, *gains, rates[1])


PARTS = 2


def exchange(part, own_part, rows_out, buffers, sems, compute, early=None, late=None):
    got_core, sent_half, got_half, own = buffers
    me, member = lax.axis_index("dp"), lax.axis_index("tensor")
    peer = (me + 1 - 2 * (me % 2), member)
    across = (me, 1 - member)
    count = part.shape[2] // PARTS

    def chunk(k):
        return pl.ds(k * count, count)

    def copy(kind, k, source, target, device):
        return send(source, target, sems[2 * kind].at[k], sems[2 * kind + 1].at[k], device)

    first = [copy(0, k, part.at[1, :, chunk(k)], got_core.at[:, chunk(k)], peer) for k in range(PARTS)]
    second = [copy(1, k, sent_half.at[chunk(k)], got_half.at[chunk(k)], across) for k in range(PARTS)]
    third = [
        copy(2, k, own.at[chunk(k)], rows_out.at[0, member, chunk(k)], across) for k in range(PARTS)
    ]
    fourth = [
        copy(3, k, own.at[chunk(k)], rows_out.at[1, member, chunk(k)], peer) for k in range(PARTS)
    ]
    fifth = [
        copy(4, k, rows_out.at[0, 1 - member, chunk(k)], rows_out.at[1, 1 - member, chunk(k)], peer)
        for k in range(PARTS)
    ]
    for k in range(PARTS):
        first[k].start()
    if early:
        early()
    for k in range(PARTS):
        first[k].wait_recv()
        total = own_part[1 - member, chunk(k)] + got_core[1 - member, chunk(k)]
        sent_half[chunk(k)] = total.astype(BF)
        second[k].start()
    for k in range(PARTS):
        second[k].wait_recv()
        total = own_part[member, chunk(k)] + got_core[member, chunk(k)] + got_half[chunk(k)].astype(F32)
        value = compute(k, chunk(k), total).astype(BF)
        own[chunk(k)] = value
        third[k].start()
        fourth[k].start()
        rows_out[0, member, chunk(k)] = value
    for k in range(PARTS):
        third[k].wait_recv()
        fifth[k].start()
    if late:
        late()
    for k in range(PARTS):
        fourth[k].wait_recv()
        fifth[k].wait_recv()
    for copies in (first, second, third, fourth, fifth):
        for one in copies:
            one.wait_send()


def exchange_scratch(rows, width):
    return [
        pltpu.VMEM((2, rows, width), F32),
        pltpu.VMEM((rows, width), BF),
        pltpu.VMEM((rows, width), BF),
        pltpu.VMEM((rows, width), BF),
    ] + [pltpu.SemaphoreType.DMA((PARTS,))] * 10


def middle_kernel(part, stream, gain, rows_out, middle, *scratch):
    me, member = lax.axis_index("dp"), lax.axis_index("tensor")
    signal_all(((me + 1 - 2 * (me % 2), member), (me, 1 - member)))

    def compute(k, rows, mixed):
        value = stream[rows].astype(F32) + mixed
        middle[rows] = value
        return value * lax.rsqrt(jnp.mean(value * value, axis=1, keepdims=True) + 1e-06) * gain[...]

    exchange(part, part.at[0], rows_out, scratch[:4], scratch[4:], compute)


def middle_rows(part, stream, gain):
    rows, width = stream.shape
    near = pl.BlockSpec(memory_space=pltpu.VMEM)
    gathered, middle = pl.pallas_call(
        middle_kernel,
        out_shape=[
            jax.ShapeDtypeStruct((2, 2, rows, width), BF),
            jax.ShapeDtypeStruct((rows, width), F32),
        ],
        in_specs=[near] * 3,
        out_specs=[near] * 2,
        scratch_shapes=exchange_scratch(rows, width),
        compiler_params=pltpu.CompilerParams(
            collective_id=1, has_side_effects=True, vmem_limit_bytes=62 << 20
        ),
        name="middle",
    )(part.reshape(2, 2, rows, width), stream, gain)
    return gathered.reshape(4 * rows, width), middle


def turn_kernel(chips, heads, ffw, early, *refs):
    refs = list(refs)

    def take(count):
        taken, refs[:] = refs[:count], refs[count:]
        return taken

    part, gain = take(2)
    small_inputs, later = take(8), take(17)
    rows_out, grad_middle, grad_gain, late = take(4)
    results = take(8)
    grad_heads, going, arrived = take(3)
    here_now, (later_sem,) = take(17), take(1)
    send_ring, recv_ring = take(2)
    me, member = lax.axis_index("dp"), lax.axis_index("tensor")
    core, chip = me % 2, me // 2
    spot = ring_spot(chip, chips)
    ways = (
        (2 * ring_chip((spot + 1) % chips, chips) + core, member),
        (2 * ring_chip((spot + chips - 1) % chips, chips) + core, member),
    )
    rows_cot, rows_mlp, hidden, grad_gate, begun, own_part, cot, middle, wout, *kept = here_now[:14]
    inputs = here_now[14:] + small_inputs
    later[5] = later[5].at[0]
    ready = staged(later, here_now, later_sem)
    signal_all((*ways, (me + 1 - 2 * core, member), (me, 1 - member)))
    half = chips // 2
    width = rows_cot.shape[1] // chips
    mid = width // 2

    def total(way, place, step):
        at = (place if way == 0 else -place) % chips * width
        value = []
        for left, right, size in ((rows_cot, hidden, ffw), (rows_mlp, grad_gate, early)):
            value.append(
                lax.dot_general(
                    left[:, at : at + width],
                    right[:, 0:size],
                    (COLS_ROWS, ((), ())),
                    preferred_element_type=F32,
                )
            )
        value = jnp.concatenate(value, axis=1)
        if step:
            return (value + arrived[way, step - 1].astype(F32)).astype(BF)
        lo = mid * way
        here = value[lo : lo + mid] + begun[way].astype(F32)
        rest = value[mid - lo : width - lo]
        return jnp.concatenate([here, rest] if way == 0 else [rest, here], axis=0).astype(BF)

    def hop(way, step):
        sems = (way, step)
        source = arrived.at[way, step - 1] if step else going.at[way]
        return send(source, arrived.at[sems], send_ring.at[sems], recv_ring.at[sems], ways[way])

    def next_hop(step):
        for way in range(2):
            if step:
                hop(way, step - 1).wait_recv()
            value = total(way, half - 1 - step, step)
            if step == half - 2:
                late[way] = value
                continue
            if step:
                arrived[way, step - 1] = value
            else:
                going[way] = value
            hop(way, step).start()

    def compute(k, rows, grad):
        value = middle[rows]
        scale = lax.rsqrt(jnp.mean(value * value, axis=1, keepdims=True) + 1e-06)
        unit_value = value * scale
        gained = jnp.sum(grad * unit_value, axis=0, keepdims=True)
        grad_gain[...] = gained if k == 0 else grad_gain[...] + gained
        grad = grad * gain[...]
        grad = scale * (grad - unit_value * jnp.mean(grad * unit_value, axis=1, keepdims=True))
        grad = grad + cot[rows].astype(F32)
        grad_middle[rows] = grad
        return grad


    def early_work():
        ready(*range(5))
        next_hop(0)
        ready(5, 6, 7)

    def late_work():
        if half > 3:
            next_hop(1)

    exchange(part, own_part, rows_out, refs[:4], refs[4:], compute, early_work, late_work)
    ready(*range(17))
    for step in range(2, half - 2):
        next_hop(step)
    for ref in results[3:]:
        ref[...] = jnp.zeros_like(ref)
    length = inputs[0].shape[0] // 2

    @pl.loop(0, 2)
    def _(s):
        at = pl.multiple_of(s * length, length)
        here = pl.ds(at, length)
        for m in range(2):
            grad_heads[pl.ds(at + m * (length // 2), length // 2)] = jnp.dot(
                rows_out[s, m], wout[...], preferred_element_type=F32
            )
        mixer_back(
            heads,
            grad_heads.at[here],
            [ref.at[here] for ref in inputs[:3]] + [ref.at[pl.ds(s, 1)] for ref in inputs[3:5]] + inputs[5:],
            [ref.at[pl.ds(s, 1)] for ref in kept[:4]] + [kept[4].at[here]],
            [ref.at[here] for ref in results[:3]] + results[3:],
        )

    next_hop(half - 2)
    for step in range(half - 2):
        for way in range(2):
            hop(way, step).wait_send()


def turn(grid, heads, early, part, cot, middle, gain, wout, rows_cot, rows_mlp, hidden, grad_gate, begun, inputs, kept):
    chips = grid.chips
    rows, width = middle.shape
    block, half = width // chips, chips // 2
    ffw = hidden.shape[1]
    n = ffw + early
    qk, rates_in, vg, _, _, cq, ck, cv, log, _, out_gain = inputs
    near = pl.BlockSpec(memory_space=pltpu.VMEM)
    far = pl.BlockSpec(memory_space=pltpu.HBM)
    dma = pltpu.SemaphoreType.DMA
    sums = [cq.shape, ck.shape, cv.shape, (2, log.shape[1]), out_gain.shape]
    part = part.reshape(2, 2, rows, width)
    near_in = (gain, *inputs[3:])
    later = (rows_cot, rows_mlp, hidden, grad_gate, begun, part, cot, middle, wout, *kept, *inputs[:3])
    held = [value.shape[1:] if value is part else value.shape for value in later]
    gathered, *rest = pl.pallas_call(
        partial(turn_kernel, chips, heads, ffw, early),
        out_shape=[
            jax.ShapeDtypeStruct((2, 2, rows, width), BF),
            jax.ShapeDtypeStruct((rows, width), F32),
            jax.ShapeDtypeStruct((1, width), F32),
            jax.ShapeDtypeStruct((2, block, n), BF),
            jax.ShapeDtypeStruct(qk.shape, BF),
            jax.ShapeDtypeStruct(rates_in.shape, BF),
            jax.ShapeDtypeStruct(vg.shape, BF),
        ]
        + [jax.ShapeDtypeStruct(shape, F32) for shape in sums],
        in_specs=[far] + [near] * len(near_in) + [far] * len(later),
        out_specs=[near] * (7 + len(sums)),
        scratch_shapes=[
            pltpu.VMEM((4 * rows, cv.shape[1]), F32),
            pltpu.VMEM((2, block, n), BF),
            pltpu.VMEM((2, half - 2, block, n), BF),
            *[pltpu.VMEM(shape, value.dtype) for shape, value in zip(held, later)],
            dma((len(later),)),
            dma((2, half - 2)),
            dma((2, half - 2)),
        ]
        + exchange_scratch(rows, width),
        compiler_params=pltpu.CompilerParams(
            collective_id=2, has_side_effects=True, vmem_limit_bytes=62 << 20
        ),
        name="turn",
    )(part, *near_in, *later)
    return gathered.reshape(4 * rows, width), *rest


def mlp_kernel(chips, ffw, early, *refs):
    rows_far, cot_far, own, right_1, left_1, right_2, left_2 = refs[:7]
    *given, begun = refs[7:14]
    hidden, gate_early, gate_rest, grad_upper, back, ahead, store_sem = refs[14:21]
    refs = refs[7:]
    rows, cot, rows_sem, weights, sums, begin, load_sem, send_ring, recv_ring, send_begin, recv_begin = refs[14:]
    me, member = lax.axis_index("dp"), lax.axis_index("tensor")
    core, chip = me % 2, me // 2
    spot = ring_spot(chip, chips)
    ways = (
        (2 * ring_chip((spot + 1) % chips, chips) + core, member),
        (2 * ring_chip((spot + chips - 1) % chips, chips) + core, member),
    )
    signal_all(ways)
    half = chips // 2
    block = own.shape[0]
    mid = block // 2

    def spots(place, lo=0, hi=block):
        return pl.ds((place % chips) * block + lo, hi - lo)

    def hop(way, step):
        cols = pl.ds(0, 3 * ffw)
        lo, hi = 0, block
        sems = (way, step - 3)
        if step >= half:
            cols = pl.ds(0, 2 * ffw) if step == half else pl.ds(2 * ffw, ffw)
            lo, hi = mid * way, mid * way + mid
            step = half
        place, to = (1 - step, -step) if way == 0 else (step - 1, step)
        if step == 3:
            source = (right_2, left_2)[way].at[pl.ds(lo, hi - lo), cols]
        else:
            source = weights.at[spots(place, lo, hi), cols]
        return send(source, weights.at[spots(to, lo, hi), cols], send_ring.at[sems], recv_ring.at[sems], ways[way])

    for way in range(2):
        hop(way, 3).start()
    loads = []
    for number, (place, source) in enumerate(((0, own), (1, left_1), (2, left_2), (-2, right_2), (-1, right_1))):
        loads.append(pltpu.make_async_copy(source, weights.at[spots(place)], load_sem.at[number]))
        loads[-1].start()

    ready = staged((rows_far, cot_far), (rows, cot), rows_sem)
    tile = ffw // 2

    def add(lo, hi, first, begins=0, ends=3 * ffw):
        inner = slice((lo % chips) * block, (lo % chips + hi - lo) * block)
        for at in range(begins, ends, tile):
            left = rows if at < 2 * ffw else cot
            value = jnp.dot(left[:, inner], weights[inner, at : at + tile], preferred_element_type=F32)
            sums[:, at : at + tile] = value if first else sums[:, at : at + tile] + value

    ready(0, 1)
    for copy in loads[:3]:
        copy.wait()
    add(0, 3, True)
    for copy in loads[3:]:
        copy.wait()
    add(-2, 0, False)
    for step in range(3, half):
        for way in range(2):
            hop(way, step).wait_recv()
            hop(way, step + 1).start()
            if step + 1 == half:
                hop(way, half + 1).start()
        add(step, step + 1, False)
        add(-step, 1 - step, False)

    starts = []

    def first_hop(lo, hi):
        number = len(starts) // 2
        for way in range(2):
            row = half * block + mid * way
            for left, right, at, size in ((cot, hidden, 0, ffw), (rows, gate_early, ffw, early)):
                begins, ends = max(lo - at, 0), min(hi - at, size)
                if begins < ends:
                    begin[way, :, at + begins : at + ends] = lax.dot_general(
                        left[:, row : row + mid],
                        right[:, begins:ends],
                        (COLS_ROWS, ((), ())),
                        preferred_element_type=F32,
                    ).astype(BF)
            cols = pl.ds(lo, hi - lo)
            sems = (way, number)
            starts.append(
                send(
                    begin.at[way, :, cols], begun.at[way, :, cols], send_begin.at[sems], recv_begin.at[sems], ways[way]
                )
            )
            starts[-1].start()

    for way in range(2):
        hop(way, half).wait_recv()
    add(half, half + 1, False, 0, 2 * ffw)
    for at in range(0, ffw, 128):
        gate, upper = sums[:, at : at + 128], sums[:, ffw + at : ffw + at + 128]
        hidden[:, at : at + 128] = (gate * jax.nn.sigmoid(gate) * upper).astype(BF)
    first_hop(0, ffw)
    stores = []

    def store(number, source, target):
        stores.append(pltpu.make_async_copy(source, target, store_sem.at[number]))
        stores[-1].start()

    def look_ahead(place):
        inner = slice(place * block, (place + 1) * block)
        ahead[:, inner] = lax.dot_general(
            hidden[...], weights[inner, 2 * ffw :], (ROWS_ROWS, ((), ())), preferred_element_type=F32
        ).astype(BF)

    store(0, hidden, given[0])
    for place in range(chips):
        if place != half:
            look_ahead(place)
    for way in range(2):
        hop(way, half + 1).wait_recv()
    add(half, half + 1, False, 2 * ffw)
    for at in range(0, ffw, 128):
        gate, upper = sums[:, at : at + 128], sums[:, ffw + at : ffw + at + 128]
        grad = sums[:, 2 * ffw + at : 2 * ffw + at + 128]
        open_gate = jax.nn.sigmoid(gate)
        part, to = (gate_early, at) if at < early else (gate_rest, at - early)
        part[:, to : to + 128] = (grad * upper * silu_back(gate, open_gate)).astype(BF)
        grad_upper[:, at : at + 128] = (grad * gate * open_gate).astype(BF)
        if at + 128 == early:
            first_hop(ffw, ffw + early)
    for number, value in ((1, gate_early), (2, gate_rest), (3, grad_upper)):
        store(number, value, given[number])
    look_ahead(half)
    store(5, ahead, given[5])
    for place in range(chips):
        inner = slice(place * block, (place + 1) * block)
        value, at = 0.0, 0
        for part in (gate_early, gate_rest, grad_upper):
            cols = slice(at, at + part.shape[1])
            value = value + lax.dot_general(
                part[...], weights[inner, cols], (ROWS_ROWS, ((), ())), preferred_element_type=F32
            )
            at += part.shape[1]
        back[:, inner] = value
        if place % (chips // 4) == chips // 4 - 1:
            quarter = pl.ds((place + 1 - chips // 4) * block, chips // 4 * block)
            store(6 + place // (chips // 4), back.at[:, quarter], given[4].at[:, quarter])
    for copy in stores:
        copy.wait()
    for copy in starts:
        copy.wait()
    for step in range(3, half + 2):
        for way in range(2):
            hop(way, step).wait_send()


def mlp(grid, rows, cot, chunks, ffw, early):
    chips = grid.chips
    count, width = rows.shape
    block, n = chunks[0].shape
    half = chips // 2
    near = pl.BlockSpec(memory_space=pltpu.VMEM)
    far = pl.BlockSpec(memory_space=pltpu.HBM)
    dma = pltpu.SemaphoreType.DMA
    inner = jax.ShapeDtypeStruct((count, ffw), BF)
    return pl.pallas_call(
        partial(mlp_kernel, chips, ffw, early),
        out_shape=[
            inner,
            jax.ShapeDtypeStruct((count, early), BF),
            jax.ShapeDtypeStruct((count, ffw - early), BF),
            inner,
            jax.ShapeDtypeStruct((count, width), F32),
            jax.ShapeDtypeStruct((count, width), BF),
            jax.ShapeDtypeStruct((2, block // 2, ffw + early), BF),
        ],
        in_specs=[far] * 7,
        out_specs=[far] * 6 + [near],
        scratch_shapes=[
            pltpu.VMEM((count, ffw), BF),
            pltpu.VMEM((count, early), BF),
            pltpu.VMEM((count, ffw - early), BF),
            pltpu.VMEM((count, ffw), BF),
            pltpu.VMEM((count, width), F32),
            pltpu.VMEM((count, width), BF),
            dma((10,)),
            pltpu.VMEM(rows.shape, BF),
            pltpu.VMEM(rows.shape, BF),
            dma((2,)),
            pltpu.VMEM((chips * block, n), BF),
            pltpu.VMEM((count, n), F32),
            pltpu.VMEM((2, block // 2, ffw + early), BF),
            dma((5,)),
            dma((2, half - 1)),
            dma((2, half - 1)),
            dma((2, 2)),
            dma((2, 2)),
        ],
        compiler_params=pltpu.CompilerParams(
            collective_id=4, has_side_effects=True, vmem_limit_bytes=62 << 20
        ),
        name="mlp",
    )(rows, cot, *chunks)


def collect_kernel(chips, steps, groups, late_parts, fields, side_of, counts, *refs):
    n_left, n_right, n_out, n_side = counts
    refs = list(refs)

    def take(count):
        taken, refs[:] = refs[:count], refs[count:]
        return taken

    far = take(n_left + n_right)
    late_out, late_left = take(2)
    weights = take(n_side)
    ahead_far, *far_tokens = take(4)
    gain, mlp_grad, rate_weights = take(3)
    grad_cq, grad_ck, grad_cv, grad_rate, grad_gain = take(5)
    outs = take(n_out)
    rates_out, out_tokens, grad_tokens, *small_outs = take(5)
    begin, arrived, late_in, final, back, got_core, sent_half, got_half, *small_ins = take(10)
    buffers = take(n_side)
    near, near_tokens = take(n_left + n_right), take(4)
    lefts, rights = near[:n_left], near[n_left:]
    ahead, stream, middle, grad_middle = near_tokens
    (far_sem,) = take(1)
    send_ring, recv_ring, own_sem, send_core, recv_core, send_late, recv_late = take(7)
    send_first, recv_first, send_second, recv_second, send_small, recv_small, weight_sem, free = take(8)
    rate_begin, rate_arrived, rate_final, send_rate, recv_rate, rate_sems = take(6)
    me, member = lax.axis_index("dp"), lax.axis_index("tensor")
    core, chip = me % 2, me // 2
    spot = ring_spot(chip, chips)
    ways = (
        (2 * ring_chip((spot + 1) % chips, chips) + core, member),
        (2 * ring_chip((spot + chips - 1) % chips, chips) + core, member),
    )
    peer = (2 * chip + 1 - core, member)
    across = (me, 1 - member)
    partners = [across] + [
        (me + (1 << k) - 2 * (1 << k) * ((me // (1 << k)) % 2), member) for k in range(steps - 1)
    ]
    signal_all(list(ways) + partners)

    half = chips // 2
    width = lefts[0].shape[1] // chips
    mid = width // 2
    starts = []
    at = 0
    for _, right in groups:
        starts.append(at)
        at += rights[right].shape[1]

    def columns(group):
        return pl.ds(starts[group], rights[groups[group][1]].shape[1])

    def piece(group, place, lo=0, hi=width):
        left, right = lefts[groups[group][0]], rights[groups[group][1]]
        at = (place % chips) * width
        return lax.dot_general(
            left[:, at + lo : at + hi], right[...], (COLS_ROWS, ((), ())), preferred_element_type=F32
        )

    def rows_of(way):
        return pl.ds(mid * way, mid)

    def hop(way, step, group):
        if step:
            source, target = arrived.at[way, step - 1], arrived.at[way, step % (half - 1)]
            source, target = source.at[:, columns(group)], target.at[:, columns(group)]
        else:
            source = begin.at[way, :, columns(group)]
            target = arrived.at[way, 0, rows_of(way), columns(group)]
        sems = (way, step, group)
        return send(source, target, send_ring.at[sems], recv_ring.at[sems], ways[way])

    rate_rows = rate_begin.shape[1]

    def rate_piece(place):
        at = (place % chips) * width
        value = lax.dot_general(
            rights[-1][:, 0:rate_rows], lefts[-1][:, at : at + width], (COLS_ROWS, ((), ())), preferred_element_type=F32
        )
        return value[:, 0:mid], value[:, mid:width]

    def rate_hop(way, step):
        source = rate_arrived.at[way, step - 1] if step else rate_begin.at[way]
        target = rate_arrived.at[way, step % (half - 1)] if step else rate_arrived.at[way, 0, way]
        sems = (way, step)
        return send(source, target, send_rate.at[sems], recv_rate.at[sems], ways[way])

    def rate_step(step, place):
        for way in range(2):
            rate_hop(way, step).wait_recv()
            for c, value in enumerate(rate_piece(place if way == 0 else -place)):
                if step or c == way:
                    value = value + rate_arrived[way, step, c].astype(F32)
                rate_arrived[way, step, c] = value.astype(BF)
            rate_hop(way, step + 1).start()

    late = [send(late_out.at[way], late_in.at[way], send_late.at[way], recv_late.at[way], ways[way]) for way in range(2)]
    sides = (back, ahead)
    first = [
        send(value.at[1], got_core.at[i], send_first.at[i], recv_first.at[i], peer)
        for i, value in enumerate((back, ahead_far))
    ]
    second = [
        send(sent_half.at[i], got_half.at[i], send_second.at[i], recv_second.at[i], across) for i in range(2)
    ]

    def fold_small(step):
        copies = []
        for i, (out, arrivals) in enumerate(zip(small_outs, small_ins)):
            source = arrivals.at[steps + step - 1] if step else out
            sems = (step, i)
            copies.append(send(source, arrivals.at[step], send_small.at[sems], recv_small.at[sems], partners[step]))
        return copies

    def put(ref, value):
        if width % 128:
            ref[...] = value
            return
        for place in range(chips):
            at = pl.multiple_of(ring_chip((spot + place) % chips, chips) * width, 128)
            ref[:, pl.ds(at, width)] = value[:, place * width : (place + 1) * width]

    def fetch(place):
        return [
            pltpu.make_async_copy(
                weight.at[pl.ds(place * width, width), pl.ds(at, buffer.shape[2])],
                buffer.at[place % 2],
                weight_sem.at[number, place % 2],
            )
            for number, (weight, (at, _), buffer) in enumerate(zip(weights, side_of, buffers))
        ]

    def side_work():
        for place in range(chips):
            if place + 1 < chips:
                for copy in fetch(place + 1):
                    copy.start()
            for copy in fetch(place):
                copy.wait()
            total = jnp.dot(
                rights[-1][:, 0:rate_rows],
                rate_weights[:, place * width : (place + 1) * width],
                preferred_element_type=F32,
            )
            for (_, right), buffer in zip(side_of, buffers):
                total = total + lax.dot_general(
                    rights[right][...],
                    buffer[place % 2],
                    (ROWS_ROWS, ((), ())),
                    preferred_element_type=F32,
                )
            back[:, :, :, place * width : (place + 1) * width] = (
                total.astype(BF).reshape(2, 2, middle.shape[0], width)
            )
            yield
        for copy in first:
            copy.start()
        yield
        ready(*range(n_left + n_right, n_left + n_right + 4))
        for i in range(2):
            first[i].wait_recv()
            total = sides[i][0, 1 - member].astype(F32) + got_core[i, 1 - member].astype(F32)
            sent_half[i] = total.astype(BF)
            second[i].start()
        yield
        total = []
        for i in range(2):
            second[i].wait_recv()
            value = sides[i][0, member].astype(F32) + got_core[i, member].astype(F32)
            total.append(value + got_half[i].astype(F32))
        put(out_tokens, middle[...] + total[1])
        value = stream[...].astype(F32)
        scale = lax.rsqrt(jnp.mean(value * value, axis=1, keepdims=True) + 1e-06)
        value = value * scale
        gained = jnp.sum(total[0] * value, axis=0, keepdims=True)
        grad = total[0] * gain[...]
        grad = scale * (grad - value * jnp.mean(grad * value, axis=1, keepdims=True))
        put(grad_tokens, grad_middle[...] + grad)
        small_out, wide = small_outs
        small_out[...] = jnp.zeros_like(small_out)
        wide[...] = jnp.zeros_like(wide)
        quarter = 2 * member + core
        taps, keyw = grad_cq.shape
        valw = grad_cv.shape[1]
        after = max(8 * keyw, 4 * valw)

        def part(at, size):
            return pl.ds(pl.multiple_of(at + quarter * size, 128), size)

        wide[0:taps, part(0, keyw)] = grad_cq[...]
        wide[0:taps, part(4 * keyw, keyw)] = grad_ck[...]
        wide[taps : 2 * taps, part(0, valw)] = grad_cv[...]
        wide[0:1, after : after + grad_gain.shape[1]] = grad_gain[...]
        wide[0:2, part(after + grad_gain.shape[1], grad_rate.shape[1])] = grad_rate[...]
        lanes = min(width, 128)
        each = width // lanes
        for i, vector in enumerate((gained, mlp_grad[...])):
            for place in range(chips):
                row = (i * chips + ring_chip((spot + place) % chips, chips)) * each
                for k in range(each):
                    at = place * width + k * lanes
                    small_out[pl.ds(row + k, 1), 0:lanes] = vector[:, at : at + lanes]
        for copy in fold_small(0):
            copy.start()
        yield
        for step in range(steps):
            for copy in fold_small(step):
                copy.wait_recv()
            for out, arrivals in zip(small_outs, small_ins):
                before = arrivals.at[steps + step - 1] if step else out
                arrivals[steps + step] = before[...] + arrivals[step]
            if step + 1 < steps:
                for copy in fold_small(step + 1):
                    copy.start()
            yield

    work = side_work()
    ready = staged([*far, ahead_far.at[pl.ds(0, 1)], *far_tokens], near + near_tokens, far_sem)
    for copy in late + fetch(0):
        copy.start()
    for group in range(len(groups)):
        ready(groups[group][0], n_left + groups[group][1])
        for way in range(2):
            begin[way, :, columns(group)] = piece(group, half, mid * way, mid * way + mid).astype(BF)
            hop(way, 0, group).start()
    ready(*range(n_left + n_right))
    for way in range(2):
        rate_begin[way] = rate_piece(half)[way].astype(BF)
        rate_hop(way, 0).start()
    for step in range(half - 1):
        place = half - 1 - step
        for group in range(len(groups)):
            next(work, None)
            next(work, None)
            for way in range(2):
                hop(way, step, group).wait_recv()
                value = piece(group, place if way == 0 else -place)
                if step:
                    value = value + arrived[way, step, :, columns(group)].astype(F32)
                    arrived[way, step, :, columns(group)] = value.astype(BF)
                else:
                    lo = mid * way
                    here = value[lo : lo + mid] + arrived[way, 0, rows_of(way), columns(group)].astype(F32)
                    arrived[way, 0, rows_of(way), columns(group)] = here.astype(BF)
                    arrived[way, 0, rows_of(1 - way), columns(group)] = value[
                        mid - lo : width - lo
                    ].astype(BF)
                if step == half - 2 and group == 0:
                    pl.semaphore_wait(free.at[way], 1)
                hop(way, step + 1, group).start()
            if group == 0:
                rate_step(step, place)
        if step == min(1, half - 3):
            for way in range(2):
                rate_hop(way, 1).wait_send()
                for group in range(len(groups)):
                    hop(way, 1, group).wait_send()
                pl.semaphore_signal(
                    free.at[way], inc=1, device_id=ways[1 - way], device_id_type=pl.DeviceIdType.MESH
                )
    for _ in work:
        pass
    for step in range(steps):
        for copy in fold_small(step):
            copy.wait_send()
    for out, arrivals in zip(small_outs, small_ins):
        out[...] = arrivals[2 * steps - 1]

    rows = width // 2
    finals, used = [], {}
    values = rate_piece(0)
    for way in range(2):
        rate_hop(way, half - 1).wait_recv()
        values = [value + rate_arrived[way, 0, c].astype(F32) for c, value in enumerate(values)]
    for c in range(2):
        rate_final[c] = values[c]
    rate_own = pltpu.make_async_copy(rate_final.at[core], rates_out.at[core], rate_sems.at[0])
    rate_far = send(rate_final.at[1 - core], rates_out.at[core], rate_sems.at[1], rate_sems.at[2], peer)
    rate_own.start()
    rate_far.start()
    for group in [len(groups)] + list(range(len(groups))):
        slot = group % 2
        for copy in used.get(slot, ()):
            copy()
        if group == len(groups):
            value = []
            for left, right in late_parts:
                left = late_left if left is None else lefts[left]
                value.append(
                    lax.dot_general(
                        left[:, 0:width],
                        rights[right][...],
                        (COLS_ROWS, ((), ())),
                        preferred_element_type=F32,
                    )
                )
            value = jnp.concatenate(value, axis=1)
        else:
            value = piece(group, 0)
        for way in range(2):
            if group == len(groups):
                late[way].wait_recv()
                value = value + late_in[way].astype(F32)
            else:
                hop(way, half - 1, group).wait_recv()
                value = value + arrived[way, 0, :, columns(group)].astype(F32)
        final[slot, :, 0 : value.shape[1]] = value
        used[slot] = []
        for number, (owner, at, out, to, whole, size) in enumerate(fields):
            if owner == group:
                own = pl.ds(pl.multiple_of(core * rows, rows), rows)
                theirs = pl.ds(pl.multiple_of((1 - core) * rows, rows), rows)
                target = outs[out].at[:, pl.ds(pl.multiple_of(core * whole + to, 128), size)]
                copy = pltpu.make_async_copy(final.at[slot, own, pl.ds(at, size)], target, own_sem.at[number])
                far = send(
                    final.at[slot, theirs, pl.ds(at, size)],
                    target,
                    send_core.at[number],
                    recv_core.at[number],
                    peer,
                )
                copy.start()
                far.start()
                finals.append(far)
                used[slot] += [copy.wait, far.wait_send]
    for slot in used:
        for copy in used[slot]:
            copy()
    for far in finals:
        far.wait_recv()
    rate_own.wait()
    rate_far.wait()
    for way in range(2):
        for step in range(half):
            if step != 1:
                rate_hop(way, step).wait_send()
    for copy in first + second + late:
        copy.wait_send()
    for step in range(half):
        for group in range(len(groups)):
            for way in range(2):
                if step != 1:
                    hop(way, step, group).wait_send()


def collect(grid, lefts, rights, groups, late, fields, sides, ahead, tokens_in, small, small_shapes, rate_weights):
    chips = grid.chips
    rows, width = tokens_in[2].shape
    steps = grid.devices.bit_length()
    n = sum(rights[right].shape[1] for _, right in groups)
    widest = max([rights[right].shape[1] for _, right in groups] + [late[0].shape[2]])
    block = width // chips
    half = chips // 2
    *late, late_parts = late
    weights = [weight for weight, _, _ in sides]
    side_of = [(at, right) for _, at, right in sides]
    stream, gain, middle, grad_middle, mlp_grad = tokens_in
    tokens_in = [ahead.reshape(2, 2, rows, width), stream, middle, grad_middle]
    inputs = [*lefts, *rights, *late, *weights, *tokens_in, gain, mlp_grad, rate_weights, *small]
    wholes = {}
    for _, _, out, _, whole in fields:
        wholes[out] = whole
    outs = [jax.ShapeDtypeStruct((block // 2, 2 * wholes[out]), F32) for out in range(len(wholes))]
    ends = [sum(rights[right].shape[1] for _, right in late_parts)]
    ends = [rights[right].shape[1] for _, right in groups] + ends
    sized = []
    for i, (group, at, out, to, whole) in enumerate(fields):
        starts = [other[1] for other in fields if other[0] == group and other[1] > at]
        sized.append((group, at, out, to, whole, min(starts + [ends[group]]) - at))
    fields = sized
    tokens = jax.ShapeDtypeStruct((rows, width), F32)
    near = pl.BlockSpec(memory_space=pltpu.VMEM)
    far = pl.BlockSpec(memory_space=pltpu.HBM)
    dma = pltpu.SemaphoreType.DMA
    ring = (2, half, len(groups))
    counts = (len(lefts), len(rights), len(outs), len(sides))
    held = [value.shape for value in (*lefts, *rights)]
    rate = (rate_weights.shape[0], block // 2)
    rates = jax.ShapeDtypeStruct((2,) + rate, F32)
    return pl.pallas_call(
        partial(collect_kernel, chips, steps, groups, late_parts, fields, side_of, counts),
        out_shape=outs + [rates, tokens, tokens] + [jax.ShapeDtypeStruct(shape, F32) for shape in small_shapes],
        in_specs=[far] * (len(held) + 1) + [near] + [far] * (len(sides) + 4) + [near] * 8,
        out_specs=[far] * (len(outs) + 1) + [near] * 4,
        scratch_shapes=[
            pltpu.VMEM((2, block // 2, n), BF),
            pltpu.VMEM((2, half - 1, block, n), BF),
            pltpu.VMEM(late[0].shape, BF),
            pltpu.VMEM((2, block, widest), F32),
            pltpu.VMEM((2, 2, rows, width), BF),
            pltpu.VMEM((2, 2, rows, width), BF),
            pltpu.VMEM((2, rows, width), BF),
            pltpu.VMEM((2, rows, width), BF),
            *[pltpu.VMEM((2 * steps,) + shape, F32) for shape in small_shapes],
        ]
        + [pltpu.VMEM((2, block, rights[right].shape[1]), BF) for _, right in side_of]
        + [pltpu.VMEM(shape, BF) for shape in held]
        + [
            pltpu.VMEM((1, 2, rows, width), BF),
            pltpu.VMEM((rows, width), BF),
            pltpu.VMEM((rows, width), F32),
            pltpu.VMEM((rows, width), F32),
            dma((len(held) + 4,)),
        ]
        + [dma(ring), dma(ring)]
        + [dma((len(fields),))] * 3
        + [dma((2,))] * 6
        + [dma((steps, 2))] * 2
        + [dma((len(sides), 2)), pltpu.SemaphoreType.REGULAR((2,))]
        + [
            pltpu.VMEM((2,) + rate, BF),
            pltpu.VMEM((2, half - 1, 2) + rate, BF),
            pltpu.VMEM((2,) + rate, F32),
            dma((2, half)),
            dma((2, half)),
            dma((3,)),
        ],
        compiler_params=pltpu.CompilerParams(
            collective_id=3, has_side_effects=True, vmem_limit_bytes=63 << 20
        ),
        name="collect",
    )(*inputs)


def finish_kernel(chips, heads, counts, *refs):
    moved, turned = counts
    refs = list(refs)

    def take(count):
        taken, refs[:] = refs[:count], refs[count:]
        return taken

    sources, turning, (rates, gains, wide) = take(moved), take(turned), take(3)
    targets, turned_out = take(moved), take(turned)
    beta, decay, norm_gain, mlp_gain, cq, ck, cv, log, bias, out_gain = take(10)
    held = take(moved)
    sem_in, sem_out = take(2)
    ready = staged(sources, held, sem_in)
    copies = []
    for i, (source, target) in enumerate(zip(held, targets)):
        if len(target.shape) > len(source.shape):
            target = target.at[0]
        ready(i)
        copies.append(pltpu.make_async_copy(source, target, sem_out.at[i]))
        copies[-1].start()
    for source, target in zip(turning, turned_out):
        target[...] = source[...].T
    for core in range(2):
        to = slice(core * heads, (core + 1) * heads)
        beta[to] = rates[core, 0:heads]
        decay[to] = rates[core, heads : 2 * heads]
    lanes = min(norm_gain.shape[1] // chips, 128)
    count = norm_gain.shape[1] // lanes
    for i, vector in enumerate((norm_gain, mlp_gain)):
        for row in range(count):
            vector[:, row * lanes : (row + 1) * lanes] = gains[i * count + row : i * count + row + 1, 0:lanes]
    taps, keyw = cq.shape
    valw = cv.shape[1]
    after = max(2 * keyw, valw)
    cq[...] = wide[0:taps, 0:keyw]
    ck[...] = wide[0:taps, keyw : 2 * keyw]
    cv[...] = wide[taps : 2 * taps, 0:valw]
    out_gain[...] = wide[0:1, after : after + out_gain.shape[1]]
    after += out_gain.shape[1]
    small = (wide.shape[1] - after) // 4
    for quarter in range(4):
        at = after + quarter * small + heads
        to = slice(quarter * heads, (quarter + 1) * heads)
        log[:, to] = wide[0:1, at : at + heads]
        bias[:, to] = wide[1:2, at : at + heads]
    for copy in copies:
        copy.wait()


def finish(grid, heads, moved, turning, rates, gains, wide, vectors, convs):
    near = pl.BlockSpec(memory_space=pltpu.VMEM)
    far = pl.BlockSpec(memory_space=pltpu.HBM)
    out_shape = [jax.ShapeDtypeStruct(shape, F32) for _, shape in moved]
    out_shape += [jax.ShapeDtypeStruct(value.shape[::-1], F32) for value in turning]
    rate = jax.ShapeDtypeStruct((2 * heads, rates.shape[2]), F32)
    vectors = [jax.ShapeDtypeStruct((1, size), F32) for size in vectors]
    convs = [jax.ShapeDtypeStruct(value.shape, F32) for value in convs]
    small = [rate, rate, *vectors[:2], *convs, *vectors[2:]]
    return pl.pallas_call(
        partial(finish_kernel, grid.chips, heads, (len(moved), len(turning))),
        out_shape=out_shape + small,
        in_specs=[far] * len(moved) + [near] * (len(turning) + 3),
        out_specs=[far] * len(moved) + [near] * (len(turning) + len(small)),
        scratch_shapes=[pltpu.VMEM(value.shape, F32) for value, _ in moved]
        + [pltpu.SemaphoreType.DMA((len(moved),))] * 2,
        compiler_params=pltpu.CompilerParams(vmem_limit_bytes=63 << 20),
        name="finish",
    )(*[value for value, _ in moved], *turning, rates, gains, wide)


def whole_rows(stack):
    return stack.reshape(-1, stack.shape[-1])


def per_device(
    tokens,
    segment_ids,
    norm_gain,
    w_query,
    w_key,
    w_value,
    w_outgate,
    w_beta,
    w_decay,
    conv_query,
    conv_key,
    conv_value,
    decay_log,
    decay_bias,
    out_gain,
    w_output,
    mlp_gain,
    w_gate,
    w_up,
    w_down,
    cotangent,
    *,
    devices,
):
    grid = Grid(devices)
    heads = w_beta.shape[1] // 2
    keyw = w_query.shape[1] // 2
    valw = w_value.shape[1] // 2
    ffw = w_gate.shape[1] // 2
    small = -(-2 * heads // 128) * 128

    rate_rows = -(-2 * heads // 16) * 16
    groups = [[w_query, w_key], [w_value, w_outgate], [(w_output,)], rate_rows, [w_gate, w_up, (w_down,)]]
    shown = (tokens[0], cotangent[0], norm_gain[None], mlp_gain[None])
    if norm_gain.shape[0] // grid.chips % 128:
        shown = [grid.into(value) for value in shown]
    *gathered, stream, cot_own, norm_row, mlp_row, rows_mix, cot_rows = spread(
        grid, groups, 4, *shown[:2], shown[2:], (w_beta.T, w_decay.T)
    )
    wqk, wvg, wout = [whole_rows(stack) for stack in gathered[:3]]
    rows_mix, cot_rows = [rows.reshape(-1, rows.shape[-1]) for rows in (rows_mix, cot_rows)]
    segments = jnp.concatenate([segment_ids, grid.over_core(segment_ids)], axis=0)

    conv_parts = [
        part_of(conv_query, grid.quarter, keyw, 1),
        part_of(conv_key, grid.quarter, keyw, 1),
        part_of(conv_value, grid.quarter, valw, 1),
        part_of(decay_log, grid.quarter, heads, 0),
        part_of(decay_bias, grid.quarter, heads, 0),
    ]
    rate_weights = gathered[3].transpose(2, 0, 1, 3).reshape(rate_rows, -1)
    pre_qk = dot(rows_mix, wqk)
    pre_rates = jnp.pad(cols_product(rows_mix, rate_weights), ((0, 0), (0, small - rate_rows)))
    pre_vg = dot(rows_mix, wvg)
    lanes = [jnp.pad(part[None], ((0, 0), (0, small - heads))) for part in conv_parts[3:]]
    mixer_in = (pre_qk, pre_rates, pre_vg, segments[:, :, None], segments[:, None, :], *conv_parts[:3], *lanes, out_gain[None])
    heads_out, kept = mixer(heads, mixer_in)
    rows_mlp, middle = middle_rows(cols_product(heads_out, wout), stream, mlp_row)
    chunk = gathered[4]
    chunks = [chunk, grid.shift(chunk, 1), grid.shift(chunk, -1)]
    pair = tied((chunks[1], chunks[2]), heads_out)
    chunks += [grid.shift(pair[0], 1), grid.shift(pair[1], -1)]
    early = ffw * 1024 // 1408 // 128 * 128
    hidden, *gate_parts, grad_upper, back_part, ahead, begun = mlp(grid, rows_mlp, cot_rows, chunks, ffw, early)
    grad_mixed, grad_middle, grad_mlp_gain, late, grad_qk, grad_rates, grad_vg, *core_grads = turn(
        grid,
        heads,
        early,
        back_part,
        cot_own,
        middle,
        mlp_row,
        wout,
        cot_rows,
        rows_mlp,
        hidden,
        gate_parts[0],
        begun,
        mixer_in,
        kept,
    )

    width = norm_gain.shape[0]
    gain_rows = width // min(width // grid.chips, 128)
    wide = max(8 * keyw, 4 * valw) + out_gain.shape[0] + 4 * small
    *weight_grads, rates, out_tokens, grad_tokens, gains, wide = collect(
        grid,
        [rows_mlp, grad_mixed, rows_mix],
        [gate_parts[1], grad_upper, grad_vg, heads_out, grad_qk, hidden, gate_parts[0], grad_rates],
        [(0, 1), (2, 2), (1, 3), (2, 4), (0, 0)],
        [late, cot_rows[:, : cot_rows.shape[1] // grid.chips], [(None, 5), (0, 6)]],
        [
            (4, 0, 0, early, ffw),
            (5, ffw, 0, 0, ffw),
            (0, 0, 1, 0, ffw),
            (1, 0, 2, 0, valw),
            (1, valw, 3, 0, valw),
            (2, 0, 4, 0, valw),
            (3, 0, 5, 0, keyw),
            (3, keyw, 6, 0, keyw),
            (5, 0, 7, 0, ffw),
        ],
        [(wvg, 0, 2), (wqk, 0, 4)],
        ahead,
        [stream, norm_row, middle, grad_middle, grad_mlp_gain],
        core_grads,
        [(2 * gain_rows, 128), (2 * conv_query.shape[0], wide)],
        rate_weights,
    )
    whole_gate, whole_up, whole_value, whole_outgate, whole_out, whole_query, whole_key, whole_down = weight_grads
    if out_tokens.shape[1] // grid.chips % 128:
        out_tokens, grad_tokens = grid.out_of(out_tokens), grid.out_of(grad_tokens)
    moved = [out_tokens, grad_tokens, whole_query, whole_key, whole_value, whole_outgate, whole_gate, whole_up]
    shapes = [(1,) + value.shape if i < 2 else value.shape for i, value in enumerate(moved)]
    sizes = [width, width, decay_log.shape[0], decay_bias.shape[0], out_gain.shape[0]]
    *moved, whole_out, whole_down, whole_beta, whole_decay, norm_row, mlp_row, cq, ck, cv, log, bias, gain = finish(
        grid,
        heads,
        list(zip(moved, shapes)),
        [whole_out, whole_down],
        rates,
        gains,
        wide,
        sizes,
        [conv_query, conv_key, conv_value],
    )
    out_tokens, grad_tokens, *moved = moved
    whole_query, whole_key, whole_value, whole_outgate, whole_gate, whole_up = moved
    return (
        out_tokens,
        grad_tokens,
        norm_row[0],
        whole_query,
        whole_key,
        whole_value,
        whole_outgate,
        whole_beta.T,
        whole_decay.T,
        cq,
        ck,
        cv,
        log[0],
        bias[0],
        gain[0],
        whole_out,
        mlp_row[0],
        whole_gate,
        whole_up,
        whole_down,
    )


def solution(mesh):
    rows = P("dp", "tensor")
    cols = P("tensor", "dp")
    tokens = P("dp", "tensor", None)
    placed = (tokens, P("dp", None), P()) + (rows,) * 6 + (P(),) * 6
    placed = placed + (cols, P(), rows, rows, cols, tokens)
    given = (tokens, tokens, P()) + (rows,) * 6 + (P(),) * 6 + (cols, P(), rows, rows, cols)
    return jax.shard_map(
        partial(per_device, devices=mesh.shape["dp"]),
        mesh=mesh,
        in_specs=placed,
        out_specs=given,
        check_vma=False,
    )
```

```python
from functools import partial
import math

import jax
import jax.numpy as jnp
from jax import lax
from jax.experimental import pallas as pl
from jax.experimental.pallas import tpu as pltpu
from jax.sharding import PartitionSpec as P

HIGH = lax.Precision.HIGH
HIGHEST = lax.Precision.HIGHEST
BF = jnp.bfloat16
F32 = jnp.float32


def scale_rows(values, factor):
    return values * lax.rsqrt(jnp.mean(values * values, axis=-1, keepdims=True) + 1e-06) * factor


def split3(value):
    high = value.astype(BF)
    return high, (value - high.astype(F32)).astype(BF)


def product(left, right, dims):
    dims = (dims, ((), ()))
    total = lax.dot_general(left[0], right[0], dims, preferred_element_type=F32)
    total = total + lax.dot_general(left[0], right[1], dims, preferred_element_type=F32)
    return total + lax.dot_general(left[1], right[0], dims, preferred_element_type=F32)


ROWS_COLS = ((1,), (0,))
ROWS_ROWS = ((1,), (1,))
COLS_ROWS = ((0,), (0,))


def exact_sum(mask, value, dims):
    high, low = split3(value)
    last = (value - high.astype(F32) - low.astype(F32)).astype(BF)
    dims = (dims, ((), ()))
    total = lax.dot_general(mask, last, dims, preferred_element_type=F32)
    total = total + lax.dot_general(mask, low, dims, preferred_element_type=F32)
    return total + lax.dot_general(mask, high, dims, preferred_element_type=F32)


def conv_parts(values, taps, keeping):
    moved = [values] + [pltpu.roll(values, j, 0) * keeping[j] for j in range(1, 4)]
    total = moved[0] * taps[0:1]
    for j in range(1, 4):
        total = total + moved[j] * taps[j : j + 1]
    return moved, total


def conv_back(grad, moved, taps, keeping):
    rows = grad.shape[0]
    total = grad * taps[0:1]
    for j in range(1, 4):
        total = total + pltpu.roll(grad * keeping[j], rows - j, 0) * taps[j : j + 1]
    parts = [jnp.sum(grad * moved[j], axis=0, keepdims=True) for j in range(4)]
    return total, jnp.concatenate(parts, axis=0)


def silu_back(total, gate):
    return gate * (1.0 + total * (1.0 - gate))


def softplus(value):
    return jnp.maximum(value, 0.0) + jnp.log1p(jnp.exp(-jnp.abs(value)))


def block_masks(seg_col, seg_row):
    size = seg_col.shape[0]
    row = lax.broadcasted_iota(jnp.int32, (size, size), 0)
    col = lax.broadcasted_iota(jnp.int32, (size, size), 1)
    masking = ((seg_col == seg_row) & (col <= row)).astype(F32)
    spot = lax.broadcasted_iota(jnp.int32, (size, 1), 0)
    keeping = [None]
    for j in range(1, 4):
        keeping.append(((pltpu.roll(seg_col, j, 0) == seg_col) & (spot >= j)).astype(F32))
    return row, col, masking, keeping


def head_rates(small, log, bias, masking, heads):
    decay_in = pltpu.roll(small, small.shape[1] - heads, 1) + bias
    factor = -jnp.exp(log)
    rates = factor * softplus(decay_in)
    betas = jax.nn.sigmoid(small)
    summed = exact_sum(masking.astype(BF), rates, ROWS_COLS)
    return decay_in, factor, rates, betas, summed


def invert(mixing, row, col):
    size = mixing.shape[0]
    result = jnp.where(row == col, 1.0, 0.0) - jnp.where((row >> 1) == (col >> 1), mixing, 0.0)
    level = 1
    while (1 << level) < size:
        picked = ((row >> (level + 1)) == (col >> (level + 1))) & ((row >> level) != (col >> level))
        part = split3(jnp.where(picked, mixing, 0.0))
        halves = split3(result)
        step = product(halves, part, ROWS_COLS)
        result = result - product(split3(step), halves, ROWS_COLS)
        level += 1
    return result


def unit(values):
    return lax.rsqrt(jnp.sum(values * values, axis=1, keepdims=True) + 1e-06)


def mixer_kernel(heads, qk, rates_in, vg, seg_col, seg_row, cq, ck, cv, log, bias, gain, *outs):
    heads_out, inverses, all_errors, all_kk, all_qk, all_raw = outs
    keyw, valw = cq.shape[1] // heads, cv.shape[1] // heads
    row, col, masking, keeping = block_masks(seg_col[0], seg_row[0])
    small = rates_in[...]
    _, _, _, betas, summed = head_rates(small, log[...], bias[...], masking, heads)
    betas_t, summed_t = betas.T, summed.T
    strict = (col < row).astype(F32)
    for h in range(heads):
        at = pl.ds(h * keyw, keyw)
        query = jax.nn.silu(conv_parts(qk[:, at], cq[:, at], keeping)[1])
        query = query * (unit(query) * (1.0 / math.sqrt(keyw)))
        key = jax.nn.silu(
            conv_parts(qk[:, pl.ds((heads + h) * keyw, keyw)], ck[:, at], keeping)[1]
        )
        key = key * unit(key)
        at = pl.ds(h * valw, valw)
        value = jax.nn.silu(conv_parts(vg[:, at], cv[:, at], keeping)[1])
        spread = summed[:, h : h + 1] - summed_t[h : h + 1]
        decays = jnp.exp(spread * masking) * masking * betas_t[h : h + 1]
        keys = split3(key)
        key_key = product(keys, keys, ROWS_ROWS)
        query_key = product(split3(query), keys, ROWS_ROWS)
        inverse = invert(decays * key_key * strict, row, col)
        errors = product(split3(inverse), split3(value), ROWS_COLS)
        raw = product(split3(decays * query_key), split3(errors), ROWS_COLS)
        inverses[0, h] = inverse
        all_errors[0, h] = errors
        all_kk[0, h] = key_key
        all_qk[0, h] = query_key
        all_raw[:, at] = raw
        scaled = raw * lax.rsqrt(jnp.mean(raw * raw, axis=1, keepdims=True) + 1e-05) * gain[...]
        gate = vg[:, pl.ds((heads + h) * valw, valw)]
        heads_out[:, at] = (scaled * jax.nn.silu(gate)).astype(BF)


def mixer_back(heads, grad, inputs, kept, results):
    qk, rates_in, vg, seg_col, seg_row, cq, ck, cv, log, bias, gain = inputs
    inverses, all_errors, all_kk, all_qk, all_raw = kept
    grad_qk, grad_small_out, grad_vg, grad_cq, grad_ck, grad_cv, grad_rate, grad_gain = results
    keyw, valw = cq.shape[1] // heads, cv.shape[1] // heads
    size = qk.shape[0]
    row, col, masking, keeping = block_masks(seg_col[0], seg_row[0])
    small = rates_in[...]
    decay_in, factor, rates, betas, summed = head_rates(small, log[...], bias[...], masking, heads)
    betas_t, summed_t = betas.T, summed.T
    strict = (col < row).astype(F32)
    lanes = lax.broadcasted_iota(jnp.int32, (1, small.shape[1]), 1)
    spots = lax.broadcasted_iota(jnp.int32, (small.shape[1], 1), 0)
    grad_summed = jnp.zeros_like(small)
    from_cols = jnp.zeros((small.shape[1], size), F32)
    for h in range(heads):
        at = pl.ds(h * valw, valw)
        raw, gate_in = all_raw[:, at], vg[:, pl.ds((heads + h) * valw, valw)]
        gate = jax.nn.sigmoid(gate_in)
        scale = lax.rsqrt(jnp.mean(raw * raw, axis=1, keepdims=True) + 1e-05)
        above = grad[:, at]
        grad_vg[:, pl.ds((heads + h) * valw, valw)] = (
            above * (raw * scale * gain[...]) * silu_back(gate_in, gate)
        ).astype(BF)
        above = above * (gate_in * gate)
        grad_gain[...] += jnp.sum(above * raw * scale, axis=0, keepdims=True)
        above = above * gain[...]
        grad_raw = scale * (above - raw * (scale * scale * jnp.mean(above * raw, axis=1, keepdims=True)))

        spread = summed[:, h : h + 1] - summed_t[h : h + 1]
        plain = jnp.exp(spread * masking) * masking
        decays = plain * betas_t[h : h + 1]
        key_key, query_key = all_kk[0, h] * strict, all_qk[0, h]
        grad_raws, errors = split3(grad_raw), split3(all_errors[0, h])
        grad_reading = product(grad_raws, errors, ROWS_ROWS)
        grad_errors = product(split3(decays * query_key), grad_raws, COLS_ROWS)
        grad_value = product(split3(inverses[0, h]), split3(grad_errors), COLS_ROWS)
        grad_mixing = -product(split3(grad_value), errors, ROWS_ROWS)
        both = (grad_mixing * key_key + grad_reading * query_key) * plain
        grad_beta = jnp.sum(both, axis=0, keepdims=True)
        both = both * betas_t[h : h + 1]
        from_rows = jnp.sum(both, axis=1, keepdims=True)
        grad_summed = grad_summed + jnp.where(lanes == heads + h, from_rows, 0.0)
        from_cols = from_cols + jnp.where(spots == h, grad_beta, 0.0)
        from_cols = from_cols - jnp.where(spots == heads + h, jnp.sum(both, axis=0, keepdims=True), 0.0)

        at = pl.ds(h * keyw, keyw)
        query_moved, query_total = conv_parts(qk[:, at], cq[:, at], keeping)
        query_gate = jax.nn.sigmoid(query_total)
        query = query_total * query_gate
        query_scale = unit(query)
        query = query * query_scale
        key_at = pl.ds((heads + h) * keyw, keyw)
        key_moved, key_total = conv_parts(qk[:, key_at], ck[:, at], keeping)
        key_gate = jax.nn.sigmoid(key_total)
        key = key_total * key_gate
        key_scale = unit(key)
        key = key * key_scale
        keys = split3(key)
        grad_kk = split3(grad_mixing * decays * strict)
        grad_qk_product = split3(grad_reading * (decays * (1.0 / math.sqrt(keyw))))
        grad_query = product(grad_qk_product, keys, ROWS_COLS)
        grad_key = product(grad_qk_product, split3(query), COLS_ROWS)
        grad_key = grad_key + product(grad_kk, keys, ROWS_COLS) + product(grad_kk, keys, COLS_ROWS)

        grad_query = query_scale * (grad_query - query * jnp.sum(grad_query * query, axis=1, keepdims=True))
        grad_query = grad_query * silu_back(query_total, query_gate)
        grad_query, taps = conv_back(grad_query, query_moved, cq[:, at], keeping)
        grad_qk[:, at] = grad_query.astype(BF)
        grad_cq[:, at] += taps
        grad_key = key_scale * (grad_key - key * jnp.sum(grad_key * key, axis=1, keepdims=True))
        grad_key = grad_key * silu_back(key_total, key_gate)
        grad_key, taps = conv_back(grad_key, key_moved, ck[:, at], keeping)
        grad_qk[:, key_at] = grad_key.astype(BF)
        grad_ck[:, at] += taps

        at = pl.ds(h * valw, valw)
        moved, total = conv_parts(vg[:, at], cv[:, at], keeping)
        grad_value = grad_value * silu_back(total, jax.nn.sigmoid(total))
        grad_value, taps = conv_back(grad_value, moved, cv[:, at], keeping)
        grad_vg[:, at] = grad_value.astype(BF)
        grad_cv[:, at] += taps

    from_cols = from_cols.T
    grad_summed = grad_summed + jnp.where(lanes >= heads, from_cols, 0.0)
    grad_rates = exact_sum(masking.astype(BF), grad_summed, COLS_ROWS)
    decay_lanes = (lanes >= heads) & (lanes < 2 * heads)
    shifted = [pltpu.roll(value, heads, 1) for value in (decay_in, rates)]
    grad_decay = grad_rates * pltpu.roll(factor, heads, 1) * jax.nn.sigmoid(shifted[0])
    grad_rate[0:1] += jnp.sum(grad_rates * shifted[1], axis=0, keepdims=True)
    grad_rate[1:2] += jnp.sum(grad_decay, axis=0, keepdims=True)
    grad_small = jnp.where(decay_lanes, grad_decay, from_cols * betas * (1.0 - betas))
    grad_small = jnp.where(lanes < 2 * heads, grad_small, 0.0)
    grad_small_out[...] = grad_small.astype(BF)


def mixer_specs(heads, qk, vg, cq, cv, small):
    length = qk.shape[0] // 2

    def by_rows(width):
        return pl.BlockSpec((length, width), lambda s: (s, 0))

    def fixed(*shape):
        return pl.BlockSpec(shape, lambda s: (0,) * len(shape))

    shared = [
        by_rows(qk.shape[1]),
        by_rows(small),
        by_rows(vg.shape[1]),
        pl.BlockSpec((1, length, 1), lambda s: (s, 0, 0)),
        pl.BlockSpec((1, 1, length), lambda s: (s, 0, 0)),
        fixed(*cq.shape),
        fixed(*cq.shape),
        fixed(*cv.shape),
        fixed(1, small),
        fixed(1, small),
        fixed(1, cv.shape[1] // heads),
    ]
    valw = cv.shape[1] // heads
    square = (heads, length, length)
    kept = [square, (heads, length, valw), square, square]
    kept_specs = [pl.BlockSpec((1,) + shape, lambda s: (s, 0, 0, 0)) for shape in kept]
    kept_specs.append(by_rows(cv.shape[1]))
    kept_shapes = [jax.ShapeDtypeStruct((2,) + shape, F32) for shape in kept]
    kept_shapes.append(jax.ShapeDtypeStruct((2 * length, cv.shape[1]), F32))
    return by_rows, fixed, shared, kept_specs, kept_shapes


def mixer(heads, inputs):
    qk, _, vg, _, _, cq, _, cv, log, _, _ = inputs
    by_rows, _, shared, kept_specs, kept_shapes = mixer_specs(heads, qk, vg, cq, cv, log.shape[1])
    heads_out, *kept = pl.pallas_call(
        partial(mixer_kernel, heads),
        grid=(2,),
        out_shape=[jax.ShapeDtypeStruct((qk.shape[0], cv.shape[1]), BF)] + kept_shapes,
        in_specs=shared,
        out_specs=[by_rows(cv.shape[1])] + kept_specs,
        compiler_params=pltpu.CompilerParams(vmem_limit_bytes=48 << 20),
        name="mixer",
    )(*inputs)
    return heads_out, kept


def rows_product(left, right):
    return lax.dot_general(left, right, (((0,), (0,)), ((), ())), preferred_element_type=F32)


def cols_product(left, right):
    return lax.dot_general(left, right, (((1,), (1,)), ((), ())), preferred_element_type=F32)


def dot(left, right):
    return jnp.dot(left, right, preferred_element_type=F32)


def tied(value, after):
    return lax.optimization_barrier((value, after))[0]


def first_of(flag, own, peer, axis):
    return jnp.concatenate([jnp.where(flag, own, peer), jnp.where(flag, peer, own)], axis=axis)


def part_of(value, index, size, axis):
    return lax.dynamic_slice_in_dim(value, index * size, size, axis)


class Grid:
    def __init__(self, devices):
        self.devices = devices
        self.chips = devices // 2
        me = lax.axis_index("dp")
        self.core = me % 2
        self.spot = ring_spot(me // 2, self.chips)
        self.member = lax.axis_index("tensor")
        self.quarter = 2 * self.member + self.core

    def swap(self, value, offset):
        pairs = [(at, at ^ offset) for at in range(self.devices)]
        return lax.ppermute(value, "dp", pairs)

    def over_core(self, value):
        return self.swap(value, 1)

    def over_tensor(self, value):
        return lax.ppermute(value, "tensor", [(0, 1), (1, 0)])

    def shift(self, value, step):
        pairs = []
        for at in range(self.devices):
            spot = (ring_spot(at // 2, self.chips) + step) % self.chips
            pairs.append((at, 2 * ring_chip(spot, self.chips) + at % 2))
        return lax.ppermute(value, "dp", pairs)

    def into(self, value):
        width = value.shape[-1] // self.chips
        blocks = []
        for place in range(self.chips):
            chip = ring_chip((self.spot + place) % self.chips, self.chips)
            blocks.append(part_of(value, chip, width, -1))
        return jnp.concatenate(blocks, axis=-1)

    def out_of(self, value):
        width = value.shape[-1] // self.chips
        blocks = []
        for chip in range(self.chips):
            place = (ring_spot(chip, self.chips) - self.spot + self.chips) % self.chips
            blocks.append(part_of(value, place, width, -1))
        return jnp.concatenate(blocks, axis=-1)

    def gather_rows(self, own):
        whole = first_of(self.member == 0, own, self.over_tensor(own), 0)
        return jnp.concatenate([whole, self.over_core(whole)], axis=0)

    def scatter_rows(self, value):
        half = value.shape[0] // 2
        whole = value[:half] + self.over_core(value[half:])
        half //= 2
        theirs = part_of(whole, 1 - self.member, half, 0)
        peer = self.over_tensor(theirs.astype(BF)).astype(F32)
        return part_of(whole, self.member, half, 0) + peer


def ring_spot(chip, chips):
    line, pair = chip // 2, chip % 2
    return line * (1 - pair) + (chips - 1 - line) * pair


def ring_chip(spot, chips):
    pair = spot // (chips // 2)
    return 2 * (spot * (1 - pair) + (chips - 1 - spot) * pair) + pair


def signal_all(devices):
    barrier = pltpu.get_barrier_semaphore()
    for device in devices:
        pl.semaphore_signal(barrier, inc=1, device_id=device, device_id_type=pl.DeviceIdType.MESH)
    pl.semaphore_wait(barrier, len(devices))


def send(source, target, send_sem, recv_sem, device):
    return pltpu.make_async_remote_copy(
        src_ref=source,
        dst_ref=target,
        send_sem=send_sem,
        recv_sem=recv_sem,
        device_id=device,
        device_id_type=pl.DeviceIdType.MESH,
    )


def staged(sources, targets, sem):
    copies = [pltpu.make_async_copy(*pair, sem.at[i]) for i, pair in enumerate(zip(sources, targets))]
    pending = set(range(len(copies)))
    for copy in copies:
        copy.start()

    def ready(*numbers):
        for i in sorted(pending.intersection(numbers)):
            copies[i].wait()
            pending.remove(i)

    return ready


def spread_kernel(chips, layout, ringed, *refs):
    count = len(layout)
    totals = 1 + max(item[0] for item in layout)
    sources, (tokens, cot, gain, gain_mlp, w_decay) = refs[:count], refs[count : count + 5]
    refs = refs[count + 5 :]
    given_out = refs[:totals]
    stream, cot_own, own_gain, own_gain_mlp, rows_mix, rows_cot = refs[totals : totals + 6]
    refs = refs[totals + 6 :]
    normed, near_sem, send_core, recv_core, send_right, recv_right, send_left, recv_left = refs[:8]
    own_sem, send_half, recv_half, send_whole, recv_whole, rate_sum, rate_own, store_sem, *turned = refs[8:]
    outs, turned = (*turned[:ringed], *given_out[ringed:]), turned[ringed:]
    me, member = lax.axis_index("dp"), lax.axis_index("tensor")
    core, chip = me % 2, me // 2
    spot = ring_spot(chip, chips)
    right = (2 * ring_chip((spot + 1) % chips, chips) + core, member)
    left = (2 * ring_chip((spot + chips - 1) % chips, chips) + core, member)
    peer = (2 * chip + 1 - core, member)
    across = (me, 1 - member)
    signal_all((right, left, peer, across))

    def home(out):
        return outs[out].at[0] if out < ringed else outs[out]

    near, far = [], []
    given = list(sources)
    turned = [(i, target) for i, target in zip([i for i, item in enumerate(layout) if item[3]], turned)]
    sources = list(sources)
    for i, target in turned:
        sources[i] = target
    for i, (out, at, width, _) in enumerate(layout):
        if width is None:
            place = home(out).at[core]
            near.append(pltpu.make_async_copy(rate_own.at[core], place, near_sem.at[i]))
            far.append(send(rate_own.at[1 - core], place, send_core.at[i], recv_core.at[i], peer))
            heads = w_decay.shape[0] // 2
            rate_sum[...] = jnp.zeros_like(rate_sum)
            for at, part in ((0, sources[i][...].astype(F32)), (heads, w_decay[...].astype(F32))):
                for c in range(2):
                    rate_sum[c, at : at + heads] = part[c * heads : (c + 1) * heads]
            rate_own[...] = rate_sum[...].astype(BF)
            continue
        rows = sources[i].shape[0]
        place = home(out).at[pl.ds(pl.multiple_of(core * rows, rows), rows), pl.ds(at, width)]
        mine = sources[i].at[:, pl.ds(pl.multiple_of(core * width, 128), width)]
        theirs = sources[i].at[:, pl.ds(pl.multiple_of((1 - core) * width, 128), width)]
        near.append(pltpu.make_async_copy(mine, place, near_sem.at[i]))
        far.append(send(theirs, place, send_core.at[i], recv_core.at[i], peer))

    def trade_halves(outs_now):
        for i, target in turned:
            if layout[i][0] in outs_now:
                target[...] = given[i][...].T
        for i, item in enumerate(layout):
            if item[0] in outs_now:
                far[i].start()
                near[i].start()

    trade_halves(range(2))

    def hop(out, step, way):
        last = step == chips // 2
        ref = outs[out]
        mid = ref.shape[1] // 2
        if way > 0:
            at, to, device, sends, receives = -(step - 1) % chips, chips - step, right, send_right, recv_right
            rows = pl.ds(0, mid)
        else:
            at, to, device, sends, receives = step - 1, step, left, send_left, recv_left
            rows = pl.ds(mid, mid)
        source, target = ref.at[at], ref.at[to]
        if last:
            source, target = source.at[rows], target.at[rows]
        return send(source, target, sends.at[out, step - 1], receives.at[out, step - 1], device)

    stored = []

    def store(out, slot):
        stored.append(pltpu.make_async_copy(outs[out].at[slot], given_out[out].at[slot], store_sem.at[out, slot]))
        stored[-1].start()

    started, own = [], []
    pairs = ((normed, rows_mix), (cot_own, rows_cot))
    halves = [
        send(value, rows.at[0, member], send_half.at[i], recv_half.at[i], across)
        for i, (value, rows) in enumerate(pairs)
    ]
    wholes = [
        send(rows.at[0], rows.at[1], send_whole.at[i], recv_whole.at[i], peer)
        for i, (_, rows) in enumerate(pairs)
    ]
    for step in range(1, chips // 2 + 1):
        for out in range(ringed):
            if step == 1:
                for i, item in enumerate(layout):
                    if item[0] == out:
                        near[i].wait()
                        far[i].wait()
            for way in (1, -1):
                if step > 1:
                    hop(out, step - 1, way).wait_recv()
                copy = hop(out, step, way)
                copy.start()
                started.append(copy)
                if step > 1:
                    store(out, chips - step + 1 if way > 0 else step - 1)
            if step == 1:
                store(out, 0)
                trade_halves((out + 2,) if out + 2 < ringed else ())
        if step == 1:
            trade_halves(range(ringed, totals))
            width = tokens.shape[1] // chips
            aligned = width % 128 == 0
            squares = jnp.zeros((tokens.shape[0], 1), F32)
            for place in range(chips):
                to = pl.ds(place * width, width)
                at = to
                if aligned:
                    at = ring_chip((spot + place) % chips, chips) * width
                    at = pl.ds(pl.multiple_of(at, 128), width)
                stream[:, to] = tokens[:, at]
                cot_own[:, to] = cot[:, at]
                own_gain[:, to] = gain[:, at]
                own_gain_mlp[:, to] = gain_mlp[:, at]
                block = stream[:, to].astype(F32)
                squares = squares + jnp.sum(block * block, axis=1, keepdims=True)
            scale = lax.rsqrt(squares / tokens.shape[1] + 1e-06)
            normed[...] = (stream[...].astype(F32) * scale * own_gain[...]).astype(BF)
            for i, (value, rows) in enumerate(pairs):
                own.append(pltpu.make_async_copy(value, rows.at[0, member], own_sem.at[i]))
                own[-1].start()
                halves[i].start()
        if step == 2:
            for i in range(2):
                own[i].wait()
                halves[i].wait()
                wholes[i].start()
    for i, item in enumerate(layout):
        if item[0] >= ringed:
            near[i].wait()
            far[i].wait()
    for copy in wholes:
        copy.wait()
    for out in range(ringed):
        for way in (1, -1):
            hop(out, chips // 2, way).wait_recv()
        store(out, chips // 2)
    for copy in stored:
        copy.wait()
    for copy in started:
        copy.wait_send()


def spread(grid, groups, ringed, tokens, cot, gains, rates):
    chips = grid.chips
    sources, layout, shapes, turned_shapes = [], [], [], []
    for out, group in enumerate(groups):
        if not isinstance(group, list):
            rate = (2, group, rates[0].shape[1])
            layout.append((out, 0, None, False))
            sources.append(rates[0])
            shapes.append(jax.ShapeDtypeStruct((chips,) + rate, BF))
            continue
        at = 0
        for shard in group:
            turned = isinstance(shard, tuple)
            if turned:
                (shard,) = shard
                turned_shapes.append(pltpu.VMEM(shard.shape[::-1], BF))
            width = shard.shape[0 if turned else 1] // 2
            layout.append((out, at, width, turned))
            sources.append(shard)
            at += width
        rows = 2 * tokens.shape[1] // grid.devices
        shapes.append(jax.ShapeDtypeStruct(((chips,) if out < ringed else ()) + (rows, at), BF))
    dma = pltpu.SemaphoreType.DMA
    hops = (ringed, chips // 2)
    anywhere = pl.BlockSpec(memory_space=pltpu.HBM)
    near = pl.BlockSpec(memory_space=pltpu.VMEM)
    own = jax.ShapeDtypeStruct(tokens.shape, BF)
    rows = jax.ShapeDtypeStruct((2, 2) + tokens.shape, BF)
    return pl.pallas_call(
        partial(spread_kernel, chips, layout, ringed),
        out_shape=shapes + [own, own] + [jax.ShapeDtypeStruct(gains[0].shape, F32)] * 2 + [rows, rows],
        in_specs=[near if item[3] or item[2] is None else anywhere for item in layout] + [near] * 5,
        out_specs=[anywhere] * len(shapes) + [near] * 4 + [anywhere] * 2,
        scratch_shapes=[pltpu.VMEM(tokens.shape, BF)]
        + [dma((len(sources),))] * 3
        + [dma(hops)] * 4
        + [dma((2,))] * 5
        + [pltpu.VMEM(rate, F32), pltpu.VMEM(rate, BF), dma((ringed, chips))]
        + [pltpu.VMEM(shape.shape, BF) for shape in shapes[:ringed]]
        + turned_shapes,
        compiler_params=pltpu.CompilerParams(
            collective_id=0, has_side_effects=True, vmem_limit_bytes=62 << 20
        ),
        name="spread",
    )(*sources, tokens, cot, *gains, rates[1])


PARTS = 4


def exchange(part, own_part, rows_out, buffers, sems, compute, early=None, late=None):
    got_core, sent_half, got_half, own = buffers
    me, member = lax.axis_index("dp"), lax.axis_index("tensor")
    peer = (me + 1 - 2 * (me % 2), member)
    across = (me, 1 - member)
    count = part.shape[2] // PARTS

    def chunk(k):
        return pl.ds(k * count, count)

    def copy(kind, k, source, target, device):
        return send(source, target, sems[2 * kind].at[k], sems[2 * kind + 1].at[k], device)

    first = [copy(0, k, part.at[1, :, chunk(k)], got_core.at[:, chunk(k)], peer) for k in range(PARTS)]
    second = [copy(1, k, sent_half.at[chunk(k)], got_half.at[chunk(k)], across) for k in range(PARTS)]
    third = [
        copy(2, k, own.at[chunk(k)], rows_out.at[0, member, chunk(k)], across) for k in range(PARTS)
    ]
    fourth = [
        copy(3, k, own.at[chunk(k)], rows_out.at[1, member, chunk(k)], peer) for k in range(PARTS)
    ]
    fifth = [
        copy(4, k, rows_out.at[0, 1 - member, chunk(k)], rows_out.at[1, 1 - member, chunk(k)], peer)
        for k in range(PARTS)
    ]
    for k in range(PARTS):
        first[k].start()
    if early:
        early()
    for k in range(PARTS):
        first[k].wait_recv()
        total = own_part[1 - member, chunk(k)] + got_core[1 - member, chunk(k)]
        sent_half[chunk(k)] = total.astype(BF)
        second[k].start()
    for k in range(PARTS):
        second[k].wait_recv()
        total = own_part[member, chunk(k)] + got_core[member, chunk(k)] + got_half[chunk(k)].astype(F32)
        value = compute(k, chunk(k), total).astype(BF)
        own[chunk(k)] = value
        third[k].start()
        fourth[k].start()
        rows_out[0, member, chunk(k)] = value
    for k in range(PARTS):
        third[k].wait_recv()
        fifth[k].start()
    if late:
        late()
    for k in range(PARTS):
        fourth[k].wait_recv()
        fifth[k].wait_recv()
    for copies in (first, second, third, fourth, fifth):
        for one in copies:
            one.wait_send()


def exchange_scratch(rows, width):
    return [
        pltpu.VMEM((2, rows, width), F32),
        pltpu.VMEM((rows, width), BF),
        pltpu.VMEM((rows, width), BF),
        pltpu.VMEM((rows, width), BF),
    ] + [pltpu.SemaphoreType.DMA((PARTS,))] * 10


def middle_kernel(part, stream, gain, rows_out, middle, *scratch):
    me, member = lax.axis_index("dp"), lax.axis_index("tensor")
    signal_all(((me + 1 - 2 * (me % 2), member), (me, 1 - member)))

    def compute(k, rows, mixed):
        value = stream[rows].astype(F32) + mixed
        middle[rows] = value
        return value * lax.rsqrt(jnp.mean(value * value, axis=1, keepdims=True) + 1e-06) * gain[...]

    exchange(part, part.at[0], rows_out, scratch[:4], scratch[4:], compute)


def middle_rows(part, stream, gain):
    rows, width = stream.shape
    near = pl.BlockSpec(memory_space=pltpu.VMEM)
    gathered, middle = pl.pallas_call(
        middle_kernel,
        out_shape=[
            jax.ShapeDtypeStruct((2, 2, rows, width), BF),
            jax.ShapeDtypeStruct((rows, width), F32),
        ],
        in_specs=[near] * 3,
        out_specs=[near] * 2,
        scratch_shapes=exchange_scratch(rows, width),
        compiler_params=pltpu.CompilerParams(
            collective_id=1, has_side_effects=True, vmem_limit_bytes=62 << 20
        ),
        name="middle",
    )(part.reshape(2, 2, rows, width), stream, gain)
    return gathered.reshape(4 * rows, width), middle


def turn_kernel(chips, heads, ffw, early, *refs):
    refs = list(refs)

    def take(count):
        taken, refs[:] = refs[:count], refs[count:]
        return taken

    part, gain = take(2)
    small_inputs, later = take(8), take(17)
    rows_out, grad_middle, grad_gain, late = take(4)
    results = take(8)
    grad_heads, going, arrived = take(3)
    here_now, (later_sem,) = take(17), take(1)
    send_ring, recv_ring = take(2)
    me, member = lax.axis_index("dp"), lax.axis_index("tensor")
    core, chip = me % 2, me // 2
    spot = ring_spot(chip, chips)
    ways = (
        (2 * ring_chip((spot + 1) % chips, chips) + core, member),
        (2 * ring_chip((spot + chips - 1) % chips, chips) + core, member),
    )
    rows_cot, rows_mlp, hidden, grad_gate, begun, own_part, cot, middle, wout, *kept = here_now[:14]
    inputs = here_now[14:] + small_inputs
    later[5] = later[5].at[0]
    ready = staged(later, here_now, later_sem)
    signal_all((*ways, (me + 1 - 2 * core, member), (me, 1 - member)))
    half = chips // 2
    width = rows_cot.shape[1] // chips
    mid = width // 2

    def total(way, place, step):
        at = (place if way == 0 else -place) % chips * width
        value = []
        for left, right, size in ((rows_cot, hidden, ffw), (rows_mlp, grad_gate, early)):
            value.append(
                lax.dot_general(
                    left[:, at : at + width],
                    right[:, 0:size],
                    (COLS_ROWS, ((), ())),
                    preferred_element_type=F32,
                )
            )
        value = jnp.concatenate(value, axis=1)
        if step:
            return (value + arrived[way, step - 1].astype(F32)).astype(BF)
        lo = mid * way
        here = value[lo : lo + mid] + begun[way].astype(F32)
        rest = value[mid - lo : width - lo]
        return jnp.concatenate([here, rest] if way == 0 else [rest, here], axis=0).astype(BF)

    def hop(way, step):
        sems = (way, step)
        source = arrived.at[way, step - 1] if step else going.at[way]
        return send(source, arrived.at[sems], send_ring.at[sems], recv_ring.at[sems], ways[way])

    def next_hop(step):
        for way in range(2):
            if step:
                hop(way, step - 1).wait_recv()
            value = total(way, half - 1 - step, step)
            if step == half - 2:
                late[way] = value
                continue
            if step:
                arrived[way, step - 1] = value
            else:
                going[way] = value
            hop(way, step).start()

    def compute(k, rows, grad):
        value = middle[rows]
        scale = lax.rsqrt(jnp.mean(value * value, axis=1, keepdims=True) + 1e-06)
        unit_value = value * scale
        gained = jnp.sum(grad * unit_value, axis=0, keepdims=True)
        grad_gain[...] = gained if k == 0 else grad_gain[...] + gained
        grad = grad * gain[...]
        grad = scale * (grad - unit_value * jnp.mean(grad * unit_value, axis=1, keepdims=True))
        grad = grad + cot[rows].astype(F32)
        grad_middle[rows] = grad
        return grad


    def early_work():
        ready(*range(5))
        next_hop(0)
        ready(5, 6, 7)

    def late_work():
        if half > 3:
            next_hop(1)

    exchange(part, own_part, rows_out, refs[:4], refs[4:], compute, early_work, late_work)
    ready(*range(17))
    for step in range(2, half - 2):
        next_hop(step)
    for ref in results[3:]:
        ref[...] = jnp.zeros_like(ref)
    length = inputs[0].shape[0] // 2

    @pl.loop(0, 2)
    def _(s):
        at = pl.multiple_of(s * length, length)
        here = pl.ds(at, length)
        for m in range(2):
            grad_heads[pl.ds(at + m * (length // 2), length // 2)] = jnp.dot(
                rows_out[s, m], wout[...], preferred_element_type=F32
            )
        mixer_back(
            heads,
            grad_heads.at[here],
            [ref.at[here] for ref in inputs[:3]] + [ref.at[pl.ds(s, 1)] for ref in inputs[3:5]] + inputs[5:],
            [ref.at[pl.ds(s, 1)] for ref in kept[:4]] + [kept[4].at[here]],
            [ref.at[here] for ref in results[:3]] + results[3:],
        )

    next_hop(half - 2)
    for step in range(half - 2):
        for way in range(2):
            hop(way, step).wait_send()


def turn(grid, heads, early, part, cot, middle, gain, wout, rows_cot, rows_mlp, hidden, grad_gate, begun, inputs, kept):
    chips = grid.chips
    rows, width = middle.shape
    block, half = width // chips, chips // 2
    ffw = hidden.shape[1]
    n = ffw + early
    qk, rates_in, vg, _, _, cq, ck, cv, log, _, out_gain = inputs
    near = pl.BlockSpec(memory_space=pltpu.VMEM)
    far = pl.BlockSpec(memory_space=pltpu.HBM)
    dma = pltpu.SemaphoreType.DMA
    sums = [cq.shape, ck.shape, cv.shape, (2, log.shape[1]), out_gain.shape]
    part = part.reshape(2, 2, rows, width)
    near_in = (gain, *inputs[3:])
    later = (rows_cot, rows_mlp, hidden, grad_gate, begun, part, cot, middle, wout, *kept, *inputs[:3])
    held = [value.shape[1:] if value is part else value.shape for value in later]
    gathered, *rest = pl.pallas_call(
        partial(turn_kernel, chips, heads, ffw, early),
        out_shape=[
            jax.ShapeDtypeStruct((2, 2, rows, width), BF),
            jax.ShapeDtypeStruct((rows, width), F32),
            jax.ShapeDtypeStruct((1, width), F32),
            jax.ShapeDtypeStruct((2, block, n), BF),
            jax.ShapeDtypeStruct(qk.shape, BF),
            jax.ShapeDtypeStruct(rates_in.shape, BF),
            jax.ShapeDtypeStruct(vg.shape, BF),
        ]
        + [jax.ShapeDtypeStruct(shape, F32) for shape in sums],
        in_specs=[far] + [near] * len(near_in) + [far] * len(later),
        out_specs=[near] * (7 + len(sums)),
        scratch_shapes=[
            pltpu.VMEM((4 * rows, cv.shape[1]), F32),
            pltpu.VMEM((2, block, n), BF),
            pltpu.VMEM((2, half - 2, block, n), BF),
            *[pltpu.VMEM(shape, value.dtype) for shape, value in zip(held, later)],
            dma((len(later),)),
            dma((2, half - 2)),
            dma((2, half - 2)),
        ]
        + exchange_scratch(rows, width),
        compiler_params=pltpu.CompilerParams(
            collective_id=2, has_side_effects=True, vmem_limit_bytes=62 << 20
        ),
        name="turn",
    )(part, *near_in, *later)
    return gathered.reshape(4 * rows, width), *rest


def mlp_kernel(chips, ffw, early, *refs):
    rows_far, cot_far, own, right_1, left_1, right_2, left_2 = refs[:7]
    *given, begun = refs[7:14]
    hidden, gate_early, gate_rest, grad_upper, back, ahead, store_sem = refs[14:21]
    refs = refs[7:]
    rows, cot, rows_sem, weights, sums, begin, load_sem, send_ring, recv_ring, send_begin, recv_begin = refs[14:]
    me, member = lax.axis_index("dp"), lax.axis_index("tensor")
    core, chip = me % 2, me // 2
    spot = ring_spot(chip, chips)
    ways = (
        (2 * ring_chip((spot + 1) % chips, chips) + core, member),
        (2 * ring_chip((spot + chips - 1) % chips, chips) + core, member),
    )
    signal_all(ways)
    half = chips // 2
    block = own.shape[0]
    mid = block // 2

    def spots(place, lo=0, hi=block):
        return pl.ds((place % chips) * block + lo, hi - lo)

    def hop(way, step):
        cols = pl.ds(0, 3 * ffw)
        lo, hi = 0, block
        sems = (way, step - 3)
        if step >= half:
            cols = pl.ds(0, 2 * ffw) if step == half else pl.ds(2 * ffw, ffw)
            lo, hi = mid * way, mid * way + mid
            step = half
        place, to = (1 - step, -step) if way == 0 else (step - 1, step)
        if step == 3:
            source = (right_2, left_2)[way].at[pl.ds(lo, hi - lo), cols]
        else:
            source = weights.at[spots(place, lo, hi), cols]
        return send(source, weights.at[spots(to, lo, hi), cols], send_ring.at[sems], recv_ring.at[sems], ways[way])

    for way in range(2):
        hop(way, 3).start()
    loads = []
    for number, (place, source) in enumerate(((0, own), (1, left_1), (2, left_2), (-2, right_2), (-1, right_1))):
        loads.append(pltpu.make_async_copy(source, weights.at[spots(place)], load_sem.at[number]))
        loads[-1].start()

    ready = staged((rows_far, cot_far), (rows, cot), rows_sem)
    tile = ffw // 2

    def add(lo, hi, first, begins=0, ends=3 * ffw):
        inner = slice((lo % chips) * block, (lo % chips + hi - lo) * block)
        for at in range(begins, ends, tile):
            left = rows if at < 2 * ffw else cot
            value = jnp.dot(left[:, inner], weights[inner, at : at + tile], preferred_element_type=F32)
            sums[:, at : at + tile] = value if first else sums[:, at : at + tile] + value

    ready(0, 1)
    for copy in loads[:3]:
        copy.wait()
    add(0, 3, True)
    for copy in loads[3:]:
        copy.wait()
    add(-2, 0, False)
    for step in range(3, half):
        for way in range(2):
            hop(way, step).wait_recv()
            hop(way, step + 1).start()
            if step + 1 == half:
                hop(way, half + 1).start()
        add(step, step + 1, False)
        add(-step, 1 - step, False)

    starts = []

    def first_hop(lo, hi):
        number = len(starts) // 2
        for way in range(2):
            row = half * block + mid * way
            for left, right, at, size in ((cot, hidden, 0, ffw), (rows, gate_early, ffw, early)):
                begins, ends = max(lo - at, 0), min(hi - at, size)
                if begins < ends:
                    begin[way, :, at + begins : at + ends] = lax.dot_general(
                        left[:, row : row + mid],
                        right[:, begins:ends],
                        (COLS_ROWS, ((), ())),
                        preferred_element_type=F32,
                    ).astype(BF)
            cols = pl.ds(lo, hi - lo)
            sems = (way, number)
            starts.append(
                send(
                    begin.at[way, :, cols], begun.at[way, :, cols], send_begin.at[sems], recv_begin.at[sems], ways[way]
                )
            )
            starts[-1].start()

    for way in range(2):
        hop(way, half).wait_recv()
    add(half, half + 1, False, 0, 2 * ffw)
    for at in range(0, ffw, 128):
        gate, upper = sums[:, at : at + 128], sums[:, ffw + at : ffw + at + 128]
        hidden[:, at : at + 128] = (gate * jax.nn.sigmoid(gate) * upper).astype(BF)
    first_hop(0, ffw)
    stores = []

    def store(number, source, target):
        stores.append(pltpu.make_async_copy(source, target, store_sem.at[number]))
        stores[-1].start()

    def look_ahead(place):
        inner = slice(place * block, (place + 1) * block)
        ahead[:, inner] = lax.dot_general(
            hidden[...], weights[inner, 2 * ffw :], (ROWS_ROWS, ((), ())), preferred_element_type=F32
        ).astype(BF)

    store(0, hidden, given[0])
    for place in range(chips):
        if place != half:
            look_ahead(place)
    for way in range(2):
        hop(way, half + 1).wait_recv()
    add(half, half + 1, False, 2 * ffw)
    for at in range(0, ffw, 128):
        gate, upper = sums[:, at : at + 128], sums[:, ffw + at : ffw + at + 128]
        grad = sums[:, 2 * ffw + at : 2 * ffw + at + 128]
        open_gate = jax.nn.sigmoid(gate)
        part, to = (gate_early, at) if at < early else (gate_rest, at - early)
        part[:, to : to + 128] = (grad * upper * silu_back(gate, open_gate)).astype(BF)
        grad_upper[:, at : at + 128] = (grad * gate * open_gate).astype(BF)
        if at + 128 == early:
            first_hop(ffw, ffw + early)
    for number, value in ((1, gate_early), (2, gate_rest), (3, grad_upper)):
        store(number, value, given[number])
    look_ahead(half)
    store(5, ahead, given[5])
    for place in range(chips):
        inner = slice(place * block, (place + 1) * block)
        value, at = 0.0, 0
        for part in (gate_early, gate_rest, grad_upper):
            cols = slice(at, at + part.shape[1])
            value = value + lax.dot_general(
                part[...], weights[inner, cols], (ROWS_ROWS, ((), ())), preferred_element_type=F32
            )
            at += part.shape[1]
        back[:, inner] = value
        if place % (chips // 4) == chips // 4 - 1:
            quarter = pl.ds((place + 1 - chips // 4) * block, chips // 4 * block)
            store(6 + place // (chips // 4), back.at[:, quarter], given[4].at[:, quarter])
    for copy in stores:
        copy.wait()
    for copy in starts:
        copy.wait()
    for step in range(3, half + 2):
        for way in range(2):
            hop(way, step).wait_send()


def mlp(grid, rows, cot, chunks, ffw, early):
    chips = grid.chips
    count, width = rows.shape
    block, n = chunks[0].shape
    half = chips // 2
    near = pl.BlockSpec(memory_space=pltpu.VMEM)
    far = pl.BlockSpec(memory_space=pltpu.HBM)
    dma = pltpu.SemaphoreType.DMA
    inner = jax.ShapeDtypeStruct((count, ffw), BF)
    return pl.pallas_call(
        partial(mlp_kernel, chips, ffw, early),
        out_shape=[
            inner,
            jax.ShapeDtypeStruct((count, early), BF),
            jax.ShapeDtypeStruct((count, ffw - early), BF),
            inner,
            jax.ShapeDtypeStruct((count, width), F32),
            jax.ShapeDtypeStruct((count, width), BF),
            jax.ShapeDtypeStruct((2, block // 2, ffw + early), BF),
        ],
        in_specs=[far] * 7,
        out_specs=[far] * 6 + [near],
        scratch_shapes=[
            pltpu.VMEM((count, ffw), BF),
            pltpu.VMEM((count, early), BF),
            pltpu.VMEM((count, ffw - early), BF),
            pltpu.VMEM((count, ffw), BF),
            pltpu.VMEM((count, width), F32),
            pltpu.VMEM((count, width), BF),
            dma((10,)),
            pltpu.VMEM(rows.shape, BF),
            pltpu.VMEM(rows.shape, BF),
            dma((2,)),
            pltpu.VMEM((chips * block, n), BF),
            pltpu.VMEM((count, n), F32),
            pltpu.VMEM((2, block // 2, ffw + early), BF),
            dma((5,)),
            dma((2, half - 1)),
            dma((2, half - 1)),
            dma((2, 2)),
            dma((2, 2)),
        ],
        compiler_params=pltpu.CompilerParams(
            collective_id=4, has_side_effects=True, vmem_limit_bytes=62 << 20
        ),
        name="mlp",
    )(rows, cot, *chunks)


def collect_kernel(chips, steps, groups, late_parts, fields, side_of, counts, *refs):
    n_left, n_right, n_out, n_side = counts
    refs = list(refs)

    def take(count):
        taken, refs[:] = refs[:count], refs[count:]
        return taken

    far = take(n_left + n_right)
    late_out, late_left = take(2)
    weights = take(n_side)
    ahead_far, *far_tokens = take(4)
    gain, mlp_grad, rate_weights = take(3)
    grad_cq, grad_ck, grad_cv, grad_rate, grad_gain = take(5)
    outs = take(n_out)
    rates_out, out_tokens, grad_tokens, *small_outs = take(5)
    begin, arrived, late_in, final, back, got_core, sent_half, got_half, *small_ins = take(10)
    buffers = take(n_side)
    near, near_tokens = take(n_left + n_right), take(4)
    lefts, rights = near[:n_left], near[n_left:]
    ahead, stream, middle, grad_middle = near_tokens
    (far_sem,) = take(1)
    send_ring, recv_ring, own_sem, send_core, recv_core, send_late, recv_late = take(7)
    send_first, recv_first, send_second, recv_second, send_small, recv_small, weight_sem, free = take(8)
    rate_begin, rate_arrived, rate_final, send_rate, recv_rate, rate_sems = take(6)
    me, member = lax.axis_index("dp"), lax.axis_index("tensor")
    core, chip = me % 2, me // 2
    spot = ring_spot(chip, chips)
    ways = (
        (2 * ring_chip((spot + 1) % chips, chips) + core, member),
        (2 * ring_chip((spot + chips - 1) % chips, chips) + core, member),
    )
    peer = (2 * chip + 1 - core, member)
    across = (me, 1 - member)
    partners = [across] + [
        (me + (1 << k) - 2 * (1 << k) * ((me // (1 << k)) % 2), member) for k in range(steps - 1)
    ]
    signal_all(list(ways) + partners)

    half = chips // 2
    width = lefts[0].shape[1] // chips
    mid = width // 2
    starts = []
    at = 0
    for _, right in groups:
        starts.append(at)
        at += rights[right].shape[1]

    def columns(group):
        return pl.ds(starts[group], rights[groups[group][1]].shape[1])

    def piece(group, place, lo=0, hi=width):
        left, right = lefts[groups[group][0]], rights[groups[group][1]]
        at = (place % chips) * width
        return lax.dot_general(
            left[:, at + lo : at + hi], right[...], (COLS_ROWS, ((), ())), preferred_element_type=F32
        )

    def rows_of(way):
        return pl.ds(mid * way, mid)

    def hop(way, step, group):
        if step:
            source, target = arrived.at[way, step - 1], arrived.at[way, step % (half - 1)]
            source, target = source.at[:, columns(group)], target.at[:, columns(group)]
        else:
            source = begin.at[way, :, columns(group)]
            target = arrived.at[way, 0, rows_of(way), columns(group)]
        sems = (way, step, group)
        return send(source, target, send_ring.at[sems], recv_ring.at[sems], ways[way])

    rate_rows = rate_begin.shape[1]

    def rate_piece(place):
        at = (place % chips) * width
        value = lax.dot_general(
            rights[-1][:, 0:rate_rows], lefts[-1][:, at : at + width], (COLS_ROWS, ((), ())), preferred_element_type=F32
        )
        return value[:, 0:mid], value[:, mid:width]

    def rate_hop(way, step):
        source = rate_arrived.at[way, step - 1] if step else rate_begin.at[way]
        target = rate_arrived.at[way, step % (half - 1)] if step else rate_arrived.at[way, 0, way]
        sems = (way, step)
        return send(source, target, send_rate.at[sems], recv_rate.at[sems], ways[way])

    def rate_step(step, place):
        for way in range(2):
            rate_hop(way, step).wait_recv()
            for c, value in enumerate(rate_piece(place if way == 0 else -place)):
                if step or c == way:
                    value = value + rate_arrived[way, step, c].astype(F32)
                rate_arrived[way, step, c] = value.astype(BF)
            rate_hop(way, step + 1).start()

    late = [send(late_out.at[way], late_in.at[way], send_late.at[way], recv_late.at[way], ways[way]) for way in range(2)]
    sides = (back, ahead)
    first = [
        send(value.at[1], got_core.at[i], send_first.at[i], recv_first.at[i], peer)
        for i, value in enumerate((back, ahead_far))
    ]
    second = [
        send(sent_half.at[i], got_half.at[i], send_second.at[i], recv_second.at[i], across) for i in range(2)
    ]

    def fold_small(step):
        copies = []
        for i, (out, arrivals) in enumerate(zip(small_outs, small_ins)):
            source = arrivals.at[steps + step - 1] if step else out
            sems = (step, i)
            copies.append(send(source, arrivals.at[step], send_small.at[sems], recv_small.at[sems], partners[step]))
        return copies

    def put(ref, value):
        if width % 128:
            ref[...] = value
            return
        for place in range(chips):
            at = pl.multiple_of(ring_chip((spot + place) % chips, chips) * width, 128)
            ref[:, pl.ds(at, width)] = value[:, place * width : (place + 1) * width]

    def fetch(place):
        return [
            pltpu.make_async_copy(
                weight.at[pl.ds(place * width, width), pl.ds(at, buffer.shape[2])],
                buffer.at[place % 2],
                weight_sem.at[number, place % 2],
            )
            for number, (weight, (at, _), buffer) in enumerate(zip(weights, side_of, buffers))
        ]

    def side_work():
        for place in range(chips):
            if place + 1 < chips:
                for copy in fetch(place + 1):
                    copy.start()
            for copy in fetch(place):
                copy.wait()
            total = jnp.dot(
                rights[-1][:, 0:rate_rows],
                rate_weights[:, place * width : (place + 1) * width],
                preferred_element_type=F32,
            )
            for (_, right), buffer in zip(side_of, buffers):
                total = total + lax.dot_general(
                    rights[right][...],
                    buffer[place % 2],
                    (ROWS_ROWS, ((), ())),
                    preferred_element_type=F32,
                )
            back[:, :, :, place * width : (place + 1) * width] = (
                total.astype(BF).reshape(2, 2, middle.shape[0], width)
            )
            yield
        for copy in first:
            copy.start()
        yield
        ready(*range(n_left + n_right, n_left + n_right + 4))
        for i in range(2):
            first[i].wait_recv()
            total = sides[i][0, 1 - member].astype(F32) + got_core[i, 1 - member].astype(F32)
            sent_half[i] = total.astype(BF)
            second[i].start()
        yield
        total = []
        for i in range(2):
            second[i].wait_recv()
            value = sides[i][0, member].astype(F32) + got_core[i, member].astype(F32)
            total.append(value + got_half[i].astype(F32))
        put(out_tokens, middle[...] + total[1])
        value = stream[...].astype(F32)
        scale = lax.rsqrt(jnp.mean(value * value, axis=1, keepdims=True) + 1e-06)
        value = value * scale
        gained = jnp.sum(total[0] * value, axis=0, keepdims=True)
        grad = total[0] * gain[...]
        grad = scale * (grad - value * jnp.mean(grad * value, axis=1, keepdims=True))
        put(grad_tokens, grad_middle[...] + grad)
        small_out, wide = small_outs
        small_out[...] = jnp.zeros_like(small_out)
        wide[...] = jnp.zeros_like(wide)
        quarter = 2 * member + core
        taps, keyw = grad_cq.shape
        valw = grad_cv.shape[1]
        after = max(8 * keyw, 4 * valw)

        def part(at, size):
            return pl.ds(pl.multiple_of(at + quarter * size, 128), size)

        wide[0:taps, part(0, keyw)] = grad_cq[...]
        wide[0:taps, part(4 * keyw, keyw)] = grad_ck[...]
        wide[taps : 2 * taps, part(0, valw)] = grad_cv[...]
        wide[0:1, after : after + grad_gain.shape[1]] = grad_gain[...]
        wide[0:2, part(after + grad_gain.shape[1], grad_rate.shape[1])] = grad_rate[...]
        lanes = min(width, 128)
        each = width // lanes
        for i, vector in enumerate((gained, mlp_grad[...])):
            for place in range(chips):
                row = (i * chips + ring_chip((spot + place) % chips, chips)) * each
                for k in range(each):
                    at = place * width + k * lanes
                    small_out[pl.ds(row + k, 1), 0:lanes] = vector[:, at : at + lanes]
        for copy in fold_small(0):
            copy.start()
        yield
        for step in range(steps):
            for copy in fold_small(step):
                copy.wait_recv()
            for out, arrivals in zip(small_outs, small_ins):
                before = arrivals.at[steps + step - 1] if step else out
                arrivals[steps + step] = before[...] + arrivals[step]
            if step + 1 < steps:
                for copy in fold_small(step + 1):
                    copy.start()
            yield

    work = side_work()
    ready = staged([*far, ahead_far.at[pl.ds(0, 1)], *far_tokens], near + near_tokens, far_sem)
    for copy in late + fetch(0):
        copy.start()
    for group in range(len(groups)):
        ready(groups[group][0], n_left + groups[group][1])
        for way in range(2):
            begin[way, :, columns(group)] = piece(group, half, mid * way, mid * way + mid).astype(BF)
            hop(way, 0, group).start()
    ready(*range(n_left + n_right))
    for way in range(2):
        rate_begin[way] = rate_piece(half)[way].astype(BF)
        rate_hop(way, 0).start()
    for step in range(half - 1):
        place = half - 1 - step
        for group in range(len(groups)):
            next(work, None)
            next(work, None)
            for way in range(2):
                hop(way, step, group).wait_recv()
                value = piece(group, place if way == 0 else -place)
                if step:
                    value = value + arrived[way, step, :, columns(group)].astype(F32)
                    arrived[way, step, :, columns(group)] = value.astype(BF)
                else:
                    lo = mid * way
                    here = value[lo : lo + mid] + arrived[way, 0, rows_of(way), columns(group)].astype(F32)
                    arrived[way, 0, rows_of(way), columns(group)] = here.astype(BF)
                    arrived[way, 0, rows_of(1 - way), columns(group)] = value[
                        mid - lo : width - lo
                    ].astype(BF)
                if step == half - 2 and group == 0:
                    pl.semaphore_wait(free.at[way], 1)
                hop(way, step + 1, group).start()
            if group == 0:
                rate_step(step, place)
        if step == min(1, half - 3):
            for way in range(2):
                rate_hop(way, 1).wait_send()
                for group in range(len(groups)):
                    hop(way, 1, group).wait_send()
                pl.semaphore_signal(
                    free.at[way], inc=1, device_id=ways[1 - way], device_id_type=pl.DeviceIdType.MESH
                )
    for _ in work:
        pass
    for step in range(steps):
        for copy in fold_small(step):
            copy.wait_send()
    for out, arrivals in zip(small_outs, small_ins):
        out[...] = arrivals[2 * steps - 1]

    rows = width // 2
    finals, used = [], {}
    values = rate_piece(0)
    for way in range(2):
        rate_hop(way, half - 1).wait_recv()
        values = [value + rate_arrived[way, 0, c].astype(F32) for c, value in enumerate(values)]
    for c in range(2):
        rate_final[c] = values[c]
    rate_own = pltpu.make_async_copy(rate_final.at[core], rates_out.at[core], rate_sems.at[0])
    rate_far = send(rate_final.at[1 - core], rates_out.at[core], rate_sems.at[1], rate_sems.at[2], peer)
    rate_own.start()
    rate_far.start()
    for group in [len(groups)] + list(range(len(groups))):
        slot = group % 2
        for copy in used.get(slot, ()):
            copy()
        if group == len(groups):
            value = []
            for left, right in late_parts:
                left = late_left if left is None else lefts[left]
                value.append(
                    lax.dot_general(
                        left[:, 0:width],
                        rights[right][...],
                        (COLS_ROWS, ((), ())),
                        preferred_element_type=F32,
                    )
                )
            value = jnp.concatenate(value, axis=1)
        else:
            value = piece(group, 0)
        for way in range(2):
            if group == len(groups):
                late[way].wait_recv()
                value = value + late_in[way].astype(F32)
            else:
                hop(way, half - 1, group).wait_recv()
                value = value + arrived[way, 0, :, columns(group)].astype(F32)
        final[slot, :, 0 : value.shape[1]] = value
        used[slot] = []
        for number, (owner, at, out, to, whole, size) in enumerate(fields):
            if owner == group:
                own = pl.ds(pl.multiple_of(core * rows, rows), rows)
                theirs = pl.ds(pl.multiple_of((1 - core) * rows, rows), rows)
                target = outs[out].at[:, pl.ds(pl.multiple_of(core * whole + to, 128), size)]
                copy = pltpu.make_async_copy(final.at[slot, own, pl.ds(at, size)], target, own_sem.at[number])
                far = send(
                    final.at[slot, theirs, pl.ds(at, size)],
                    target,
                    send_core.at[number],
                    recv_core.at[number],
                    peer,
                )
                copy.start()
                far.start()
                finals.append(far)
                used[slot] += [copy.wait, far.wait_send]
    for slot in used:
        for copy in used[slot]:
            copy()
    for far in finals:
        far.wait_recv()
    rate_own.wait()
    rate_far.wait()
    for way in range(2):
        for step in range(half):
            if step != 1:
                rate_hop(way, step).wait_send()
    for copy in first + second + late:
        copy.wait_send()
    for step in range(half):
        for group in range(len(groups)):
            for way in range(2):
                if step != 1:
                    hop(way, step, group).wait_send()


def collect(grid, lefts, rights, groups, late, fields, sides, ahead, tokens_in, small, small_shapes, rate_weights):
    chips = grid.chips
    rows, width = tokens_in[2].shape
    steps = grid.devices.bit_length()
    n = sum(rights[right].shape[1] for _, right in groups)
    widest = max([rights[right].shape[1] for _, right in groups] + [late[0].shape[2]])
    block = width // chips
    half = chips // 2
    *late, late_parts = late
    weights = [weight for weight, _, _ in sides]
    side_of = [(at, right) for _, at, right in sides]
    stream, gain, middle, grad_middle, mlp_grad = tokens_in
    tokens_in = [ahead.reshape(2, 2, rows, width), stream, middle, grad_middle]
    inputs = [*lefts, *rights, *late, *weights, *tokens_in, gain, mlp_grad, rate_weights, *small]
    wholes = {}
    for _, _, out, _, whole in fields:
        wholes[out] = whole
    outs = [jax.ShapeDtypeStruct((block // 2, 2 * wholes[out]), F32) for out in range(len(wholes))]
    ends = [sum(rights[right].shape[1] for _, right in late_parts)]
    ends = [rights[right].shape[1] for _, right in groups] + ends
    sized = []
    for i, (group, at, out, to, whole) in enumerate(fields):
        starts = [other[1] for other in fields if other[0] == group and other[1] > at]
        sized.append((group, at, out, to, whole, min(starts + [ends[group]]) - at))
    fields = sized
    tokens = jax.ShapeDtypeStruct((rows, width), F32)
    near = pl.BlockSpec(memory_space=pltpu.VMEM)
    far = pl.BlockSpec(memory_space=pltpu.HBM)
    dma = pltpu.SemaphoreType.DMA
    ring = (2, half, len(groups))
    counts = (len(lefts), len(rights), len(outs), len(sides))
    held = [value.shape for value in (*lefts, *rights)]
    rate = (rate_weights.shape[0], block // 2)
    rates = jax.ShapeDtypeStruct((2,) + rate, F32)
    return pl.pallas_call(
        partial(collect_kernel, chips, steps, groups, late_parts, fields, side_of, counts),
        out_shape=outs + [rates, tokens, tokens] + [jax.ShapeDtypeStruct(shape, F32) for shape in small_shapes],
        in_specs=[far] * (len(held) + 1) + [near] + [far] * (len(sides) + 4) + [near] * 8,
        out_specs=[far] * (len(outs) + 1) + [near] * 4,
        scratch_shapes=[
            pltpu.VMEM((2, block // 2, n), BF),
            pltpu.VMEM((2, half - 1, block, n), BF),
            pltpu.VMEM(late[0].shape, BF),
            pltpu.VMEM((2, block, widest), F32),
            pltpu.VMEM((2, 2, rows, width), BF),
            pltpu.VMEM((2, 2, rows, width), BF),
            pltpu.VMEM((2, rows, width), BF),
            pltpu.VMEM((2, rows, width), BF),
            *[pltpu.VMEM((2 * steps,) + shape, F32) for shape in small_shapes],
        ]
        + [pltpu.VMEM((2, block, rights[right].shape[1]), BF) for _, right in side_of]
        + [pltpu.VMEM(shape, BF) for shape in held]
        + [
            pltpu.VMEM((1, 2, rows, width), BF),
            pltpu.VMEM((rows, width), BF),
            pltpu.VMEM((rows, width), F32),
            pltpu.VMEM((rows, width), F32),
            dma((len(held) + 4,)),
        ]
        + [dma(ring), dma(ring)]
        + [dma((len(fields),))] * 3
        + [dma((2,))] * 6
        + [dma((steps, 2))] * 2
        + [dma((len(sides), 2)), pltpu.SemaphoreType.REGULAR((2,))]
        + [
            pltpu.VMEM((2,) + rate, BF),
            pltpu.VMEM((2, half - 1, 2) + rate, BF),
            pltpu.VMEM((2,) + rate, F32),
            dma((2, half)),
            dma((2, half)),
            dma((3,)),
        ],
        compiler_params=pltpu.CompilerParams(
            collective_id=3, has_side_effects=True, vmem_limit_bytes=63 << 20
        ),
        name="collect",
    )(*inputs)


def finish_kernel(chips, heads, counts, *refs):
    moved, turned = counts
    refs = list(refs)

    def take(count):
        taken, refs[:] = refs[:count], refs[count:]
        return taken

    sources, turning, (rates, gains, wide) = take(moved), take(turned), take(3)
    targets, turned_out = take(moved), take(turned)
    beta, decay, norm_gain, mlp_gain, cq, ck, cv, log, bias, out_gain = take(10)
    held = take(moved)
    sem_in, sem_out = take(2)
    ready = staged(sources, held, sem_in)
    copies = []
    for i, (source, target) in enumerate(zip(held, targets)):
        if len(target.shape) > len(source.shape):
            target = target.at[0]
        ready(i)
        copies.append(pltpu.make_async_copy(source, target, sem_out.at[i]))
        copies[-1].start()
    for source, target in zip(turning, turned_out):
        target[...] = source[...].T
    for core in range(2):
        to = slice(core * heads, (core + 1) * heads)
        beta[to] = rates[core, 0:heads]
        decay[to] = rates[core, heads : 2 * heads]
    lanes = min(norm_gain.shape[1] // chips, 128)
    count = norm_gain.shape[1] // lanes
    for i, vector in enumerate((norm_gain, mlp_gain)):
        for row in range(count):
            vector[:, row * lanes : (row + 1) * lanes] = gains[i * count + row : i * count + row + 1, 0:lanes]
    taps, keyw = cq.shape
    valw = cv.shape[1]
    after = max(2 * keyw, valw)
    cq[...] = wide[0:taps, 0:keyw]
    ck[...] = wide[0:taps, keyw : 2 * keyw]
    cv[...] = wide[taps : 2 * taps, 0:valw]
    out_gain[...] = wide[0:1, after : after + out_gain.shape[1]]
    after += out_gain.shape[1]
    small = (wide.shape[1] - after) // 4
    for quarter in range(4):
        at = after + quarter * small + heads
        to = slice(quarter * heads, (quarter + 1) * heads)
        log[:, to] = wide[0:1, at : at + heads]
        bias[:, to] = wide[1:2, at : at + heads]
    for copy in copies:
        copy.wait()


def finish(grid, heads, moved, turning, rates, gains, wide, vectors, convs):
    near = pl.BlockSpec(memory_space=pltpu.VMEM)
    far = pl.BlockSpec(memory_space=pltpu.HBM)
    out_shape = [jax.ShapeDtypeStruct(shape, F32) for _, shape in moved]
    out_shape += [jax.ShapeDtypeStruct(value.shape[::-1], F32) for value in turning]
    rate = jax.ShapeDtypeStruct((2 * heads, rates.shape[2]), F32)
    vectors = [jax.ShapeDtypeStruct((1, size), F32) for size in vectors]
    convs = [jax.ShapeDtypeStruct(value.shape, F32) for value in convs]
    small = [rate, rate, *vectors[:2], *convs, *vectors[2:]]
    return pl.pallas_call(
        partial(finish_kernel, grid.chips, heads, (len(moved), len(turning))),
        out_shape=out_shape + small,
        in_specs=[far] * len(moved) + [near] * (len(turning) + 3),
        out_specs=[far] * len(moved) + [near] * (len(turning) + len(small)),
        scratch_shapes=[pltpu.VMEM(value.shape, F32) for value, _ in moved]
        + [pltpu.SemaphoreType.DMA((len(moved),))] * 2,
        compiler_params=pltpu.CompilerParams(vmem_limit_bytes=63 << 20),
        name="finish",
    )(*[value for value, _ in moved], *turning, rates, gains, wide)


def whole_rows(stack):
    return stack.reshape(-1, stack.shape[-1])


def per_device(
    tokens,
    segment_ids,
    norm_gain,
    w_query,
    w_key,
    w_value,
    w_outgate,
    w_beta,
    w_decay,
    conv_query,
    conv_key,
    conv_value,
    decay_log,
    decay_bias,
    out_gain,
    w_output,
    mlp_gain,
    w_gate,
    w_up,
    w_down,
    cotangent,
    *,
    devices,
):
    grid = Grid(devices)
    heads = w_beta.shape[1] // 2
    keyw = w_query.shape[1] // 2
    valw = w_value.shape[1] // 2
    ffw = w_gate.shape[1] // 2
    small = -(-2 * heads // 128) * 128

    rate_rows = -(-2 * heads // 16) * 16
    groups = [[w_query, w_key], [w_value, w_outgate], [(w_output,)], rate_rows, [w_gate, w_up, (w_down,)]]
    shown = (tokens[0], cotangent[0], norm_gain[None], mlp_gain[None])
    if norm_gain.shape[0] // grid.chips % 128:
        shown = [grid.into(value) for value in shown]
    *gathered, stream, cot_own, norm_row, mlp_row, rows_mix, cot_rows = spread(
        grid, groups, 4, *shown[:2], shown[2:], (w_beta.T, w_decay.T)
    )
    wqk, wvg, wout = [whole_rows(stack) for stack in gathered[:3]]
    rows_mix, cot_rows = [rows.reshape(-1, rows.shape[-1]) for rows in (rows_mix, cot_rows)]
    segments = jnp.concatenate([segment_ids, grid.over_core(segment_ids)], axis=0)

    conv_parts = [
        part_of(conv_query, grid.quarter, keyw, 1),
        part_of(conv_key, grid.quarter, keyw, 1),
        part_of(conv_value, grid.quarter, valw, 1),
        part_of(decay_log, grid.quarter, heads, 0),
        part_of(decay_bias, grid.quarter, heads, 0),
    ]
    rate_weights = gathered[3].transpose(2, 0, 1, 3).reshape(rate_rows, -1)
    pre_qk = dot(rows_mix, wqk)
    pre_rates = jnp.pad(cols_product(rows_mix, rate_weights), ((0, 0), (0, small - rate_rows)))
    pre_vg = dot(rows_mix, wvg)
    lanes = [jnp.pad(part[None], ((0, 0), (0, small - heads))) for part in conv_parts[3:]]
    mixer_in = (pre_qk, pre_rates, pre_vg, segments[:, :, None], segments[:, None, :], *conv_parts[:3], *lanes, out_gain[None])
    heads_out, kept = mixer(heads, mixer_in)
    rows_mlp, middle = middle_rows(cols_product(heads_out, wout), stream, mlp_row)
    chunk = gathered[4]
    chunks = [chunk, grid.shift(chunk, 1), grid.shift(chunk, -1)]
    pair = tied((chunks[1], chunks[2]), heads_out)
    chunks += [grid.shift(pair[0], 1), grid.shift(pair[1], -1)]
    early = ffw * 1024 // 1408 // 128 * 128
    hidden, *gate_parts, grad_upper, back_part, ahead, begun = mlp(grid, rows_mlp, cot_rows, chunks, ffw, early)
    grad_mixed, grad_middle, grad_mlp_gain, late, grad_qk, grad_rates, grad_vg, *core_grads = turn(
        grid,
        heads,
        early,
        back_part,
        cot_own,
        middle,
        mlp_row,
        wout,
        cot_rows,
        rows_mlp,
        hidden,
        gate_parts[0],
        begun,
        mixer_in,
        kept,
    )

    width = norm_gain.shape[0]
    gain_rows = width // min(width // grid.chips, 128)
    wide = max(8 * keyw, 4 * valw) + out_gain.shape[0] + 4 * small
    *weight_grads, rates, out_tokens, grad_tokens, gains, wide = collect(
        grid,
        [rows_mlp, grad_mixed, rows_mix],
        [gate_parts[1], grad_upper, grad_vg, heads_out, grad_qk, hidden, gate_parts[0], grad_rates],
        [(0, 1), (2, 2), (1, 3), (2, 4), (0, 0)],
        [late, cot_rows[:, : cot_rows.shape[1] // grid.chips], [(None, 5), (0, 6)]],
        [
            (4, 0, 0, early, ffw),
            (5, ffw, 0, 0, ffw),
            (0, 0, 1, 0, ffw),
            (1, 0, 2, 0, valw),
            (1, valw, 3, 0, valw),
            (2, 0, 4, 0, valw),
            (3, 0, 5, 0, keyw),
            (3, keyw, 6, 0, keyw),
            (5, 0, 7, 0, ffw),
        ],
        [(wvg, 0, 2), (wqk, 0, 4)],
        ahead,
        [stream, norm_row, middle, grad_middle, grad_mlp_gain],
        core_grads,
        [(2 * gain_rows, 128), (2 * conv_query.shape[0], wide)],
        rate_weights,
    )
    whole_gate, whole_up, whole_value, whole_outgate, whole_out, whole_query, whole_key, whole_down = weight_grads
    if out_tokens.shape[1] // grid.chips % 128:
        out_tokens, grad_tokens = grid.out_of(out_tokens), grid.out_of(grad_tokens)
    moved = [out_tokens, grad_tokens, whole_query, whole_key, whole_value, whole_outgate, whole_gate, whole_up]
    shapes = [(1,) + value.shape if i < 2 else value.shape for i, value in enumerate(moved)]
    sizes = [width, width, decay_log.shape[0], decay_bias.shape[0], out_gain.shape[0]]
    *moved, whole_out, whole_down, whole_beta, whole_decay, norm_row, mlp_row, cq, ck, cv, log, bias, gain = finish(
        grid,
        heads,
        list(zip(moved, shapes)),
        [whole_out, whole_down],
        rates,
        gains,
        wide,
        sizes,
        [conv_query, conv_key, conv_value],
    )
    out_tokens, grad_tokens, *moved = moved
    whole_query, whole_key, whole_value, whole_outgate, whole_gate, whole_up = moved
    return (
        out_tokens,
        grad_tokens,
        norm_row[0],
        whole_query,
        whole_key,
        whole_value,
        whole_outgate,
        whole_beta.T,
        whole_decay.T,
        cq,
        ck,
        cv,
        log[0],
        bias[0],
        gain[0],
        whole_out,
        mlp_row[0],
        whole_gate,
        whole_up,
        whole_down,
    )


def solution(mesh):
    rows = P("dp", "tensor")
    cols = P("tensor", "dp")
    tokens = P("dp", "tensor", None)
    placed = (tokens, P("dp", None), P()) + (rows,) * 6 + (P(),) * 6
    placed = placed + (cols, P(), rows, rows, cols, tokens)
    given = (tokens, tokens, P()) + (rows,) * 6 + (P(),) * 6 + (cols, P(), rows, rows, cols)
    return jax.shard_map(
        partial(per_device, devices=mesh.shape["dp"]),
        mesh=mesh,
        in_specs=placed,
        out_specs=given,
        check_vma=False,
    )
```
